128 devices in a mesh: row: 16 (over y, z), col: 8 (over x, core).
Axes of the slice: x: 4, y: 4, z: 4, core: 2. Of those that a mesh axis runs over, the one named last changes fastest.
Arguments:
- blocks: bfloat16 [16, 8, 128, 4096], P('row', 'col'), may hold values from -0.25 to 0.25
- block_row: int32 [16, 8, 128], P('row', 'col'), may hold values from 0 to 15
- block_col: int32 [16, 8, 128], P('row', 'col'), may hold values from 0 to 31
- counts: int32 [16, 8], P('row', 'col'), may hold values from 0 to 128, as said below
- vectors: float32 [256, 4096], P(('col', 'row')), may hold values from -6 to 6
- row_mass: float32 [256, 64], P(('row', 'col')), may hold values from 0.25 to 4
- col_mass: float32 [256, 64], P(('col', 'row')), may hold values from 0.25 to 4
Outputs:
- subspace: float32 [256, 4096], P(('col', 'row'))
The draws below stay inside these ranges and needn't reach their ends.
Inputs may be any that keep to these rules, and one draw needn't show every extreme that they name: `counts`: in every row panel one tile uses all 128 slots; every other tile uses at most 8.
All inputs are finite; a program needn't handle non-finite values.
Results may differ from the reference program's by a relative error of at most 0.0085.
Values may be sent and summed in bfloat16 or wider, within the bound.
A program may use at most 64 MiB of HBM per device.

```python
import math
import jax
import jax.numpy as jnp
from jax import lax

BS = 64
K = 64
ITERS = 4
BAND = 16
BLK_DEV = 2
NB_CAP = 128
NB = 256
N_ROW = 16
N_COL = 8


def sparse_layout(key):
    rblk = BLK_DEV * N_COL
    cblk = BLK_DEV * N_ROW
    tile_r = jnp.arange(N_ROW, dtype=jnp.int32)[:, None]
    tile_c = jnp.arange(N_COL, dtype=jnp.int32)[None, :]
    home_col = (tile_r * rblk + rblk // 2) // cblk
    is_home = tile_c == home_col
    shape = (N_ROW, N_COL, NB_CAP)
    rows = jax.random.randint(jax.random.fold_in(key, 11), shape, 0, rblk).astype(jnp.int32)
    global_row = tile_r[:, :, None] * rblk + rows
    offset = jax.random.randint(jax.random.fold_in(key, 12), shape, -BAND, BAND + 1).astype(jnp.int32)
    near = jnp.clip(global_row + offset - tile_c[:, :, None] * cblk, 0, cblk - 1)
    far = jax.random.randint(jax.random.fold_in(key, 13), shape, 0, cblk).astype(jnp.int32)
    cols = jnp.where(is_home[:, :, None], near, far).astype(jnp.int32)
    sparse = jax.random.randint(jax.random.fold_in(key, 14), (N_ROW, N_COL), 0, NB_CAP // 16 + 1)
    filled = jnp.where(is_home, NB_CAP, sparse).astype(jnp.int32)
    return (rows, cols, filled)


def draw_block_row(key, part):
    return sparse_layout(key)[0]


def draw_block_col(key, part):
    return sparse_layout(key)[1]


def draw_counts(key, part):
    return sparse_layout(key)[2]


def block_scale(key, extent, shards, least, largest):
    loudness, own = 1.0, jax.random.fold_in(key, 6)
    for dim, blocks in shards:
        draws = jnp.exp(jax.random.uniform(jax.random.fold_in(own, dim), (blocks,), jnp.float32, least / len(shards), largest / len(shards)))
        loudness = loudness * jnp.repeat(draws, extent[dim] // blocks).reshape([-1 if axis == dim else 1 for axis in range(len(extent))])
    return loudness


def scatter_about(rng, dims, width, bound, shards=(), kind=jnp.bfloat16):
    loudness = block_scale(rng, dims, shards, -0.22, 0.18) if shards else 1.0
    result = jax.random.normal(rng, dims, jnp.float32) * width * loudness
    return jnp.minimum(jnp.maximum(result, -bound), bound).astype(kind)


def setup_inputs(seed: int = 0) -> dict:
    arg_keys = jax.random.split(jax.random.key(seed), 8)
    blocks = scatter_about(arg_keys[0], (N_ROW, N_COL, NB_CAP, BS * BS), (8 * BS) ** -0.5, 0.25, ((0, 16), (1, 8)))
    block_row = draw_block_row(jax.random.fold_in(arg_keys[7], 71), 0)
    block_col = draw_block_col(jax.random.fold_in(arg_keys[7], 71), 0)
    counts = draw_counts(jax.random.fold_in(arg_keys[7], 71), 0)
    vectors = scatter_about(arg_keys[4], (NB, K * BS), 1.0, 6.0, ((0, 128),), jnp.float32)
    row_mass = jnp.clip(jnp.exp(math.log(4.0) - 2.7725887 * jax.random.uniform(arg_keys[5], (NB, BS), jnp.float32) ** block_scale(arg_keys[5], (NB, BS), ((0, 128),), -0.2, 0.2)), 0.25, 4.0)
    col_mass = jnp.clip(jnp.exp(math.log(4.0) - 2.7725887 * jax.random.uniform(arg_keys[6], (NB, BS), jnp.float32) ** block_scale(arg_keys[6], (NB, BS), ((0, 128),), -0.2, 0.2)), 0.25, 4.0)
    return dict(blocks=blocks, block_row=block_row, block_col=block_col, counts=counts, vectors=vectors, row_mass=row_mass, col_mass=col_mass)


def reference(blocks, block_row, block_col, counts, vectors, row_mass, col_mass):
    rblk = BLK_DEV * N_COL
    cblk = BLK_DEV * N_ROW
    nblk = BLK_DEV * N_ROW * N_COL
    ntile = N_ROW * N_COL
    tiles = blocks.reshape(ntile, NB_CAP, BS, BS)
    rows_all = block_row.reshape(ntile, NB_CAP)
    cols_all = block_col.reshape(ntile, NB_CAP)
    live = jnp.arange(NB_CAP)[None, :] < counts.reshape(-1)[:, None]
    fwd_ids = jnp.where(live, rows_all, rblk).astype(jnp.int32)
    bwd_ids = jnp.where(live, cols_all, cblk).astype(jnp.int32)
    tile_row = (jnp.arange(ntile) // N_COL).astype(jnp.int32)
    tile_col = (jnp.arange(ntile) % N_COL).astype(jnp.int32)
    inv_col = 1.0 / jnp.sqrt(col_mass)
    current = vectors.reshape(nblk, K, BS)
    for step in range(ITERS):
        scaled = (current * inv_col[:, None, :]).astype(jnp.bfloat16)

        def fstep(carry, item):
            tile, cols, ids, rpos, cpos = item
            panel = lax.dynamic_slice_in_dim(scaled, (cpos * cblk).astype(jnp.int32), cblk, 0)
            taken = jnp.take(panel, cols, axis=0).astype(jnp.float32)
            prod = jnp.einsum('bij,bkj->bki', tile.astype(jnp.float32), taken)
            seg = jax.ops.segment_sum(prod, ids, num_segments=rblk + 1)[:rblk]
            start = (rpos * rblk).astype(jnp.int32)
            old = lax.dynamic_slice_in_dim(carry, start, rblk, 0)
            return (lax.dynamic_update_slice_in_dim(carry, old + seg, start, 0), None)
        rows_sum, unused = lax.scan(fstep, jnp.zeros((nblk, K, BS), jnp.float32), (tiles, cols_all, fwd_ids, tile_row, tile_col))
        weighted = (rows_sum * row_mass[:, None, :]).astype(jnp.bfloat16)

        def bstep(carry, item):
            tile, rows, ids, rpos, cpos = item
            panel = lax.dynamic_slice_in_dim(weighted, (rpos * rblk).astype(jnp.int32), rblk, 0)
            taken = jnp.take(panel, rows, axis=0).astype(jnp.float32)
            prod = jnp.einsum('bij,bki->bkj', tile.astype(jnp.float32), taken)
            seg = jax.ops.segment_sum(prod, ids, num_segments=cblk + 1)[:cblk]
            start = (cpos * cblk).astype(jnp.int32)
            old = lax.dynamic_slice_in_dim(carry, start, cblk, 0)
            return (lax.dynamic_update_slice_in_dim(carry, old + seg, start, 0), None)
        cols_sum, unused = lax.scan(bstep, jnp.zeros((nblk, K, BS), jnp.float32), (tiles, rows_all, bwd_ids, tile_row, tile_col))
        projected = cols_sum * inv_col[:, None, :]
        gram = jnp.einsum('bki,bli->kl', projected, projected, precision=lax.Precision.HIGHEST) / (nblk * BS)
        lower = jnp.linalg.cholesky(gram)
        inverse = lax.linalg.triangular_solve(lower, jnp.eye(K, dtype=jnp.float32), left_side=True, lower=True)
        current = jnp.einsum('kl,bli->bki', inverse, projected, precision=lax.Precision.HIGHEST)
    return current.reshape(nblk, K * BS)
```

```python
import jax
import jax.numpy as jnp
from jax import lax
from jax.sharding import PartitionSpec as P

ITERS = 4


def rotate(projected, gram):
    lower = jnp.linalg.cholesky(gram)
    inverse = lax.linalg.triangular_solve(
        lower, jnp.eye(gram.shape[0], dtype=jnp.float32), left_side=True, lower=True
    )
    return jnp.einsum(
        "kl,bli->bki",
        inverse,
        projected,
        precision=lax.Precision.HIGHEST,
        preferred_element_type=jnp.float32,
    )


def local_gram(projected):
    return jnp.einsum(
        "bki,bli->kl",
        projected,
        projected,
        precision=lax.Precision.HIGHEST,
        preferred_element_type=jnp.float32,
    )


def per_device(blocks, block_row, block_col, counts, vectors, row_mass, col_mass):
    tile = blocks[0, 0]
    n_cap = tile.shape[0]
    bsize = row_mass.shape[1]
    vecs = vectors.shape[1] // bsize
    own = vectors.shape[0]
    n_row = lax.axis_size("row")
    n_col = lax.axis_size("col")
    row_panel = own * n_col
    col_panel = own * n_row
    total_boxes = float(own * bsize * n_row * n_col)
    rows_idx = block_row[0, 0]
    cols_idx = block_col[0, 0]
    live = jnp.arange(n_cap) < counts[0, 0]
    fwd_ids = jnp.where(live, rows_idx, row_panel)
    bwd_ids = jnp.where(live, cols_idx, col_panel)
    square = tile.reshape(n_cap, bsize, bsize)
    col_mass_panel = lax.all_gather(col_mass, "row", axis=0, tiled=True)
    row_mass_panel = lax.all_gather(row_mass, "col", axis=0, tiled=True)
    inv_col = 1.0 / jnp.sqrt(col_mass_panel)
    current = lax.all_gather(vectors, "row", axis=0, tiled=True).reshape(col_panel, vecs, bsize)
    for step in range(ITERS):
        scaled = (current * inv_col[:, None, :]).astype(jnp.bfloat16)
        forward_taken = jnp.take(scaled, cols_idx, axis=0)
        forward_product = jnp.einsum(
            "bij,bkj->bki", square, forward_taken, preferred_element_type=jnp.float32
        )
        forward_summed = jax.ops.segment_sum(forward_product, fwd_ids, num_segments=row_panel + 1)
        rows_sum = lax.psum(forward_summed[:row_panel], "col")
        weighted = (rows_sum * row_mass_panel[:, None, :]).astype(jnp.bfloat16)
        taken = jnp.take(weighted, rows_idx, axis=0)
        product = jnp.einsum("bij,bki->bkj", square, taken, preferred_element_type=jnp.float32)
        summed = jax.ops.segment_sum(product, bwd_ids, num_segments=col_panel + 1)
        cols_sum = lax.psum(summed[:col_panel], "row")
        projected = cols_sum * inv_col[:, None, :]
        gram = lax.psum(local_gram(projected), "col") / total_boxes
        current = rotate(projected, gram)
    me = lax.axis_index("row")
    mine = lax.dynamic_slice_in_dim(current, me * own, own, 0)
    return mine.reshape(own, vecs * bsize)


def solution(mesh):
    in_specs = (
        P("row", "col", None, None),
        P("row", "col", None),
        P("row", "col", None),
        P("row", "col"),
        P(("col", "row"), None),
        P(("row", "col"), None),
        P(("col", "row"), None),
    )
    out_specs = P(("col", "row"), None)
    return jax.shard_map(
        per_device, mesh=mesh, in_specs=in_specs, out_specs=out_specs, check_vma=False
    )
```

```python
import functools

import jax
import jax.numpy as jnp
from jax import lax
from jax.experimental import pallas as pl
from jax.experimental.pallas import tpu as pltpu
from jax.sharding import PartitionSpec as P

ITERS = 4
LANES = 512
MESH_ID = pl.DeviceIdType.MESH


def _peer(axis, other, p):
    them = lax.axis_index(other)
    return (p, them) if axis == "row" else (them, p)


def _reduce_kernel(axis, other, n, ch, two_phase, x_ref, o_ref, recv, mine, gath, s1, r1, s2, r2):
    me = lax.axis_index(axis)
    barrier = pltpu.get_barrier_semaphore()
    for d in range(1, n):
        pl.semaphore_signal(
            barrier, 1, device_id=_peer(axis, other, (me + d) % n), device_id_type=MESH_ID
        )
    pl.semaphore_wait(barrier, n - 1)
    if not two_phase:
        sends = []
        for d in range(1, n):
            c = pltpu.make_async_remote_copy(
                x_ref, recv.at[d], s1.at[d], r1.at[d],
                device_id=_peer(axis, other, (me + d) % n), device_id_type=MESH_ID,
            )
            c.start()
            sends.append(c)
        for c in sends:
            c.wait()
        recv[0] = x_ref[...]
        acc = recv[me % n]
        for p in range(1, n):
            acc = acc + recv[(me - p + n) % n]
        o_ref[...] = acc
        return
    sends = []
    for d in range(1, n):
        peer = (me + d) % n
        start = pl.multiple_of(peer * ch, ch)
        c = pltpu.make_async_remote_copy(
            x_ref.at[pl.ds(start, ch)], recv.at[d], s1.at[d], r1.at[d],
            device_id=_peer(axis, other, peer), device_id_type=MESH_ID,
        )
        c.start()
        sends.append(c)
    own = pl.multiple_of(me * ch, ch)
    acc = x_ref[pl.ds(own, ch), :]
    for d, c in enumerate(sends, 1):
        c.wait()
        acc = acc + recv[d]
    mine[...] = acc
    gathers = []
    for d in range(1, n):
        c = pltpu.make_async_remote_copy(
            mine, gath.at[d], s2.at[d], r2.at[d],
            device_id=_peer(axis, other, (me + d) % n), device_id_type=MESH_ID,
        )
        c.start()
        gathers.append(c)
    o_ref[pl.ds(own, ch), :] = acc
    for d, c in enumerate(gathers, 1):
        c.wait()
        src = pl.multiple_of(((me - d + n) % n) * ch, ch)
        o_ref[pl.ds(src, ch), :] = gath[d]


def _gather_kernel(axis, other, n, x_ref, o_ref, gath, s2, r2):
    me = lax.axis_index(axis)
    ch = x_ref.shape[0]
    barrier = pltpu.get_barrier_semaphore()
    for d in range(1, n):
        pl.semaphore_signal(
            barrier, 1, device_id=_peer(axis, other, (me + d) % n), device_id_type=MESH_ID
        )
    pl.semaphore_wait(barrier, n - 1)
    gathers = []
    for d in range(1, n):
        c = pltpu.make_async_remote_copy(
            x_ref, gath.at[d], s2.at[d], r2.at[d],
            device_id=_peer(axis, other, (me + d) % n), device_id_type=MESH_ID,
        )
        c.start()
        gathers.append(c)
    o_ref[pl.ds(pl.multiple_of(me * ch, ch), ch), :] = x_ref[...]
    for d, c in enumerate(gathers, 1):
        c.wait()
        src = pl.multiple_of(((me - d + n) % n) * ch, ch)
        o_ref[pl.ds(src, ch), :] = gath[d]


def all_gather(x, axis, other, n, collective_id):
    ch, lanes = x.shape
    return pl.pallas_call(
        functools.partial(_gather_kernel, axis, other, n),
        out_shape=jax.ShapeDtypeStruct((n * ch, lanes), x.dtype),
        in_specs=[pl.BlockSpec(memory_space=pltpu.VMEM)],
        out_specs=pl.BlockSpec(memory_space=pltpu.VMEM),
        scratch_shapes=[
            pltpu.VMEM((n, ch, lanes), x.dtype),
            pltpu.SemaphoreType.DMA((n,)),
            pltpu.SemaphoreType.DMA((n,)),
        ],
        compiler_params=pltpu.CompilerParams(collective_id=collective_id, has_side_effects=True),
    )(x)


def all_reduce(x, axis, other, n, collective_id, two_phase=True):
    rows, lanes = x.shape
    ch = rows // n if two_phase else rows
    slots = ch if two_phase else rows
    return pl.pallas_call(
        functools.partial(_reduce_kernel, axis, other, n, ch, two_phase),
        out_shape=jax.ShapeDtypeStruct(x.shape, x.dtype),
        in_specs=[pl.BlockSpec(memory_space=pltpu.VMEM)],
        out_specs=pl.BlockSpec(memory_space=pltpu.VMEM),
        scratch_shapes=[
            pltpu.VMEM((n, slots, lanes), x.dtype),
            pltpu.VMEM((ch, lanes), x.dtype),
            pltpu.VMEM((n, ch, lanes), x.dtype),
            pltpu.SemaphoreType.DMA((n,)),
            pltpu.SemaphoreType.DMA((n,)),
            pltpu.SemaphoreType.DMA((n,)),
            pltpu.SemaphoreType.DMA((n,)),
        ],
        compiler_params=pltpu.CompilerParams(collective_id=collective_id, has_side_effects=True),
    )(x)


def rotate(projected, gram):
    lower = jnp.linalg.cholesky(gram)
    inverse = lax.linalg.triangular_solve(
        lower, jnp.eye(gram.shape[0], dtype=jnp.float32), left_side=True, lower=True
    )
    return jnp.einsum(
        "kl,bli->bki",
        inverse,
        projected,
        precision=lax.Precision.HIGHEST,
        preferred_element_type=jnp.float32,
    )


def local_gram(projected):
    return jnp.einsum(
        "bki,bli->kl",
        projected,
        projected,
        precision=lax.Precision.HIGHEST,
        preferred_element_type=jnp.float32,
    )


def panel_sum(partial, axis, other, n, collective_id):
    blocks, vecs, bsize = partial.shape
    flat = partial.reshape(blocks * vecs * bsize // LANES, LANES)
    return all_reduce(flat, axis, other, n, collective_id).reshape(blocks, vecs, bsize)


def per_device(blocks, block_row, block_col, counts, vectors, row_mass, col_mass):
    tile = blocks[0, 0]
    n_cap = tile.shape[0]
    bsize = row_mass.shape[1]
    vecs = vectors.shape[1] // bsize
    own = vectors.shape[0]
    n_row = lax.axis_size("row")
    n_col = lax.axis_size("col")
    row_panel = own * n_col
    col_panel = own * n_row
    total_boxes = float(own * bsize * n_row * n_col)
    rows_idx = block_row[0, 0]
    cols_idx = block_col[0, 0]
    live = jnp.arange(n_cap) < counts[0, 0]
    fwd_ids = jnp.where(live, rows_idx, row_panel)
    bwd_ids = jnp.where(live, cols_idx, col_panel)
    square = tile.reshape(n_cap, bsize, bsize)
    vec_rows = own * vecs * bsize // LANES
    mass_pad = jnp.zeros((8, LANES), jnp.float32).at[0, : own * bsize].set(col_mass.reshape(-1))
    packed = jnp.concatenate([vectors.reshape(vec_rows, LANES), mass_pad], axis=0)
    got = all_gather(packed, "row", "col", n_row, 4).reshape(n_row, vec_rows + 8, LANES)
    current = got[:, :vec_rows].reshape(col_panel, vecs, bsize)
    col_mass_panel = got[:, vec_rows, : own * bsize].reshape(col_panel, bsize)
    row_pad = jnp.zeros((8, 128), jnp.float32).at[0, : own * bsize].set(row_mass.reshape(-1))
    row_got = all_gather(row_pad, "col", "row", n_col, 5).reshape(n_col, 8, 128)
    row_mass_panel = row_got[:, 0, : own * bsize].reshape(row_panel, bsize)
    inv_col = 1.0 / jnp.sqrt(col_mass_panel)
    fwd_hot = (fwd_ids[None, :] == jnp.arange(row_panel)[:, None]).astype(jnp.float32)
    bwd_hot = (bwd_ids[None, :] == jnp.arange(col_panel)[:, None]).astype(jnp.float32)
    for step in range(ITERS):
        scaled = (current * inv_col[:, None, :]).astype(jnp.bfloat16)
        forward_taken = jnp.take(scaled, cols_idx, axis=0)
        forward_product = jnp.einsum(
            "bij,bkj->bki", square, forward_taken, preferred_element_type=jnp.float32
        )
        forward_summed = jnp.einsum(
            "rs,ski->rki", fwd_hot, forward_product, precision=lax.Precision.HIGHEST,
            preferred_element_type=jnp.float32,
        )
        rows_sum = panel_sum(forward_summed, "col", "row", n_col, 1)
        weighted = (rows_sum * row_mass_panel[:, None, :]).astype(jnp.bfloat16)
        taken = jnp.take(weighted, rows_idx, axis=0)
        product = jnp.einsum("bij,bki->bkj", square, taken, preferred_element_type=jnp.float32)
        summed = jnp.einsum(
            "cs,skj->ckj", bwd_hot, product, precision=lax.Precision.HIGHEST,
            preferred_element_type=jnp.float32,
        )
        cols_sum = panel_sum(summed, "row", "col", n_row, 2)
        projected = cols_sum * inv_col[:, None, :]
        partial_gram = local_gram(projected)
        gram = all_reduce(partial_gram, "col", "row", n_col, 3, two_phase=False) / total_boxes
        current = rotate(projected, gram)
    me = lax.axis_index("row")
    mine = lax.dynamic_slice_in_dim(current, me * own, own, 0)
    return mine.reshape(own, vecs * bsize)


def solution(mesh):
    in_specs = (
        P("row", "col", None, None),
        P("row", "col", None),
        P("row", "col", None),
        P("row", "col"),
        P(("col", "row"), None),
        P(("row", "col"), None),
        P(("col", "row"), None),
    )
    out_specs = P(("col", "row"), None)
    return jax.shard_map(
        per_device, mesh=mesh, in_specs=in_specs, out_specs=out_specs, check_vma=False
    )
```

```python
import functools

import jax
import jax.numpy as jnp
from jax import lax
from jax.experimental import pallas as pl
from jax.experimental.pallas import tpu as pltpu
from jax.sharding import PartitionSpec as P

ITERS = 4
LANES = 512
MESH_ID = pl.DeviceIdType.MESH


def _peer(axis, other, p):
    them = lax.axis_index(other)
    return (p, them) if axis == "row" else (them, p)


def _reduce_kernel(axis, other, n, ch, two_phase, x_ref, o_ref, recv, mine, gath, s1, r1, s2, r2):
    me = lax.axis_index(axis)
    barrier = pltpu.get_barrier_semaphore()
    for d in range(1, n):
        pl.semaphore_signal(
            barrier, 1, device_id=_peer(axis, other, (me + d) % n), device_id_type=MESH_ID
        )
    pl.semaphore_wait(barrier, n - 1)
    if not two_phase:
        sends = []
        for d in range(1, n):
            c = pltpu.make_async_remote_copy(
                x_ref, recv.at[d], s1.at[d], r1.at[d],
                device_id=_peer(axis, other, (me + d) % n), device_id_type=MESH_ID,
            )
            c.start()
            sends.append(c)
        for c in sends:
            c.wait()
        recv[0] = x_ref[...]
        acc = recv[me % n]
        for p in range(1, n):
            acc = acc + recv[(me - p + n) % n]
        o_ref[...] = acc
        return
    sends = []
    for d in range(1, n):
        peer = (me + d) % n
        start = pl.multiple_of(peer * ch, ch)
        c = pltpu.make_async_remote_copy(
            x_ref.at[pl.ds(start, ch)], recv.at[d], s1.at[d], r1.at[d],
            device_id=_peer(axis, other, peer), device_id_type=MESH_ID,
        )
        c.start()
        sends.append(c)
    own = pl.multiple_of(me * ch, ch)
    acc = x_ref[pl.ds(own, ch), :]
    for d, c in enumerate(sends, 1):
        c.wait()
        acc = acc + recv[d]
    mine[...] = acc
    gathers = []
    for d in range(1, n):
        c = pltpu.make_async_remote_copy(
            mine, gath.at[d], s2.at[d], r2.at[d],
            device_id=_peer(axis, other, (me + d) % n), device_id_type=MESH_ID,
        )
        c.start()
        gathers.append(c)
    o_ref[pl.ds(own, ch), :] = acc
    for d, c in enumerate(gathers, 1):
        c.wait()
        src = pl.multiple_of(((me - d + n) % n) * ch, ch)
        o_ref[pl.ds(src, ch), :] = gath[d]


def _gather_kernel(axis, other, n, x_ref, o_ref, gath, s2, r2):
    me = lax.axis_index(axis)
    ch = x_ref.shape[0]
    barrier = pltpu.get_barrier_semaphore()
    for d in range(1, n):
        pl.semaphore_signal(
            barrier, 1, device_id=_peer(axis, other, (me + d) % n), device_id_type=MESH_ID
        )
    pl.semaphore_wait(barrier, n - 1)
    gathers = []
    for d in range(1, n):
        c = pltpu.make_async_remote_copy(
            x_ref, gath.at[d], s2.at[d], r2.at[d],
            device_id=_peer(axis, other, (me + d) % n), device_id_type=MESH_ID,
        )
        c.start()
        gathers.append(c)
    o_ref[pl.ds(pl.multiple_of(me * ch, ch), ch), :] = x_ref[...]
    for d, c in enumerate(gathers, 1):
        c.wait()
        src = pl.multiple_of(((me - d + n) % n) * ch, ch)
        o_ref[pl.ds(src, ch), :] = gath[d]


def all_gather(x, axis, other, n, collective_id):
    ch, lanes = x.shape
    return pl.pallas_call(
        functools.partial(_gather_kernel, axis, other, n),
        out_shape=jax.ShapeDtypeStruct((n * ch, lanes), x.dtype),
        in_specs=[pl.BlockSpec(memory_space=pltpu.VMEM)],
        out_specs=pl.BlockSpec(memory_space=pltpu.VMEM),
        scratch_shapes=[
            pltpu.VMEM((n, ch, lanes), x.dtype),
            pltpu.SemaphoreType.DMA((n,)),
            pltpu.SemaphoreType.DMA((n,)),
        ],
        compiler_params=pltpu.CompilerParams(collective_id=collective_id, has_side_effects=True),
    )(x)


def all_reduce(x, axis, other, n, collective_id, two_phase=True):
    rows, lanes = x.shape
    ch = rows // n if two_phase else rows
    slots = ch if two_phase else rows
    return pl.pallas_call(
        functools.partial(_reduce_kernel, axis, other, n, ch, two_phase),
        out_shape=jax.ShapeDtypeStruct(x.shape, x.dtype),
        in_specs=[pl.BlockSpec(memory_space=pltpu.VMEM)],
        out_specs=pl.BlockSpec(memory_space=pltpu.VMEM),
        scratch_shapes=[
            pltpu.VMEM((n, slots, lanes), x.dtype),
            pltpu.VMEM((ch, lanes), x.dtype),
            pltpu.VMEM((n, ch, lanes), x.dtype),
            pltpu.SemaphoreType.DMA((n,)),
            pltpu.SemaphoreType.DMA((n,)),
            pltpu.SemaphoreType.DMA((n,)),
            pltpu.SemaphoreType.DMA((n,)),
        ],
        compiler_params=pltpu.CompilerParams(collective_id=collective_id, has_side_effects=True),
    )(x)


def rotate(projected, gram):
    lower = jnp.linalg.cholesky(gram)
    inverse = lax.linalg.triangular_solve(
        lower, jnp.eye(gram.shape[0], dtype=jnp.float32), left_side=True, lower=True
    )
    return jnp.einsum(
        "kl,bli->bki",
        inverse,
        projected,
        precision=lax.Precision.HIGHEST,
        preferred_element_type=jnp.float32,
    )


def local_gram(projected):
    return jnp.einsum(
        "bki,bli->kl",
        projected,
        projected,
        precision=lax.Precision.HIGHEST,
        preferred_element_type=jnp.float32,
    )


def panel_sum(partial, axis, other, n, collective_id):
    blocks, vecs, bsize = partial.shape
    flat = partial.reshape(blocks * vecs * bsize // LANES, LANES)
    return all_reduce(flat, axis, other, n, collective_id).reshape(blocks, vecs, bsize)


def per_device(blocks, block_row, block_col, counts, vectors, row_mass, col_mass):
    tile = blocks[0, 0]
    n_cap = tile.shape[0]
    bsize = row_mass.shape[1]
    vecs = vectors.shape[1] // bsize
    own = vectors.shape[0]
    n_row = lax.axis_size("row")
    n_col = lax.axis_size("col")
    row_panel = own * n_col
    col_panel = own * n_row
    total_boxes = float(own * bsize * n_row * n_col)
    rows_idx = block_row[0, 0]
    cols_idx = block_col[0, 0]
    live = jnp.arange(n_cap) < counts[0, 0]
    vec_rows = own * vecs * bsize // LANES
    mass_pad = jnp.zeros((8, LANES), jnp.float32).at[0, : own * bsize].set(col_mass.reshape(-1))
    packed = jnp.concatenate([vectors.reshape(vec_rows, LANES), mass_pad], axis=0)
    got = all_gather(packed, "row", "col", n_row, 4).reshape(n_row, vec_rows + 8, LANES)
    current = got[:, :vec_rows].reshape(col_panel, vecs, bsize)
    col_mass_panel = got[:, vec_rows, : own * bsize].reshape(col_panel, bsize)
    row_pad = jnp.zeros((8, 128), jnp.float32).at[0, : own * bsize].set(row_mass.reshape(-1))
    row_got = all_gather(row_pad, "col", "row", n_col, 5).reshape(n_col, 8, 128)
    row_mass_panel = row_got[:, 0, : own * bsize].reshape(row_panel, bsize)
    inv_col = 1.0 / jnp.sqrt(col_mass_panel)
    pair = jnp.where(live, rows_idx * col_panel + cols_idx, row_panel * col_panel)
    hot = (pair[None, :] == jnp.arange(row_panel * col_panel)[:, None]).astype(jnp.bfloat16)
    dense = jnp.dot(hot, tile, preferred_element_type=jnp.float32)
    dense_hi = dense.astype(jnp.bfloat16)
    dense_lo = (dense - dense_hi.astype(jnp.float32)).astype(jnp.bfloat16)
    dense_hi = dense_hi.reshape(row_panel, col_panel, bsize, bsize)
    dense_lo = dense_lo.reshape(row_panel, col_panel, bsize, bsize)
    for step in range(ITERS):
        scaled = (current * inv_col[:, None, :]).astype(jnp.bfloat16)
        forward_summed = jnp.einsum(
            "ckj,rcij->rki", scaled, dense_hi, preferred_element_type=jnp.float32
        ) + jnp.einsum("ckj,rcij->rki", scaled, dense_lo, preferred_element_type=jnp.float32)
        rows_sum = panel_sum(forward_summed, "col", "row", n_col, 1)
        weighted = (rows_sum * row_mass_panel[:, None, :]).astype(jnp.bfloat16)
        summed = jnp.einsum(
            "rki,rcij->ckj", weighted, dense_hi, preferred_element_type=jnp.float32
        ) + jnp.einsum("rki,rcij->ckj", weighted, dense_lo, preferred_element_type=jnp.float32)
        cols_sum = panel_sum(summed, "row", "col", n_row, 2)
        projected = cols_sum * inv_col[:, None, :]
        partial_gram = local_gram(projected)
        gram = all_reduce(partial_gram, "col", "row", n_col, 3, two_phase=False) / total_boxes
        current = rotate(projected, gram)
    me = lax.axis_index("row")
    mine = lax.dynamic_slice_in_dim(current, me * own, own, 0)
    return mine.reshape(own, vecs * bsize)


def solution(mesh):
    in_specs = (
        P("row", "col", None, None),
        P("row", "col", None),
        P("row", "col", None),
        P("row", "col"),
        P(("col", "row"), None),
        P(("row", "col"), None),
        P(("col", "row"), None),
    )
    out_specs = P(("col", "row"), None)
    return jax.shard_map(
        per_device, mesh=mesh, in_specs=in_specs, out_specs=out_specs, check_vma=False
    )
```

```python
import functools

import jax
import jax.numpy as jnp
from jax import lax
from jax.experimental import pallas as pl
from jax.experimental.pallas import tpu as pltpu
from jax.sharding import PartitionSpec as P

ITERS = 4
LANES = 512
MESH_ID = pl.DeviceIdType.MESH


def _peer(axis, other, p):
    them = lax.axis_index(other)
    return (p, them) if axis == "row" else (them, p)


def _reduce_kernel(axis, other, n, ch, two_phase, x_ref, o_ref, recv, mine, gath, s1, r1, s2, r2):
    me = lax.axis_index(axis)
    barrier = pltpu.get_barrier_semaphore()
    for d in range(1, n):
        pl.semaphore_signal(
            barrier, 1, device_id=_peer(axis, other, (me + d) % n), device_id_type=MESH_ID
        )
    pl.semaphore_wait(barrier, n - 1)
    if not two_phase:
        sends = []
        for d in range(1, n):
            c = pltpu.make_async_remote_copy(
                x_ref, recv.at[d], s1.at[d], r1.at[d],
                device_id=_peer(axis, other, (me + d) % n), device_id_type=MESH_ID,
            )
            c.start()
            sends.append(c)
        for c in sends:
            c.wait()
        recv[0] = x_ref[...]
        acc = recv[me % n]
        for p in range(1, n):
            acc = acc + recv[(me - p + n) % n]
        o_ref[...] = acc
        return
    sends = []
    for d in range(1, n):
        peer = (me + d) % n
        start = pl.multiple_of(peer * ch, ch)
        c = pltpu.make_async_remote_copy(
            x_ref.at[pl.ds(start, ch)], recv.at[d], s1.at[d], r1.at[d],
            device_id=_peer(axis, other, peer), device_id_type=MESH_ID,
        )
        c.start()
        sends.append(c)
    own = pl.multiple_of(me * ch, ch)
    acc = x_ref[pl.ds(own, ch), :]
    for d, c in enumerate(sends, 1):
        c.wait()
        acc = acc + recv[d]
    mine[...] = acc
    gathers = []
    for d in range(1, n):
        c = pltpu.make_async_remote_copy(
            mine, gath.at[d], s2.at[d], r2.at[d],
            device_id=_peer(axis, other, (me + d) % n), device_id_type=MESH_ID,
        )
        c.start()
        gathers.append(c)
    o_ref[pl.ds(own, ch), :] = acc
    for d, c in enumerate(gathers, 1):
        c.wait()
        src = pl.multiple_of(((me - d + n) % n) * ch, ch)
        o_ref[pl.ds(src, ch), :] = gath[d]


def _gather_kernel(axis, other, n, x_ref, o_ref, gath, s2, r2):
    me = lax.axis_index(axis)
    ch = x_ref.shape[0]
    barrier = pltpu.get_barrier_semaphore()
    for d in range(1, n):
        pl.semaphore_signal(
            barrier, 1, device_id=_peer(axis, other, (me + d) % n), device_id_type=MESH_ID
        )
    pl.semaphore_wait(barrier, n - 1)
    gathers = []
    for d in range(1, n):
        c = pltpu.make_async_remote_copy(
            x_ref, gath.at[d], s2.at[d], r2.at[d],
            device_id=_peer(axis, other, (me + d) % n), device_id_type=MESH_ID,
        )
        c.start()
        gathers.append(c)
    o_ref[pl.ds(pl.multiple_of(me * ch, ch), ch), :] = x_ref[...]
    for d, c in enumerate(gathers, 1):
        c.wait()
        src = pl.multiple_of(((me - d + n) % n) * ch, ch)
        o_ref[pl.ds(src, ch), :] = gath[d]


def all_gather(x, axis, other, n, collective_id):
    ch, lanes = x.shape
    return pl.pallas_call(
        functools.partial(_gather_kernel, axis, other, n),
        out_shape=jax.ShapeDtypeStruct((n * ch, lanes), x.dtype),
        in_specs=[pl.BlockSpec(memory_space=pltpu.VMEM)],
        out_specs=pl.BlockSpec(memory_space=pltpu.VMEM),
        scratch_shapes=[
            pltpu.VMEM((n, ch, lanes), x.dtype),
            pltpu.SemaphoreType.DMA((n,)),
            pltpu.SemaphoreType.DMA((n,)),
        ],
        compiler_params=pltpu.CompilerParams(collective_id=collective_id, has_side_effects=True),
    )(x)


def _forward_kernel(n, ch, x_ref, mass_ref, o_ref, recv, mine, gath, s1, r1, s2, r2):
    axis, other = "col", "row"
    me = lax.axis_index(axis)
    barrier = pltpu.get_barrier_semaphore()
    for d in range(1, n):
        pl.semaphore_signal(
            barrier, 1, device_id=_peer(axis, other, (me + d) % n), device_id_type=MESH_ID
        )
    pl.semaphore_wait(barrier, n - 1)
    sends = []
    for d in range(1, n):
        peer = (me + d) % n
        start = pl.multiple_of(peer * ch, ch)
        c = pltpu.make_async_remote_copy(
            x_ref.at[pl.ds(start, ch)], recv.at[d], s1.at[d], r1.at[d],
            device_id=_peer(axis, other, peer), device_id_type=MESH_ID,
        )
        c.start()
        sends.append(c)
    own = pl.multiple_of(me * ch, ch)
    acc = x_ref[pl.ds(own, ch), :]
    for d, c in enumerate(sends, 1):
        c.wait()
        acc = acc + recv[d]
    mine[...] = (acc * mass_ref[...]).astype(mine.dtype)
    gathers = []
    for d in range(1, n):
        c = pltpu.make_async_remote_copy(
            mine, gath.at[d], s2.at[d], r2.at[d],
            device_id=_peer(axis, other, (me + d) % n), device_id_type=MESH_ID,
        )
        c.start()
        gathers.append(c)
    o_ref[pl.ds(own, ch), :] = mine[...]
    for d, c in enumerate(gathers, 1):
        c.wait()
        src = pl.multiple_of(((me - d + n) % n) * ch, ch)
        o_ref[pl.ds(src, ch), :] = gath[d]


def forward_reduce(x, mass, n, collective_id):
    rows, lanes = x.shape
    ch = rows // n
    return pl.pallas_call(
        functools.partial(_forward_kernel, n, ch),
        out_shape=jax.ShapeDtypeStruct(x.shape, jnp.bfloat16),
        in_specs=[pl.BlockSpec(memory_space=pltpu.VMEM)] * 2,
        out_specs=pl.BlockSpec(memory_space=pltpu.VMEM),
        scratch_shapes=[
            pltpu.VMEM((n, ch, lanes), x.dtype),
            pltpu.VMEM((ch, lanes), jnp.bfloat16),
            pltpu.VMEM((n, ch, lanes), jnp.bfloat16),
            pltpu.SemaphoreType.DMA((n,)),
            pltpu.SemaphoreType.DMA((n,)),
            pltpu.SemaphoreType.DMA((n,)),
            pltpu.SemaphoreType.DMA((n,)),
        ],
        compiler_params=pltpu.CompilerParams(collective_id=collective_id, has_side_effects=True),
    )(x, mass)


def _gather2_kernel(axis, other, n, x_ref, y_ref, o_ref, p_ref, gx, gy, sx, rx, sy, ry):
    me = lax.axis_index(axis)
    cx = x_ref.shape[0]
    cy = y_ref.shape[0]
    barrier = pltpu.get_barrier_semaphore()
    for d in range(1, n):
        pl.semaphore_signal(
            barrier, 1, device_id=_peer(axis, other, (me + d) % n), device_id_type=MESH_ID
        )
    pl.semaphore_wait(barrier, n - 1)
    copies = []
    for d in range(1, n):
        peer = _peer(axis, other, (me + d) % n)
        a = pltpu.make_async_remote_copy(
            x_ref, gx.at[d], sx.at[d], rx.at[d], device_id=peer, device_id_type=MESH_ID
        )
        b = pltpu.make_async_remote_copy(
            y_ref, gy.at[d], sy.at[d], ry.at[d], device_id=peer, device_id_type=MESH_ID
        )
        a.start()
        b.start()
        copies.append((a, b))
    o_ref[pl.ds(pl.multiple_of(me * cx, cx), cx), :] = x_ref[...]
    p_ref[pl.ds(pl.multiple_of(me * cy, cy), cy), :] = y_ref[...]
    for d, (a, b) in enumerate(copies, 1):
        a.wait()
        b.wait()
        src = (me - d + n) % n
        o_ref[pl.ds(pl.multiple_of(src * cx, cx), cx), :] = gx[d]
        p_ref[pl.ds(pl.multiple_of(src * cy, cy), cy), :] = gy[d]


def all_gather2(x, y, axis, other, n, collective_id):
    return pl.pallas_call(
        functools.partial(_gather2_kernel, axis, other, n),
        out_shape=(
            jax.ShapeDtypeStruct((n * x.shape[0], x.shape[1]), x.dtype),
            jax.ShapeDtypeStruct((n * y.shape[0], y.shape[1]), y.dtype),
        ),
        in_specs=[pl.BlockSpec(memory_space=pltpu.VMEM)] * 2,
        out_specs=(pl.BlockSpec(memory_space=pltpu.VMEM),) * 2,
        scratch_shapes=[
            pltpu.VMEM((n,) + x.shape, x.dtype),
            pltpu.VMEM((n,) + y.shape, y.dtype),
            pltpu.SemaphoreType.DMA((n,)),
            pltpu.SemaphoreType.DMA((n,)),
            pltpu.SemaphoreType.DMA((n,)),
            pltpu.SemaphoreType.DMA((n,)),
        ],
        compiler_params=pltpu.CompilerParams(collective_id=collective_id, has_side_effects=True),
    )(x, y)


def all_reduce(x, axis, other, n, collective_id, two_phase=True):
    rows, lanes = x.shape
    ch = rows // n if two_phase else rows
    slots = ch if two_phase else rows
    return pl.pallas_call(
        functools.partial(_reduce_kernel, axis, other, n, ch, two_phase),
        out_shape=jax.ShapeDtypeStruct(x.shape, x.dtype),
        in_specs=[pl.BlockSpec(memory_space=pltpu.VMEM)],
        out_specs=pl.BlockSpec(memory_space=pltpu.VMEM),
        scratch_shapes=[
            pltpu.VMEM((n, slots, lanes), x.dtype),
            pltpu.VMEM((ch, lanes), x.dtype),
            pltpu.VMEM((n, ch, lanes), x.dtype),
            pltpu.SemaphoreType.DMA((n,)),
            pltpu.SemaphoreType.DMA((n,)),
            pltpu.SemaphoreType.DMA((n,)),
            pltpu.SemaphoreType.DMA((n,)),
        ],
        compiler_params=pltpu.CompilerParams(collective_id=collective_id, has_side_effects=True),
    )(x)


def rotate(projected, gram):
    lower = jnp.linalg.cholesky(gram)
    inverse = lax.linalg.triangular_solve(
        lower, jnp.eye(gram.shape[0], dtype=jnp.float32), left_side=True, lower=True
    )
    return jnp.einsum(
        "kl,bli->bki",
        inverse,
        projected,
        precision=lax.Precision.HIGHEST,
        preferred_element_type=jnp.float32,
    )


def local_gram(projected):
    return jnp.einsum(
        "bki,bli->kl",
        projected,
        projected,
        precision=lax.Precision.HIGHEST,
        preferred_element_type=jnp.float32,
    )


def panel_sum(partial, axis, other, n, collective_id):
    blocks, vecs, bsize = partial.shape
    flat = partial.reshape(blocks * vecs * bsize // LANES, LANES)
    return all_reduce(flat, axis, other, n, collective_id).reshape(blocks, vecs, bsize)


def per_device(blocks, block_row, block_col, counts, vectors, row_mass, col_mass):
    tile = blocks[0, 0]
    n_cap = tile.shape[0]
    bsize = row_mass.shape[1]
    vecs = vectors.shape[1] // bsize
    own = vectors.shape[0]
    n_row = lax.axis_size("row")
    n_col = lax.axis_size("col")
    row_panel = own * n_col
    col_panel = own * n_row
    total_boxes = float(own * bsize * n_row * n_col)
    rows_idx = block_row[0, 0]
    cols_idx = block_col[0, 0]
    live = jnp.arange(n_cap) < counts[0, 0]
    fwd_ids = jnp.where(live, rows_idx, row_panel)
    bwd_ids = jnp.where(live, cols_idx, col_panel)
    square = tile.reshape(n_cap, bsize, bsize)
    vec_rows = own * vecs * bsize // LANES
    own_inv = 1.0 / jnp.sqrt(col_mass)
    first = (vectors.reshape(own, vecs, bsize) * own_inv[:, None, :]).astype(jnp.bfloat16)
    mass_pad = jnp.zeros((8, 128), jnp.float32).at[0, : own * bsize].set(col_mass.reshape(-1))
    got, mass_got = all_gather2(first.reshape(vec_rows, LANES), mass_pad, "row", "col", n_row, 4)
    first_panel = got.reshape(col_panel, vecs, bsize)
    col_mass_panel = mass_got.reshape(n_row, 8, 128)[:, 0, : own * bsize].reshape(col_panel, bsize)
    inv_col = 1.0 / jnp.sqrt(col_mass_panel)
    row_mass_spread = jnp.broadcast_to(row_mass[:, None, :], (own, vecs, bsize)).reshape(vec_rows, LANES)
    fwd_hot = (fwd_ids[None, :] == jnp.arange(row_panel)[:, None]).astype(jnp.float32)
    bwd_hot = (bwd_ids[None, :] == jnp.arange(col_panel)[:, None]).astype(jnp.float32)
    for step in range(ITERS):
        if step == 0:
            scaled = first_panel
        else:
            scaled = (current * inv_col[:, None, :]).astype(jnp.bfloat16)
        forward_taken = jnp.take(scaled, cols_idx, axis=0)
        forward_product = jnp.einsum(
            "bij,bkj->bki", square, forward_taken, preferred_element_type=jnp.float32
        )
        forward_summed = jnp.einsum(
            "rs,ski->rki", fwd_hot, forward_product, precision=lax.Precision.HIGHEST,
            preferred_element_type=jnp.float32,
        )
        flat = forward_summed.reshape(row_panel * vecs * bsize // LANES, LANES)
        weighted = forward_reduce(flat, row_mass_spread, n_col, 1).reshape(row_panel, vecs, bsize)
        taken = jnp.take(weighted, rows_idx, axis=0)
        product = jnp.einsum("bij,bki->bkj", square, taken, preferred_element_type=jnp.float32)
        summed = jnp.einsum(
            "cs,skj->ckj", bwd_hot, product, precision=lax.Precision.HIGHEST,
            preferred_element_type=jnp.float32,
        )
        cols_sum = panel_sum(summed, "row", "col", n_row, 2)
        projected = cols_sum * inv_col[:, None, :]
        partial_gram = local_gram(projected)
        gram = all_reduce(partial_gram, "col", "row", n_col, 3, two_phase=False) / total_boxes
        current = rotate(projected, gram)
    me = lax.axis_index("row")
    mine = lax.dynamic_slice_in_dim(current, me * own, own, 0)
    return mine.reshape(own, vecs * bsize)


def solution(mesh):
    in_specs = (
        P("row", "col", None, None),
        P("row", "col", None),
        P("row", "col", None),
        P("row", "col"),
        P(("col", "row"), None),
        P(("row", "col"), None),
        P(("col", "row"), None),
    )
    out_specs = P(("col", "row"), None)
    return jax.shard_map(
        per_device, mesh=mesh, in_specs=in_specs, out_specs=out_specs, check_vma=False
    )
```

```python
import functools

import jax
import jax.numpy as jnp
from jax import lax
from jax.experimental import pallas as pl
from jax.experimental.pallas import tpu as pltpu
from jax.sharding import PartitionSpec as P

ITERS = 4
LANES = 512
MESH_ID = pl.DeviceIdType.MESH


def _peer(axis, other, p):
    them = lax.axis_index(other)
    return (p, them) if axis == "row" else (them, p)


def _reduce_kernel(axis, other, n, ch, two_phase, x_ref, o_ref, recv, mine, gath, s1, r1, s2, r2):
    me = lax.axis_index(axis)
    barrier = pltpu.get_barrier_semaphore()
    for d in range(1, n):
        pl.semaphore_signal(
            barrier, 1, device_id=_peer(axis, other, (me + d) % n), device_id_type=MESH_ID
        )
    pl.semaphore_wait(barrier, n - 1)
    if not two_phase:
        sends = []
        for d in range(1, n):
            c = pltpu.make_async_remote_copy(
                x_ref, recv.at[d], s1.at[d], r1.at[d],
                device_id=_peer(axis, other, (me + d) % n), device_id_type=MESH_ID,
            )
            c.start()
            sends.append(c)
        for c in sends:
            c.wait()
        recv[0] = x_ref[...]
        acc = recv[me % n]
        for p in range(1, n):
            acc = acc + recv[(me - p + n) % n]
        o_ref[...] = acc
        return
    sends = []
    for d in range(1, n):
        peer = (me + d) % n
        start = pl.multiple_of(peer * ch, ch)
        c = pltpu.make_async_remote_copy(
            x_ref.at[pl.ds(start, ch)], recv.at[d], s1.at[d], r1.at[d],
            device_id=_peer(axis, other, peer), device_id_type=MESH_ID,
        )
        c.start()
        sends.append(c)
    own = pl.multiple_of(me * ch, ch)
    acc = x_ref[pl.ds(own, ch), :]
    for d, c in enumerate(sends, 1):
        c.wait()
        acc = acc + recv[d]
    mine[...] = acc
    gathers = []
    for d in range(1, n):
        c = pltpu.make_async_remote_copy(
            mine, gath.at[d], s2.at[d], r2.at[d],
            device_id=_peer(axis, other, (me + d) % n), device_id_type=MESH_ID,
        )
        c.start()
        gathers.append(c)
    o_ref[pl.ds(own, ch), :] = acc
    for d, c in enumerate(gathers, 1):
        c.wait()
        src = pl.multiple_of(((me - d + n) % n) * ch, ch)
        o_ref[pl.ds(src, ch), :] = gath[d]


def _gather_kernel(axis, other, n, x_ref, o_ref, gath, s2, r2):
    me = lax.axis_index(axis)
    ch = x_ref.shape[0]
    barrier = pltpu.get_barrier_semaphore()
    for d in range(1, n):
        pl.semaphore_signal(
            barrier, 1, device_id=_peer(axis, other, (me + d) % n), device_id_type=MESH_ID
        )
    pl.semaphore_wait(barrier, n - 1)
    gathers = []
    for d in range(1, n):
        c = pltpu.make_async_remote_copy(
            x_ref, gath.at[d], s2.at[d], r2.at[d],
            device_id=_peer(axis, other, (me + d) % n), device_id_type=MESH_ID,
        )
        c.start()
        gathers.append(c)
    o_ref[pl.ds(pl.multiple_of(me * ch, ch), ch), :] = x_ref[...]
    for d, c in enumerate(gathers, 1):
        c.wait()
        src = pl.multiple_of(((me - d + n) % n) * ch, ch)
        o_ref[pl.ds(src, ch), :] = gath[d]


def all_gather(x, axis, other, n, collective_id):
    ch, lanes = x.shape
    return pl.pallas_call(
        functools.partial(_gather_kernel, axis, other, n),
        out_shape=jax.ShapeDtypeStruct((n * ch, lanes), x.dtype),
        in_specs=[pl.BlockSpec(memory_space=pltpu.VMEM)],
        out_specs=pl.BlockSpec(memory_space=pltpu.VMEM),
        scratch_shapes=[
            pltpu.VMEM((n, ch, lanes), x.dtype),
            pltpu.SemaphoreType.DMA((n,)),
            pltpu.SemaphoreType.DMA((n,)),
        ],
        compiler_params=pltpu.CompilerParams(collective_id=collective_id, has_side_effects=True),
    )(x)


def _forward_kernel(n, ch, x_ref, mass_ref, o_ref, recv, mine, gath, s1, r1, s2, r2):
    axis, other = "col", "row"
    me = lax.axis_index(axis)
    barrier = pltpu.get_barrier_semaphore()
    for d in range(1, n):
        pl.semaphore_signal(
            barrier, 1, device_id=_peer(axis, other, (me + d) % n), device_id_type=MESH_ID
        )
    pl.semaphore_wait(barrier, n - 1)
    sends = []
    for d in range(1, n):
        peer = (me + d) % n
        start = pl.multiple_of(peer * ch, ch)
        c = pltpu.make_async_remote_copy(
            x_ref.at[pl.ds(start, ch)], recv.at[d], s1.at[d], r1.at[d],
            device_id=_peer(axis, other, peer), device_id_type=MESH_ID,
        )
        c.start()
        sends.append(c)
    own = pl.multiple_of(me * ch, ch)
    acc = x_ref[pl.ds(own, ch), :]
    for d, c in enumerate(sends, 1):
        c.wait()
        acc = acc + recv[d]
    mine[...] = (acc * mass_ref[...]).astype(mine.dtype)
    gathers = []
    for d in range(1, n):
        c = pltpu.make_async_remote_copy(
            mine, gath.at[d], s2.at[d], r2.at[d],
            device_id=_peer(axis, other, (me + d) % n), device_id_type=MESH_ID,
        )
        c.start()
        gathers.append(c)
    o_ref[pl.ds(own, ch), :] = mine[...]
    for d, c in enumerate(gathers, 1):
        c.wait()
        src = pl.multiple_of(((me - d + n) % n) * ch, ch)
        o_ref[pl.ds(src, ch), :] = gath[d]


def forward_reduce(x, mass, n, collective_id):
    rows, lanes = x.shape
    ch = rows // n
    return pl.pallas_call(
        functools.partial(_forward_kernel, n, ch),
        out_shape=jax.ShapeDtypeStruct(x.shape, jnp.bfloat16),
        in_specs=[pl.BlockSpec(memory_space=pltpu.VMEM)] * 2,
        out_specs=pl.BlockSpec(memory_space=pltpu.VMEM),
        scratch_shapes=[
            pltpu.VMEM((n, ch, lanes), x.dtype),
            pltpu.VMEM((ch, lanes), jnp.bfloat16),
            pltpu.VMEM((n, ch, lanes), jnp.bfloat16),
            pltpu.SemaphoreType.DMA((n,)),
            pltpu.SemaphoreType.DMA((n,)),
            pltpu.SemaphoreType.DMA((n,)),
            pltpu.SemaphoreType.DMA((n,)),
        ],
        compiler_params=pltpu.CompilerParams(collective_id=collective_id, has_side_effects=True),
    )(x, mass)


def _gather2_kernel(axis, other, n, x_ref, y_ref, o_ref, p_ref, gx, gy, sx, rx, sy, ry):
    me = lax.axis_index(axis)
    cx = x_ref.shape[0]
    cy = y_ref.shape[0]
    barrier = pltpu.get_barrier_semaphore()
    for d in range(1, n):
        pl.semaphore_signal(
            barrier, 1, device_id=_peer(axis, other, (me + d) % n), device_id_type=MESH_ID
        )
    pl.semaphore_wait(barrier, n - 1)
    copies = []
    for d in range(1, n):
        peer = _peer(axis, other, (me + d) % n)
        a = pltpu.make_async_remote_copy(
            x_ref, gx.at[d], sx.at[d], rx.at[d], device_id=peer, device_id_type=MESH_ID
        )
        b = pltpu.make_async_remote_copy(
            y_ref, gy.at[d], sy.at[d], ry.at[d], device_id=peer, device_id_type=MESH_ID
        )
        a.start()
        b.start()
        copies.append((a, b))
    o_ref[pl.ds(pl.multiple_of(me * cx, cx), cx), :] = x_ref[...]
    p_ref[pl.ds(pl.multiple_of(me * cy, cy), cy), :] = y_ref[...]
    for d, (a, b) in enumerate(copies, 1):
        a.wait()
        b.wait()
        src = (me - d + n) % n
        o_ref[pl.ds(pl.multiple_of(src * cx, cx), cx), :] = gx[d]
        p_ref[pl.ds(pl.multiple_of(src * cy, cy), cy), :] = gy[d]


def all_gather2(x, y, axis, other, n, collective_id):
    return pl.pallas_call(
        functools.partial(_gather2_kernel, axis, other, n),
        out_shape=(
            jax.ShapeDtypeStruct((n * x.shape[0], x.shape[1]), x.dtype),
            jax.ShapeDtypeStruct((n * y.shape[0], y.shape[1]), y.dtype),
        ),
        in_specs=[pl.BlockSpec(memory_space=pltpu.VMEM)] * 2,
        out_specs=(pl.BlockSpec(memory_space=pltpu.VMEM),) * 2,
        scratch_shapes=[
            pltpu.VMEM((n,) + x.shape, x.dtype),
            pltpu.VMEM((n,) + y.shape, y.dtype),
            pltpu.SemaphoreType.DMA((n,)),
            pltpu.SemaphoreType.DMA((n,)),
            pltpu.SemaphoreType.DMA((n,)),
            pltpu.SemaphoreType.DMA((n,)),
        ],
        compiler_params=pltpu.CompilerParams(collective_id=collective_id, has_side_effects=True),
    )(x, y)


def _gram_of(a):
    return lax.dot_general(
        a, a, (((1,), (1,)), ((), ())), precision=lax.Precision.HIGHEST,
        preferred_element_type=jnp.float32,
    )


def _backward_kernel(n, m, x_ref, icol_ref, o_ref, g_ref, recv, gath, g3, s1, r1, s2, r2, s3, r3):
    me = lax.axis_index("row")
    mc = lax.axis_index("col")
    barrier = pltpu.get_barrier_semaphore()
    for d in range(1, n):
        pl.semaphore_signal(barrier, 1, device_id=((me + d) % n, mc), device_id_type=MESH_ID)
    for d in range(1, m):
        pl.semaphore_signal(barrier, 1, device_id=(me, (mc + d) % m), device_id_type=MESH_ID)
    pl.semaphore_wait(barrier, n - 1 + m - 1)
    sends = []
    for d in range(1, n):
        peer = (me + d) % n
        c = pltpu.make_async_remote_copy(
            x_ref.at[peer], recv.at[d], s1.at[d], r1.at[d],
            device_id=(peer, mc), device_id_type=MESH_ID,
        )
        c.start()
        sends.append(c)
    acc = x_ref[me]
    for d, c in enumerate(sends, 1):
        c.wait()
        acc = acc + recv[d]
    gath[0] = acc * icol_ref[...]
    gathers = []
    for d in range(1, n):
        c = pltpu.make_async_remote_copy(
            gath.at[0], gath.at[d], s2.at[d], r2.at[d],
            device_id=((me + d) % n, mc), device_id_type=MESH_ID,
        )
        c.start()
        gathers.append(c)
    for c in gathers:
        c.wait()
    g = None
    for p in range(n):
        chunk = gath[(me - p + n) % n]
        o_ref[p] = chunk
        term = _gram_of(chunk)
        g = term if g is None else g + term
    g3[0] = g
    grams = []
    for d in range(1, m):
        c = pltpu.make_async_remote_copy(
            g3.at[0], g3.at[d], s3.at[d], r3.at[d],
            device_id=(me, (mc + d) % m), device_id_type=MESH_ID,
        )
        c.start()
        grams.append(c)
    for c in grams:
        c.wait()
    total = g3[mc % m]
    for q in range(1, m):
        total = total + g3[(mc - q + m) % m]
    g_ref[...] = total


def backward_reduce(x, icol, n, m, collective_id):
    chunks, vecs, lanes = x.shape
    return pl.pallas_call(
        functools.partial(_backward_kernel, n, m),
        out_shape=(
            jax.ShapeDtypeStruct(x.shape, jnp.float32),
            jax.ShapeDtypeStruct((vecs, vecs), jnp.float32),
        ),
        in_specs=[pl.BlockSpec(memory_space=pltpu.VMEM)] * 2,
        out_specs=(pl.BlockSpec(memory_space=pltpu.VMEM),) * 2,
        scratch_shapes=[
            pltpu.VMEM((n, vecs, lanes), jnp.float32),
            pltpu.VMEM((n, vecs, lanes), jnp.float32),
            pltpu.VMEM((m, vecs, vecs), jnp.float32),
            pltpu.SemaphoreType.DMA((n,)),
            pltpu.SemaphoreType.DMA((n,)),
            pltpu.SemaphoreType.DMA((n,)),
            pltpu.SemaphoreType.DMA((n,)),
            pltpu.SemaphoreType.DMA((m,)),
            pltpu.SemaphoreType.DMA((m,)),
        ],
        compiler_params=pltpu.CompilerParams(collective_id=collective_id, has_side_effects=True),
    )(x, icol)


def all_reduce(x, axis, other, n, collective_id, two_phase=True):
    rows, lanes = x.shape
    ch = rows // n if two_phase else rows
    slots = ch if two_phase else rows
    return pl.pallas_call(
        functools.partial(_reduce_kernel, axis, other, n, ch, two_phase),
        out_shape=jax.ShapeDtypeStruct(x.shape, x.dtype),
        in_specs=[pl.BlockSpec(memory_space=pltpu.VMEM)],
        out_specs=pl.BlockSpec(memory_space=pltpu.VMEM),
        scratch_shapes=[
            pltpu.VMEM((n, slots, lanes), x.dtype),
            pltpu.VMEM((ch, lanes), x.dtype),
            pltpu.VMEM((n, ch, lanes), x.dtype),
            pltpu.SemaphoreType.DMA((n,)),
            pltpu.SemaphoreType.DMA((n,)),
            pltpu.SemaphoreType.DMA((n,)),
            pltpu.SemaphoreType.DMA((n,)),
        ],
        compiler_params=pltpu.CompilerParams(collective_id=collective_id, has_side_effects=True),
    )(x)


def rotate(projected, gram):
    lower = jnp.linalg.cholesky(gram)
    inverse = lax.linalg.triangular_solve(
        lower, jnp.eye(gram.shape[0], dtype=jnp.float32), left_side=True, lower=True
    )
    return jnp.einsum(
        "kl,bli->bki",
        inverse,
        projected,
        precision=lax.Precision.HIGHEST,
        preferred_element_type=jnp.float32,
    )


def rotate_pairs(projected, gram):
    lower = jnp.linalg.cholesky(gram)
    inverse = lax.linalg.triangular_solve(
        lower, jnp.eye(gram.shape[0], dtype=jnp.float32), left_side=True, lower=True
    )
    return jnp.einsum(
        "kl,plx->pkx",
        inverse,
        projected,
        precision=lax.Precision.HIGHEST,
        preferred_element_type=jnp.float32,
    )


def local_gram(projected):
    return jnp.einsum(
        "bki,bli->kl",
        projected,
        projected,
        precision=lax.Precision.HIGHEST,
        preferred_element_type=jnp.float32,
    )


def panel_sum(partial, axis, other, n, collective_id):
    blocks, vecs, bsize = partial.shape
    flat = partial.reshape(blocks * vecs * bsize // LANES, LANES)
    return all_reduce(flat, axis, other, n, collective_id).reshape(blocks, vecs, bsize)


def per_device(blocks, block_row, block_col, counts, vectors, row_mass, col_mass):
    tile = blocks[0, 0]
    n_cap = tile.shape[0]
    bsize = row_mass.shape[1]
    vecs = vectors.shape[1] // bsize
    own = vectors.shape[0]
    n_row = lax.axis_size("row")
    n_col = lax.axis_size("col")
    row_panel = own * n_col
    col_panel = own * n_row
    total_boxes = float(own * bsize * n_row * n_col)
    rows_idx = block_row[0, 0]
    cols_idx = block_col[0, 0]
    live = jnp.arange(n_cap) < counts[0, 0]
    fwd_ids = jnp.where(live, rows_idx, row_panel)
    bwd_ids = jnp.where(live, cols_idx, col_panel)
    square = tile.reshape(n_cap, bsize, bsize)
    vec_rows = own * vecs * bsize // LANES
    own_inv = 1.0 / jnp.sqrt(col_mass)
    first = (vectors.reshape(own, vecs, bsize) * own_inv[:, None, :]).astype(jnp.bfloat16)
    mass_pad = jnp.zeros((8, 128), jnp.float32).at[0, : own * bsize].set(col_mass.reshape(-1))
    got, mass_got = all_gather2(first.reshape(vec_rows, LANES), mass_pad, "row", "col", n_row, 4)
    first_panel = got.reshape(col_panel, vecs, bsize)
    col_mass_panel = mass_got.reshape(n_row, 8, 128)[:, 0, : own * bsize].reshape(col_panel, bsize)
    inv_col = 1.0 / jnp.sqrt(col_mass_panel)
    pairs = col_panel // 2
    inv_pairs = inv_col.reshape(pairs, 1, 2 * bsize)
    own_pair = jnp.broadcast_to(own_inv.reshape(1, own * bsize), (vecs, own * bsize))
    row_mass_spread = jnp.broadcast_to(row_mass[:, None, :], (own, vecs, bsize)).reshape(vec_rows, LANES)
    fwd_hot = (fwd_ids[None, :] == jnp.arange(row_panel)[:, None]).astype(jnp.float32)
    bwd_hot = (bwd_ids[None, :] == jnp.arange(col_panel)[:, None]).astype(jnp.float32)
    for step in range(ITERS):
        if step == 0:
            scaled = first_panel
        else:
            paired = (current * inv_pairs).astype(jnp.bfloat16)
            scaled = paired.reshape(pairs, vecs, 2, bsize).transpose(0, 2, 1, 3).reshape(col_panel, vecs, bsize)
        forward_taken = jnp.take(scaled, cols_idx, axis=0)
        forward_product = jnp.einsum(
            "bij,bkj->bki", square, forward_taken, preferred_element_type=jnp.float32
        )
        forward_summed = jnp.einsum(
            "rs,ski->rki", fwd_hot, forward_product, precision=lax.Precision.HIGHEST,
            preferred_element_type=jnp.float32,
        )
        flat = forward_summed.reshape(row_panel * vecs * bsize // LANES, LANES)
        weighted = forward_reduce(flat, row_mass_spread, n_col, 1).reshape(row_panel, vecs, bsize)
        taken = jnp.take(weighted, rows_idx, axis=0)
        product = jnp.einsum("bij,bki->bkj", square, taken, preferred_element_type=jnp.float32)
        summed = jnp.einsum(
            "pbs,skj->pkbj", bwd_hot.reshape(pairs, 2, n_cap), product,
            precision=lax.Precision.HIGHEST, preferred_element_type=jnp.float32,
        ).reshape(pairs, vecs, 2 * bsize)
        projected, gram = backward_reduce(summed, own_pair, n_row, n_col, 2)
        current = rotate_pairs(projected, gram / total_boxes)
    me = lax.axis_index("row")
    mine = lax.dynamic_index_in_dim(current, me, 0, keepdims=False)
    return mine.reshape(vecs, own, bsize).transpose(1, 0, 2).reshape(own, vecs * bsize)


def solution(mesh):
    in_specs = (
        P("row", "col", None, None),
        P("row", "col", None),
        P("row", "col", None),
        P("row", "col"),
        P(("col", "row"), None),
        P(("row", "col"), None),
        P(("col", "row"), None),
    )
    out_specs = P(("col", "row"), None)
    return jax.shard_map(
        per_device, mesh=mesh, in_specs=in_specs, out_specs=out_specs, check_vma=False
    )
```

```python
import functools

import jax
import jax.numpy as jnp
from jax import lax
from jax.experimental import pallas as pl
from jax.experimental.pallas import tpu as pltpu
from jax.sharding import PartitionSpec as P

ITERS = 4
LANES = 512
MESH_ID = pl.DeviceIdType.MESH


def _peer(axis, other, p):
    them = lax.axis_index(other)
    return (p, them) if axis == "row" else (them, p)


def _reduce_kernel(axis, other, n, ch, two_phase, x_ref, o_ref, recv, mine, gath, s1, r1, s2, r2):
    me = lax.axis_index(axis)
    barrier = pltpu.get_barrier_semaphore()
    for d in range(1, n):
        pl.semaphore_signal(
            barrier, 1, device_id=_peer(axis, other, (me + d) % n), device_id_type=MESH_ID
        )
    pl.semaphore_wait(barrier, n - 1)
    if not two_phase:
        sends = []
        for d in range(1, n):
            c = pltpu.make_async_remote_copy(
                x_ref, recv.at[d], s1.at[d], r1.at[d],
                device_id=_peer(axis, other, (me + d) % n), device_id_type=MESH_ID,
            )
            c.start()
            sends.append(c)
        for c in sends:
            c.wait()
        recv[0] = x_ref[...]
        acc = recv[me % n]
        for p in range(1, n):
            acc = acc + recv[(me - p + n) % n]
        o_ref[...] = acc
        return
    sends = []
    for d in range(1, n):
        peer = (me + d) % n
        start = pl.multiple_of(peer * ch, ch)
        c = pltpu.make_async_remote_copy(
            x_ref.at[pl.ds(start, ch)], recv.at[d], s1.at[d], r1.at[d],
            device_id=_peer(axis, other, peer), device_id_type=MESH_ID,
        )
        c.start()
        sends.append(c)
    own = pl.multiple_of(me * ch, ch)
    acc = x_ref[pl.ds(own, ch), :]
    for d, c in enumerate(sends, 1):
        c.wait()
        acc = acc + recv[d]
    mine[...] = acc
    gathers = []
    for d in range(1, n):
        c = pltpu.make_async_remote_copy(
            mine, gath.at[d], s2.at[d], r2.at[d],
            device_id=_peer(axis, other, (me + d) % n), device_id_type=MESH_ID,
        )
        c.start()
        gathers.append(c)
    o_ref[pl.ds(own, ch), :] = acc
    for d, c in enumerate(gathers, 1):
        c.wait()
        src = pl.multiple_of(((me - d + n) % n) * ch, ch)
        o_ref[pl.ds(src, ch), :] = gath[d]


def _gather_kernel(axis, other, n, x_ref, o_ref, gath, s2, r2):
    me = lax.axis_index(axis)
    ch = x_ref.shape[0]
    barrier = pltpu.get_barrier_semaphore()
    for d in range(1, n):
        pl.semaphore_signal(
            barrier, 1, device_id=_peer(axis, other, (me + d) % n), device_id_type=MESH_ID
        )
    pl.semaphore_wait(barrier, n - 1)
    gathers = []
    for d in range(1, n):
        c = pltpu.make_async_remote_copy(
            x_ref, gath.at[d], s2.at[d], r2.at[d],
            device_id=_peer(axis, other, (me + d) % n), device_id_type=MESH_ID,
        )
        c.start()
        gathers.append(c)
    o_ref[pl.ds(pl.multiple_of(me * ch, ch), ch), :] = x_ref[...]
    for d, c in enumerate(gathers, 1):
        c.wait()
        src = pl.multiple_of(((me - d + n) % n) * ch, ch)
        o_ref[pl.ds(src, ch), :] = gath[d]


def all_gather(x, axis, other, n, collective_id):
    ch, lanes = x.shape
    return pl.pallas_call(
        functools.partial(_gather_kernel, axis, other, n),
        out_shape=jax.ShapeDtypeStruct((n * ch, lanes), x.dtype),
        in_specs=[pl.BlockSpec(memory_space=pltpu.VMEM)],
        out_specs=pl.BlockSpec(memory_space=pltpu.VMEM),
        scratch_shapes=[
            pltpu.VMEM((n, ch, lanes), x.dtype),
            pltpu.SemaphoreType.DMA((n,)),
            pltpu.SemaphoreType.DMA((n,)),
        ],
        compiler_params=pltpu.CompilerParams(collective_id=collective_id, has_side_effects=True),
    )(x)


def _forward_kernel(n, ch, x_ref, mass_ref, o_ref, recv, mine, gath, s1, r1, s2, r2):
    axis, other = "col", "row"
    me = lax.axis_index(axis)
    barrier = pltpu.get_barrier_semaphore()
    for d in range(1, n):
        pl.semaphore_signal(
            barrier, 1, device_id=_peer(axis, other, (me + d) % n), device_id_type=MESH_ID
        )
    pl.semaphore_wait(barrier, n - 1)
    sends = []
    for d in range(1, n):
        peer = (me + d) % n
        start = pl.multiple_of(peer * ch, ch)
        c = pltpu.make_async_remote_copy(
            x_ref.at[pl.ds(start, ch)], recv.at[d], s1.at[d], r1.at[d],
            device_id=_peer(axis, other, peer), device_id_type=MESH_ID,
        )
        c.start()
        sends.append(c)
    own = pl.multiple_of(me * ch, ch)
    acc = x_ref[pl.ds(own, ch), :]
    for d, c in enumerate(sends, 1):
        c.wait()
        acc = acc + recv[d]
    mine[...] = (acc * mass_ref[...]).astype(mine.dtype)
    gathers = []
    for d in range(1, n):
        c = pltpu.make_async_remote_copy(
            mine, gath.at[d], s2.at[d], r2.at[d],
            device_id=_peer(axis, other, (me + d) % n), device_id_type=MESH_ID,
        )
        c.start()
        gathers.append(c)
    o_ref[pl.ds(own, ch), :] = mine[...]
    for d, c in enumerate(gathers, 1):
        c.wait()
        src = pl.multiple_of(((me - d + n) % n) * ch, ch)
        o_ref[pl.ds(src, ch), :] = gath[d]


def forward_reduce(x, mass, n, collective_id):
    rows, lanes = x.shape
    ch = rows // n
    return pl.pallas_call(
        functools.partial(_forward_kernel, n, ch),
        out_shape=jax.ShapeDtypeStruct(x.shape, jnp.bfloat16),
        in_specs=[pl.BlockSpec(memory_space=pltpu.VMEM)] * 2,
        out_specs=pl.BlockSpec(memory_space=pltpu.VMEM),
        scratch_shapes=[
            pltpu.VMEM((n, ch, lanes), x.dtype),
            pltpu.VMEM((ch, lanes), jnp.bfloat16),
            pltpu.VMEM((n, ch, lanes), jnp.bfloat16),
            pltpu.SemaphoreType.DMA((n,)),
            pltpu.SemaphoreType.DMA((n,)),
            pltpu.SemaphoreType.DMA((n,)),
            pltpu.SemaphoreType.DMA((n,)),
        ],
        compiler_params=pltpu.CompilerParams(collective_id=collective_id, has_side_effects=True),
    )(x, mass)


def _gather2_kernel(axis, other, n, x_ref, y_ref, o_ref, p_ref, gx, gy, sx, rx, sy, ry):
    me = lax.axis_index(axis)
    cx = x_ref.shape[0]
    cy = y_ref.shape[0]
    barrier = pltpu.get_barrier_semaphore()
    for d in range(1, n):
        pl.semaphore_signal(
            barrier, 1, device_id=_peer(axis, other, (me + d) % n), device_id_type=MESH_ID
        )
    pl.semaphore_wait(barrier, n - 1)
    copies = []
    for d in range(1, n):
        peer = _peer(axis, other, (me + d) % n)
        a = pltpu.make_async_remote_copy(
            x_ref, gx.at[d], sx.at[d], rx.at[d], device_id=peer, device_id_type=MESH_ID
        )
        b = pltpu.make_async_remote_copy(
            y_ref, gy.at[d], sy.at[d], ry.at[d], device_id=peer, device_id_type=MESH_ID
        )
        a.start()
        b.start()
        copies.append((a, b))
    o_ref[pl.ds(pl.multiple_of(me * cx, cx), cx), :] = x_ref[...]
    p_ref[pl.ds(pl.multiple_of(me * cy, cy), cy), :] = y_ref[...]
    for d, (a, b) in enumerate(copies, 1):
        a.wait()
        b.wait()
        src = (me - d + n) % n
        o_ref[pl.ds(pl.multiple_of(src * cx, cx), cx), :] = gx[d]
        p_ref[pl.ds(pl.multiple_of(src * cy, cy), cy), :] = gy[d]


def all_gather2(x, y, axis, other, n, collective_id):
    return pl.pallas_call(
        functools.partial(_gather2_kernel, axis, other, n),
        out_shape=(
            jax.ShapeDtypeStruct((n * x.shape[0], x.shape[1]), x.dtype),
            jax.ShapeDtypeStruct((n * y.shape[0], y.shape[1]), y.dtype),
        ),
        in_specs=[pl.BlockSpec(memory_space=pltpu.VMEM)] * 2,
        out_specs=(pl.BlockSpec(memory_space=pltpu.VMEM),) * 2,
        scratch_shapes=[
            pltpu.VMEM((n,) + x.shape, x.dtype),
            pltpu.VMEM((n,) + y.shape, y.dtype),
            pltpu.SemaphoreType.DMA((n,)),
            pltpu.SemaphoreType.DMA((n,)),
            pltpu.SemaphoreType.DMA((n,)),
            pltpu.SemaphoreType.DMA((n,)),
        ],
        compiler_params=pltpu.CompilerParams(collective_id=collective_id, has_side_effects=True),
    )(x, y)


def _gram_of(a):
    return lax.dot_general(
        a, a, (((1,), (1,)), ((), ())), precision=lax.Precision.HIGHEST,
        preferred_element_type=jnp.float32,
    )


def _backward_kernel(n, m, x_ref, icol_ref, o_ref, g_ref, recv, gath, g3, s1, r1, s2, r2, s3, r3):
    me = lax.axis_index("row")
    mc = lax.axis_index("col")
    barrier = pltpu.get_barrier_semaphore()
    for d in range(1, n):
        pl.semaphore_signal(barrier, 1, device_id=((me + d) % n, mc), device_id_type=MESH_ID)
    for d in range(1, m):
        pl.semaphore_signal(barrier, 1, device_id=(me, (mc + d) % m), device_id_type=MESH_ID)
    pl.semaphore_wait(barrier, n - 1 + m - 1)
    sends = []
    for d in range(1, n):
        peer = (me + d) % n
        c = pltpu.make_async_remote_copy(
            x_ref.at[peer], recv.at[d], s1.at[d], r1.at[d],
            device_id=(peer, mc), device_id_type=MESH_ID,
        )
        c.start()
        sends.append(c)
    acc = x_ref[me]
    for d, c in enumerate(sends, 1):
        c.wait()
        acc = acc + recv[d]
    gath[0] = acc * icol_ref[...]
    gathers = []
    for d in range(1, n):
        c = pltpu.make_async_remote_copy(
            gath.at[0], gath.at[d], s2.at[d], r2.at[d],
            device_id=((me + d) % n, mc), device_id_type=MESH_ID,
        )
        c.start()
        gathers.append(c)
    for c in gathers:
        c.wait()
    g = None
    for p in range(n):
        chunk = gath[(me - p + n) % n]
        o_ref[p] = chunk
        term = _gram_of(chunk)
        g = term if g is None else g + term
    g3[0] = g
    grams = []
    for d in range(1, m):
        c = pltpu.make_async_remote_copy(
            g3.at[0], g3.at[d], s3.at[d], r3.at[d],
            device_id=(me, (mc + d) % m), device_id_type=MESH_ID,
        )
        c.start()
        grams.append(c)
    for c in grams:
        c.wait()
    total = g3[mc % m]
    for q in range(1, m):
        total = total + g3[(mc - q + m) % m]
    g_ref[...] = total


def backward_reduce(x, icol, n, m, collective_id):
    chunks, vecs, lanes = x.shape
    return pl.pallas_call(
        functools.partial(_backward_kernel, n, m),
        out_shape=(
            jax.ShapeDtypeStruct(x.shape, jnp.float32),
            jax.ShapeDtypeStruct((vecs, vecs), jnp.float32),
        ),
        in_specs=[pl.BlockSpec(memory_space=pltpu.VMEM)] * 2,
        out_specs=(pl.BlockSpec(memory_space=pltpu.VMEM),) * 2,
        scratch_shapes=[
            pltpu.VMEM((n, vecs, lanes), jnp.float32),
            pltpu.VMEM((n, vecs, lanes), jnp.float32),
            pltpu.VMEM((m, vecs, vecs), jnp.float32),
            pltpu.SemaphoreType.DMA((n,)),
            pltpu.SemaphoreType.DMA((n,)),
            pltpu.SemaphoreType.DMA((n,)),
            pltpu.SemaphoreType.DMA((n,)),
            pltpu.SemaphoreType.DMA((m,)),
            pltpu.SemaphoreType.DMA((m,)),
        ],
        compiler_params=pltpu.CompilerParams(collective_id=collective_id, has_side_effects=True),
    )(x, icol)


def all_reduce(x, axis, other, n, collective_id, two_phase=True):
    rows, lanes = x.shape
    ch = rows // n if two_phase else rows
    slots = ch if two_phase else rows
    return pl.pallas_call(
        functools.partial(_reduce_kernel, axis, other, n, ch, two_phase),
        out_shape=jax.ShapeDtypeStruct(x.shape, x.dtype),
        in_specs=[pl.BlockSpec(memory_space=pltpu.VMEM)],
        out_specs=pl.BlockSpec(memory_space=pltpu.VMEM),
        scratch_shapes=[
            pltpu.VMEM((n, slots, lanes), x.dtype),
            pltpu.VMEM((ch, lanes), x.dtype),
            pltpu.VMEM((n, ch, lanes), x.dtype),
            pltpu.SemaphoreType.DMA((n,)),
            pltpu.SemaphoreType.DMA((n,)),
            pltpu.SemaphoreType.DMA((n,)),
            pltpu.SemaphoreType.DMA((n,)),
        ],
        compiler_params=pltpu.CompilerParams(collective_id=collective_id, has_side_effects=True),
    )(x)


def rotate(projected, gram):
    lower = jnp.linalg.cholesky(gram)
    inverse = lax.linalg.triangular_solve(
        lower, jnp.eye(gram.shape[0], dtype=jnp.float32), left_side=True, lower=True
    )
    return jnp.einsum(
        "kl,bli->bki",
        inverse,
        projected,
        precision=lax.Precision.HIGHEST,
        preferred_element_type=jnp.float32,
    )


def rotate_pairs(projected, gram):
    lower = jnp.linalg.cholesky(gram)
    inverse = lax.linalg.triangular_solve(
        lower, jnp.eye(gram.shape[0], dtype=jnp.float32), left_side=True, lower=True
    )
    return jnp.einsum(
        "kl,plx->pkx",
        inverse,
        projected,
        precision=lax.Precision.HIGHEST,
        preferred_element_type=jnp.float32,
    )


def local_gram(projected):
    return jnp.einsum(
        "bki,bli->kl",
        projected,
        projected,
        precision=lax.Precision.HIGHEST,
        preferred_element_type=jnp.float32,
    )


def panel_sum(partial, axis, other, n, collective_id):
    blocks, vecs, bsize = partial.shape
    flat = partial.reshape(blocks * vecs * bsize // LANES, LANES)
    return all_reduce(flat, axis, other, n, collective_id).reshape(blocks, vecs, bsize)


def per_device(blocks, block_row, block_col, counts, vectors, row_mass, col_mass):
    tile = blocks[0, 0]
    n_cap = tile.shape[0]
    bsize = row_mass.shape[1]
    vecs = vectors.shape[1] // bsize
    own = vectors.shape[0]
    n_row = lax.axis_size("row")
    n_col = lax.axis_size("col")
    row_panel = own * n_col
    col_panel = own * n_row
    total_boxes = float(own * bsize * n_row * n_col)
    rows_idx = block_row[0, 0]
    cols_idx = block_col[0, 0]
    live = jnp.arange(n_cap) < counts[0, 0]
    fwd_ids = jnp.where(live, rows_idx, row_panel)
    bwd_ids = jnp.where(live, cols_idx, col_panel)
    square = tile.reshape(n_cap, bsize, bsize)
    vec_rows = own * vecs * bsize // LANES
    own_inv = 1.0 / jnp.sqrt(col_mass)
    first = (vectors.reshape(own, vecs, bsize) * own_inv[:, None, :]).astype(jnp.bfloat16)
    mass_pad = jnp.zeros((8, 128), jnp.float32).at[0, : own * bsize].set(col_mass.reshape(-1))
    got, mass_got = all_gather2(first.reshape(vec_rows, LANES), mass_pad, "row", "col", n_row, 4)
    first_panel = got.reshape(col_panel, vecs, bsize)
    col_mass_panel = mass_got.reshape(n_row, 8, 128)[:, 0, : own * bsize].reshape(col_panel, bsize)
    inv_col = 1.0 / jnp.sqrt(col_mass_panel)
    pairs = col_panel // 2
    inv_pairs = inv_col.reshape(pairs, 1, 2 * bsize)
    own_pair = jnp.broadcast_to(own_inv.reshape(1, own * bsize), (vecs, own * bsize))
    row_mass_spread = jnp.broadcast_to(row_mass[:, None, :], (own, vecs, bsize)).reshape(vec_rows, LANES)
    fwd_hot = (fwd_ids[None, :] == jnp.arange(row_panel)[:, None]).astype(jnp.float32)
    bwd_hot = (bwd_ids[None, :] == jnp.arange(col_panel)[:, None]).astype(jnp.float32)
    for step in range(ITERS):
        if step == 0:
            scaled = first_panel
        else:
            paired = (current * inv_pairs).astype(jnp.bfloat16)
            scaled = paired.reshape(pairs, vecs, 2, bsize).transpose(0, 2, 1, 3).reshape(col_panel, vecs, bsize)
        forward_taken = jnp.take(scaled, cols_idx, axis=0)
        forward_product = jnp.einsum(
            "bij,bkj->bki", square, forward_taken, preferred_element_type=jnp.float32
        )
        forward_summed = jnp.einsum(
            "rs,ski->rki", fwd_hot, forward_product, precision=lax.Precision.HIGH,
            preferred_element_type=jnp.float32,
        )
        flat = forward_summed.reshape(row_panel * vecs * bsize // LANES, LANES)
        weighted = forward_reduce(flat, row_mass_spread, n_col, 1).reshape(row_panel, vecs, bsize)
        taken = jnp.take(weighted, rows_idx, axis=0)
        product = jnp.einsum("bij,bki->bkj", square, taken, preferred_element_type=jnp.float32)
        summed = jnp.einsum(
            "pbs,skj->pkbj", bwd_hot.reshape(pairs, 2, n_cap), product,
            precision=lax.Precision.HIGH, preferred_element_type=jnp.float32,
        ).reshape(pairs, vecs, 2 * bsize)
        projected, gram = backward_reduce(summed, own_pair, n_row, n_col, 2)
        current = rotate_pairs(projected, gram / total_boxes)
    me = lax.axis_index("row")
    mine = lax.dynamic_index_in_dim(current, me, 0, keepdims=False)
    return mine.reshape(vecs, own, bsize).transpose(1, 0, 2).reshape(own, vecs * bsize)


def solution(mesh):
    in_specs = (
        P("row", "col", None, None),
        P("row", "col", None),
        P("row", "col", None),
        P("row", "col"),
        P(("col", "row"), None),
        P(("row", "col"), None),
        P(("col", "row"), None),
    )
    out_specs = P(("col", "row"), None)
    return jax.shard_map(
        per_device, mesh=mesh, in_specs=in_specs, out_specs=out_specs, check_vma=False
    )
```

```python
import functools

import jax
import jax.numpy as jnp
from jax import lax
from jax.experimental import pallas as pl
from jax.experimental.pallas import tpu as pltpu
from jax.sharding import PartitionSpec as P

ITERS = 4
LANES = 512
MESH_ID = pl.DeviceIdType.MESH


def _peer(axis, other, p):
    them = lax.axis_index(other)
    return (p, them) if axis == "row" else (them, p)


def _reduce_kernel(axis, other, n, ch, two_phase, x_ref, o_ref, recv, mine, gath, s1, r1, s2, r2):
    me = lax.axis_index(axis)
    barrier = pltpu.get_barrier_semaphore()
    for d in range(1, n):
        pl.semaphore_signal(
            barrier, 1, device_id=_peer(axis, other, (me + d) % n), device_id_type=MESH_ID
        )
    pl.semaphore_wait(barrier, n - 1)
    if not two_phase:
        sends = []
        for d in range(1, n):
            c = pltpu.make_async_remote_copy(
                x_ref, recv.at[d], s1.at[d], r1.at[d],
                device_id=_peer(axis, other, (me + d) % n), device_id_type=MESH_ID,
            )
            c.start()
            sends.append(c)
        for c in sends:
            c.wait()
        recv[0] = x_ref[...]
        acc = recv[me % n]
        for p in range(1, n):
            acc = acc + recv[(me - p + n) % n]
        o_ref[...] = acc
        return
    sends = []
    for d in range(1, n):
        peer = (me + d) % n
        start = pl.multiple_of(peer * ch, ch)
        c = pltpu.make_async_remote_copy(
            x_ref.at[pl.ds(start, ch)], recv.at[d], s1.at[d], r1.at[d],
            device_id=_peer(axis, other, peer), device_id_type=MESH_ID,
        )
        c.start()
        sends.append(c)
    own = pl.multiple_of(me * ch, ch)
    acc = x_ref[pl.ds(own, ch), :]
    for d, c in enumerate(sends, 1):
        c.wait()
        acc = acc + recv[d]
    mine[...] = acc
    gathers = []
    for d in range(1, n):
        c = pltpu.make_async_remote_copy(
            mine, gath.at[d], s2.at[d], r2.at[d],
            device_id=_peer(axis, other, (me + d) % n), device_id_type=MESH_ID,
        )
        c.start()
        gathers.append(c)
    o_ref[pl.ds(own, ch), :] = acc
    for d, c in enumerate(gathers, 1):
        c.wait()
        src = pl.multiple_of(((me - d + n) % n) * ch, ch)
        o_ref[pl.ds(src, ch), :] = gath[d]


def _gather_kernel(axis, other, n, x_ref, o_ref, gath, s2, r2):
    me = lax.axis_index(axis)
    ch = x_ref.shape[0]
    barrier = pltpu.get_barrier_semaphore()
    for d in range(1, n):
        pl.semaphore_signal(
            barrier, 1, device_id=_peer(axis, other, (me + d) % n), device_id_type=MESH_ID
        )
    pl.semaphore_wait(barrier, n - 1)
    gathers = []
    for d in range(1, n):
        c = pltpu.make_async_remote_copy(
            x_ref, gath.at[d], s2.at[d], r2.at[d],
            device_id=_peer(axis, other, (me + d) % n), device_id_type=MESH_ID,
        )
        c.start()
        gathers.append(c)
    o_ref[pl.ds(pl.multiple_of(me * ch, ch), ch), :] = x_ref[...]
    for d, c in enumerate(gathers, 1):
        c.wait()
        src = pl.multiple_of(((me - d + n) % n) * ch, ch)
        o_ref[pl.ds(src, ch), :] = gath[d]


def all_gather(x, axis, other, n, collective_id):
    ch, lanes = x.shape
    return pl.pallas_call(
        functools.partial(_gather_kernel, axis, other, n),
        out_shape=jax.ShapeDtypeStruct((n * ch, lanes), x.dtype),
        in_specs=[pl.BlockSpec(memory_space=pltpu.VMEM)],
        out_specs=pl.BlockSpec(memory_space=pltpu.VMEM),
        scratch_shapes=[
            pltpu.VMEM((n, ch, lanes), x.dtype),
            pltpu.SemaphoreType.DMA((n,)),
            pltpu.SemaphoreType.DMA((n,)),
        ],
        compiler_params=pltpu.CompilerParams(collective_id=collective_id, has_side_effects=True),
    )(x)


def _forward_kernel(n, ch, x_ref, mass_ref, o_ref, recv, mine, gath, s1, r1, s2, r2):
    axis, other = "col", "row"
    me = lax.axis_index(axis)
    barrier = pltpu.get_barrier_semaphore()
    for d in range(1, n):
        pl.semaphore_signal(
            barrier, 1, device_id=_peer(axis, other, (me + d) % n), device_id_type=MESH_ID
        )
    pl.semaphore_wait(barrier, n - 1)
    sends = []
    for d in range(1, n):
        peer = (me + d) % n
        start = pl.multiple_of(peer * ch, ch)
        c = pltpu.make_async_remote_copy(
            x_ref.at[pl.ds(start, ch)], recv.at[d], s1.at[d], r1.at[d],
            device_id=_peer(axis, other, peer), device_id_type=MESH_ID,
        )
        c.start()
        sends.append(c)
    own = pl.multiple_of(me * ch, ch)
    acc = x_ref[pl.ds(own, ch), :]
    for d, c in enumerate(sends, 1):
        c.wait()
        acc = acc + recv[d]
    mine[...] = (acc * mass_ref[...]).astype(mine.dtype)
    gathers = []
    for d in range(1, n):
        c = pltpu.make_async_remote_copy(
            mine, gath.at[d], s2.at[d], r2.at[d],
            device_id=_peer(axis, other, (me + d) % n), device_id_type=MESH_ID,
        )
        c.start()
        gathers.append(c)
    o_ref[pl.ds(own, ch), :] = mine[...]
    for d, c in enumerate(gathers, 1):
        c.wait()
        src = pl.multiple_of(((me - d + n) % n) * ch, ch)
        o_ref[pl.ds(src, ch), :] = gath[d]


def forward_reduce(x, mass, n, collective_id):
    rows, lanes = x.shape
    ch = rows // n
    return pl.pallas_call(
        functools.partial(_forward_kernel, n, ch),
        out_shape=jax.ShapeDtypeStruct(x.shape, jnp.bfloat16),
        in_specs=[pl.BlockSpec(memory_space=pltpu.VMEM)] * 2,
        out_specs=pl.BlockSpec(memory_space=pltpu.VMEM),
        scratch_shapes=[
            pltpu.VMEM((n, ch, lanes), x.dtype),
            pltpu.VMEM((ch, lanes), jnp.bfloat16),
            pltpu.VMEM((n, ch, lanes), jnp.bfloat16),
            pltpu.SemaphoreType.DMA((n,)),
            pltpu.SemaphoreType.DMA((n,)),
            pltpu.SemaphoreType.DMA((n,)),
            pltpu.SemaphoreType.DMA((n,)),
        ],
        compiler_params=pltpu.CompilerParams(collective_id=collective_id, has_side_effects=True),
    )(x, mass)


def _gather2_kernel(axis, other, n, x_ref, y_ref, o_ref, p_ref, gx, gy, sx, rx, sy, ry):
    me = lax.axis_index(axis)
    cx = x_ref.shape[0]
    cy = y_ref.shape[0]
    barrier = pltpu.get_barrier_semaphore()
    for d in range(1, n):
        pl.semaphore_signal(
            barrier, 1, device_id=_peer(axis, other, (me + d) % n), device_id_type=MESH_ID
        )
    pl.semaphore_wait(barrier, n - 1)
    copies = []
    for d in range(1, n):
        peer = _peer(axis, other, (me + d) % n)
        a = pltpu.make_async_remote_copy(
            x_ref, gx.at[d], sx.at[d], rx.at[d], device_id=peer, device_id_type=MESH_ID
        )
        b = pltpu.make_async_remote_copy(
            y_ref, gy.at[d], sy.at[d], ry.at[d], device_id=peer, device_id_type=MESH_ID
        )
        a.start()
        b.start()
        copies.append((a, b))
    o_ref[pl.ds(pl.multiple_of(me * cx, cx), cx), :] = x_ref[...]
    p_ref[pl.ds(pl.multiple_of(me * cy, cy), cy), :] = y_ref[...]
    for d, (a, b) in enumerate(copies, 1):
        a.wait()
        b.wait()
        src = (me - d + n) % n
        o_ref[pl.ds(pl.multiple_of(src * cx, cx), cx), :] = gx[d]
        p_ref[pl.ds(pl.multiple_of(src * cy, cy), cy), :] = gy[d]


def all_gather2(x, y, axis, other, n, collective_id):
    return pl.pallas_call(
        functools.partial(_gather2_kernel, axis, other, n),
        out_shape=(
            jax.ShapeDtypeStruct((n * x.shape[0], x.shape[1]), x.dtype),
            jax.ShapeDtypeStruct((n * y.shape[0], y.shape[1]), y.dtype),
        ),
        in_specs=[pl.BlockSpec(memory_space=pltpu.VMEM)] * 2,
        out_specs=(pl.BlockSpec(memory_space=pltpu.VMEM),) * 2,
        scratch_shapes=[
            pltpu.VMEM((n,) + x.shape, x.dtype),
            pltpu.VMEM((n,) + y.shape, y.dtype),
            pltpu.SemaphoreType.DMA((n,)),
            pltpu.SemaphoreType.DMA((n,)),
            pltpu.SemaphoreType.DMA((n,)),
            pltpu.SemaphoreType.DMA((n,)),
        ],
        compiler_params=pltpu.CompilerParams(collective_id=collective_id, has_side_effects=True),
    )(x, y)


def _gram_of(a):
    return lax.dot_general(
        a, a, (((1,), (1,)), ((), ())), precision=lax.Precision.HIGHEST,
        preferred_element_type=jnp.float32,
    )


def chol_inverse(a):
    n = a.shape[0]
    r = lax.broadcasted_iota(jnp.int32, (n, n), 0)
    c = lax.broadcasted_iota(jnp.int32, (n, n), 1)
    r1 = lax.broadcasted_iota(jnp.int32, (n, 1), 0)
    c1 = lax.broadcasted_iota(jnp.int32, (1, n), 1)
    x0 = jnp.where(r == c, 1.0, 0.0).astype(jnp.float32)

    def step(j, carry):
        m, x = carry
        col = jnp.sum(jnp.where(c == j, m, 0.0), axis=1, keepdims=True)
        row = jnp.sum(jnp.where(r == j, m, 0.0), axis=0, keepdims=True)
        piv = jnp.sqrt(jnp.sum(jnp.where(r1 == j, col, 0.0), axis=0, keepdims=True))
        lcol = jnp.where(r1 >= j, col / piv, 0.0)
        lrow = jnp.where(c1 >= j, row / piv, 0.0)
        m = m - lcol * lrow
        xrow = jnp.sum(jnp.where(r == j, x, 0.0), axis=0, keepdims=True) / piv
        x = jnp.where(r == j, xrow, x)
        x = x - jnp.where(r1 > j, lcol, 0.0) * xrow
        return m, x

    m, x = lax.fori_loop(0, n, step, (a, x0))
    return x


def _backward_kernel(n, m, scale, x_ref, icol_ref, o_ref, recv, gath, g3, s1, r1, s2, r2, s3, r3):
    me = lax.axis_index("row")
    mc = lax.axis_index("col")
    barrier = pltpu.get_barrier_semaphore()
    for d in range(1, n):
        pl.semaphore_signal(barrier, 1, device_id=((me + d) % n, mc), device_id_type=MESH_ID)
    for d in range(1, m):
        pl.semaphore_signal(barrier, 1, device_id=(me, (mc + d) % m), device_id_type=MESH_ID)
    pl.semaphore_wait(barrier, n - 1 + m - 1)
    sends = []
    for d in range(1, n):
        peer = (me + d) % n
        c = pltpu.make_async_remote_copy(
            x_ref.at[peer], recv.at[d], s1.at[d], r1.at[d],
            device_id=(peer, mc), device_id_type=MESH_ID,
        )
        c.start()
        sends.append(c)
    acc = x_ref[me]
    for d, c in enumerate(sends, 1):
        c.wait()
        acc = acc + recv[d]
    gath[0] = acc * icol_ref[...]
    gathers = []
    for d in range(1, n):
        c = pltpu.make_async_remote_copy(
            gath.at[0], gath.at[d], s2.at[d], r2.at[d],
            device_id=((me + d) % n, mc), device_id_type=MESH_ID,
        )
        c.start()
        gathers.append(c)
    for c in gathers:
        c.wait()
    g = None
    for p in range(n):
        term = _gram_of(gath[(me - p + n) % n])
        g = term if g is None else g + term
    g3[0] = g
    grams = []
    for d in range(1, m):
        c = pltpu.make_async_remote_copy(
            g3.at[0], g3.at[d], s3.at[d], r3.at[d],
            device_id=(me, (mc + d) % m), device_id_type=MESH_ID,
        )
        c.start()
        grams.append(c)
    for c in grams:
        c.wait()
    total = g3[mc % m]
    for q in range(1, m):
        total = total + g3[(mc - q + m) % m]
    inverse = chol_inverse(total * scale)
    for p in range(n):
        o_ref[p] = lax.dot_general(
            inverse, gath[(me - p + n) % n], (((1,), (0,)), ((), ())),
            precision=lax.Precision.HIGHEST, preferred_element_type=jnp.float32,
        )


def backward_reduce(x, icol, n, m, scale, collective_id):
    chunks, vecs, lanes = x.shape
    return pl.pallas_call(
        functools.partial(_backward_kernel, n, m, scale),
        out_shape=jax.ShapeDtypeStruct(x.shape, jnp.float32),
        in_specs=[pl.BlockSpec(memory_space=pltpu.VMEM)] * 2,
        out_specs=pl.BlockSpec(memory_space=pltpu.VMEM),
        scratch_shapes=[
            pltpu.VMEM((n, vecs, lanes), jnp.float32),
            pltpu.VMEM((n, vecs, lanes), jnp.float32),
            pltpu.VMEM((m, vecs, vecs), jnp.float32),
            pltpu.SemaphoreType.DMA((n,)),
            pltpu.SemaphoreType.DMA((n,)),
            pltpu.SemaphoreType.DMA((n,)),
            pltpu.SemaphoreType.DMA((n,)),
            pltpu.SemaphoreType.DMA((m,)),
            pltpu.SemaphoreType.DMA((m,)),
        ],
        compiler_params=pltpu.CompilerParams(collective_id=collective_id, has_side_effects=True),
    )(x, icol)


def all_reduce(x, axis, other, n, collective_id, two_phase=True):
    rows, lanes = x.shape
    ch = rows // n if two_phase else rows
    slots = ch if two_phase else rows
    return pl.pallas_call(
        functools.partial(_reduce_kernel, axis, other, n, ch, two_phase),
        out_shape=jax.ShapeDtypeStruct(x.shape, x.dtype),
        in_specs=[pl.BlockSpec(memory_space=pltpu.VMEM)],
        out_specs=pl.BlockSpec(memory_space=pltpu.VMEM),
        scratch_shapes=[
            pltpu.VMEM((n, slots, lanes), x.dtype),
            pltpu.VMEM((ch, lanes), x.dtype),
            pltpu.VMEM((n, ch, lanes), x.dtype),
            pltpu.SemaphoreType.DMA((n,)),
            pltpu.SemaphoreType.DMA((n,)),
            pltpu.SemaphoreType.DMA((n,)),
            pltpu.SemaphoreType.DMA((n,)),
        ],
        compiler_params=pltpu.CompilerParams(collective_id=collective_id, has_side_effects=True),
    )(x)


def rotate(projected, gram):
    lower = jnp.linalg.cholesky(gram)
    inverse = lax.linalg.triangular_solve(
        lower, jnp.eye(gram.shape[0], dtype=jnp.float32), left_side=True, lower=True
    )
    return jnp.einsum(
        "kl,bli->bki",
        inverse,
        projected,
        precision=lax.Precision.HIGHEST,
        preferred_element_type=jnp.float32,
    )


def rotate_pairs(projected, gram):
    lower = jnp.linalg.cholesky(gram)
    inverse = lax.linalg.triangular_solve(
        lower, jnp.eye(gram.shape[0], dtype=jnp.float32), left_side=True, lower=True
    )
    return jnp.einsum(
        "kl,plx->pkx",
        inverse,
        projected,
        precision=lax.Precision.HIGHEST,
        preferred_element_type=jnp.float32,
    )


def local_gram(projected):
    return jnp.einsum(
        "bki,bli->kl",
        projected,
        projected,
        precision=lax.Precision.HIGHEST,
        preferred_element_type=jnp.float32,
    )


def panel_sum(partial, axis, other, n, collective_id):
    blocks, vecs, bsize = partial.shape
    flat = partial.reshape(blocks * vecs * bsize // LANES, LANES)
    return all_reduce(flat, axis, other, n, collective_id).reshape(blocks, vecs, bsize)


def per_device(blocks, block_row, block_col, counts, vectors, row_mass, col_mass):
    tile = blocks[0, 0]
    n_cap = tile.shape[0]
    bsize = row_mass.shape[1]
    vecs = vectors.shape[1] // bsize
    own = vectors.shape[0]
    n_row = lax.axis_size("row")
    n_col = lax.axis_size("col")
    row_panel = own * n_col
    col_panel = own * n_row
    total_boxes = float(own * bsize * n_row * n_col)
    rows_idx = block_row[0, 0]
    cols_idx = block_col[0, 0]
    live = jnp.arange(n_cap) < counts[0, 0]
    fwd_ids = jnp.where(live, rows_idx, row_panel)
    bwd_ids = jnp.where(live, cols_idx, col_panel)
    square = tile.reshape(n_cap, bsize, bsize)
    vec_rows = own * vecs * bsize // LANES
    own_inv = 1.0 / jnp.sqrt(col_mass)
    first = (vectors.reshape(own, vecs, bsize) * own_inv[:, None, :]).astype(jnp.bfloat16)
    mass_pad = jnp.zeros((8, 128), jnp.float32).at[0, : own * bsize].set(col_mass.reshape(-1))
    got, mass_got = all_gather2(first.reshape(vec_rows, LANES), mass_pad, "row", "col", n_row, 4)
    first_panel = got.reshape(col_panel, vecs, bsize)
    col_mass_panel = mass_got.reshape(n_row, 8, 128)[:, 0, : own * bsize].reshape(col_panel, bsize)
    inv_col = 1.0 / jnp.sqrt(col_mass_panel)
    pairs = col_panel // 2
    inv_pairs = inv_col.reshape(pairs, 1, 2 * bsize)
    own_pair = jnp.broadcast_to(own_inv.reshape(1, own * bsize), (vecs, own * bsize))
    row_mass_spread = jnp.broadcast_to(row_mass[:, None, :], (own, vecs, bsize)).reshape(vec_rows, LANES)
    fwd_hot = (fwd_ids[None, :] == jnp.arange(row_panel)[:, None]).astype(jnp.float32)
    bwd_hot = (bwd_ids[None, :] == jnp.arange(col_panel)[:, None]).astype(jnp.float32)
    for step in range(ITERS):
        if step == 0:
            scaled = first_panel
        else:
            paired = (current * inv_pairs).astype(jnp.bfloat16)
            scaled = paired.reshape(pairs, vecs, 2, bsize).transpose(0, 2, 1, 3).reshape(col_panel, vecs, bsize)
        forward_taken = jnp.take(scaled, cols_idx, axis=0)
        forward_product = jnp.einsum(
            "bij,bkj->bki", square, forward_taken, preferred_element_type=jnp.float32
        )
        forward_summed = jnp.einsum(
            "rs,ski->rki", fwd_hot, forward_product, precision=lax.Precision.HIGH,
            preferred_element_type=jnp.float32,
        )
        flat = forward_summed.reshape(row_panel * vecs * bsize // LANES, LANES)
        weighted = forward_reduce(flat, row_mass_spread, n_col, 1).reshape(row_panel, vecs, bsize)
        taken = jnp.take(weighted, rows_idx, axis=0)
        product = jnp.einsum("bij,bki->bkj", square, taken, preferred_element_type=jnp.float32)
        summed = jnp.einsum(
            "pbs,skj->pkbj", bwd_hot.reshape(pairs, 2, n_cap), product,
            precision=lax.Precision.HIGH, preferred_element_type=jnp.float32,
        ).reshape(pairs, vecs, 2 * bsize)
        current = backward_reduce(summed, own_pair, n_row, n_col, 1.0 / total_boxes, 2)
    me = lax.axis_index("row")
    mine = lax.dynamic_index_in_dim(current, me, 0, keepdims=False)
    return mine.reshape(vecs, own, bsize).transpose(1, 0, 2).reshape(own, vecs * bsize)


def solution(mesh):
    in_specs = (
        P("row", "col", None, None),
        P("row", "col", None),
        P("row", "col", None),
        P("row", "col"),
        P(("col", "row"), None),
        P(("row", "col"), None),
        P(("col", "row"), None),
    )
    out_specs = P(("col", "row"), None)
    return jax.shard_map(
        per_device, mesh=mesh, in_specs=in_specs, out_specs=out_specs, check_vma=False
    )
```

```python
import functools

import jax
import jax.numpy as jnp
from jax import lax
from jax.experimental import pallas as pl
from jax.experimental.pallas import tpu as pltpu
from jax.sharding import PartitionSpec as P

ITERS = 4
LANES = 512
MESH_ID = pl.DeviceIdType.MESH


def _peer(axis, other, p):
    them = lax.axis_index(other)
    return (p, them) if axis == "row" else (them, p)


def _reduce_kernel(axis, other, n, ch, two_phase, x_ref, o_ref, recv, mine, gath, s1, r1, s2, r2):
    me = lax.axis_index(axis)
    barrier = pltpu.get_barrier_semaphore()
    for d in range(1, n):
        pl.semaphore_signal(
            barrier, 1, device_id=_peer(axis, other, (me + d) % n), device_id_type=MESH_ID
        )
    pl.semaphore_wait(barrier, n - 1)
    if not two_phase:
        sends = []
        for d in range(1, n):
            c = pltpu.make_async_remote_copy(
                x_ref, recv.at[d], s1.at[d], r1.at[d],
                device_id=_peer(axis, other, (me + d) % n), device_id_type=MESH_ID,
            )
            c.start()
            sends.append(c)
        for c in sends:
            c.wait()
        recv[0] = x_ref[...]
        acc = recv[me % n]
        for p in range(1, n):
            acc = acc + recv[(me - p + n) % n]
        o_ref[...] = acc
        return
    sends = []
    for d in range(1, n):
        peer = (me + d) % n
        start = pl.multiple_of(peer * ch, ch)
        c = pltpu.make_async_remote_copy(
            x_ref.at[pl.ds(start, ch)], recv.at[d], s1.at[d], r1.at[d],
            device_id=_peer(axis, other, peer), device_id_type=MESH_ID,
        )
        c.start()
        sends.append(c)
    own = pl.multiple_of(me * ch, ch)
    acc = x_ref[pl.ds(own, ch), :]
    for d, c in enumerate(sends, 1):
        c.wait()
        acc = acc + recv[d]
    mine[...] = acc
    gathers = []
    for d in range(1, n):
        c = pltpu.make_async_remote_copy(
            mine, gath.at[d], s2.at[d], r2.at[d],
            device_id=_peer(axis, other, (me + d) % n), device_id_type=MESH_ID,
        )
        c.start()
        gathers.append(c)
    o_ref[pl.ds(own, ch), :] = acc
    for d, c in enumerate(gathers, 1):
        c.wait()
        src = pl.multiple_of(((me - d + n) % n) * ch, ch)
        o_ref[pl.ds(src, ch), :] = gath[d]


def _gather_kernel(axis, other, n, x_ref, o_ref, gath, s2, r2):
    me = lax.axis_index(axis)
    ch = x_ref.shape[0]
    barrier = pltpu.get_barrier_semaphore()
    for d in range(1, n):
        pl.semaphore_signal(
            barrier, 1, device_id=_peer(axis, other, (me + d) % n), device_id_type=MESH_ID
        )
    pl.semaphore_wait(barrier, n - 1)
    gathers = []
    for d in range(1, n):
        c = pltpu.make_async_remote_copy(
            x_ref, gath.at[d], s2.at[d], r2.at[d],
            device_id=_peer(axis, other, (me + d) % n), device_id_type=MESH_ID,
        )
        c.start()
        gathers.append(c)
    o_ref[pl.ds(pl.multiple_of(me * ch, ch), ch), :] = x_ref[...]
    for d, c in enumerate(gathers, 1):
        c.wait()
        src = pl.multiple_of(((me - d + n) % n) * ch, ch)
        o_ref[pl.ds(src, ch), :] = gath[d]


def all_gather(x, axis, other, n, collective_id):
    ch, lanes = x.shape
    return pl.pallas_call(
        functools.partial(_gather_kernel, axis, other, n),
        out_shape=jax.ShapeDtypeStruct((n * ch, lanes), x.dtype),
        in_specs=[pl.BlockSpec(memory_space=pltpu.VMEM)],
        out_specs=pl.BlockSpec(memory_space=pltpu.VMEM),
        scratch_shapes=[
            pltpu.VMEM((n, ch, lanes), x.dtype),
            pltpu.SemaphoreType.DMA((n,)),
            pltpu.SemaphoreType.DMA((n,)),
        ],
        compiler_params=pltpu.CompilerParams(collective_id=collective_id, has_side_effects=True),
    )(x)


def _forward_kernel(n, ch, x_ref, mass_ref, o_ref, recv, mine, gath, s1, r1, s2, r2):
    axis, other = "col", "row"
    me = lax.axis_index(axis)
    barrier = pltpu.get_barrier_semaphore()
    for d in range(1, n):
        pl.semaphore_signal(
            barrier, 1, device_id=_peer(axis, other, (me + d) % n), device_id_type=MESH_ID
        )
    pl.semaphore_wait(barrier, n - 1)
    sends = []
    for d in range(1, n):
        peer = (me + d) % n
        start = pl.multiple_of(peer * ch, ch)
        c = pltpu.make_async_remote_copy(
            x_ref.at[pl.ds(start, ch)], recv.at[d], s1.at[d], r1.at[d],
            device_id=_peer(axis, other, peer), device_id_type=MESH_ID,
        )
        c.start()
        sends.append(c)
    own = pl.multiple_of(me * ch, ch)
    acc = x_ref[pl.ds(own, ch), :]
    for d, c in enumerate(sends, 1):
        c.wait()
        acc = acc + recv[d]
    mine[...] = (acc * mass_ref[...]).astype(mine.dtype)
    gathers = []
    for d in range(1, n):
        c = pltpu.make_async_remote_copy(
            mine, gath.at[d], s2.at[d], r2.at[d],
            device_id=_peer(axis, other, (me + d) % n), device_id_type=MESH_ID,
        )
        c.start()
        gathers.append(c)
    o_ref[pl.ds(own, ch), :] = mine[...]
    for d, c in enumerate(gathers, 1):
        c.wait()
        src = pl.multiple_of(((me - d + n) % n) * ch, ch)
        o_ref[pl.ds(src, ch), :] = gath[d]


def forward_reduce(x, mass, n, collective_id):
    rows, lanes = x.shape
    ch = rows // n
    return pl.pallas_call(
        functools.partial(_forward_kernel, n, ch),
        out_shape=jax.ShapeDtypeStruct(x.shape, jnp.bfloat16),
        in_specs=[pl.BlockSpec(memory_space=pltpu.VMEM)] * 2,
        out_specs=pl.BlockSpec(memory_space=pltpu.VMEM),
        scratch_shapes=[
            pltpu.VMEM((n, ch, lanes), x.dtype),
            pltpu.VMEM((ch, lanes), jnp.bfloat16),
            pltpu.VMEM((n, ch, lanes), jnp.bfloat16),
            pltpu.SemaphoreType.DMA((n,)),
            pltpu.SemaphoreType.DMA((n,)),
            pltpu.SemaphoreType.DMA((n,)),
            pltpu.SemaphoreType.DMA((n,)),
        ],
        compiler_params=pltpu.CompilerParams(collective_id=collective_id, has_side_effects=True),
    )(x, mass)


def _gather2_kernel(axis, other, n, x_ref, y_ref, o_ref, p_ref, gx, gy, sx, rx, sy, ry):
    me = lax.axis_index(axis)
    cx = x_ref.shape[0]
    cy = y_ref.shape[0]
    barrier = pltpu.get_barrier_semaphore()
    for d in range(1, n):
        pl.semaphore_signal(
            barrier, 1, device_id=_peer(axis, other, (me + d) % n), device_id_type=MESH_ID
        )
    pl.semaphore_wait(barrier, n - 1)
    copies = []
    for d in range(1, n):
        peer = _peer(axis, other, (me + d) % n)
        a = pltpu.make_async_remote_copy(
            x_ref, gx.at[d], sx.at[d], rx.at[d], device_id=peer, device_id_type=MESH_ID
        )
        b = pltpu.make_async_remote_copy(
            y_ref, gy.at[d], sy.at[d], ry.at[d], device_id=peer, device_id_type=MESH_ID
        )
        a.start()
        b.start()
        copies.append((a, b))
    o_ref[pl.ds(pl.multiple_of(me * cx, cx), cx), :] = x_ref[...]
    p_ref[pl.ds(pl.multiple_of(me * cy, cy), cy), :] = y_ref[...]
    for d, (a, b) in enumerate(copies, 1):
        a.wait()
        b.wait()
        src = (me - d + n) % n
        o_ref[pl.ds(pl.multiple_of(src * cx, cx), cx), :] = gx[d]
        p_ref[pl.ds(pl.multiple_of(src * cy, cy), cy), :] = gy[d]


def all_gather2(x, y, axis, other, n, collective_id):
    return pl.pallas_call(
        functools.partial(_gather2_kernel, axis, other, n),
        out_shape=(
            jax.ShapeDtypeStruct((n * x.shape[0], x.shape[1]), x.dtype),
            jax.ShapeDtypeStruct((n * y.shape[0], y.shape[1]), y.dtype),
        ),
        in_specs=[pl.BlockSpec(memory_space=pltpu.VMEM)] * 2,
        out_specs=(pl.BlockSpec(memory_space=pltpu.VMEM),) * 2,
        scratch_shapes=[
            pltpu.VMEM((n,) + x.shape, x.dtype),
            pltpu.VMEM((n,) + y.shape, y.dtype),
            pltpu.SemaphoreType.DMA((n,)),
            pltpu.SemaphoreType.DMA((n,)),
            pltpu.SemaphoreType.DMA((n,)),
            pltpu.SemaphoreType.DMA((n,)),
        ],
        compiler_params=pltpu.CompilerParams(collective_id=collective_id, has_side_effects=True),
    )(x, y)


def _gram_of(a):
    return lax.dot_general(
        a, a, (((1,), (1,)), ((), ())), precision=lax.Precision.HIGHEST,
        preferred_element_type=jnp.float32,
    )


def chol_inverse(a):
    n = a.shape[0]
    r = lax.broadcasted_iota(jnp.int32, (n, n), 0)
    c = lax.broadcasted_iota(jnp.int32, (n, n), 1)
    r1 = lax.broadcasted_iota(jnp.int32, (n, 1), 0)
    c1 = lax.broadcasted_iota(jnp.int32, (1, n), 1)
    x0 = jnp.where(r == c, 1.0, 0.0).astype(jnp.float32)

    def step(j, carry):
        m, x = carry
        col = jnp.sum(jnp.where(c == j, m, 0.0), axis=1, keepdims=True)
        row = jnp.sum(jnp.where(r == j, m, 0.0), axis=0, keepdims=True)
        inv = 1.0 / jnp.sqrt(jnp.sum(jnp.where(c1 == j, row, 0.0), axis=1, keepdims=True))
        lcol = jnp.where(r1 >= j, col * inv, 0.0)
        lrow = jnp.where(c1 >= j, row * inv, 0.0)
        m = m - lcol * lrow
        xrow = jnp.sum(jnp.where(r == j, x, 0.0), axis=0, keepdims=True) * inv
        x = jnp.where(r == j, xrow, x)
        x = x - jnp.where(r1 > j, lcol, 0.0) * xrow
        return m, x

    m, x = lax.fori_loop(0, n, step, (a, x0))
    return x


def _backward_kernel(n, m, scale, x_ref, icol_ref, o_ref, recv, gath, g3, s1, r1, s2, r2, s3, r3):
    me = lax.axis_index("row")
    mc = lax.axis_index("col")
    barrier = pltpu.get_barrier_semaphore()
    for d in range(1, n):
        pl.semaphore_signal(barrier, 1, device_id=((me + d) % n, mc), device_id_type=MESH_ID)
    for d in range(1, m):
        pl.semaphore_signal(barrier, 1, device_id=(me, (mc + d) % m), device_id_type=MESH_ID)
    pl.semaphore_wait(barrier, n - 1 + m - 1)
    sends = []
    for d in range(1, n):
        peer = (me + d) % n
        c = pltpu.make_async_remote_copy(
            x_ref.at[peer], recv.at[d], s1.at[d], r1.at[d],
            device_id=(peer, mc), device_id_type=MESH_ID,
        )
        c.start()
        sends.append(c)
    acc = x_ref[me]
    for d, c in enumerate(sends, 1):
        c.wait()
        acc = acc + recv[d]
    gath[0] = acc * icol_ref[...]
    gathers = []
    for d in range(1, n):
        c = pltpu.make_async_remote_copy(
            gath.at[0], gath.at[d], s2.at[d], r2.at[d],
            device_id=((me + d) % n, mc), device_id_type=MESH_ID,
        )
        c.start()
        gathers.append(c)
    for c in gathers:
        c.wait()
    g = None
    for p in range(n):
        term = _gram_of(gath[(me - p + n) % n])
        g = term if g is None else g + term
    g3[0] = g
    grams = []
    for d in range(1, m):
        c = pltpu.make_async_remote_copy(
            g3.at[0], g3.at[d], s3.at[d], r3.at[d],
            device_id=(me, (mc + d) % m), device_id_type=MESH_ID,
        )
        c.start()
        grams.append(c)
    for c in grams:
        c.wait()
    total = g3[mc % m]
    for q in range(1, m):
        total = total + g3[(mc - q + m) % m]
    inverse = chol_inverse(total * scale)
    for p in range(n):
        o_ref[p] = lax.dot_general(
            inverse, gath[(me - p + n) % n], (((1,), (0,)), ((), ())),
            precision=lax.Precision.HIGHEST, preferred_element_type=jnp.float32,
        )


def backward_reduce(x, icol, n, m, scale, collective_id):
    chunks, vecs, lanes = x.shape
    return pl.pallas_call(
        functools.partial(_backward_kernel, n, m, scale),
        out_shape=jax.ShapeDtypeStruct(x.shape, jnp.float32),
        in_specs=[pl.BlockSpec(memory_space=pltpu.VMEM)] * 2,
        out_specs=pl.BlockSpec(memory_space=pltpu.VMEM),
        scratch_shapes=[
            pltpu.VMEM((n, vecs, lanes), jnp.float32),
            pltpu.VMEM((n, vecs, lanes), jnp.float32),
            pltpu.VMEM((m, vecs, vecs), jnp.float32),
            pltpu.SemaphoreType.DMA((n,)),
            pltpu.SemaphoreType.DMA((n,)),
            pltpu.SemaphoreType.DMA((n,)),
            pltpu.SemaphoreType.DMA((n,)),
            pltpu.SemaphoreType.DMA((m,)),
            pltpu.SemaphoreType.DMA((m,)),
        ],
        compiler_params=pltpu.CompilerParams(collective_id=collective_id, has_side_effects=True),
    )(x, icol)


def all_reduce(x, axis, other, n, collective_id, two_phase=True):
    rows, lanes = x.shape
    ch = rows // n if two_phase else rows
    slots = ch if two_phase else rows
    return pl.pallas_call(
        functools.partial(_reduce_kernel, axis, other, n, ch, two_phase),
        out_shape=jax.ShapeDtypeStruct(x.shape, x.dtype),
        in_specs=[pl.BlockSpec(memory_space=pltpu.VMEM)],
        out_specs=pl.BlockSpec(memory_space=pltpu.VMEM),
        scratch_shapes=[
            pltpu.VMEM((n, slots, lanes), x.dtype),
            pltpu.VMEM((ch, lanes), x.dtype),
            pltpu.VMEM((n, ch, lanes), x.dtype),
            pltpu.SemaphoreType.DMA((n,)),
            pltpu.SemaphoreType.DMA((n,)),
            pltpu.SemaphoreType.DMA((n,)),
            pltpu.SemaphoreType.DMA((n,)),
        ],
        compiler_params=pltpu.CompilerParams(collective_id=collective_id, has_side_effects=True),
    )(x)


def rotate(projected, gram):
    lower = jnp.linalg.cholesky(gram)
    inverse = lax.linalg.triangular_solve(
        lower, jnp.eye(gram.shape[0], dtype=jnp.float32), left_side=True, lower=True
    )
    return jnp.einsum(
        "kl,bli->bki",
        inverse,
        projected,
        precision=lax.Precision.HIGHEST,
        preferred_element_type=jnp.float32,
    )


def rotate_pairs(projected, gram):
    lower = jnp.linalg.cholesky(gram)
    inverse = lax.linalg.triangular_solve(
        lower, jnp.eye(gram.shape[0], dtype=jnp.float32), left_side=True, lower=True
    )
    return jnp.einsum(
        "kl,plx->pkx",
        inverse,
        projected,
        precision=lax.Precision.HIGHEST,
        preferred_element_type=jnp.float32,
    )


def local_gram(projected):
    return jnp.einsum(
        "bki,bli->kl",
        projected,
        projected,
        precision=lax.Precision.HIGHEST,
        preferred_element_type=jnp.float32,
    )


def panel_sum(partial, axis, other, n, collective_id):
    blocks, vecs, bsize = partial.shape
    flat = partial.reshape(blocks * vecs * bsize // LANES, LANES)
    return all_reduce(flat, axis, other, n, collective_id).reshape(blocks, vecs, bsize)


def per_device(blocks, block_row, block_col, counts, vectors, row_mass, col_mass):
    tile = blocks[0, 0]
    n_cap = tile.shape[0]
    bsize = row_mass.shape[1]
    vecs = vectors.shape[1] // bsize
    own = vectors.shape[0]
    n_row = lax.axis_size("row")
    n_col = lax.axis_size("col")
    row_panel = own * n_col
    col_panel = own * n_row
    total_boxes = float(own * bsize * n_row * n_col)
    rows_idx = block_row[0, 0]
    cols_idx = block_col[0, 0]
    live = jnp.arange(n_cap) < counts[0, 0]
    fwd_ids = jnp.where(live, rows_idx, row_panel)
    bwd_ids = jnp.where(live, cols_idx, col_panel)
    square = tile.reshape(n_cap, bsize, bsize)
    vec_rows = own * vecs * bsize // LANES
    own_inv = 1.0 / jnp.sqrt(col_mass)
    first = (vectors.reshape(own, vecs, bsize) * own_inv[:, None, :]).astype(jnp.bfloat16)
    mass_pad = jnp.zeros((8, 128), jnp.float32).at[0, : own * bsize].set(col_mass.reshape(-1))
    got, mass_got = all_gather2(first.reshape(vec_rows, LANES), mass_pad, "row", "col", n_row, 4)
    first_panel = got.reshape(col_panel, vecs, bsize)
    col_mass_panel = mass_got.reshape(n_row, 8, 128)[:, 0, : own * bsize].reshape(col_panel, bsize)
    inv_col = 1.0 / jnp.sqrt(col_mass_panel)
    pairs = col_panel // 2
    inv_pairs = inv_col.reshape(pairs, 1, 2 * bsize)
    own_pair = jnp.broadcast_to(own_inv.reshape(1, own * bsize), (vecs, own * bsize))
    row_mass_spread = jnp.broadcast_to(row_mass[:, None, :], (own, vecs, bsize)).reshape(vec_rows, LANES)
    fwd_hot = (fwd_ids[None, :] == jnp.arange(row_panel)[:, None]).astype(jnp.float32)
    bwd_hot = (bwd_ids[None, :] == jnp.arange(col_panel)[:, None]).astype(jnp.float32)
    for step in range(ITERS):
        if step == 0:
            scaled = first_panel
        else:
            paired = (current * inv_pairs).astype(jnp.bfloat16)
            scaled = paired.reshape(pairs, vecs, 2, bsize).transpose(0, 2, 1, 3).reshape(col_panel, vecs, bsize)
        forward_taken = jnp.take(scaled, cols_idx, axis=0)
        forward_product = jnp.einsum(
            "bij,bkj->bki", square, forward_taken, preferred_element_type=jnp.float32
        )
        forward_summed = jnp.einsum(
            "rs,ski->rki", fwd_hot, forward_product, precision=lax.Precision.HIGH,
            preferred_element_type=jnp.float32,
        )
        flat = forward_summed.reshape(row_panel * vecs * bsize // LANES, LANES)
        weighted = forward_reduce(flat, row_mass_spread, n_col, 1).reshape(row_panel, vecs, bsize)
        taken = jnp.take(weighted, rows_idx, axis=0)
        product = jnp.einsum("bij,bki->bkj", square, taken, preferred_element_type=jnp.float32)
        summed = jnp.einsum(
            "pbs,skj->pkbj", bwd_hot.reshape(pairs, 2, n_cap), product,
            precision=lax.Precision.HIGH, preferred_element_type=jnp.float32,
        ).reshape(pairs, vecs, 2 * bsize)
        current = backward_reduce(summed, own_pair, n_row, n_col, 1.0 / total_boxes, 2)
    me = lax.axis_index("row")
    mine = lax.dynamic_index_in_dim(current, me, 0, keepdims=False)
    return mine.reshape(vecs, own, bsize).transpose(1, 0, 2).reshape(own, vecs * bsize)


def solution(mesh):
    in_specs = (
        P("row", "col", None, None),
        P("row", "col", None),
        P("row", "col", None),
        P("row", "col"),
        P(("col", "row"), None),
        P(("row", "col"), None),
        P(("col", "row"), None),
    )
    out_specs = P(("col", "row"), None)
    return jax.shard_map(
        per_device, mesh=mesh, in_specs=in_specs, out_specs=out_specs, check_vma=False
    )
```

```python
import functools

import jax
import jax.numpy as jnp
from jax import lax
from jax.experimental import pallas as pl
from jax.experimental.pallas import tpu as pltpu
from jax.sharding import PartitionSpec as P

ITERS = 4
LANES = 512
MESH_ID = pl.DeviceIdType.MESH


def _peer(axis, other, p):
    them = lax.axis_index(other)
    return (p, them) if axis == "row" else (them, p)


def _reduce_kernel(axis, other, n, ch, two_phase, x_ref, o_ref, recv, mine, gath, s1, r1, s2, r2):
    me = lax.axis_index(axis)
    barrier = pltpu.get_barrier_semaphore()
    for d in range(1, n):
        pl.semaphore_signal(
            barrier, 1, device_id=_peer(axis, other, (me + d) % n), device_id_type=MESH_ID
        )
    pl.semaphore_wait(barrier, n - 1)
    if not two_phase:
        sends = []
        for d in range(1, n):
            c = pltpu.make_async_remote_copy(
                x_ref, recv.at[d], s1.at[d], r1.at[d],
                device_id=_peer(axis, other, (me + d) % n), device_id_type=MESH_ID,
            )
            c.start()
            sends.append(c)
        for c in sends:
            c.wait()
        recv[0] = x_ref[...]
        acc = recv[me % n]
        for p in range(1, n):
            acc = acc + recv[(me - p + n) % n]
        o_ref[...] = acc
        return
    sends = []
    for d in range(1, n):
        peer = (me + d) % n
        start = pl.multiple_of(peer * ch, ch)
        c = pltpu.make_async_remote_copy(
            x_ref.at[pl.ds(start, ch)], recv.at[d], s1.at[d], r1.at[d],
            device_id=_peer(axis, other, peer), device_id_type=MESH_ID,
        )
        c.start()
        sends.append(c)
    own = pl.multiple_of(me * ch, ch)
    acc = x_ref[pl.ds(own, ch), :]
    for d, c in enumerate(sends, 1):
        c.wait()
        acc = acc + recv[d]
    mine[...] = acc
    gathers = []
    for d in range(1, n):
        c = pltpu.make_async_remote_copy(
            mine, gath.at[d], s2.at[d], r2.at[d],
            device_id=_peer(axis, other, (me + d) % n), device_id_type=MESH_ID,
        )
        c.start()
        gathers.append(c)
    o_ref[pl.ds(own, ch), :] = acc
    for d, c in enumerate(gathers, 1):
        c.wait()
        src = pl.multiple_of(((me - d + n) % n) * ch, ch)
        o_ref[pl.ds(src, ch), :] = gath[d]


def _gather_kernel(axis, other, n, x_ref, o_ref, gath, s2, r2):
    me = lax.axis_index(axis)
    ch = x_ref.shape[0]
    barrier = pltpu.get_barrier_semaphore()
    for d in range(1, n):
        pl.semaphore_signal(
            barrier, 1, device_id=_peer(axis, other, (me + d) % n), device_id_type=MESH_ID
        )
    pl.semaphore_wait(barrier, n - 1)
    gathers = []
    for d in range(1, n):
        c = pltpu.make_async_remote_copy(
            x_ref, gath.at[d], s2.at[d], r2.at[d],
            device_id=_peer(axis, other, (me + d) % n), device_id_type=MESH_ID,
        )
        c.start()
        gathers.append(c)
    o_ref[pl.ds(pl.multiple_of(me * ch, ch), ch), :] = x_ref[...]
    for d, c in enumerate(gathers, 1):
        c.wait()
        src = pl.multiple_of(((me - d + n) % n) * ch, ch)
        o_ref[pl.ds(src, ch), :] = gath[d]


def all_gather(x, axis, other, n, collective_id):
    ch, lanes = x.shape
    return pl.pallas_call(
        functools.partial(_gather_kernel, axis, other, n),
        out_shape=jax.ShapeDtypeStruct((n * ch, lanes), x.dtype),
        in_specs=[pl.BlockSpec(memory_space=pltpu.VMEM)],
        out_specs=pl.BlockSpec(memory_space=pltpu.VMEM),
        scratch_shapes=[
            pltpu.VMEM((n, ch, lanes), x.dtype),
            pltpu.SemaphoreType.DMA((n,)),
            pltpu.SemaphoreType.DMA((n,)),
        ],
        compiler_params=pltpu.CompilerParams(collective_id=collective_id, has_side_effects=True),
    )(x)


def _forward_kernel(n, ch, x_ref, mass_ref, o_ref, recv, mine, gath, s1, r1, s2, r2):
    axis, other = "col", "row"
    me = lax.axis_index(axis)
    barrier = pltpu.get_barrier_semaphore()
    for d in range(1, n):
        pl.semaphore_signal(
            barrier, 1, device_id=_peer(axis, other, (me + d) % n), device_id_type=MESH_ID
        )
    pl.semaphore_wait(barrier, n - 1)
    sends = []
    for d in range(1, n):
        peer = (me + d) % n
        start = pl.multiple_of(peer * ch, ch)
        c = pltpu.make_async_remote_copy(
            x_ref.at[pl.ds(start, ch)], recv.at[d], s1.at[d], r1.at[d],
            device_id=_peer(axis, other, peer), device_id_type=MESH_ID,
        )
        c.start()
        sends.append(c)
    own = pl.multiple_of(me * ch, ch)
    acc = x_ref[pl.ds(own, ch), :]
    for d, c in enumerate(sends, 1):
        c.wait()
        acc = acc + recv[d]
    mine[...] = (acc * mass_ref[...]).astype(mine.dtype)
    gathers = []
    for d in range(1, n):
        c = pltpu.make_async_remote_copy(
            mine, gath.at[d], s2.at[d], r2.at[d],
            device_id=_peer(axis, other, (me + d) % n), device_id_type=MESH_ID,
        )
        c.start()
        gathers.append(c)
    o_ref[pl.ds(own, ch), :] = mine[...]
    for d, c in enumerate(gathers, 1):
        c.wait()
        src = pl.multiple_of(((me - d + n) % n) * ch, ch)
        o_ref[pl.ds(src, ch), :] = gath[d]


def forward_reduce(x, mass, n, collective_id):
    rows, lanes = x.shape
    ch = rows // n
    return pl.pallas_call(
        functools.partial(_forward_kernel, n, ch),
        out_shape=jax.ShapeDtypeStruct(x.shape, jnp.bfloat16),
        in_specs=[pl.BlockSpec(memory_space=pltpu.VMEM)] * 2,
        out_specs=pl.BlockSpec(memory_space=pltpu.VMEM),
        scratch_shapes=[
            pltpu.VMEM((n, ch, lanes), x.dtype),
            pltpu.VMEM((ch, lanes), jnp.bfloat16),
            pltpu.VMEM((n, ch, lanes), jnp.bfloat16),
            pltpu.SemaphoreType.DMA((n,)),
            pltpu.SemaphoreType.DMA((n,)),
            pltpu.SemaphoreType.DMA((n,)),
            pltpu.SemaphoreType.DMA((n,)),
        ],
        compiler_params=pltpu.CompilerParams(collective_id=collective_id, has_side_effects=True),
    )(x, mass)


def _gather2_kernel(axis, other, n, x_ref, y_ref, o_ref, p_ref, gx, gy, sx, rx, sy, ry):
    me = lax.axis_index(axis)
    cx = x_ref.shape[0]
    cy = y_ref.shape[0]
    barrier = pltpu.get_barrier_semaphore()
    for d in range(1, n):
        pl.semaphore_signal(
            barrier, 1, device_id=_peer(axis, other, (me + d) % n), device_id_type=MESH_ID
        )
    pl.semaphore_wait(barrier, n - 1)
    copies = []
    for d in range(1, n):
        peer = _peer(axis, other, (me + d) % n)
        a = pltpu.make_async_remote_copy(
            x_ref, gx.at[d], sx.at[d], rx.at[d], device_id=peer, device_id_type=MESH_ID
        )
        b = pltpu.make_async_remote_copy(
            y_ref, gy.at[d], sy.at[d], ry.at[d], device_id=peer, device_id_type=MESH_ID
        )
        a.start()
        b.start()
        copies.append((a, b))
    o_ref[pl.ds(pl.multiple_of(me * cx, cx), cx), :] = x_ref[...]
    p_ref[pl.ds(pl.multiple_of(me * cy, cy), cy), :] = y_ref[...]
    for d, (a, b) in enumerate(copies, 1):
        a.wait()
        b.wait()
        src = (me - d + n) % n
        o_ref[pl.ds(pl.multiple_of(src * cx, cx), cx), :] = gx[d]
        p_ref[pl.ds(pl.multiple_of(src * cy, cy), cy), :] = gy[d]


def all_gather2(x, y, axis, other, n, collective_id):
    return pl.pallas_call(
        functools.partial(_gather2_kernel, axis, other, n),
        out_shape=(
            jax.ShapeDtypeStruct((n * x.shape[0], x.shape[1]), x.dtype),
            jax.ShapeDtypeStruct((n * y.shape[0], y.shape[1]), y.dtype),
        ),
        in_specs=[pl.BlockSpec(memory_space=pltpu.VMEM)] * 2,
        out_specs=(pl.BlockSpec(memory_space=pltpu.VMEM),) * 2,
        scratch_shapes=[
            pltpu.VMEM((n,) + x.shape, x.dtype),
            pltpu.VMEM((n,) + y.shape, y.dtype),
            pltpu.SemaphoreType.DMA((n,)),
            pltpu.SemaphoreType.DMA((n,)),
            pltpu.SemaphoreType.DMA((n,)),
            pltpu.SemaphoreType.DMA((n,)),
        ],
        compiler_params=pltpu.CompilerParams(collective_id=collective_id, has_side_effects=True),
    )(x, y)


def _gram_of(a):
    return lax.dot_general(
        a, a, (((1,), (1,)), ((), ())), precision=lax.Precision.HIGHEST,
        preferred_element_type=jnp.float32,
    )


def chol_inverse(a):
    n = a.shape[0]
    r = lax.broadcasted_iota(jnp.int32, (n, n), 0)
    c = lax.broadcasted_iota(jnp.int32, (n, n), 1)
    r1 = lax.broadcasted_iota(jnp.int32, (n, 1), 0)
    c1 = lax.broadcasted_iota(jnp.int32, (1, n), 1)
    x0 = jnp.where(r == c, 1.0, 0.0).astype(jnp.float32)

    def step(j, carry):
        m, x = carry
        col = jnp.sum(jnp.where(c == j, m, 0.0), axis=1, keepdims=True)
        row = jnp.sum(jnp.where(r == j, m, 0.0), axis=0, keepdims=True)
        piv = jnp.sqrt(jnp.sum(jnp.where(r1 == j, col, 0.0), axis=0, keepdims=True))
        lcol = jnp.where(r1 >= j, col / piv, 0.0)
        lrow = jnp.where(c1 >= j, row / piv, 0.0)
        m = m - lcol * lrow
        xrow = jnp.sum(jnp.where(r == j, x, 0.0), axis=0, keepdims=True) / piv
        x = jnp.where(r == j, xrow, x)
        x = x - jnp.where(r1 > j, lcol, 0.0) * xrow
        return m, x

    m, x = lax.fori_loop(0, n, step, (a, x0))
    return x


def _backward_kernel(n, m, scale, x_ref, icol_ref, o_ref, recv, gath, gp, g3, s1, r1, s2, r2, s3, r3, s4, r4):
    me = lax.axis_index("row")
    mc = lax.axis_index("col")
    barrier = pltpu.get_barrier_semaphore()
    for d in range(1, n):
        pl.semaphore_signal(barrier, 1, device_id=((me + d) % n, mc), device_id_type=MESH_ID)
    for d in range(1, m):
        pl.semaphore_signal(barrier, 1, device_id=(me, (mc + d) % m), device_id_type=MESH_ID)
    pl.semaphore_wait(barrier, n - 1 + m - 1)
    sends = []
    for d in range(1, n):
        peer = (me + d) % n
        c = pltpu.make_async_remote_copy(
            x_ref.at[peer], recv.at[d], s1.at[d], r1.at[d],
            device_id=(peer, mc), device_id_type=MESH_ID,
        )
        c.start()
        sends.append(c)
    acc = x_ref[me]
    for d, c in enumerate(sends, 1):
        c.wait()
        acc = acc + recv[d]
    gath[0] = acc * icol_ref[...]
    gp[0] = _gram_of(gath[0])
    grams = []
    for d in range(1, n):
        c = pltpu.make_async_remote_copy(
            gp.at[0], gp.at[d], s4.at[d], r4.at[d],
            device_id=((me + d) % n, mc), device_id_type=MESH_ID,
        )
        c.start()
        grams.append(c)
    gathers = []
    for d in range(1, n):
        c = pltpu.make_async_remote_copy(
            gath.at[0], gath.at[d], s2.at[d], r2.at[d],
            device_id=((me + d) % n, mc), device_id_type=MESH_ID,
        )
        c.start()
        gathers.append(c)
    for c in grams:
        c.wait()
    g = gp[me % n]
    for p in range(1, n):
        g = g + gp[(me - p + n) % n]
    g3[0] = g
    cols = []
    for d in range(1, m):
        c = pltpu.make_async_remote_copy(
            g3.at[0], g3.at[d], s3.at[d], r3.at[d],
            device_id=(me, (mc + d) % m), device_id_type=MESH_ID,
        )
        c.start()
        cols.append(c)
    for c in cols:
        c.wait()
    total = g3[mc % m]
    for q in range(1, m):
        total = total + g3[(mc - q + m) % m]
    inverse = chol_inverse(total * scale)
    for c in gathers:
        c.wait()
    for p in range(n):
        o_ref[p] = lax.dot_general(
            inverse, gath[(me - p + n) % n], (((1,), (0,)), ((), ())),
            precision=lax.Precision.HIGHEST, preferred_element_type=jnp.float32,
        )


def backward_reduce(x, icol, n, m, scale, collective_id):
    chunks, vecs, lanes = x.shape
    return pl.pallas_call(
        functools.partial(_backward_kernel, n, m, scale),
        out_shape=jax.ShapeDtypeStruct(x.shape, jnp.float32),
        in_specs=[pl.BlockSpec(memory_space=pltpu.VMEM)] * 2,
        out_specs=pl.BlockSpec(memory_space=pltpu.VMEM),
        scratch_shapes=[
            pltpu.VMEM((n, vecs, lanes), jnp.float32),
            pltpu.VMEM((n, vecs, lanes), jnp.float32),
            pltpu.VMEM((n, vecs, vecs), jnp.float32),
            pltpu.VMEM((m, vecs, vecs), jnp.float32),
            pltpu.SemaphoreType.DMA((n,)),
            pltpu.SemaphoreType.DMA((n,)),
            pltpu.SemaphoreType.DMA((n,)),
            pltpu.SemaphoreType.DMA((n,)),
            pltpu.SemaphoreType.DMA((m,)),
            pltpu.SemaphoreType.DMA((m,)),
            pltpu.SemaphoreType.DMA((n,)),
            pltpu.SemaphoreType.DMA((n,)),
        ],
        compiler_params=pltpu.CompilerParams(collective_id=collective_id, has_side_effects=True),
    )(x, icol)


def all_reduce(x, axis, other, n, collective_id, two_phase=True):
    rows, lanes = x.shape
    ch = rows // n if two_phase else rows
    slots = ch if two_phase else rows
    return pl.pallas_call(
        functools.partial(_reduce_kernel, axis, other, n, ch, two_phase),
        out_shape=jax.ShapeDtypeStruct(x.shape, x.dtype),
        in_specs=[pl.BlockSpec(memory_space=pltpu.VMEM)],
        out_specs=pl.BlockSpec(memory_space=pltpu.VMEM),
        scratch_shapes=[
            pltpu.VMEM((n, slots, lanes), x.dtype),
            pltpu.VMEM((ch, lanes), x.dtype),
            pltpu.VMEM((n, ch, lanes), x.dtype),
            pltpu.SemaphoreType.DMA((n,)),
            pltpu.SemaphoreType.DMA((n,)),
            pltpu.SemaphoreType.DMA((n,)),
            pltpu.SemaphoreType.DMA((n,)),
        ],
        compiler_params=pltpu.CompilerParams(collective_id=collective_id, has_side_effects=True),
    )(x)


def rotate(projected, gram):
    lower = jnp.linalg.cholesky(gram)
    inverse = lax.linalg.triangular_solve(
        lower, jnp.eye(gram.shape[0], dtype=jnp.float32), left_side=True, lower=True
    )
    return jnp.einsum(
        "kl,bli->bki",
        inverse,
        projected,
        precision=lax.Precision.HIGHEST,
        preferred_element_type=jnp.float32,
    )


def rotate_pairs(projected, gram):
    lower = jnp.linalg.cholesky(gram)
    inverse = lax.linalg.triangular_solve(
        lower, jnp.eye(gram.shape[0], dtype=jnp.float32), left_side=True, lower=True
    )
    return jnp.einsum(
        "kl,plx->pkx",
        inverse,
        projected,
        precision=lax.Precision.HIGHEST,
        preferred_element_type=jnp.float32,
    )


def local_gram(projected):
    return jnp.einsum(
        "bki,bli->kl",
        projected,
        projected,
        precision=lax.Precision.HIGHEST,
        preferred_element_type=jnp.float32,
    )


def panel_sum(partial, axis, other, n, collective_id):
    blocks, vecs, bsize = partial.shape
    flat = partial.reshape(blocks * vecs * bsize // LANES, LANES)
    return all_reduce(flat, axis, other, n, collective_id).reshape(blocks, vecs, bsize)


def per_device(blocks, block_row, block_col, counts, vectors, row_mass, col_mass):
    tile = blocks[0, 0]
    n_cap = tile.shape[0]
    bsize = row_mass.shape[1]
    vecs = vectors.shape[1] // bsize
    own = vectors.shape[0]
    n_row = lax.axis_size("row")
    n_col = lax.axis_size("col")
    row_panel = own * n_col
    col_panel = own * n_row
    total_boxes = float(own * bsize * n_row * n_col)
    rows_idx = block_row[0, 0]
    cols_idx = block_col[0, 0]
    live = jnp.arange(n_cap) < counts[0, 0]
    fwd_ids = jnp.where(live, rows_idx, row_panel)
    bwd_ids = jnp.where(live, cols_idx, col_panel)
    square = tile.reshape(n_cap, bsize, bsize)
    vec_rows = own * vecs * bsize // LANES
    own_inv = 1.0 / jnp.sqrt(col_mass)
    first = (vectors.reshape(own, vecs, bsize) * own_inv[:, None, :]).astype(jnp.bfloat16)
    mass_pad = jnp.zeros((8, 128), jnp.float32).at[0, : own * bsize].set(col_mass.reshape(-1))
    got, mass_got = all_gather2(first.reshape(vec_rows, LANES), mass_pad, "row", "col", n_row, 4)
    first_panel = got.reshape(col_panel, vecs, bsize)
    col_mass_panel = mass_got.reshape(n_row, 8, 128)[:, 0, : own * bsize].reshape(col_panel, bsize)
    inv_col = 1.0 / jnp.sqrt(col_mass_panel)
    pairs = col_panel // 2
    inv_pairs = inv_col.reshape(pairs, 1, 2 * bsize)
    own_pair = jnp.broadcast_to(own_inv.reshape(1, own * bsize), (vecs, own * bsize))
    row_mass_spread = jnp.broadcast_to(row_mass[:, None, :], (own, vecs, bsize)).reshape(vec_rows, LANES)
    fwd_hot = (fwd_ids[None, :] == jnp.arange(row_panel)[:, None]).astype(jnp.float32)
    bwd_hot = (bwd_ids[None, :] == jnp.arange(col_panel)[:, None]).astype(jnp.float32)
    for step in range(ITERS):
        if step == 0:
            scaled = first_panel
        else:
            paired = (current * inv_pairs).astype(jnp.bfloat16)
            scaled = paired.reshape(pairs, vecs, 2, bsize).transpose(0, 2, 1, 3).reshape(col_panel, vecs, bsize)
        forward_taken = jnp.take(scaled, cols_idx, axis=0)
        forward_product = jnp.einsum(
            "bij,bkj->bki", square, forward_taken, preferred_element_type=jnp.float32
        )
        forward_summed = jnp.einsum(
            "rs,ski->rki", fwd_hot, forward_product, precision=lax.Precision.HIGH,
            preferred_element_type=jnp.float32,
        )
        flat = forward_summed.reshape(row_panel * vecs * bsize // LANES, LANES)
        weighted = forward_reduce(flat, row_mass_spread, n_col, 1).reshape(row_panel, vecs, bsize)
        taken = jnp.take(weighted, rows_idx, axis=0)
        product = jnp.einsum("bij,bki->bkj", square, taken, preferred_element_type=jnp.float32)
        summed = jnp.einsum(
            "pbs,skj->pkbj", bwd_hot.reshape(pairs, 2, n_cap), product,
            precision=lax.Precision.HIGH, preferred_element_type=jnp.float32,
        ).reshape(pairs, vecs, 2 * bsize)
        current = backward_reduce(summed, own_pair, n_row, n_col, 1.0 / total_boxes, 2)
    me = lax.axis_index("row")
    mine = lax.dynamic_index_in_dim(current, me, 0, keepdims=False)
    return mine.reshape(vecs, own, bsize).transpose(1, 0, 2).reshape(own, vecs * bsize)


def solution(mesh):
    in_specs = (
        P("row", "col", None, None),
        P("row", "col", None),
        P("row", "col", None),
        P("row", "col"),
        P(("col", "row"), None),
        P(("row", "col"), None),
        P(("col", "row"), None),
    )
    out_specs = P(("col", "row"), None)
    return jax.shard_map(
        per_device, mesh=mesh, in_specs=in_specs, out_specs=out_specs, check_vma=False
    )
```

```python
import functools

import jax
import jax.numpy as jnp
from jax import lax
from jax.experimental import pallas as pl
from jax.experimental.pallas import tpu as pltpu
from jax.sharding import PartitionSpec as P

ITERS = 4
LANES = 512
MESH_ID = pl.DeviceIdType.MESH


def _peer(axis, other, p):
    them = lax.axis_index(other)
    return (p, them) if axis == "row" else (them, p)


def _reduce_kernel(axis, other, n, ch, two_phase, x_ref, o_ref, recv, mine, gath, s1, r1, s2, r2):
    me = lax.axis_index(axis)
    barrier = pltpu.get_barrier_semaphore()
    for d in range(1, n):
        pl.semaphore_signal(
            barrier, 1, device_id=_peer(axis, other, (me + d) % n), device_id_type=MESH_ID
        )
    pl.semaphore_wait(barrier, n - 1)
    if not two_phase:
        sends = []
        for d in range(1, n):
            c = pltpu.make_async_remote_copy(
                x_ref, recv.at[d], s1.at[d], r1.at[d],
                device_id=_peer(axis, other, (me + d) % n), device_id_type=MESH_ID,
            )
            c.start()
            sends.append(c)
        for c in sends:
            c.wait()
        recv[0] = x_ref[...]
        acc = recv[me % n]
        for p in range(1, n):
            acc = acc + recv[(me - p + n) % n]
        o_ref[...] = acc
        return
    sends = []
    for d in range(1, n):
        peer = (me + d) % n
        start = pl.multiple_of(peer * ch, ch)
        c = pltpu.make_async_remote_copy(
            x_ref.at[pl.ds(start, ch)], recv.at[d], s1.at[d], r1.at[d],
            device_id=_peer(axis, other, peer), device_id_type=MESH_ID,
        )
        c.start()
        sends.append(c)
    own = pl.multiple_of(me * ch, ch)
    acc = x_ref[pl.ds(own, ch), :]
    for d, c in enumerate(sends, 1):
        c.wait()
        acc = acc + recv[d]
    mine[...] = acc
    gathers = []
    for d in range(1, n):
        c = pltpu.make_async_remote_copy(
            mine, gath.at[d], s2.at[d], r2.at[d],
            device_id=_peer(axis, other, (me + d) % n), device_id_type=MESH_ID,
        )
        c.start()
        gathers.append(c)
    o_ref[pl.ds(own, ch), :] = acc
    for d, c in enumerate(gathers, 1):
        c.wait()
        src = pl.multiple_of(((me - d + n) % n) * ch, ch)
        o_ref[pl.ds(src, ch), :] = gath[d]


def _gather_kernel(axis, other, n, x_ref, o_ref, gath, s2, r2):
    me = lax.axis_index(axis)
    ch = x_ref.shape[0]
    barrier = pltpu.get_barrier_semaphore()
    for d in range(1, n):
        pl.semaphore_signal(
            barrier, 1, device_id=_peer(axis, other, (me + d) % n), device_id_type=MESH_ID
        )
    pl.semaphore_wait(barrier, n - 1)
    gathers = []
    for d in range(1, n):
        c = pltpu.make_async_remote_copy(
            x_ref, gath.at[d], s2.at[d], r2.at[d],
            device_id=_peer(axis, other, (me + d) % n), device_id_type=MESH_ID,
        )
        c.start()
        gathers.append(c)
    o_ref[pl.ds(pl.multiple_of(me * ch, ch), ch), :] = x_ref[...]
    for d, c in enumerate(gathers, 1):
        c.wait()
        src = pl.multiple_of(((me - d + n) % n) * ch, ch)
        o_ref[pl.ds(src, ch), :] = gath[d]


def all_gather(x, axis, other, n, collective_id):
    ch, lanes = x.shape
    return pl.pallas_call(
        functools.partial(_gather_kernel, axis, other, n),
        out_shape=jax.ShapeDtypeStruct((n * ch, lanes), x.dtype),
        in_specs=[pl.BlockSpec(memory_space=pltpu.VMEM)],
        out_specs=pl.BlockSpec(memory_space=pltpu.VMEM),
        scratch_shapes=[
            pltpu.VMEM((n, ch, lanes), x.dtype),
            pltpu.SemaphoreType.DMA((n,)),
            pltpu.SemaphoreType.DMA((n,)),
        ],
        compiler_params=pltpu.CompilerParams(collective_id=collective_id, has_side_effects=True),
    )(x)


def _forward_kernel(n, ch, x_ref, mass_ref, o_ref, recv, mine, gath, s1, r1, s2, r2):
    axis, other = "col", "row"
    me = lax.axis_index(axis)
    barrier = pltpu.get_barrier_semaphore()
    for d in range(1, n):
        pl.semaphore_signal(
            barrier, 1, device_id=_peer(axis, other, (me + d) % n), device_id_type=MESH_ID
        )
    pl.semaphore_wait(barrier, n - 1)
    sends = []
    for d in range(1, n):
        peer = (me + d) % n
        start = pl.multiple_of(peer * ch, ch)
        c = pltpu.make_async_remote_copy(
            x_ref.at[pl.ds(start, ch)], recv.at[d], s1.at[d], r1.at[d],
            device_id=_peer(axis, other, peer), device_id_type=MESH_ID,
        )
        c.start()
        sends.append(c)
    own = pl.multiple_of(me * ch, ch)
    acc = x_ref[pl.ds(own, ch), :]
    for d, c in enumerate(sends, 1):
        c.wait()
        acc = acc + recv[d]
    mine[...] = (acc * mass_ref[...]).astype(mine.dtype)
    gathers = []
    for d in range(1, n):
        c = pltpu.make_async_remote_copy(
            mine, gath.at[d], s2.at[d], r2.at[d],
            device_id=_peer(axis, other, (me + d) % n), device_id_type=MESH_ID,
        )
        c.start()
        gathers.append(c)
    o_ref[pl.ds(own, ch), :] = mine[...]
    for d, c in enumerate(gathers, 1):
        c.wait()
        src = pl.multiple_of(((me - d + n) % n) * ch, ch)
        o_ref[pl.ds(src, ch), :] = gath[d]


def forward_reduce(x, mass, n, collective_id):
    rows, lanes = x.shape
    ch = rows // n
    return pl.pallas_call(
        functools.partial(_forward_kernel, n, ch),
        out_shape=jax.ShapeDtypeStruct(x.shape, jnp.bfloat16),
        in_specs=[pl.BlockSpec(memory_space=pltpu.VMEM)] * 2,
        out_specs=pl.BlockSpec(memory_space=pltpu.VMEM),
        scratch_shapes=[
            pltpu.VMEM((n, ch, lanes), x.dtype),
            pltpu.VMEM((ch, lanes), jnp.bfloat16),
            pltpu.VMEM((n, ch, lanes), jnp.bfloat16),
            pltpu.SemaphoreType.DMA((n,)),
            pltpu.SemaphoreType.DMA((n,)),
            pltpu.SemaphoreType.DMA((n,)),
            pltpu.SemaphoreType.DMA((n,)),
        ],
        compiler_params=pltpu.CompilerParams(collective_id=collective_id, has_side_effects=True),
    )(x, mass)


def _gather2_kernel(axis, other, n, x_ref, y_ref, o_ref, p_ref, gx, gy, sx, rx, sy, ry):
    me = lax.axis_index(axis)
    cx = x_ref.shape[0]
    cy = y_ref.shape[0]
    barrier = pltpu.get_barrier_semaphore()
    for d in range(1, n):
        pl.semaphore_signal(
            barrier, 1, device_id=_peer(axis, other, (me + d) % n), device_id_type=MESH_ID
        )
    pl.semaphore_wait(barrier, n - 1)
    copies = []
    for d in range(1, n):
        peer = _peer(axis, other, (me + d) % n)
        a = pltpu.make_async_remote_copy(
            x_ref, gx.at[d], sx.at[d], rx.at[d], device_id=peer, device_id_type=MESH_ID
        )
        b = pltpu.make_async_remote_copy(
            y_ref, gy.at[d], sy.at[d], ry.at[d], device_id=peer, device_id_type=MESH_ID
        )
        a.start()
        b.start()
        copies.append((a, b))
    o_ref[pl.ds(pl.multiple_of(me * cx, cx), cx), :] = x_ref[...]
    p_ref[pl.ds(pl.multiple_of(me * cy, cy), cy), :] = y_ref[...]
    for d, (a, b) in enumerate(copies, 1):
        a.wait()
        b.wait()
        src = (me - d + n) % n
        o_ref[pl.ds(pl.multiple_of(src * cx, cx), cx), :] = gx[d]
        p_ref[pl.ds(pl.multiple_of(src * cy, cy), cy), :] = gy[d]


def all_gather2(x, y, axis, other, n, collective_id):
    return pl.pallas_call(
        functools.partial(_gather2_kernel, axis, other, n),
        out_shape=(
            jax.ShapeDtypeStruct((n * x.shape[0], x.shape[1]), x.dtype),
            jax.ShapeDtypeStruct((n * y.shape[0], y.shape[1]), y.dtype),
        ),
        in_specs=[pl.BlockSpec(memory_space=pltpu.VMEM)] * 2,
        out_specs=(pl.BlockSpec(memory_space=pltpu.VMEM),) * 2,
        scratch_shapes=[
            pltpu.VMEM((n,) + x.shape, x.dtype),
            pltpu.VMEM((n,) + y.shape, y.dtype),
            pltpu.SemaphoreType.DMA((n,)),
            pltpu.SemaphoreType.DMA((n,)),
            pltpu.SemaphoreType.DMA((n,)),
            pltpu.SemaphoreType.DMA((n,)),
        ],
        compiler_params=pltpu.CompilerParams(collective_id=collective_id, has_side_effects=True),
    )(x, y)


def _gram_of(a):
    return lax.dot_general(
        a, a, (((1,), (1,)), ((), ())), precision=lax.Precision.HIGHEST,
        preferred_element_type=jnp.float32,
    )


def chol_inverse(a):
    n = a.shape[0]
    r = lax.broadcasted_iota(jnp.int32, (n, n), 0)
    c = lax.broadcasted_iota(jnp.int32, (n, n), 1)
    r1 = lax.broadcasted_iota(jnp.int32, (n, 1), 0)
    c1 = lax.broadcasted_iota(jnp.int32, (1, n), 1)
    x0 = jnp.where(r == c, 1.0, 0.0).astype(jnp.float32)

    def step(j, carry):
        m, x = carry
        col = jnp.sum(jnp.where(c == j, m, 0.0), axis=1, keepdims=True)
        row = jnp.sum(jnp.where(r == j, m, 0.0), axis=0, keepdims=True)
        piv = jnp.sqrt(jnp.sum(jnp.where(r1 == j, col, 0.0), axis=0, keepdims=True))
        lcol = jnp.where(r1 >= j, col / piv, 0.0)
        lrow = jnp.where(c1 >= j, row / piv, 0.0)
        m = m - lcol * lrow
        xrow = jnp.sum(jnp.where(r == j, x, 0.0), axis=0, keepdims=True) / piv
        x = jnp.where(r == j, xrow, x)
        x = x - jnp.where(r1 > j, lcol, 0.0) * xrow
        return m, x

    m, x = lax.fori_loop(0, n, step, (a, x0))
    return x


def _backward_kernel(n, m, scale, x_ref, icol_ref, o_ref, recv, gath, g3, s1, r1, s2, r2, s3, r3):
    me = lax.axis_index("row")
    mc = lax.axis_index("col")
    barrier = pltpu.get_barrier_semaphore()
    for d in range(1, n):
        pl.semaphore_signal(barrier, 1, device_id=((me + d) % n, mc), device_id_type=MESH_ID)
    for d in range(1, m):
        pl.semaphore_signal(barrier, 1, device_id=(me, (mc + d) % m), device_id_type=MESH_ID)
    pl.semaphore_wait(barrier, n - 1 + m - 1)
    sends = []
    for d in range(1, n):
        peer = (me + d) % n
        c = pltpu.make_async_remote_copy(
            x_ref.at[peer], recv.at[d], s1.at[d], r1.at[d],
            device_id=(peer, mc), device_id_type=MESH_ID,
        )
        c.start()
        sends.append(c)
    acc = x_ref[me]
    for d, c in enumerate(sends, 1):
        c.wait()
        acc = acc + recv[d]
    gath[0] = acc * icol_ref[...]
    gathers = []
    for d in range(1, n):
        c = pltpu.make_async_remote_copy(
            gath.at[0], gath.at[d], s2.at[d], r2.at[d],
            device_id=((me + d) % n, mc), device_id_type=MESH_ID,
        )
        c.start()
        gathers.append(c)
    for c in gathers:
        c.wait()
    g = None
    for p in range(n):
        term = _gram_of(gath[(me - p + n) % n])
        g = term if g is None else g + term
    g3[0] = g
    grams = []
    for d in range(1, m):
        c = pltpu.make_async_remote_copy(
            g3.at[0], g3.at[d], s3.at[d], r3.at[d],
            device_id=(me, (mc + d) % m), device_id_type=MESH_ID,
        )
        c.start()
        grams.append(c)
    for c in grams:
        c.wait()
    total = g3[mc % m]
    for q in range(1, m):
        total = total + g3[(mc - q + m) % m]
    inverse = chol_inverse(total * scale)
    for p in range(n):
        o_ref[p] = lax.dot_general(
            inverse, gath[(me - p + n) % n], (((1,), (0,)), ((), ())),
            precision=lax.Precision.HIGHEST, preferred_element_type=jnp.float32,
        )


def backward_reduce(x, icol, n, m, scale, collective_id):
    chunks, vecs, lanes = x.shape
    return pl.pallas_call(
        functools.partial(_backward_kernel, n, m, scale),
        out_shape=jax.ShapeDtypeStruct(x.shape, jnp.float32),
        in_specs=[pl.BlockSpec(memory_space=pltpu.VMEM)] * 2,
        out_specs=pl.BlockSpec(memory_space=pltpu.VMEM),
        scratch_shapes=[
            pltpu.VMEM((n, vecs, lanes), jnp.float32),
            pltpu.VMEM((n, vecs, lanes), jnp.float32),
            pltpu.VMEM((m, vecs, vecs), jnp.float32),
            pltpu.SemaphoreType.DMA((n,)),
            pltpu.SemaphoreType.DMA((n,)),
            pltpu.SemaphoreType.DMA((n,)),
            pltpu.SemaphoreType.DMA((n,)),
            pltpu.SemaphoreType.DMA((m,)),
            pltpu.SemaphoreType.DMA((m,)),
        ],
        compiler_params=pltpu.CompilerParams(collective_id=collective_id, has_side_effects=True),
    )(x, icol)


def all_reduce(x, axis, other, n, collective_id, two_phase=True):
    rows, lanes = x.shape
    ch = rows // n if two_phase else rows
    slots = ch if two_phase else rows
    return pl.pallas_call(
        functools.partial(_reduce_kernel, axis, other, n, ch, two_phase),
        out_shape=jax.ShapeDtypeStruct(x.shape, x.dtype),
        in_specs=[pl.BlockSpec(memory_space=pltpu.VMEM)],
        out_specs=pl.BlockSpec(memory_space=pltpu.VMEM),
        scratch_shapes=[
            pltpu.VMEM((n, slots, lanes), x.dtype),
            pltpu.VMEM((ch, lanes), x.dtype),
            pltpu.VMEM((n, ch, lanes), x.dtype),
            pltpu.SemaphoreType.DMA((n,)),
            pltpu.SemaphoreType.DMA((n,)),
            pltpu.SemaphoreType.DMA((n,)),
            pltpu.SemaphoreType.DMA((n,)),
        ],
        compiler_params=pltpu.CompilerParams(collective_id=collective_id, has_side_effects=True),
    )(x)


def rotate(projected, gram):
    lower = jnp.linalg.cholesky(gram)
    inverse = lax.linalg.triangular_solve(
        lower, jnp.eye(gram.shape[0], dtype=jnp.float32), left_side=True, lower=True
    )
    return jnp.einsum(
        "kl,bli->bki",
        inverse,
        projected,
        precision=lax.Precision.HIGHEST,
        preferred_element_type=jnp.float32,
    )


def rotate_pairs(projected, gram):
    lower = jnp.linalg.cholesky(gram)
    inverse = lax.linalg.triangular_solve(
        lower, jnp.eye(gram.shape[0], dtype=jnp.float32), left_side=True, lower=True
    )
    return jnp.einsum(
        "kl,plx->pkx",
        inverse,
        projected,
        precision=lax.Precision.HIGHEST,
        preferred_element_type=jnp.float32,
    )


def local_gram(projected):
    return jnp.einsum(
        "bki,bli->kl",
        projected,
        projected,
        precision=lax.Precision.HIGHEST,
        preferred_element_type=jnp.float32,
    )


def panel_sum(partial, axis, other, n, collective_id):
    blocks, vecs, bsize = partial.shape
    flat = partial.reshape(blocks * vecs * bsize // LANES, LANES)
    return all_reduce(flat, axis, other, n, collective_id).reshape(blocks, vecs, bsize)


def per_device(blocks, block_row, block_col, counts, vectors, row_mass, col_mass):
    tile = blocks[0, 0]
    n_cap = tile.shape[0]
    bsize = row_mass.shape[1]
    vecs = vectors.shape[1] // bsize
    own = vectors.shape[0]
    n_row = lax.axis_size("row")
    n_col = lax.axis_size("col")
    row_panel = own * n_col
    col_panel = own * n_row
    total_boxes = float(own * bsize * n_row * n_col)
    rows_idx = block_row[0, 0]
    cols_idx = block_col[0, 0]
    live = jnp.arange(n_cap) < counts[0, 0]
    fwd_ids = jnp.where(live, rows_idx, row_panel)
    bwd_ids = jnp.where(live, cols_idx, col_panel)
    square = tile.reshape(n_cap, bsize, bsize)
    vec_rows = own * vecs * bsize // LANES
    own_inv = 1.0 / jnp.sqrt(col_mass)
    first = (vectors.reshape(own, vecs, bsize) * own_inv[:, None, :]).astype(jnp.bfloat16)
    mass_pad = jnp.zeros((8, 128), jnp.float32).at[0, : own * bsize].set(col_mass.reshape(-1))
    got, mass_got = all_gather2(first.reshape(vec_rows, LANES), mass_pad, "row", "col", n_row, 4)
    first_panel = got.reshape(col_panel, vecs, bsize)
    col_mass_panel = mass_got.reshape(n_row, 8, 128)[:, 0, : own * bsize].reshape(col_panel, bsize)
    inv_col = 1.0 / jnp.sqrt(col_mass_panel)
    pairs = col_panel // 2
    inv_pairs = inv_col.reshape(pairs, 1, 2 * bsize)
    own_pair = jnp.broadcast_to(own_inv.reshape(1, own * bsize), (vecs, own * bsize))
    row_mass_spread = jnp.broadcast_to(row_mass[:, None, :], (own, vecs, bsize)).reshape(vec_rows, LANES)
    fwd_hot = (fwd_ids[None, :] == jnp.arange(row_panel)[:, None]).astype(jnp.float32)
    bwd_hot = (bwd_ids[None, :] == jnp.arange(col_panel)[:, None]).astype(jnp.float32)
    def iteration(step, carry):
        scaled, unused = carry
        forward_taken = jnp.take(scaled, cols_idx, axis=0)
        forward_product = jnp.einsum(
            "bij,bkj->bki", square, forward_taken, preferred_element_type=jnp.float32
        )
        forward_summed = jnp.einsum(
            "rs,ski->rki", fwd_hot, forward_product, precision=lax.Precision.HIGH,
            preferred_element_type=jnp.float32,
        )
        flat = forward_summed.reshape(row_panel * vecs * bsize // LANES, LANES)
        weighted = forward_reduce(flat, row_mass_spread, n_col, 1).reshape(row_panel, vecs, bsize)
        taken = jnp.take(weighted, rows_idx, axis=0)
        product = jnp.einsum("bij,bki->bkj", square, taken, preferred_element_type=jnp.float32)
        summed = jnp.einsum(
            "pbs,skj->pkbj", bwd_hot.reshape(pairs, 2, n_cap), product,
            precision=lax.Precision.HIGH, preferred_element_type=jnp.float32,
        ).reshape(pairs, vecs, 2 * bsize)
        current = backward_reduce(summed, own_pair, n_row, n_col, 1.0 / total_boxes, 2)
        paired = (current * inv_pairs).astype(jnp.bfloat16)
        scaled = paired.reshape(pairs, vecs, 2, bsize).transpose(0, 2, 1, 3).reshape(col_panel, vecs, bsize)
        return scaled, current

    start = jnp.zeros((pairs, vecs, 2 * bsize), jnp.float32)
    unused, current = lax.fori_loop(0, ITERS, iteration, (first_panel, start))
    me = lax.axis_index("row")
    mine = lax.dynamic_index_in_dim(current, me, 0, keepdims=False)
    return mine.reshape(vecs, own, bsize).transpose(1, 0, 2).reshape(own, vecs * bsize)


def solution(mesh):
    in_specs = (
        P("row", "col", None, None),
        P("row", "col", None),
        P("row", "col", None),
        P("row", "col"),
        P(("col", "row"), None),
        P(("row", "col"), None),
        P(("col", "row"), None),
    )
    out_specs = P(("col", "row"), None)
    return jax.shard_map(
        per_device, mesh=mesh, in_specs=in_specs, out_specs=out_specs, check_vma=False
    )
```

```python
import functools

import jax
import jax.numpy as jnp
from jax import lax
from jax.experimental import pallas as pl
from jax.experimental.pallas import tpu as pltpu
from jax.sharding import PartitionSpec as P

ITERS = 4
LANES = 512
MESH_ID = pl.DeviceIdType.MESH


def _peer(axis, other, p):
    them = lax.axis_index(other)
    return (p, them) if axis == "row" else (them, p)


def _reduce_kernel(axis, other, n, ch, two_phase, x_ref, o_ref, recv, mine, gath, s1, r1, s2, r2):
    me = lax.axis_index(axis)
    barrier = pltpu.get_barrier_semaphore()
    for d in range(1, n):
        pl.semaphore_signal(
            barrier, 1, device_id=_peer(axis, other, (me + d) % n), device_id_type=MESH_ID
        )
    pl.semaphore_wait(barrier, n - 1)
    if not two_phase:
        sends = []
        for d in range(1, n):
            c = pltpu.make_async_remote_copy(
                x_ref, recv.at[d], s1.at[d], r1.at[d],
                device_id=_peer(axis, other, (me + d) % n), device_id_type=MESH_ID,
            )
            c.start()
            sends.append(c)
        for c in sends:
            c.wait()
        recv[0] = x_ref[...]
        acc = recv[me % n]
        for p in range(1, n):
            acc = acc + recv[(me - p + n) % n]
        o_ref[...] = acc
        return
    sends = []
    for d in range(1, n):
        peer = (me + d) % n
        start = pl.multiple_of(peer * ch, ch)
        c = pltpu.make_async_remote_copy(
            x_ref.at[pl.ds(start, ch)], recv.at[d], s1.at[d], r1.at[d],
            device_id=_peer(axis, other, peer), device_id_type=MESH_ID,
        )
        c.start()
        sends.append(c)
    own = pl.multiple_of(me * ch, ch)
    acc = x_ref[pl.ds(own, ch), :]
    for d, c in enumerate(sends, 1):
        c.wait()
        acc = acc + recv[d]
    mine[...] = acc
    gathers = []
    for d in range(1, n):
        c = pltpu.make_async_remote_copy(
            mine, gath.at[d], s2.at[d], r2.at[d],
            device_id=_peer(axis, other, (me + d) % n), device_id_type=MESH_ID,
        )
        c.start()
        gathers.append(c)
    o_ref[pl.ds(own, ch), :] = acc
    for d, c in enumerate(gathers, 1):
        c.wait()
        src = pl.multiple_of(((me - d + n) % n) * ch, ch)
        o_ref[pl.ds(src, ch), :] = gath[d]


def _gather_kernel(axis, other, n, x_ref, o_ref, gath, s2, r2):
    me = lax.axis_index(axis)
    ch = x_ref.shape[0]
    barrier = pltpu.get_barrier_semaphore()
    for d in range(1, n):
        pl.semaphore_signal(
            barrier, 1, device_id=_peer(axis, other, (me + d) % n), device_id_type=MESH_ID
        )
    pl.semaphore_wait(barrier, n - 1)
    gathers = []
    for d in range(1, n):
        c = pltpu.make_async_remote_copy(
            x_ref, gath.at[d], s2.at[d], r2.at[d],
            device_id=_peer(axis, other, (me + d) % n), device_id_type=MESH_ID,
        )
        c.start()
        gathers.append(c)
    o_ref[pl.ds(pl.multiple_of(me * ch, ch), ch), :] = x_ref[...]
    for d, c in enumerate(gathers, 1):
        c.wait()
        src = pl.multiple_of(((me - d + n) % n) * ch, ch)
        o_ref[pl.ds(src, ch), :] = gath[d]


def all_gather(x, axis, other, n, collective_id):
    ch, lanes = x.shape
    return pl.pallas_call(
        functools.partial(_gather_kernel, axis, other, n),
        out_shape=jax.ShapeDtypeStruct((n * ch, lanes), x.dtype),
        in_specs=[pl.BlockSpec(memory_space=pltpu.VMEM)],
        out_specs=pl.BlockSpec(memory_space=pltpu.VMEM),
        scratch_shapes=[
            pltpu.VMEM((n, ch, lanes), x.dtype),
            pltpu.SemaphoreType.DMA((n,)),
            pltpu.SemaphoreType.DMA((n,)),
        ],
        compiler_params=pltpu.CompilerParams(collective_id=collective_id, has_side_effects=True),
    )(x)


def _forward_kernel(n, ch, x_ref, mass_ref, o_ref, recv, mine, gath, s1, r1, s2, r2):
    axis, other = "col", "row"
    me = lax.axis_index(axis)
    barrier = pltpu.get_barrier_semaphore()
    for d in range(1, n):
        pl.semaphore_signal(
            barrier, 1, device_id=_peer(axis, other, (me + d) % n), device_id_type=MESH_ID
        )
    pl.semaphore_wait(barrier, n - 1)
    sends = []
    for d in range(1, n):
        peer = (me + d) % n
        start = pl.multiple_of(peer * ch, ch)
        c = pltpu.make_async_remote_copy(
            x_ref.at[pl.ds(start, ch)], recv.at[d], s1.at[d], r1.at[d],
            device_id=_peer(axis, other, peer), device_id_type=MESH_ID,
        )
        c.start()
        sends.append(c)
    own = pl.multiple_of(me * ch, ch)
    acc = x_ref[pl.ds(own, ch), :]
    for d, c in enumerate(sends, 1):
        c.wait()
        acc = acc + recv[d]
    mine[...] = (acc * mass_ref[...]).astype(mine.dtype)
    gathers = []
    for d in range(1, n):
        c = pltpu.make_async_remote_copy(
            mine, gath.at[d], s2.at[d], r2.at[d],
            device_id=_peer(axis, other, (me + d) % n), device_id_type=MESH_ID,
        )
        c.start()
        gathers.append(c)
    o_ref[pl.ds(own, ch), :] = mine[...]
    for d, c in enumerate(gathers, 1):
        c.wait()
        src = pl.multiple_of(((me - d + n) % n) * ch, ch)
        o_ref[pl.ds(src, ch), :] = gath[d]


def forward_reduce(x, mass, n, collective_id):
    rows, lanes = x.shape
    ch = rows // n
    return pl.pallas_call(
        functools.partial(_forward_kernel, n, ch),
        out_shape=jax.ShapeDtypeStruct(x.shape, jnp.bfloat16),
        in_specs=[pl.BlockSpec(memory_space=pltpu.VMEM)] * 2,
        out_specs=pl.BlockSpec(memory_space=pltpu.VMEM),
        scratch_shapes=[
            pltpu.VMEM((n, ch, lanes), x.dtype),
            pltpu.VMEM((ch, lanes), jnp.bfloat16),
            pltpu.VMEM((n, ch, lanes), jnp.bfloat16),
            pltpu.SemaphoreType.DMA((n,)),
            pltpu.SemaphoreType.DMA((n,)),
            pltpu.SemaphoreType.DMA((n,)),
            pltpu.SemaphoreType.DMA((n,)),
        ],
        compiler_params=pltpu.CompilerParams(collective_id=collective_id, has_side_effects=True),
    )(x, mass)


def _gather2_kernel(axis, other, n, x_ref, y_ref, o_ref, p_ref, gx, gy, sx, rx, sy, ry):
    me = lax.axis_index(axis)
    cx = x_ref.shape[0]
    cy = y_ref.shape[0]
    barrier = pltpu.get_barrier_semaphore()
    for d in range(1, n):
        pl.semaphore_signal(
            barrier, 1, device_id=_peer(axis, other, (me + d) % n), device_id_type=MESH_ID
        )
    pl.semaphore_wait(barrier, n - 1)
    copies = []
    for d in range(1, n):
        peer = _peer(axis, other, (me + d) % n)
        a = pltpu.make_async_remote_copy(
            x_ref, gx.at[d], sx.at[d], rx.at[d], device_id=peer, device_id_type=MESH_ID
        )
        b = pltpu.make_async_remote_copy(
            y_ref, gy.at[d], sy.at[d], ry.at[d], device_id=peer, device_id_type=MESH_ID
        )
        a.start()
        b.start()
        copies.append((a, b))
    o_ref[pl.ds(pl.multiple_of(me * cx, cx), cx), :] = x_ref[...]
    p_ref[pl.ds(pl.multiple_of(me * cy, cy), cy), :] = y_ref[...]
    for d, (a, b) in enumerate(copies, 1):
        a.wait()
        b.wait()
        src = (me - d + n) % n
        o_ref[pl.ds(pl.multiple_of(src * cx, cx), cx), :] = gx[d]
        p_ref[pl.ds(pl.multiple_of(src * cy, cy), cy), :] = gy[d]


def all_gather2(x, y, axis, other, n, collective_id):
    return pl.pallas_call(
        functools.partial(_gather2_kernel, axis, other, n),
        out_shape=(
            jax.ShapeDtypeStruct((n * x.shape[0], x.shape[1]), x.dtype),
            jax.ShapeDtypeStruct((n * y.shape[0], y.shape[1]), y.dtype),
        ),
        in_specs=[pl.BlockSpec(memory_space=pltpu.VMEM)] * 2,
        out_specs=(pl.BlockSpec(memory_space=pltpu.VMEM),) * 2,
        scratch_shapes=[
            pltpu.VMEM((n,) + x.shape, x.dtype),
            pltpu.VMEM((n,) + y.shape, y.dtype),
            pltpu.SemaphoreType.DMA((n,)),
            pltpu.SemaphoreType.DMA((n,)),
            pltpu.SemaphoreType.DMA((n,)),
            pltpu.SemaphoreType.DMA((n,)),
        ],
        compiler_params=pltpu.CompilerParams(collective_id=collective_id, has_side_effects=True),
    )(x, y)


def _gram_of(a):
    return lax.dot_general(
        a, a, (((1,), (1,)), ((), ())), precision=lax.Precision.HIGHEST,
        preferred_element_type=jnp.float32,
    )


def chol_inverse(a):
    n = a.shape[0]
    r = lax.broadcasted_iota(jnp.int32, (n, n), 0)
    c = lax.broadcasted_iota(jnp.int32, (n, n), 1)
    r1 = lax.broadcasted_iota(jnp.int32, (n, 1), 0)
    c1 = lax.broadcasted_iota(jnp.int32, (1, n), 1)
    x0 = jnp.where(r == c, 1.0, 0.0).astype(jnp.float32)

    def step(j, carry):
        m, x = carry
        col = jnp.sum(jnp.where(c == j, m, 0.0), axis=1, keepdims=True)
        row = jnp.sum(jnp.where(r == j, m, 0.0), axis=0, keepdims=True)
        piv = jnp.sqrt(jnp.sum(jnp.where(r1 == j, col, 0.0), axis=0, keepdims=True))
        lcol = jnp.where(r1 >= j, col / piv, 0.0)
        lrow = jnp.where(c1 >= j, row / piv, 0.0)
        m = m - lcol * lrow
        xrow = jnp.sum(jnp.where(r == j, x, 0.0), axis=0, keepdims=True) / piv
        x = jnp.where(r == j, xrow, x)
        x = x - jnp.where(r1 > j, lcol, 0.0) * xrow
        return m, x

    m, x = lax.fori_loop(0, n, step, (a, x0))
    return x


def _backward_kernel(n, m, scale, x_ref, icol_ref, o_ref, recv, gath, g3, s1, r1, s2, r2, s3, r3):
    me = lax.axis_index("row")
    mc = lax.axis_index("col")
    barrier = pltpu.get_barrier_semaphore()
    for d in range(1, n):
        pl.semaphore_signal(barrier, 1, device_id=((me + d) % n, mc), device_id_type=MESH_ID)
    for d in range(1, m):
        pl.semaphore_signal(barrier, 1, device_id=(me, (mc + d) % m), device_id_type=MESH_ID)
    pl.semaphore_wait(barrier, n - 1 + m - 1)
    sends = []
    for d in range(1, n):
        peer = (me + d) % n
        c = pltpu.make_async_remote_copy(
            x_ref.at[peer], recv.at[d], s1.at[d], r1.at[d],
            device_id=(peer, mc), device_id_type=MESH_ID,
        )
        c.start()
        sends.append(c)
    acc = x_ref[me]
    for d, c in enumerate(sends, 1):
        c.wait()
        acc = acc + recv[d]
    gath[0] = acc * icol_ref[...]
    gathers = []
    for d in range(1, n):
        c = pltpu.make_async_remote_copy(
            gath.at[0], gath.at[d], s2.at[d], r2.at[d],
            device_id=((me + d) % n, mc), device_id_type=MESH_ID,
        )
        c.start()
        gathers.append(c)
    for c in gathers:
        c.wait()
    g = None
    for p in range(n):
        term = _gram_of(gath[(me - p + n) % n])
        g = term if g is None else g + term
    g3[0] = g
    grams = []
    for d in range(1, m):
        c = pltpu.make_async_remote_copy(
            g3.at[0], g3.at[d], s3.at[d], r3.at[d],
            device_id=(me, (mc + d) % m), device_id_type=MESH_ID,
        )
        c.start()
        grams.append(c)
    for c in grams:
        c.wait()
    total = g3[mc % m]
    for q in range(1, m):
        total = total + g3[(mc - q + m) % m]
    inverse = chol_inverse(total * scale)
    for p in range(n):
        o_ref[p] = lax.dot_general(
            inverse, gath[(me - p + n) % n], (((1,), (0,)), ((), ())),
            precision=lax.Precision.HIGHEST, preferred_element_type=jnp.float32,
        )


def backward_reduce(x, icol, n, m, scale, collective_id):
    chunks, vecs, lanes = x.shape
    return pl.pallas_call(
        functools.partial(_backward_kernel, n, m, scale),
        out_shape=jax.ShapeDtypeStruct(x.shape, jnp.float32),
        in_specs=[pl.BlockSpec(memory_space=pltpu.VMEM)] * 2,
        out_specs=pl.BlockSpec(memory_space=pltpu.VMEM),
        scratch_shapes=[
            pltpu.VMEM((n, vecs, lanes), jnp.float32),
            pltpu.VMEM((n, vecs, lanes), jnp.float32),
            pltpu.VMEM((m, vecs, vecs), jnp.float32),
            pltpu.SemaphoreType.DMA((n,)),
            pltpu.SemaphoreType.DMA((n,)),
            pltpu.SemaphoreType.DMA((n,)),
            pltpu.SemaphoreType.DMA((n,)),
            pltpu.SemaphoreType.DMA((m,)),
            pltpu.SemaphoreType.DMA((m,)),
        ],
        compiler_params=pltpu.CompilerParams(collective_id=collective_id, has_side_effects=True),
    )(x, icol)


def all_reduce(x, axis, other, n, collective_id, two_phase=True):
    rows, lanes = x.shape
    ch = rows // n if two_phase else rows
    slots = ch if two_phase else rows
    return pl.pallas_call(
        functools.partial(_reduce_kernel, axis, other, n, ch, two_phase),
        out_shape=jax.ShapeDtypeStruct(x.shape, x.dtype),
        in_specs=[pl.BlockSpec(memory_space=pltpu.VMEM)],
        out_specs=pl.BlockSpec(memory_space=pltpu.VMEM),
        scratch_shapes=[
            pltpu.VMEM((n, slots, lanes), x.dtype),
            pltpu.VMEM((ch, lanes), x.dtype),
            pltpu.VMEM((n, ch, lanes), x.dtype),
            pltpu.SemaphoreType.DMA((n,)),
            pltpu.SemaphoreType.DMA((n,)),
            pltpu.SemaphoreType.DMA((n,)),
            pltpu.SemaphoreType.DMA((n,)),
        ],
        compiler_params=pltpu.CompilerParams(collective_id=collective_id, has_side_effects=True),
    )(x)


def rotate(projected, gram):
    lower = jnp.linalg.cholesky(gram)
    inverse = lax.linalg.triangular_solve(
        lower, jnp.eye(gram.shape[0], dtype=jnp.float32), left_side=True, lower=True
    )
    return jnp.einsum(
        "kl,bli->bki",
        inverse,
        projected,
        precision=lax.Precision.HIGHEST,
        preferred_element_type=jnp.float32,
    )


def rotate_pairs(projected, gram):
    lower = jnp.linalg.cholesky(gram)
    inverse = lax.linalg.triangular_solve(
        lower, jnp.eye(gram.shape[0], dtype=jnp.float32), left_side=True, lower=True
    )
    return jnp.einsum(
        "kl,plx->pkx",
        inverse,
        projected,
        precision=lax.Precision.HIGHEST,
        preferred_element_type=jnp.float32,
    )


def local_gram(projected):
    return jnp.einsum(
        "bki,bli->kl",
        projected,
        projected,
        precision=lax.Precision.HIGHEST,
        preferred_element_type=jnp.float32,
    )


def panel_sum(partial, axis, other, n, collective_id):
    blocks, vecs, bsize = partial.shape
    flat = partial.reshape(blocks * vecs * bsize // LANES, LANES)
    return all_reduce(flat, axis, other, n, collective_id).reshape(blocks, vecs, bsize)


def per_device(blocks, block_row, block_col, counts, vectors, row_mass, col_mass):
    tile = blocks[0, 0]
    n_cap = tile.shape[0]
    bsize = row_mass.shape[1]
    vecs = vectors.shape[1] // bsize
    own = vectors.shape[0]
    n_row = lax.axis_size("row")
    n_col = lax.axis_size("col")
    row_panel = own * n_col
    col_panel = own * n_row
    total_boxes = float(own * bsize * n_row * n_col)
    rows_idx = block_row[0, 0]
    cols_idx = block_col[0, 0]
    live = jnp.arange(n_cap) < counts[0, 0]
    fwd_ids = jnp.where(live, rows_idx, row_panel)
    bwd_ids = jnp.where(live, cols_idx, col_panel)
    square = tile.reshape(n_cap, bsize, bsize)
    vec_rows = own * vecs * bsize // LANES
    own_inv = 1.0 / jnp.sqrt(col_mass)
    first = (vectors.reshape(own, vecs, bsize) * own_inv[:, None, :]).astype(jnp.bfloat16)
    mass_pad = jnp.zeros((8, 128), jnp.float32).at[0, : own * bsize].set(col_mass.reshape(-1))
    got, mass_got = all_gather2(first.reshape(vec_rows, LANES), mass_pad, "row", "col", n_row, 4)
    first_panel = got.reshape(col_panel, vecs, bsize)
    col_mass_panel = mass_got.reshape(n_row, 8, 128)[:, 0, : own * bsize].reshape(col_panel, bsize)
    inv_col = 1.0 / jnp.sqrt(col_mass_panel)
    pairs = col_panel // 2
    inv_pairs = inv_col.reshape(pairs, 1, 2 * bsize)
    own_pair = jnp.broadcast_to(own_inv.reshape(1, own * bsize), (vecs, own * bsize))
    row_mass_spread = jnp.broadcast_to(row_mass[:, None, :], (own, vecs, bsize)).reshape(vec_rows, LANES)
    fwd_hot = (fwd_ids[None, :] == jnp.arange(row_panel)[:, None]).astype(jnp.bfloat16)
    bwd_hot = (bwd_ids[None, :] == jnp.arange(col_panel)[:, None]).astype(jnp.bfloat16)
    for step in range(ITERS):
        if step == 0:
            scaled = first_panel
        else:
            paired = (current * inv_pairs).astype(jnp.bfloat16)
            scaled = paired.reshape(pairs, vecs, 2, bsize).transpose(0, 2, 1, 3).reshape(col_panel, vecs, bsize)
        forward_taken = jnp.take(scaled, cols_idx, axis=0)
        forward_product = jnp.einsum(
            "bij,bkj->bki", square, forward_taken, preferred_element_type=jnp.bfloat16
        )
        forward_summed = jnp.einsum(
            "rs,ski->rki", fwd_hot, forward_product, preferred_element_type=jnp.float32
        )
        flat = forward_summed.reshape(row_panel * vecs * bsize // LANES, LANES)
        weighted = forward_reduce(flat, row_mass_spread, n_col, 1).reshape(row_panel, vecs, bsize)
        taken = jnp.take(weighted, rows_idx, axis=0)
        product = jnp.einsum("bij,bki->bkj", square, taken, preferred_element_type=jnp.bfloat16)
        summed = jnp.einsum(
            "pbs,skj->pkbj", bwd_hot.reshape(pairs, 2, n_cap), product,
            preferred_element_type=jnp.float32,
        ).reshape(pairs, vecs, 2 * bsize)
        current = backward_reduce(summed, own_pair, n_row, n_col, 1.0 / total_boxes, 2)
    me = lax.axis_index("row")
    mine = lax.dynamic_index_in_dim(current, me, 0, keepdims=False)
    return mine.reshape(vecs, own, bsize).transpose(1, 0, 2).reshape(own, vecs * bsize)


def solution(mesh):
    in_specs = (
        P("row", "col", None, None),
        P("row", "col", None),
        P("row", "col", None),
        P("row", "col"),
        P(("col", "row"), None),
        P(("row", "col"), None),
        P(("col", "row"), None),
    )
    out_specs = P(("col", "row"), None)
    return jax.shard_map(
        per_device, mesh=mesh, in_specs=in_specs, out_specs=out_specs, check_vma=False
    )
```

```python
import functools

import jax
import jax.numpy as jnp
from jax import lax
from jax.experimental import pallas as pl
from jax.experimental.pallas import tpu as pltpu
from jax.sharding import PartitionSpec as P

ITERS = 4
LANES = 512
MESH_ID = pl.DeviceIdType.MESH


def _peer(axis, other, p):
    them = lax.axis_index(other)
    return (p, them) if axis == "row" else (them, p)


def _reduce_kernel(axis, other, n, ch, two_phase, x_ref, o_ref, recv, mine, gath, s1, r1, s2, r2):
    me = lax.axis_index(axis)
    barrier = pltpu.get_barrier_semaphore()
    for d in range(1, n):
        pl.semaphore_signal(
            barrier, 1, device_id=_peer(axis, other, (me + d) % n), device_id_type=MESH_ID
        )
    pl.semaphore_wait(barrier, n - 1)
    if not two_phase:
        sends = []
        for d in range(1, n):
            c = pltpu.make_async_remote_copy(
                x_ref, recv.at[d], s1.at[d], r1.at[d],
                device_id=_peer(axis, other, (me + d) % n), device_id_type=MESH_ID,
            )
            c.start()
            sends.append(c)
        for c in sends:
            c.wait()
        recv[0] = x_ref[...]
        acc = recv[me % n]
        for p in range(1, n):
            acc = acc + recv[(me - p + n) % n]
        o_ref[...] = acc
        return
    sends = []
    for d in range(1, n):
        peer = (me + d) % n
        start = pl.multiple_of(peer * ch, ch)
        c = pltpu.make_async_remote_copy(
            x_ref.at[pl.ds(start, ch)], recv.at[d], s1.at[d], r1.at[d],
            device_id=_peer(axis, other, peer), device_id_type=MESH_ID,
        )
        c.start()
        sends.append(c)
    own = pl.multiple_of(me * ch, ch)
    acc = x_ref[pl.ds(own, ch), :]
    for d, c in enumerate(sends, 1):
        c.wait()
        acc = acc + recv[d]
    mine[...] = acc
    gathers = []
    for d in range(1, n):
        c = pltpu.make_async_remote_copy(
            mine, gath.at[d], s2.at[d], r2.at[d],
            device_id=_peer(axis, other, (me + d) % n), device_id_type=MESH_ID,
        )
        c.start()
        gathers.append(c)
    o_ref[pl.ds(own, ch), :] = acc
    for d, c in enumerate(gathers, 1):
        c.wait()
        src = pl.multiple_of(((me - d + n) % n) * ch, ch)
        o_ref[pl.ds(src, ch), :] = gath[d]


def _gather_kernel(axis, other, n, x_ref, o_ref, gath, s2, r2):
    me = lax.axis_index(axis)
    ch = x_ref.shape[0]
    barrier = pltpu.get_barrier_semaphore()
    for d in range(1, n):
        pl.semaphore_signal(
            barrier, 1, device_id=_peer(axis, other, (me + d) % n), device_id_type=MESH_ID
        )
    pl.semaphore_wait(barrier, n - 1)
    gathers = []
    for d in range(1, n):
        c = pltpu.make_async_remote_copy(
            x_ref, gath.at[d], s2.at[d], r2.at[d],
            device_id=_peer(axis, other, (me + d) % n), device_id_type=MESH_ID,
        )
        c.start()
        gathers.append(c)
    o_ref[pl.ds(pl.multiple_of(me * ch, ch), ch), :] = x_ref[...]
    for d, c in enumerate(gathers, 1):
        c.wait()
        src = pl.multiple_of(((me - d + n) % n) * ch, ch)
        o_ref[pl.ds(src, ch), :] = gath[d]


def all_gather(x, axis, other, n, collective_id):
    ch, lanes = x.shape
    return pl.pallas_call(
        functools.partial(_gather_kernel, axis, other, n),
        out_shape=jax.ShapeDtypeStruct((n * ch, lanes), x.dtype),
        in_specs=[pl.BlockSpec(memory_space=pltpu.VMEM)],
        out_specs=pl.BlockSpec(memory_space=pltpu.VMEM),
        scratch_shapes=[
            pltpu.VMEM((n, ch, lanes), x.dtype),
            pltpu.SemaphoreType.DMA((n,)),
            pltpu.SemaphoreType.DMA((n,)),
        ],
        compiler_params=pltpu.CompilerParams(collective_id=collective_id, has_side_effects=True),
    )(x)


def _forward_kernel(n, ch, x_ref, mass_ref, o_ref, recv, mine, gath, s1, r1, s2, r2):
    axis, other = "col", "row"
    me = lax.axis_index(axis)
    barrier = pltpu.get_barrier_semaphore()
    for d in range(1, n):
        pl.semaphore_signal(
            barrier, 1, device_id=_peer(axis, other, (me + d) % n), device_id_type=MESH_ID
        )
    pl.semaphore_wait(barrier, n - 1)
    sends = []
    for d in range(1, n):
        peer = (me + d) % n
        start = pl.multiple_of(peer * ch, ch)
        c = pltpu.make_async_remote_copy(
            x_ref.at[pl.ds(start, ch)], recv.at[d], s1.at[d], r1.at[d],
            device_id=_peer(axis, other, peer), device_id_type=MESH_ID,
        )
        c.start()
        sends.append(c)
    own = pl.multiple_of(me * ch, ch)
    acc = x_ref[pl.ds(own, ch), :]
    for d, c in enumerate(sends, 1):
        c.wait()
        acc = acc + recv[d]
    mine[...] = (acc * mass_ref[...]).astype(mine.dtype)
    gathers = []
    for d in range(1, n):
        c = pltpu.make_async_remote_copy(
            mine, gath.at[d], s2.at[d], r2.at[d],
            device_id=_peer(axis, other, (me + d) % n), device_id_type=MESH_ID,
        )
        c.start()
        gathers.append(c)
    o_ref[pl.ds(own, ch), :] = mine[...]
    for d, c in enumerate(gathers, 1):
        c.wait()
        src = pl.multiple_of(((me - d + n) % n) * ch, ch)
        o_ref[pl.ds(src, ch), :] = gath[d]


def forward_reduce(x, mass, n, collective_id):
    rows, lanes = x.shape
    ch = rows // n
    return pl.pallas_call(
        functools.partial(_forward_kernel, n, ch),
        out_shape=jax.ShapeDtypeStruct(x.shape, jnp.bfloat16),
        in_specs=[pl.BlockSpec(memory_space=pltpu.VMEM)] * 2,
        out_specs=pl.BlockSpec(memory_space=pltpu.VMEM),
        scratch_shapes=[
            pltpu.VMEM((n, ch, lanes), x.dtype),
            pltpu.VMEM((ch, lanes), jnp.bfloat16),
            pltpu.VMEM((n, ch, lanes), jnp.bfloat16),
            pltpu.SemaphoreType.DMA((n,)),
            pltpu.SemaphoreType.DMA((n,)),
            pltpu.SemaphoreType.DMA((n,)),
            pltpu.SemaphoreType.DMA((n,)),
        ],
        compiler_params=pltpu.CompilerParams(collective_id=collective_id, has_side_effects=True),
    )(x, mass)


def _gather2_kernel(axis, other, n, x_ref, y_ref, o_ref, p_ref, gx, gy, sx, rx, sy, ry):
    me = lax.axis_index(axis)
    cx = x_ref.shape[0]
    cy = y_ref.shape[0]
    barrier = pltpu.get_barrier_semaphore()
    for d in range(1, n):
        pl.semaphore_signal(
            barrier, 1, device_id=_peer(axis, other, (me + d) % n), device_id_type=MESH_ID
        )
    pl.semaphore_wait(barrier, n - 1)
    copies = []
    for d in range(1, n):
        peer = _peer(axis, other, (me + d) % n)
        a = pltpu.make_async_remote_copy(
            x_ref, gx.at[d], sx.at[d], rx.at[d], device_id=peer, device_id_type=MESH_ID
        )
        b = pltpu.make_async_remote_copy(
            y_ref, gy.at[d], sy.at[d], ry.at[d], device_id=peer, device_id_type=MESH_ID
        )
        a.start()
        b.start()
        copies.append((a, b))
    o_ref[pl.ds(pl.multiple_of(me * cx, cx), cx), :] = x_ref[...]
    p_ref[pl.ds(pl.multiple_of(me * cy, cy), cy), :] = y_ref[...]
    for d, (a, b) in enumerate(copies, 1):
        a.wait()
        b.wait()
        src = (me - d + n) % n
        o_ref[pl.ds(pl.multiple_of(src * cx, cx), cx), :] = gx[d]
        p_ref[pl.ds(pl.multiple_of(src * cy, cy), cy), :] = gy[d]


def all_gather2(x, y, axis, other, n, collective_id):
    return pl.pallas_call(
        functools.partial(_gather2_kernel, axis, other, n),
        out_shape=(
            jax.ShapeDtypeStruct((n * x.shape[0], x.shape[1]), x.dtype),
            jax.ShapeDtypeStruct((n * y.shape[0], y.shape[1]), y.dtype),
        ),
        in_specs=[pl.BlockSpec(memory_space=pltpu.VMEM)] * 2,
        out_specs=(pl.BlockSpec(memory_space=pltpu.VMEM),) * 2,
        scratch_shapes=[
            pltpu.VMEM((n,) + x.shape, x.dtype),
            pltpu.VMEM((n,) + y.shape, y.dtype),
            pltpu.SemaphoreType.DMA((n,)),
            pltpu.SemaphoreType.DMA((n,)),
            pltpu.SemaphoreType.DMA((n,)),
            pltpu.SemaphoreType.DMA((n,)),
        ],
        compiler_params=pltpu.CompilerParams(collective_id=collective_id, has_side_effects=True),
    )(x, y)


def _gram_of(a):
    return lax.dot_general(
        a, a, (((1,), (1,)), ((), ())), precision=lax.Precision.HIGHEST,
        preferred_element_type=jnp.float32,
    )


def chol_inverse(a):
    n = a.shape[0]
    r = lax.broadcasted_iota(jnp.int32, (n, n), 0)
    c = lax.broadcasted_iota(jnp.int32, (n, n), 1)
    r1 = lax.broadcasted_iota(jnp.int32, (n, 1), 0)
    c1 = lax.broadcasted_iota(jnp.int32, (1, n), 1)
    x0 = jnp.where(r == c, 1.0, 0.0).astype(jnp.float32)

    def step(j, carry):
        m, x = carry
        col = jnp.sum(jnp.where(c == j, m, 0.0), axis=1, keepdims=True)
        row = jnp.sum(jnp.where(r == j, m, 0.0), axis=0, keepdims=True)
        piv = jnp.sqrt(jnp.sum(jnp.where(r1 == j, col, 0.0), axis=0, keepdims=True))
        lcol = jnp.where(r1 >= j, col / piv, 0.0)
        lrow = jnp.where(c1 >= j, row / piv, 0.0)
        m = m - lcol * lrow
        xrow = jnp.sum(jnp.where(r == j, x, 0.0), axis=0, keepdims=True) / piv
        x = jnp.where(r == j, xrow, x)
        x = x - jnp.where(r1 > j, lcol, 0.0) * xrow
        return m, x

    m, x = lax.fori_loop(0, n, step, (a, x0))
    return x


def _backward_kernel(n, m, scale, x_ref, icol_ref, o_ref, recv, gath, g3, s1, r1, s2, r2, s3, r3):
    me = lax.axis_index("row")
    mc = lax.axis_index("col")
    barrier = pltpu.get_barrier_semaphore()
    for d in range(1, n):
        pl.semaphore_signal(barrier, 1, device_id=((me + d) % n, mc), device_id_type=MESH_ID)
    for d in range(1, m):
        pl.semaphore_signal(barrier, 1, device_id=(me, (mc + d) % m), device_id_type=MESH_ID)
    pl.semaphore_wait(barrier, n - 1 + m - 1)
    sends = []
    for d in range(1, n):
        peer = (me + d) % n
        c = pltpu.make_async_remote_copy(
            x_ref.at[peer], recv.at[d], s1.at[d], r1.at[d],
            device_id=(peer, mc), device_id_type=MESH_ID,
        )
        c.start()
        sends.append(c)
    acc = x_ref[me]
    for d, c in enumerate(sends, 1):
        c.wait()
        acc = acc + recv[d]
    gath[0] = acc * icol_ref[...]
    gathers = []
    for d in range(1, n):
        c = pltpu.make_async_remote_copy(
            gath.at[0], gath.at[d], s2.at[d], r2.at[d],
            device_id=((me + d) % n, mc), device_id_type=MESH_ID,
        )
        c.start()
        gathers.append(c)
    for c in gathers:
        c.wait()
    g = None
    for p in range(n):
        term = _gram_of(gath[(me - p + n) % n])
        g = term if g is None else g + term
    g3[0] = g
    grams = []
    for d in range(1, m):
        c = pltpu.make_async_remote_copy(
            g3.at[0], g3.at[d], s3.at[d], r3.at[d],
            device_id=(me, (mc + d) % m), device_id_type=MESH_ID,
        )
        c.start()
        grams.append(c)
    for c in grams:
        c.wait()
    total = g3[mc % m]
    for q in range(1, m):
        total = total + g3[(mc - q + m) % m]
    inverse = chol_inverse(total * scale)
    for p in range(n):
        o_ref[p] = lax.dot_general(
            inverse, gath[(me - p + n) % n], (((1,), (0,)), ((), ())),
            precision=lax.Precision.HIGHEST, preferred_element_type=jnp.float32,
        )


def backward_reduce(x, icol, n, m, scale, collective_id):
    chunks, vecs, lanes = x.shape
    return pl.pallas_call(
        functools.partial(_backward_kernel, n, m, scale),
        out_shape=jax.ShapeDtypeStruct(x.shape, jnp.float32),
        in_specs=[pl.BlockSpec(memory_space=pltpu.VMEM)] * 2,
        out_specs=pl.BlockSpec(memory_space=pltpu.VMEM),
        scratch_shapes=[
            pltpu.VMEM((n, vecs, lanes), jnp.float32),
            pltpu.VMEM((n, vecs, lanes), jnp.float32),
            pltpu.VMEM((m, vecs, vecs), jnp.float32),
            pltpu.SemaphoreType.DMA((n,)),
            pltpu.SemaphoreType.DMA((n,)),
            pltpu.SemaphoreType.DMA((n,)),
            pltpu.SemaphoreType.DMA((n,)),
            pltpu.SemaphoreType.DMA((m,)),
            pltpu.SemaphoreType.DMA((m,)),
        ],
        compiler_params=pltpu.CompilerParams(collective_id=collective_id, has_side_effects=True),
    )(x, icol)


def all_reduce(x, axis, other, n, collective_id, two_phase=True):
    rows, lanes = x.shape
    ch = rows // n if two_phase else rows
    slots = ch if two_phase else rows
    return pl.pallas_call(
        functools.partial(_reduce_kernel, axis, other, n, ch, two_phase),
        out_shape=jax.ShapeDtypeStruct(x.shape, x.dtype),
        in_specs=[pl.BlockSpec(memory_space=pltpu.VMEM)],
        out_specs=pl.BlockSpec(memory_space=pltpu.VMEM),
        scratch_shapes=[
            pltpu.VMEM((n, slots, lanes), x.dtype),
            pltpu.VMEM((ch, lanes), x.dtype),
            pltpu.VMEM((n, ch, lanes), x.dtype),
            pltpu.SemaphoreType.DMA((n,)),
            pltpu.SemaphoreType.DMA((n,)),
            pltpu.SemaphoreType.DMA((n,)),
            pltpu.SemaphoreType.DMA((n,)),
        ],
        compiler_params=pltpu.CompilerParams(collective_id=collective_id, has_side_effects=True),
    )(x)


def rotate(projected, gram):
    lower = jnp.linalg.cholesky(gram)
    inverse = lax.linalg.triangular_solve(
        lower, jnp.eye(gram.shape[0], dtype=jnp.float32), left_side=True, lower=True
    )
    return jnp.einsum(
        "kl,bli->bki",
        inverse,
        projected,
        precision=lax.Precision.HIGHEST,
        preferred_element_type=jnp.float32,
    )


def rotate_pairs(projected, gram):
    lower = jnp.linalg.cholesky(gram)
    inverse = lax.linalg.triangular_solve(
        lower, jnp.eye(gram.shape[0], dtype=jnp.float32), left_side=True, lower=True
    )
    return jnp.einsum(
        "kl,plx->pkx",
        inverse,
        projected,
        precision=lax.Precision.HIGHEST,
        preferred_element_type=jnp.float32,
    )


def local_gram(projected):
    return jnp.einsum(
        "bki,bli->kl",
        projected,
        projected,
        precision=lax.Precision.HIGHEST,
        preferred_element_type=jnp.float32,
    )


def panel_sum(partial, axis, other, n, collective_id):
    blocks, vecs, bsize = partial.shape
    flat = partial.reshape(blocks * vecs * bsize // LANES, LANES)
    return all_reduce(flat, axis, other, n, collective_id).reshape(blocks, vecs, bsize)


def per_device(blocks, block_row, block_col, counts, vectors, row_mass, col_mass):
    tile = blocks[0, 0]
    n_cap = tile.shape[0]
    bsize = row_mass.shape[1]
    vecs = vectors.shape[1] // bsize
    own = vectors.shape[0]
    n_row = lax.axis_size("row")
    n_col = lax.axis_size("col")
    row_panel = own * n_col
    col_panel = own * n_row
    total_boxes = float(own * bsize * n_row * n_col)
    rows_idx = block_row[0, 0]
    cols_idx = block_col[0, 0]
    live = jnp.arange(n_cap) < counts[0, 0]
    fwd_ids = jnp.where(live, rows_idx, row_panel)
    bwd_ids = jnp.where(live, cols_idx, col_panel)
    square = tile.reshape(n_cap, bsize, bsize)
    vec_rows = own * vecs * bsize // LANES
    own_inv = 1.0 / jnp.sqrt(col_mass)
    first = (vectors.reshape(own, vecs, bsize) * own_inv[:, None, :]).astype(jnp.bfloat16)
    mass_pad = jnp.zeros((8, 128), jnp.float32).at[0, : own * bsize].set(col_mass.reshape(-1))
    got, mass_got = all_gather2(first.reshape(vec_rows, LANES), mass_pad, "row", "col", n_row, 4)
    first_panel = got.reshape(col_panel, vecs, bsize)
    col_mass_panel = mass_got.reshape(n_row, 8, 128)[:, 0, : own * bsize].reshape(col_panel, bsize)
    inv_col = 1.0 / jnp.sqrt(col_mass_panel)
    pairs = col_panel // 2
    inv_pairs = inv_col.reshape(pairs, 1, 2 * bsize)
    own_pair = jnp.broadcast_to(own_inv.reshape(1, own * bsize), (vecs, own * bsize))
    row_mass_spread = jnp.broadcast_to(row_mass[:, None, :], (own, vecs, bsize)).reshape(vec_rows, LANES)
    fwd_hot = (fwd_ids[None, :] == jnp.arange(row_panel)[:, None]).astype(jnp.bfloat16)
    bwd_hot = (bwd_ids[None, :] == jnp.arange(col_panel)[:, None]).astype(jnp.bfloat16)
    for step in range(ITERS):
        if step == 0:
            scaled = first_panel
        else:
            paired = (current * inv_pairs).astype(jnp.bfloat16)
            scaled = paired.reshape(pairs, vecs, 2, bsize).transpose(0, 2, 1, 3).reshape(col_panel, vecs, bsize)
        forward_taken = jnp.take(scaled, cols_idx, axis=0)
        forward_product = jnp.einsum(
            "bij,bkj->bki", square, forward_taken, preferred_element_type=jnp.bfloat16
        )
        forward_summed = jnp.einsum(
            "rs,ski->rki", fwd_hot, forward_product, preferred_element_type=jnp.float32
        )
        flat = forward_summed.reshape(row_panel * vecs * bsize // LANES, LANES)
        weighted = forward_reduce(flat, row_mass_spread, n_col, 1).reshape(row_panel, vecs, bsize)
        taken = jnp.take(weighted, rows_idx, axis=0)
        product = jnp.einsum("bij,bki->bkj", square, taken, preferred_element_type=jnp.float32)
        summed = jnp.einsum(
            "pbs,skj->pkbj", bwd_hot.reshape(pairs, 2, n_cap).astype(jnp.float32), product,
            precision=lax.Precision.HIGH, preferred_element_type=jnp.float32,
        ).reshape(pairs, vecs, 2 * bsize)
        current = backward_reduce(summed, own_pair, n_row, n_col, 1.0 / total_boxes, 2)
    me = lax.axis_index("row")
    mine = lax.dynamic_index_in_dim(current, me, 0, keepdims=False)
    return mine.reshape(vecs, own, bsize).transpose(1, 0, 2).reshape(own, vecs * bsize)


def solution(mesh):
    in_specs = (
        P("row", "col", None, None),
        P("row", "col", None),
        P("row", "col", None),
        P("row", "col"),
        P(("col", "row"), None),
        P(("row", "col"), None),
        P(("col", "row"), None),
    )
    out_specs = P(("col", "row"), None)
    return jax.shard_map(
        per_device, mesh=mesh, in_specs=in_specs, out_specs=out_specs, check_vma=False
    )
```

```python
import functools

import jax
import jax.numpy as jnp
from jax import lax
from jax.experimental import pallas as pl
from jax.experimental.pallas import tpu as pltpu
from jax.sharding import PartitionSpec as P

ITERS = 4
LANES = 512
MESH_ID = pl.DeviceIdType.MESH


def _peer(axis, other, p):
    them = lax.axis_index(other)
    return (p, them) if axis == "row" else (them, p)


def _reduce_kernel(axis, other, n, ch, two_phase, x_ref, o_ref, recv, mine, gath, s1, r1, s2, r2):
    me = lax.axis_index(axis)
    barrier = pltpu.get_barrier_semaphore()
    for d in range(1, n):
        pl.semaphore_signal(
            barrier, 1, device_id=_peer(axis, other, (me + d) % n), device_id_type=MESH_ID
        )
    pl.semaphore_wait(barrier, n - 1)
    if not two_phase:
        sends = []
        for d in range(1, n):
            c = pltpu.make_async_remote_copy(
                x_ref, recv.at[d], s1.at[d], r1.at[d],
                device_id=_peer(axis, other, (me + d) % n), device_id_type=MESH_ID,
            )
            c.start()
            sends.append(c)
        for c in sends:
            c.wait()
        recv[0] = x_ref[...]
        acc = recv[me % n]
        for p in range(1, n):
            acc = acc + recv[(me - p + n) % n]
        o_ref[...] = acc
        return
    sends = []
    for d in range(1, n):
        peer = (me + d) % n
        start = pl.multiple_of(peer * ch, ch)
        c = pltpu.make_async_remote_copy(
            x_ref.at[pl.ds(start, ch)], recv.at[d], s1.at[d], r1.at[d],
            device_id=_peer(axis, other, peer), device_id_type=MESH_ID,
        )
        c.start()
        sends.append(c)
    own = pl.multiple_of(me * ch, ch)
    acc = x_ref[pl.ds(own, ch), :]
    for d, c in enumerate(sends, 1):
        c.wait()
        acc = acc + recv[d]
    mine[...] = acc
    gathers = []
    for d in range(1, n):
        c = pltpu.make_async_remote_copy(
            mine, gath.at[d], s2.at[d], r2.at[d],
            device_id=_peer(axis, other, (me + d) % n), device_id_type=MESH_ID,
        )
        c.start()
        gathers.append(c)
    o_ref[pl.ds(own, ch), :] = acc
    for d, c in enumerate(gathers, 1):
        c.wait()
        src = pl.multiple_of(((me - d + n) % n) * ch, ch)
        o_ref[pl.ds(src, ch), :] = gath[d]


def _gather_kernel(axis, other, n, x_ref, o_ref, gath, s2, r2):
    me = lax.axis_index(axis)
    ch = x_ref.shape[0]
    barrier = pltpu.get_barrier_semaphore()
    for d in range(1, n):
        pl.semaphore_signal(
            barrier, 1, device_id=_peer(axis, other, (me + d) % n), device_id_type=MESH_ID
        )
    pl.semaphore_wait(barrier, n - 1)
    gathers = []
    for d in range(1, n):
        c = pltpu.make_async_remote_copy(
            x_ref, gath.at[d], s2.at[d], r2.at[d],
            device_id=_peer(axis, other, (me + d) % n), device_id_type=MESH_ID,
        )
        c.start()
        gathers.append(c)
    o_ref[pl.ds(pl.multiple_of(me * ch, ch), ch), :] = x_ref[...]
    for d, c in enumerate(gathers, 1):
        c.wait()
        src = pl.multiple_of(((me - d + n) % n) * ch, ch)
        o_ref[pl.ds(src, ch), :] = gath[d]


def all_gather(x, axis, other, n, collective_id):
    ch, lanes = x.shape
    return pl.pallas_call(
        functools.partial(_gather_kernel, axis, other, n),
        out_shape=jax.ShapeDtypeStruct((n * ch, lanes), x.dtype),
        in_specs=[pl.BlockSpec(memory_space=pltpu.VMEM)],
        out_specs=pl.BlockSpec(memory_space=pltpu.VMEM),
        scratch_shapes=[
            pltpu.VMEM((n, ch, lanes), x.dtype),
            pltpu.SemaphoreType.DMA((n,)),
            pltpu.SemaphoreType.DMA((n,)),
        ],
        compiler_params=pltpu.CompilerParams(collective_id=collective_id, has_side_effects=True),
    )(x)


def _forward_kernel(n, ch, x_ref, mass_ref, o_ref, recv, mine, gath, s1, r1, s2, r2):
    axis, other = "col", "row"
    me = lax.axis_index(axis)
    barrier = pltpu.get_barrier_semaphore()
    for d in range(1, n):
        pl.semaphore_signal(
            barrier, 1, device_id=_peer(axis, other, (me + d) % n), device_id_type=MESH_ID
        )
    pl.semaphore_wait(barrier, n - 1)
    sends = []
    for d in range(1, n):
        peer = (me + d) % n
        start = pl.multiple_of(peer * ch, ch)
        c = pltpu.make_async_remote_copy(
            x_ref.at[pl.ds(start, ch)], recv.at[d], s1.at[d], r1.at[d],
            device_id=_peer(axis, other, peer), device_id_type=MESH_ID,
        )
        c.start()
        sends.append(c)
    own = pl.multiple_of(me * ch, ch)
    acc = x_ref[pl.ds(own, ch), :]
    for d, c in enumerate(sends, 1):
        c.wait()
        acc = acc + recv[d]
    mine[...] = (acc * mass_ref[...]).astype(mine.dtype)
    gathers = []
    for d in range(1, n):
        c = pltpu.make_async_remote_copy(
            mine, gath.at[d], s2.at[d], r2.at[d],
            device_id=_peer(axis, other, (me + d) % n), device_id_type=MESH_ID,
        )
        c.start()
        gathers.append(c)
    o_ref[pl.ds(own, ch), :] = mine[...]
    for d, c in enumerate(gathers, 1):
        c.wait()
        src = pl.multiple_of(((me - d + n) % n) * ch, ch)
        o_ref[pl.ds(src, ch), :] = gath[d]


def forward_reduce(x, mass, n, collective_id):
    rows, lanes = x.shape
    ch = rows // n
    return pl.pallas_call(
        functools.partial(_forward_kernel, n, ch),
        out_shape=jax.ShapeDtypeStruct(x.shape, jnp.bfloat16),
        in_specs=[pl.BlockSpec(memory_space=pltpu.VMEM)] * 2,
        out_specs=pl.BlockSpec(memory_space=pltpu.VMEM),
        scratch_shapes=[
            pltpu.VMEM((n, ch, lanes), x.dtype),
            pltpu.VMEM((ch, lanes), jnp.bfloat16),
            pltpu.VMEM((n, ch, lanes), jnp.bfloat16),
            pltpu.SemaphoreType.DMA((n,)),
            pltpu.SemaphoreType.DMA((n,)),
            pltpu.SemaphoreType.DMA((n,)),
            pltpu.SemaphoreType.DMA((n,)),
        ],
        compiler_params=pltpu.CompilerParams(collective_id=collective_id, has_side_effects=True),
    )(x, mass)


def _gather2_kernel(axis, other, n, x_ref, y_ref, o_ref, p_ref, gx, gy, sx, rx, sy, ry):
    me = lax.axis_index(axis)
    cx = x_ref.shape[0]
    cy = y_ref.shape[0]
    barrier = pltpu.get_barrier_semaphore()
    for d in range(1, n):
        pl.semaphore_signal(
            barrier, 1, device_id=_peer(axis, other, (me + d) % n), device_id_type=MESH_ID
        )
    pl.semaphore_wait(barrier, n - 1)
    copies = []
    for d in range(1, n):
        peer = _peer(axis, other, (me + d) % n)
        a = pltpu.make_async_remote_copy(
            x_ref, gx.at[d], sx.at[d], rx.at[d], device_id=peer, device_id_type=MESH_ID
        )
        b = pltpu.make_async_remote_copy(
            y_ref, gy.at[d], sy.at[d], ry.at[d], device_id=peer, device_id_type=MESH_ID
        )
        a.start()
        b.start()
        copies.append((a, b))
    o_ref[pl.ds(pl.multiple_of(me * cx, cx), cx), :] = x_ref[...]
    p_ref[pl.ds(pl.multiple_of(me * cy, cy), cy), :] = y_ref[...]
    for d, (a, b) in enumerate(copies, 1):
        a.wait()
        b.wait()
        src = (me - d + n) % n
        o_ref[pl.ds(pl.multiple_of(src * cx, cx), cx), :] = gx[d]
        p_ref[pl.ds(pl.multiple_of(src * cy, cy), cy), :] = gy[d]


def all_gather2(x, y, axis, other, n, collective_id):
    return pl.pallas_call(
        functools.partial(_gather2_kernel, axis, other, n),
        out_shape=(
            jax.ShapeDtypeStruct((n * x.shape[0], x.shape[1]), x.dtype),
            jax.ShapeDtypeStruct((n * y.shape[0], y.shape[1]), y.dtype),
        ),
        in_specs=[pl.BlockSpec(memory_space=pltpu.VMEM)] * 2,
        out_specs=(pl.BlockSpec(memory_space=pltpu.VMEM),) * 2,
        scratch_shapes=[
            pltpu.VMEM((n,) + x.shape, x.dtype),
            pltpu.VMEM((n,) + y.shape, y.dtype),
            pltpu.SemaphoreType.DMA((n,)),
            pltpu.SemaphoreType.DMA((n,)),
            pltpu.SemaphoreType.DMA((n,)),
            pltpu.SemaphoreType.DMA((n,)),
        ],
        compiler_params=pltpu.CompilerParams(collective_id=collective_id, has_side_effects=True),
    )(x, y)


def _gram_of(a):
    return lax.dot_general(
        a, a, (((1,), (1,)), ((), ())), precision=lax.Precision.HIGHEST,
        preferred_element_type=jnp.float32,
    )


def chol_inverse(a):
    n = a.shape[0]
    r = lax.broadcasted_iota(jnp.int32, (n, n), 0)
    c = lax.broadcasted_iota(jnp.int32, (n, n), 1)
    r1 = lax.broadcasted_iota(jnp.int32, (n, 1), 0)
    c1 = lax.broadcasted_iota(jnp.int32, (1, n), 1)
    x0 = jnp.where(r == c, 1.0, 0.0).astype(jnp.float32)

    def step(j, carry):
        m, x = carry
        col = jnp.sum(jnp.where(c == j, m, 0.0), axis=1, keepdims=True)
        row = jnp.sum(jnp.where(r == j, m, 0.0), axis=0, keepdims=True)
        piv = jnp.sqrt(jnp.sum(jnp.where(r1 == j, col, 0.0), axis=0, keepdims=True))
        lcol = jnp.where(r1 >= j, col / piv, 0.0)
        lrow = jnp.where(c1 >= j, row / piv, 0.0)
        m = m - lcol * lrow
        xrow = jnp.sum(jnp.where(r == j, x, 0.0), axis=0, keepdims=True) / piv
        x = jnp.where(r == j, xrow, x)
        x = x - jnp.where(r1 > j, lcol, 0.0) * xrow
        return m, x

    m, x = lax.fori_loop(0, n, step, (a, x0))
    return x


def _backward_kernel(n, m, scale, x_ref, icol_ref, o_ref, recv, gath, g3, s1, r1, s2, r2, s3, r3):
    me = lax.axis_index("row")
    mc = lax.axis_index("col")
    barrier = pltpu.get_barrier_semaphore()
    for d in range(1, n):
        pl.semaphore_signal(barrier, 1, device_id=((me + d) % n, mc), device_id_type=MESH_ID)
    for d in range(1, m):
        pl.semaphore_signal(barrier, 1, device_id=(me, (mc + d) % m), device_id_type=MESH_ID)
    pl.semaphore_wait(barrier, n - 1 + m - 1)
    sends = []
    for d in range(1, n):
        peer = (me + d) % n
        c = pltpu.make_async_remote_copy(
            x_ref.at[peer], recv.at[d], s1.at[d], r1.at[d],
            device_id=(peer, mc), device_id_type=MESH_ID,
        )
        c.start()
        sends.append(c)
    acc = x_ref[me]
    for d, c in enumerate(sends, 1):
        c.wait()
        acc = acc + recv[d]
    gath[0] = acc * icol_ref[...]
    gathers = []
    for d in range(1, n):
        c = pltpu.make_async_remote_copy(
            gath.at[0], gath.at[d], s2.at[d], r2.at[d],
            device_id=((me + d) % n, mc), device_id_type=MESH_ID,
        )
        c.start()
        gathers.append(c)
    for c in gathers:
        c.wait()
    g = None
    for p in range(n):
        term = _gram_of(gath[(me - p + n) % n])
        g = term if g is None else g + term
    g3[0] = g
    grams = []
    for d in range(1, m):
        c = pltpu.make_async_remote_copy(
            g3.at[0], g3.at[d], s3.at[d], r3.at[d],
            device_id=(me, (mc + d) % m), device_id_type=MESH_ID,
        )
        c.start()
        grams.append(c)
    for c in grams:
        c.wait()
    total = g3[mc % m]
    for q in range(1, m):
        total = total + g3[(mc - q + m) % m]
    inverse = chol_inverse(total * scale)
    for p in range(n):
        o_ref[p] = lax.dot_general(
            inverse, gath[(me - p + n) % n], (((1,), (0,)), ((), ())),
            precision=lax.Precision.HIGHEST, preferred_element_type=jnp.float32,
        )


def backward_reduce(x, icol, n, m, scale, collective_id):
    chunks, vecs, lanes = x.shape
    return pl.pallas_call(
        functools.partial(_backward_kernel, n, m, scale),
        out_shape=jax.ShapeDtypeStruct(x.shape, jnp.float32),
        in_specs=[pl.BlockSpec(memory_space=pltpu.VMEM)] * 2,
        out_specs=pl.BlockSpec(memory_space=pltpu.VMEM),
        scratch_shapes=[
            pltpu.VMEM((n, vecs, lanes), jnp.float32),
            pltpu.VMEM((n, vecs, lanes), jnp.float32),
            pltpu.VMEM((m, vecs, vecs), jnp.float32),
            pltpu.SemaphoreType.DMA((n,)),
            pltpu.SemaphoreType.DMA((n,)),
            pltpu.SemaphoreType.DMA((n,)),
            pltpu.SemaphoreType.DMA((n,)),
            pltpu.SemaphoreType.DMA((m,)),
            pltpu.SemaphoreType.DMA((m,)),
        ],
        compiler_params=pltpu.CompilerParams(collective_id=collective_id, has_side_effects=True),
    )(x, icol)


def all_reduce(x, axis, other, n, collective_id, two_phase=True):
    rows, lanes = x.shape
    ch = rows // n if two_phase else rows
    slots = ch if two_phase else rows
    return pl.pallas_call(
        functools.partial(_reduce_kernel, axis, other, n, ch, two_phase),
        out_shape=jax.ShapeDtypeStruct(x.shape, x.dtype),
        in_specs=[pl.BlockSpec(memory_space=pltpu.VMEM)],
        out_specs=pl.BlockSpec(memory_space=pltpu.VMEM),
        scratch_shapes=[
            pltpu.VMEM((n, slots, lanes), x.dtype),
            pltpu.VMEM((ch, lanes), x.dtype),
            pltpu.VMEM((n, ch, lanes), x.dtype),
            pltpu.SemaphoreType.DMA((n,)),
            pltpu.SemaphoreType.DMA((n,)),
            pltpu.SemaphoreType.DMA((n,)),
            pltpu.SemaphoreType.DMA((n,)),
        ],
        compiler_params=pltpu.CompilerParams(collective_id=collective_id, has_side_effects=True),
    )(x)


def rotate(projected, gram):
    lower = jnp.linalg.cholesky(gram)
    inverse = lax.linalg.triangular_solve(
        lower, jnp.eye(gram.shape[0], dtype=jnp.float32), left_side=True, lower=True
    )
    return jnp.einsum(
        "kl,bli->bki",
        inverse,
        projected,
        precision=lax.Precision.HIGHEST,
        preferred_element_type=jnp.float32,
    )


def rotate_pairs(projected, gram):
    lower = jnp.linalg.cholesky(gram)
    inverse = lax.linalg.triangular_solve(
        lower, jnp.eye(gram.shape[0], dtype=jnp.float32), left_side=True, lower=True
    )
    return jnp.einsum(
        "kl,plx->pkx",
        inverse,
        projected,
        precision=lax.Precision.HIGHEST,
        preferred_element_type=jnp.float32,
    )


def local_gram(projected):
    return jnp.einsum(
        "bki,bli->kl",
        projected,
        projected,
        precision=lax.Precision.HIGHEST,
        preferred_element_type=jnp.float32,
    )


def panel_sum(partial, axis, other, n, collective_id):
    blocks, vecs, bsize = partial.shape
    flat = partial.reshape(blocks * vecs * bsize // LANES, LANES)
    return all_reduce(flat, axis, other, n, collective_id).reshape(blocks, vecs, bsize)


def per_device(blocks, block_row, block_col, counts, vectors, row_mass, col_mass):
    tile = blocks[0, 0]
    n_cap = tile.shape[0]
    bsize = row_mass.shape[1]
    vecs = vectors.shape[1] // bsize
    own = vectors.shape[0]
    n_row = lax.axis_size("row")
    n_col = lax.axis_size("col")
    row_panel = own * n_col
    col_panel = own * n_row
    total_boxes = float(own * bsize * n_row * n_col)
    rows_idx = block_row[0, 0]
    cols_idx = block_col[0, 0]
    live = jnp.arange(n_cap) < counts[0, 0]
    fwd_ids = jnp.where(live, rows_idx, row_panel)
    bwd_ids = jnp.where(live, cols_idx, col_panel)
    square = tile.reshape(n_cap, bsize, bsize)
    vec_rows = own * vecs * bsize // LANES
    own_inv = 1.0 / jnp.sqrt(col_mass)
    first = (vectors.reshape(own, vecs, bsize) * own_inv[:, None, :]).astype(jnp.bfloat16)
    mass_pad = jnp.zeros((8, 128), jnp.float32).at[0, : own * bsize].set(col_mass.reshape(-1))
    got, mass_got = all_gather2(first.reshape(vec_rows, LANES), mass_pad, "row", "col", n_row, 4)
    first_panel = got.reshape(col_panel, vecs, bsize)
    col_mass_panel = mass_got.reshape(n_row, 8, 128)[:, 0, : own * bsize].reshape(col_panel, bsize)
    inv_col = 1.0 / jnp.sqrt(col_mass_panel)
    pairs = col_panel // 2
    inv_pairs = inv_col.reshape(pairs, 1, 2 * bsize)
    own_pair = jnp.broadcast_to(own_inv.reshape(1, own * bsize), (vecs, own * bsize))
    row_mass_spread = jnp.broadcast_to(row_mass[:, None, :], (own, vecs, bsize)).reshape(vec_rows, LANES)
    fwd_hot = (fwd_ids[None, :] == jnp.arange(row_panel)[:, None]).astype(jnp.bfloat16)
    bwd_hot = (bwd_ids[None, :] == jnp.arange(col_panel)[:, None]).astype(jnp.bfloat16)
    for step in range(ITERS):
        if step == 0:
            scaled = first_panel
        else:
            paired = (current * inv_pairs).astype(jnp.bfloat16)
            scaled = paired.reshape(pairs, vecs, 2, bsize).transpose(0, 2, 1, 3).reshape(col_panel, vecs, bsize)
        forward_taken = jnp.take(scaled, cols_idx, axis=0)
        forward_product = jnp.einsum(
            "bij,bkj->bki", square, forward_taken, preferred_element_type=jnp.float32
        )
        forward_summed = jnp.einsum(
            "rs,ski->rki", fwd_hot.astype(jnp.float32), forward_product,
            precision=lax.Precision.HIGH, preferred_element_type=jnp.float32,
        )
        flat = forward_summed.reshape(row_panel * vecs * bsize // LANES, LANES)
        weighted = forward_reduce(flat, row_mass_spread, n_col, 1).reshape(row_panel, vecs, bsize)
        taken = jnp.take(weighted, rows_idx, axis=0)
        product = jnp.einsum("bij,bki->bkj", square, taken, preferred_element_type=jnp.bfloat16)
        summed = jnp.einsum(
            "pbs,skj->pkbj", bwd_hot.reshape(pairs, 2, n_cap), product,
            preferred_element_type=jnp.float32,
        ).reshape(pairs, vecs, 2 * bsize)
        current = backward_reduce(summed, own_pair, n_row, n_col, 1.0 / total_boxes, 2)
    me = lax.axis_index("row")
    mine = lax.dynamic_index_in_dim(current, me, 0, keepdims=False)
    return mine.reshape(vecs, own, bsize).transpose(1, 0, 2).reshape(own, vecs * bsize)


def solution(mesh):
    in_specs = (
        P("row", "col", None, None),
        P("row", "col", None),
        P("row", "col", None),
        P("row", "col"),
        P(("col", "row"), None),
        P(("row", "col"), None),
        P(("col", "row"), None),
    )
    out_specs = P(("col", "row"), None)
    return jax.shard_map(
        per_device, mesh=mesh, in_specs=in_specs, out_specs=out_specs, check_vma=False
    )
```

```python
import functools

import jax
import jax.numpy as jnp
from jax import lax
from jax.experimental import pallas as pl
from jax.experimental.pallas import tpu as pltpu
from jax.sharding import PartitionSpec as P

ITERS = 4
LANES = 512
MESH_ID = pl.DeviceIdType.MESH


def _peer(axis, other, p):
    them = lax.axis_index(other)
    return (p, them) if axis == "row" else (them, p)


def _reduce_kernel(axis, other, n, ch, two_phase, x_ref, o_ref, recv, mine, gath, s1, r1, s2, r2):
    me = lax.axis_index(axis)
    barrier = pltpu.get_barrier_semaphore()
    for d in range(1, n):
        pl.semaphore_signal(
            barrier, 1, device_id=_peer(axis, other, (me + d) % n), device_id_type=MESH_ID
        )
    pl.semaphore_wait(barrier, n - 1)
    if not two_phase:
        sends = []
        for d in range(1, n):
            c = pltpu.make_async_remote_copy(
                x_ref, recv.at[d], s1.at[d], r1.at[d],
                device_id=_peer(axis, other, (me + d) % n), device_id_type=MESH_ID,
            )
            c.start()
            sends.append(c)
        for c in sends:
            c.wait()
        recv[0] = x_ref[...]
        acc = recv[me % n]
        for p in range(1, n):
            acc = acc + recv[(me - p + n) % n]
        o_ref[...] = acc
        return
    sends = []
    for d in range(1, n):
        peer = (me + d) % n
        start = pl.multiple_of(peer * ch, ch)
        c = pltpu.make_async_remote_copy(
            x_ref.at[pl.ds(start, ch)], recv.at[d], s1.at[d], r1.at[d],
            device_id=_peer(axis, other, peer), device_id_type=MESH_ID,
        )
        c.start()
        sends.append(c)
    own = pl.multiple_of(me * ch, ch)
    acc = x_ref[pl.ds(own, ch), :]
    for d, c in enumerate(sends, 1):
        c.wait()
        acc = acc + recv[d]
    mine[...] = acc
    gathers = []
    for d in range(1, n):
        c = pltpu.make_async_remote_copy(
            mine, gath.at[d], s2.at[d], r2.at[d],
            device_id=_peer(axis, other, (me + d) % n), device_id_type=MESH_ID,
        )
        c.start()
        gathers.append(c)
    o_ref[pl.ds(own, ch), :] = acc
    for d, c in enumerate(gathers, 1):
        c.wait()
        src = pl.multiple_of(((me - d + n) % n) * ch, ch)
        o_ref[pl.ds(src, ch), :] = gath[d]


def _gather_kernel(axis, other, n, x_ref, o_ref, gath, s2, r2):
    me = lax.axis_index(axis)
    ch = x_ref.shape[0]
    barrier = pltpu.get_barrier_semaphore()
    for d in range(1, n):
        pl.semaphore_signal(
            barrier, 1, device_id=_peer(axis, other, (me + d) % n), device_id_type=MESH_ID
        )
    pl.semaphore_wait(barrier, n - 1)
    gathers = []
    for d in range(1, n):
        c = pltpu.make_async_remote_copy(
            x_ref, gath.at[d], s2.at[d], r2.at[d],
            device_id=_peer(axis, other, (me + d) % n), device_id_type=MESH_ID,
        )
        c.start()
        gathers.append(c)
    o_ref[pl.ds(pl.multiple_of(me * ch, ch), ch), :] = x_ref[...]
    for d, c in enumerate(gathers, 1):
        c.wait()
        src = pl.multiple_of(((me - d + n) % n) * ch, ch)
        o_ref[pl.ds(src, ch), :] = gath[d]


def all_gather(x, axis, other, n, collective_id):
    ch, lanes = x.shape
    return pl.pallas_call(
        functools.partial(_gather_kernel, axis, other, n),
        out_shape=jax.ShapeDtypeStruct((n * ch, lanes), x.dtype),
        in_specs=[pl.BlockSpec(memory_space=pltpu.VMEM)],
        out_specs=pl.BlockSpec(memory_space=pltpu.VMEM),
        scratch_shapes=[
            pltpu.VMEM((n, ch, lanes), x.dtype),
            pltpu.SemaphoreType.DMA((n,)),
            pltpu.SemaphoreType.DMA((n,)),
        ],
        compiler_params=pltpu.CompilerParams(collective_id=collective_id, has_side_effects=True),
    )(x)


def _forward_kernel(n, ch, x_ref, mass_ref, o_ref, recv, mine, gath, s1, r1, s2, r2):
    axis, other = "col", "row"
    me = lax.axis_index(axis)
    barrier = pltpu.get_barrier_semaphore()
    for d in range(1, n):
        pl.semaphore_signal(
            barrier, 1, device_id=_peer(axis, other, (me + d) % n), device_id_type=MESH_ID
        )
    pl.semaphore_wait(barrier, n - 1)
    sends = []
    for d in range(1, n):
        peer = (me + d) % n
        start = pl.multiple_of(peer * ch, ch)
        c = pltpu.make_async_remote_copy(
            x_ref.at[pl.ds(start, ch)], recv.at[d], s1.at[d], r1.at[d],
            device_id=_peer(axis, other, peer), device_id_type=MESH_ID,
        )
        c.start()
        sends.append(c)
    own = pl.multiple_of(me * ch, ch)
    acc = x_ref[pl.ds(own, ch), :]
    for d, c in enumerate(sends, 1):
        c.wait()
        acc = acc + recv[d]
    mine[...] = (acc * mass_ref[...]).astype(mine.dtype)
    gathers = []
    for d in range(1, n):
        c = pltpu.make_async_remote_copy(
            mine, gath.at[d], s2.at[d], r2.at[d],
            device_id=_peer(axis, other, (me + d) % n), device_id_type=MESH_ID,
        )
        c.start()
        gathers.append(c)
    o_ref[pl.ds(own, ch), :] = mine[...]
    for d, c in enumerate(gathers, 1):
        c.wait()
        src = pl.multiple_of(((me - d + n) % n) * ch, ch)
        o_ref[pl.ds(src, ch), :] = gath[d]


def forward_reduce(x, mass, n, collective_id):
    rows, lanes = x.shape
    ch = rows // n
    return pl.pallas_call(
        functools.partial(_forward_kernel, n, ch),
        out_shape=jax.ShapeDtypeStruct(x.shape, jnp.bfloat16),
        in_specs=[pl.BlockSpec(memory_space=pltpu.VMEM)] * 2,
        out_specs=pl.BlockSpec(memory_space=pltpu.VMEM),
        scratch_shapes=[
            pltpu.VMEM((n, ch, lanes), x.dtype),
            pltpu.VMEM((ch, lanes), jnp.bfloat16),
            pltpu.VMEM((n, ch, lanes), jnp.bfloat16),
            pltpu.SemaphoreType.DMA((n,)),
            pltpu.SemaphoreType.DMA((n,)),
            pltpu.SemaphoreType.DMA((n,)),
            pltpu.SemaphoreType.DMA((n,)),
        ],
        compiler_params=pltpu.CompilerParams(collective_id=collective_id, has_side_effects=True),
    )(x, mass)


def _gather2_kernel(axis, other, n, x_ref, y_ref, o_ref, p_ref, gx, gy, sx, rx, sy, ry):
    me = lax.axis_index(axis)
    cx = x_ref.shape[0]
    cy = y_ref.shape[0]
    barrier = pltpu.get_barrier_semaphore()
    for d in range(1, n):
        pl.semaphore_signal(
            barrier, 1, device_id=_peer(axis, other, (me + d) % n), device_id_type=MESH_ID
        )
    pl.semaphore_wait(barrier, n - 1)
    copies = []
    for d in range(1, n):
        peer = _peer(axis, other, (me + d) % n)
        a = pltpu.make_async_remote_copy(
            x_ref, gx.at[d], sx.at[d], rx.at[d], device_id=peer, device_id_type=MESH_ID
        )
        b = pltpu.make_async_remote_copy(
            y_ref, gy.at[d], sy.at[d], ry.at[d], device_id=peer, device_id_type=MESH_ID
        )
        a.start()
        b.start()
        copies.append((a, b))
    o_ref[pl.ds(pl.multiple_of(me * cx, cx), cx), :] = x_ref[...]
    p_ref[pl.ds(pl.multiple_of(me * cy, cy), cy), :] = y_ref[...]
    for d, (a, b) in enumerate(copies, 1):
        a.wait()
        b.wait()
        src = (me - d + n) % n
        o_ref[pl.ds(pl.multiple_of(src * cx, cx), cx), :] = gx[d]
        p_ref[pl.ds(pl.multiple_of(src * cy, cy), cy), :] = gy[d]


def all_gather2(x, y, axis, other, n, collective_id):
    return pl.pallas_call(
        functools.partial(_gather2_kernel, axis, other, n),
        out_shape=(
            jax.ShapeDtypeStruct((n * x.shape[0], x.shape[1]), x.dtype),
            jax.ShapeDtypeStruct((n * y.shape[0], y.shape[1]), y.dtype),
        ),
        in_specs=[pl.BlockSpec(memory_space=pltpu.VMEM)] * 2,
        out_specs=(pl.BlockSpec(memory_space=pltpu.VMEM),) * 2,
        scratch_shapes=[
            pltpu.VMEM((n,) + x.shape, x.dtype),
            pltpu.VMEM((n,) + y.shape, y.dtype),
            pltpu.SemaphoreType.DMA((n,)),
            pltpu.SemaphoreType.DMA((n,)),
            pltpu.SemaphoreType.DMA((n,)),
            pltpu.SemaphoreType.DMA((n,)),
        ],
        compiler_params=pltpu.CompilerParams(collective_id=collective_id, has_side_effects=True),
    )(x, y)


def _gram_of(a):
    return lax.dot_general(
        a, a, (((1,), (1,)), ((), ())), precision=lax.Precision.HIGHEST,
        preferred_element_type=jnp.float32,
    )


def chol_inverse(a):
    n = a.shape[0]
    r = lax.broadcasted_iota(jnp.int32, (n, n), 0)
    c = lax.broadcasted_iota(jnp.int32, (n, n), 1)
    r1 = lax.broadcasted_iota(jnp.int32, (n, 1), 0)
    c1 = lax.broadcasted_iota(jnp.int32, (1, n), 1)
    x0 = jnp.where(r == c, 1.0, 0.0).astype(jnp.float32)
    d0 = jnp.sum(jnp.where(r == c, a, 0.0), axis=0, keepdims=True)

    def step(j, carry):
        m, x, d = carry
        inv = 1.0 / jnp.sqrt(jnp.sum(jnp.where(c1 == j, d, 0.0), axis=1, keepdims=True))
        col = jnp.sum(jnp.where(c == j, m, 0.0), axis=1, keepdims=True)
        row = jnp.sum(jnp.where(r == j, m, 0.0), axis=0, keepdims=True)
        lcol = jnp.where(r1 >= j, col * inv, 0.0)
        lrow = jnp.where(c1 >= j, row * inv, 0.0)
        m = m - lcol * lrow
        d = d - lrow * lrow
        xrow = jnp.sum(jnp.where(r == j, x, 0.0), axis=0, keepdims=True) * inv
        x = jnp.where(r == j, xrow, x)
        x = x - jnp.where(r1 > j, lcol, 0.0) * xrow
        return m, x, d

    m, x, d = lax.fori_loop(0, n, step, (a, x0, d0))
    return x


def _backward_kernel(n, m, scale, x_ref, icol_ref, o_ref, recv, gath, g3, s1, r1, s2, r2, s3, r3):
    me = lax.axis_index("row")
    mc = lax.axis_index("col")
    barrier = pltpu.get_barrier_semaphore()
    for d in range(1, n):
        pl.semaphore_signal(barrier, 1, device_id=((me + d) % n, mc), device_id_type=MESH_ID)
    for d in range(1, m):
        pl.semaphore_signal(barrier, 1, device_id=(me, (mc + d) % m), device_id_type=MESH_ID)
    pl.semaphore_wait(barrier, n - 1 + m - 1)
    sends = []
    for d in range(1, n):
        peer = (me + d) % n
        c = pltpu.make_async_remote_copy(
            x_ref.at[peer], recv.at[d], s1.at[d], r1.at[d],
            device_id=(peer, mc), device_id_type=MESH_ID,
        )
        c.start()
        sends.append(c)
    acc = x_ref[me]
    for d, c in enumerate(sends, 1):
        c.wait()
        acc = acc + recv[d]
    gath[0] = acc * icol_ref[...]
    gathers = []
    for d in range(1, n):
        c = pltpu.make_async_remote_copy(
            gath.at[0], gath.at[d], s2.at[d], r2.at[d],
            device_id=((me + d) % n, mc), device_id_type=MESH_ID,
        )
        c.start()
        gathers.append(c)
    for c in gathers:
        c.wait()
    g = None
    for p in range(n):
        term = _gram_of(gath[(me - p + n) % n])
        g = term if g is None else g + term
    g3[0] = g
    grams = []
    for d in range(1, m):
        c = pltpu.make_async_remote_copy(
            g3.at[0], g3.at[d], s3.at[d], r3.at[d],
            device_id=(me, (mc + d) % m), device_id_type=MESH_ID,
        )
        c.start()
        grams.append(c)
    for c in grams:
        c.wait()
    total = g3[mc % m]
    for q in range(1, m):
        total = total + g3[(mc - q + m) % m]
    inverse = chol_inverse(total * scale)
    for p in range(n):
        o_ref[p] = lax.dot_general(
            inverse, gath[(me - p + n) % n], (((1,), (0,)), ((), ())),
            precision=lax.Precision.HIGHEST, preferred_element_type=jnp.float32,
        )


def backward_reduce(x, icol, n, m, scale, collective_id):
    chunks, vecs, lanes = x.shape
    return pl.pallas_call(
        functools.partial(_backward_kernel, n, m, scale),
        out_shape=jax.ShapeDtypeStruct(x.shape, jnp.float32),
        in_specs=[pl.BlockSpec(memory_space=pltpu.VMEM)] * 2,
        out_specs=pl.BlockSpec(memory_space=pltpu.VMEM),
        scratch_shapes=[
            pltpu.VMEM((n, vecs, lanes), jnp.float32),
            pltpu.VMEM((n, vecs, lanes), jnp.float32),
            pltpu.VMEM((m, vecs, vecs), jnp.float32),
            pltpu.SemaphoreType.DMA((n,)),
            pltpu.SemaphoreType.DMA((n,)),
            pltpu.SemaphoreType.DMA((n,)),
            pltpu.SemaphoreType.DMA((n,)),
            pltpu.SemaphoreType.DMA((m,)),
            pltpu.SemaphoreType.DMA((m,)),
        ],
        compiler_params=pltpu.CompilerParams(collective_id=collective_id, has_side_effects=True),
    )(x, icol)


def all_reduce(x, axis, other, n, collective_id, two_phase=True):
    rows, lanes = x.shape
    ch = rows // n if two_phase else rows
    slots = ch if two_phase else rows
    return pl.pallas_call(
        functools.partial(_reduce_kernel, axis, other, n, ch, two_phase),
        out_shape=jax.ShapeDtypeStruct(x.shape, x.dtype),
        in_specs=[pl.BlockSpec(memory_space=pltpu.VMEM)],
        out_specs=pl.BlockSpec(memory_space=pltpu.VMEM),
        scratch_shapes=[
            pltpu.VMEM((n, slots, lanes), x.dtype),
            pltpu.VMEM((ch, lanes), x.dtype),
            pltpu.VMEM((n, ch, lanes), x.dtype),
            pltpu.SemaphoreType.DMA((n,)),
            pltpu.SemaphoreType.DMA((n,)),
            pltpu.SemaphoreType.DMA((n,)),
            pltpu.SemaphoreType.DMA((n,)),
        ],
        compiler_params=pltpu.CompilerParams(collective_id=collective_id, has_side_effects=True),
    )(x)


def rotate(projected, gram):
    lower = jnp.linalg.cholesky(gram)
    inverse = lax.linalg.triangular_solve(
        lower, jnp.eye(gram.shape[0], dtype=jnp.float32), left_side=True, lower=True
    )
    return jnp.einsum(
        "kl,bli->bki",
        inverse,
        projected,
        precision=lax.Precision.HIGHEST,
        preferred_element_type=jnp.float32,
    )


def rotate_pairs(projected, gram):
    lower = jnp.linalg.cholesky(gram)
    inverse = lax.linalg.triangular_solve(
        lower, jnp.eye(gram.shape[0], dtype=jnp.float32), left_side=True, lower=True
    )
    return jnp.einsum(
        "kl,plx->pkx",
        inverse,
        projected,
        precision=lax.Precision.HIGHEST,
        preferred_element_type=jnp.float32,
    )


def local_gram(projected):
    return jnp.einsum(
        "bki,bli->kl",
        projected,
        projected,
        precision=lax.Precision.HIGHEST,
        preferred_element_type=jnp.float32,
    )


def panel_sum(partial, axis, other, n, collective_id):
    blocks, vecs, bsize = partial.shape
    flat = partial.reshape(blocks * vecs * bsize // LANES, LANES)
    return all_reduce(flat, axis, other, n, collective_id).reshape(blocks, vecs, bsize)


def per_device(blocks, block_row, block_col, counts, vectors, row_mass, col_mass):
    tile = blocks[0, 0]
    n_cap = tile.shape[0]
    bsize = row_mass.shape[1]
    vecs = vectors.shape[1] // bsize
    own = vectors.shape[0]
    n_row = lax.axis_size("row")
    n_col = lax.axis_size("col")
    row_panel = own * n_col
    col_panel = own * n_row
    total_boxes = float(own * bsize * n_row * n_col)
    rows_idx = block_row[0, 0]
    cols_idx = block_col[0, 0]
    live = jnp.arange(n_cap) < counts[0, 0]
    fwd_ids = jnp.where(live, rows_idx, row_panel)
    bwd_ids = jnp.where(live, cols_idx, col_panel)
    square = tile.reshape(n_cap, bsize, bsize)
    vec_rows = own * vecs * bsize // LANES
    own_inv = 1.0 / jnp.sqrt(col_mass)
    first = (vectors.reshape(own, vecs, bsize) * own_inv[:, None, :]).astype(jnp.bfloat16)
    mass_pad = jnp.zeros((8, 128), jnp.float32).at[0, : own * bsize].set(col_mass.reshape(-1))
    got, mass_got = all_gather2(first.reshape(vec_rows, LANES), mass_pad, "row", "col", n_row, 4)
    first_panel = got.reshape(col_panel, vecs, bsize)
    col_mass_panel = mass_got.reshape(n_row, 8, 128)[:, 0, : own * bsize].reshape(col_panel, bsize)
    inv_col = 1.0 / jnp.sqrt(col_mass_panel)
    pairs = col_panel // 2
    inv_pairs = inv_col.reshape(pairs, 1, 2 * bsize)
    own_pair = jnp.broadcast_to(own_inv.reshape(1, own * bsize), (vecs, own * bsize))
    row_mass_spread = jnp.broadcast_to(row_mass[:, None, :], (own, vecs, bsize)).reshape(vec_rows, LANES)
    fwd_hot = (fwd_ids[None, :] == jnp.arange(row_panel)[:, None]).astype(jnp.bfloat16)
    bwd_hot = (bwd_ids[None, :] == jnp.arange(col_panel)[:, None]).astype(jnp.bfloat16)
    for step in range(ITERS):
        if step == 0:
            scaled = first_panel
        else:
            paired = (current * inv_pairs).astype(jnp.bfloat16)
            scaled = paired.reshape(pairs, vecs, 2, bsize).transpose(0, 2, 1, 3).reshape(col_panel, vecs, bsize)
        forward_taken = jnp.take(scaled, cols_idx, axis=0)
        forward_product = jnp.einsum(
            "bij,bkj->bki", square, forward_taken, preferred_element_type=jnp.bfloat16
        )
        forward_summed = jnp.einsum(
            "rs,ski->rki", fwd_hot, forward_product, preferred_element_type=jnp.float32
        )
        flat = forward_summed.reshape(row_panel * vecs * bsize // LANES, LANES)
        weighted = forward_reduce(flat, row_mass_spread, n_col, 1).reshape(row_panel, vecs, bsize)
        taken = jnp.take(weighted, rows_idx, axis=0)
        product = jnp.einsum("bij,bki->bkj", square, taken, preferred_element_type=jnp.bfloat16)
        summed = jnp.einsum(
            "pbs,skj->pkbj", bwd_hot.reshape(pairs, 2, n_cap), product,
            preferred_element_type=jnp.float32,
        ).reshape(pairs, vecs, 2 * bsize)
        current = backward_reduce(summed, own_pair, n_row, n_col, 1.0 / total_boxes, 2)
    me = lax.axis_index("row")
    mine = lax.dynamic_index_in_dim(current, me, 0, keepdims=False)
    return mine.reshape(vecs, own, bsize).transpose(1, 0, 2).reshape(own, vecs * bsize)


def solution(mesh):
    in_specs = (
        P("row", "col", None, None),
        P("row", "col", None),
        P("row", "col", None),
        P("row", "col"),
        P(("col", "row"), None),
        P(("row", "col"), None),
        P(("col", "row"), None),
    )
    out_specs = P(("col", "row"), None)
    return jax.shard_map(
        per_device, mesh=mesh, in_specs=in_specs, out_specs=out_specs, check_vma=False
    )
```

```python
import functools

import jax
import jax.numpy as jnp
from jax import lax
from jax.experimental import pallas as pl
from jax.experimental.pallas import tpu as pltpu
from jax.sharding import PartitionSpec as P

ITERS = 4
LANES = 512
MESH_ID = pl.DeviceIdType.MESH


def _peer(axis, other, p):
    them = lax.axis_index(other)
    return (p, them) if axis == "row" else (them, p)


def _reduce_kernel(axis, other, n, ch, two_phase, x_ref, o_ref, recv, mine, gath, s1, r1, s2, r2):
    me = lax.axis_index(axis)
    barrier = pltpu.get_barrier_semaphore()
    for d in range(1, n):
        pl.semaphore_signal(
            barrier, 1, device_id=_peer(axis, other, (me + d) % n), device_id_type=MESH_ID
        )
    pl.semaphore_wait(barrier, n - 1)
    if not two_phase:
        sends = []
        for d in range(1, n):
            c = pltpu.make_async_remote_copy(
                x_ref, recv.at[d], s1.at[d], r1.at[d],
                device_id=_peer(axis, other, (me + d) % n), device_id_type=MESH_ID,
            )
            c.start()
            sends.append(c)
        for c in sends:
            c.wait()
        recv[0] = x_ref[...]
        acc = recv[me % n]
        for p in range(1, n):
            acc = acc + recv[(me - p + n) % n]
        o_ref[...] = acc
        return
    sends = []
    for d in range(1, n):
        peer = (me + d) % n
        start = pl.multiple_of(peer * ch, ch)
        c = pltpu.make_async_remote_copy(
            x_ref.at[pl.ds(start, ch)], recv.at[d], s1.at[d], r1.at[d],
            device_id=_peer(axis, other, peer), device_id_type=MESH_ID,
        )
        c.start()
        sends.append(c)
    own = pl.multiple_of(me * ch, ch)
    acc = x_ref[pl.ds(own, ch), :]
    for d, c in enumerate(sends, 1):
        c.wait()
        acc = acc + recv[d]
    mine[...] = acc
    gathers = []
    for d in range(1, n):
        c = pltpu.make_async_remote_copy(
            mine, gath.at[d], s2.at[d], r2.at[d],
            device_id=_peer(axis, other, (me + d) % n), device_id_type=MESH_ID,
        )
        c.start()
        gathers.append(c)
    o_ref[pl.ds(own, ch), :] = acc
    for d, c in enumerate(gathers, 1):
        c.wait()
        src = pl.multiple_of(((me - d + n) % n) * ch, ch)
        o_ref[pl.ds(src, ch), :] = gath[d]


def _gather_kernel(axis, other, n, x_ref, o_ref, gath, s2, r2):
    me = lax.axis_index(axis)
    ch = x_ref.shape[0]
    barrier = pltpu.get_barrier_semaphore()
    for d in range(1, n):
        pl.semaphore_signal(
            barrier, 1, device_id=_peer(axis, other, (me + d) % n), device_id_type=MESH_ID
        )
    pl.semaphore_wait(barrier, n - 1)
    gathers = []
    for d in range(1, n):
        c = pltpu.make_async_remote_copy(
            x_ref, gath.at[d], s2.at[d], r2.at[d],
            device_id=_peer(axis, other, (me + d) % n), device_id_type=MESH_ID,
        )
        c.start()
        gathers.append(c)
    o_ref[pl.ds(pl.multiple_of(me * ch, ch), ch), :] = x_ref[...]
    for d, c in enumerate(gathers, 1):
        c.wait()
        src = pl.multiple_of(((me - d + n) % n) * ch, ch)
        o_ref[pl.ds(src, ch), :] = gath[d]


def all_gather(x, axis, other, n, collective_id):
    ch, lanes = x.shape
    return pl.pallas_call(
        functools.partial(_gather_kernel, axis, other, n),
        out_shape=jax.ShapeDtypeStruct((n * ch, lanes), x.dtype),
        in_specs=[pl.BlockSpec(memory_space=pltpu.VMEM)],
        out_specs=pl.BlockSpec(memory_space=pltpu.VMEM),
        scratch_shapes=[
            pltpu.VMEM((n, ch, lanes), x.dtype),
            pltpu.SemaphoreType.DMA((n,)),
            pltpu.SemaphoreType.DMA((n,)),
        ],
        compiler_params=pltpu.CompilerParams(collective_id=collective_id, has_side_effects=True),
    )(x)


def _forward_kernel(n, ch, x_ref, mass_ref, o_ref, recv, mine, gath, s1, r1, s2, r2):
    axis, other = "col", "row"
    me = lax.axis_index(axis)
    barrier = pltpu.get_barrier_semaphore()
    for d in range(1, n):
        pl.semaphore_signal(
            barrier, 1, device_id=_peer(axis, other, (me + d) % n), device_id_type=MESH_ID
        )
    pl.semaphore_wait(barrier, n - 1)
    sends = []
    for d in range(1, n):
        peer = (me + d) % n
        start = pl.multiple_of(peer * ch, ch)
        c = pltpu.make_async_remote_copy(
            x_ref.at[pl.ds(start, ch)], recv.at[d], s1.at[d], r1.at[d],
            device_id=_peer(axis, other, peer), device_id_type=MESH_ID,
        )
        c.start()
        sends.append(c)
    own = pl.multiple_of(me * ch, ch)
    acc = x_ref[pl.ds(own, ch), :]
    for d, c in enumerate(sends, 1):
        c.wait()
        acc = acc + recv[d]
    mine[...] = (acc * mass_ref[...]).astype(mine.dtype)
    gathers = []
    for d in range(1, n):
        c = pltpu.make_async_remote_copy(
            mine, gath.at[d], s2.at[d], r2.at[d],
            device_id=_peer(axis, other, (me + d) % n), device_id_type=MESH_ID,
        )
        c.start()
        gathers.append(c)
    o_ref[pl.ds(own, ch), :] = mine[...]
    for d, c in enumerate(gathers, 1):
        c.wait()
        src = pl.multiple_of(((me - d + n) % n) * ch, ch)
        o_ref[pl.ds(src, ch), :] = gath[d]


def forward_reduce(x, mass, n, collective_id):
    rows, lanes = x.shape
    ch = rows // n
    return pl.pallas_call(
        functools.partial(_forward_kernel, n, ch),
        out_shape=jax.ShapeDtypeStruct(x.shape, jnp.bfloat16),
        in_specs=[pl.BlockSpec(memory_space=pltpu.VMEM)] * 2,
        out_specs=pl.BlockSpec(memory_space=pltpu.VMEM),
        scratch_shapes=[
            pltpu.VMEM((n, ch, lanes), x.dtype),
            pltpu.VMEM((ch, lanes), jnp.bfloat16),
            pltpu.VMEM((n, ch, lanes), jnp.bfloat16),
            pltpu.SemaphoreType.DMA((n,)),
            pltpu.SemaphoreType.DMA((n,)),
            pltpu.SemaphoreType.DMA((n,)),
            pltpu.SemaphoreType.DMA((n,)),
        ],
        compiler_params=pltpu.CompilerParams(collective_id=collective_id, has_side_effects=True),
    )(x, mass)


def _gather2_kernel(axis, other, n, x_ref, y_ref, o_ref, p_ref, gx, gy, sx, rx, sy, ry):
    me = lax.axis_index(axis)
    cx = x_ref.shape[0]
    cy = y_ref.shape[0]
    barrier = pltpu.get_barrier_semaphore()
    for d in range(1, n):
        pl.semaphore_signal(
            barrier, 1, device_id=_peer(axis, other, (me + d) % n), device_id_type=MESH_ID
        )
    pl.semaphore_wait(barrier, n - 1)
    copies = []
    for d in range(1, n):
        peer = _peer(axis, other, (me + d) % n)
        a = pltpu.make_async_remote_copy(
            x_ref, gx.at[d], sx.at[d], rx.at[d], device_id=peer, device_id_type=MESH_ID
        )
        b = pltpu.make_async_remote_copy(
            y_ref, gy.at[d], sy.at[d], ry.at[d], device_id=peer, device_id_type=MESH_ID
        )
        a.start()
        b.start()
        copies.append((a, b))
    o_ref[pl.ds(pl.multiple_of(me * cx, cx), cx), :] = x_ref[...]
    p_ref[pl.ds(pl.multiple_of(me * cy, cy), cy), :] = y_ref[...]
    for d, (a, b) in enumerate(copies, 1):
        a.wait()
        b.wait()
        src = (me - d + n) % n
        o_ref[pl.ds(pl.multiple_of(src * cx, cx), cx), :] = gx[d]
        p_ref[pl.ds(pl.multiple_of(src * cy, cy), cy), :] = gy[d]


def all_gather2(x, y, axis, other, n, collective_id):
    return pl.pallas_call(
        functools.partial(_gather2_kernel, axis, other, n),
        out_shape=(
            jax.ShapeDtypeStruct((n * x.shape[0], x.shape[1]), x.dtype),
            jax.ShapeDtypeStruct((n * y.shape[0], y.shape[1]), y.dtype),
        ),
        in_specs=[pl.BlockSpec(memory_space=pltpu.VMEM)] * 2,
        out_specs=(pl.BlockSpec(memory_space=pltpu.VMEM),) * 2,
        scratch_shapes=[
            pltpu.VMEM((n,) + x.shape, x.dtype),
            pltpu.VMEM((n,) + y.shape, y.dtype),
            pltpu.SemaphoreType.DMA((n,)),
            pltpu.SemaphoreType.DMA((n,)),
            pltpu.SemaphoreType.DMA((n,)),
            pltpu.SemaphoreType.DMA((n,)),
        ],
        compiler_params=pltpu.CompilerParams(collective_id=collective_id, has_side_effects=True),
    )(x, y)


def _gram_of(a):
    return lax.dot_general(
        a, a, (((1,), (1,)), ((), ())), precision=lax.Precision.HIGHEST,
        preferred_element_type=jnp.float32,
    )


def chol_inverse(a):
    n = a.shape[0]
    r = lax.broadcasted_iota(jnp.int32, (n, n), 0)
    c = lax.broadcasted_iota(jnp.int32, (n, n), 1)
    r1 = lax.broadcasted_iota(jnp.int32, (n, 1), 0)
    c1 = lax.broadcasted_iota(jnp.int32, (1, n), 1)
    x0 = jnp.where(r == c, 1.0, 0.0).astype(jnp.float32)
    d0 = jnp.sum(jnp.where(r == c, a, 0.0), axis=0, keepdims=True)

    def step(j, carry):
        m, x, d = carry
        inv = 1.0 / jnp.sqrt(jnp.sum(jnp.where(c1 == j, d, 0.0), axis=1, keepdims=True))
        row = jnp.sum(jnp.where(r == j, m, 0.0), axis=0, keepdims=True)
        lrow = jnp.where(c1 >= j, row * inv, 0.0)
        lcol = jnp.transpose(lrow)
        m = m - lcol * lrow
        d = d - lrow * lrow
        xrow = jnp.sum(jnp.where(r == j, x, 0.0), axis=0, keepdims=True) * inv
        x = jnp.where(r == j, xrow, x)
        x = x - jnp.where(r1 > j, lcol, 0.0) * xrow
        return m, x, d

    m, x, d = lax.fori_loop(0, n, step, (a, x0, d0))
    return x


def _backward_kernel(n, m, scale, x_ref, icol_ref, o_ref, recv, gath, g3, s1, r1, s2, r2, s3, r3):
    me = lax.axis_index("row")
    mc = lax.axis_index("col")
    barrier = pltpu.get_barrier_semaphore()
    for d in range(1, n):
        pl.semaphore_signal(barrier, 1, device_id=((me + d) % n, mc), device_id_type=MESH_ID)
    for d in range(1, m):
        pl.semaphore_signal(barrier, 1, device_id=(me, (mc + d) % m), device_id_type=MESH_ID)
    pl.semaphore_wait(barrier, n - 1 + m - 1)
    sends = []
    for d in range(1, n):
        peer = (me + d) % n
        c = pltpu.make_async_remote_copy(
            x_ref.at[peer], recv.at[d], s1.at[d], r1.at[d],
            device_id=(peer, mc), device_id_type=MESH_ID,
        )
        c.start()
        sends.append(c)
    acc = x_ref[me]
    for d, c in enumerate(sends, 1):
        c.wait()
        acc = acc + recv[d]
    gath[0] = acc * icol_ref[...]
    gathers = []
    for d in range(1, n):
        c = pltpu.make_async_remote_copy(
            gath.at[0], gath.at[d], s2.at[d], r2.at[d],
            device_id=((me + d) % n, mc), device_id_type=MESH_ID,
        )
        c.start()
        gathers.append(c)
    for c in gathers:
        c.wait()
    g = None
    for p in range(n):
        term = _gram_of(gath[(me - p + n) % n])
        g = term if g is None else g + term
    g3[0] = g
    grams = []
    for d in range(1, m):
        c = pltpu.make_async_remote_copy(
            g3.at[0], g3.at[d], s3.at[d], r3.at[d],
            device_id=(me, (mc + d) % m), device_id_type=MESH_ID,
        )
        c.start()
        grams.append(c)
    for c in grams:
        c.wait()
    total = g3[mc % m]
    for q in range(1, m):
        total = total + g3[(mc - q + m) % m]
    inverse = chol_inverse(total * scale)
    for p in range(n):
        o_ref[p] = lax.dot_general(
            inverse, gath[(me - p + n) % n], (((1,), (0,)), ((), ())),
            precision=lax.Precision.HIGHEST, preferred_element_type=jnp.float32,
        )


def backward_reduce(x, icol, n, m, scale, collective_id):
    chunks, vecs, lanes = x.shape
    return pl.pallas_call(
        functools.partial(_backward_kernel, n, m, scale),
        out_shape=jax.ShapeDtypeStruct(x.shape, jnp.float32),
        in_specs=[pl.BlockSpec(memory_space=pltpu.VMEM)] * 2,
        out_specs=pl.BlockSpec(memory_space=pltpu.VMEM),
        scratch_shapes=[
            pltpu.VMEM((n, vecs, lanes), jnp.float32),
            pltpu.VMEM((n, vecs, lanes), jnp.float32),
            pltpu.VMEM((m, vecs, vecs), jnp.float32),
            pltpu.SemaphoreType.DMA((n,)),
            pltpu.SemaphoreType.DMA((n,)),
            pltpu.SemaphoreType.DMA((n,)),
            pltpu.SemaphoreType.DMA((n,)),
            pltpu.SemaphoreType.DMA((m,)),
            pltpu.SemaphoreType.DMA((m,)),
        ],
        compiler_params=pltpu.CompilerParams(collective_id=collective_id, has_side_effects=True),
    )(x, icol)


def all_reduce(x, axis, other, n, collective_id, two_phase=True):
    rows, lanes = x.shape
    ch = rows // n if two_phase else rows
    slots = ch if two_phase else rows
    return pl.pallas_call(
        functools.partial(_reduce_kernel, axis, other, n, ch, two_phase),
        out_shape=jax.ShapeDtypeStruct(x.shape, x.dtype),
        in_specs=[pl.BlockSpec(memory_space=pltpu.VMEM)],
        out_specs=pl.BlockSpec(memory_space=pltpu.VMEM),
        scratch_shapes=[
            pltpu.VMEM((n, slots, lanes), x.dtype),
            pltpu.VMEM((ch, lanes), x.dtype),
            pltpu.VMEM((n, ch, lanes), x.dtype),
            pltpu.SemaphoreType.DMA((n,)),
            pltpu.SemaphoreType.DMA((n,)),
            pltpu.SemaphoreType.DMA((n,)),
            pltpu.SemaphoreType.DMA((n,)),
        ],
        compiler_params=pltpu.CompilerParams(collective_id=collective_id, has_side_effects=True),
    )(x)


def rotate(projected, gram):
    lower = jnp.linalg.cholesky(gram)
    inverse = lax.linalg.triangular_solve(
        lower, jnp.eye(gram.shape[0], dtype=jnp.float32), left_side=True, lower=True
    )
    return jnp.einsum(
        "kl,bli->bki",
        inverse,
        projected,
        precision=lax.Precision.HIGHEST,
        preferred_element_type=jnp.float32,
    )


def rotate_pairs(projected, gram):
    lower = jnp.linalg.cholesky(gram)
    inverse = lax.linalg.triangular_solve(
        lower, jnp.eye(gram.shape[0], dtype=jnp.float32), left_side=True, lower=True
    )
    return jnp.einsum(
        "kl,plx->pkx",
        inverse,
        projected,
        precision=lax.Precision.HIGHEST,
        preferred_element_type=jnp.float32,
    )


def local_gram(projected):
    return jnp.einsum(
        "bki,bli->kl",
        projected,
        projected,
        precision=lax.Precision.HIGHEST,
        preferred_element_type=jnp.float32,
    )


def panel_sum(partial, axis, other, n, collective_id):
    blocks, vecs, bsize = partial.shape
    flat = partial.reshape(blocks * vecs * bsize // LANES, LANES)
    return all_reduce(flat, axis, other, n, collective_id).reshape(blocks, vecs, bsize)


def per_device(blocks, block_row, block_col, counts, vectors, row_mass, col_mass):
    tile = blocks[0, 0]
    n_cap = tile.shape[0]
    bsize = row_mass.shape[1]
    vecs = vectors.shape[1] // bsize
    own = vectors.shape[0]
    n_row = lax.axis_size("row")
    n_col = lax.axis_size("col")
    row_panel = own * n_col
    col_panel = own * n_row
    total_boxes = float(own * bsize * n_row * n_col)
    rows_idx = block_row[0, 0]
    cols_idx = block_col[0, 0]
    live = jnp.arange(n_cap) < counts[0, 0]
    fwd_ids = jnp.where(live, rows_idx, row_panel)
    bwd_ids = jnp.where(live, cols_idx, col_panel)
    square = tile.reshape(n_cap, bsize, bsize)
    vec_rows = own * vecs * bsize // LANES
    own_inv = 1.0 / jnp.sqrt(col_mass)
    first = (vectors.reshape(own, vecs, bsize) * own_inv[:, None, :]).astype(jnp.bfloat16)
    mass_pad = jnp.zeros((8, 128), jnp.float32).at[0, : own * bsize].set(col_mass.reshape(-1))
    got, mass_got = all_gather2(first.reshape(vec_rows, LANES), mass_pad, "row", "col", n_row, 4)
    first_panel = got.reshape(col_panel, vecs, bsize)
    col_mass_panel = mass_got.reshape(n_row, 8, 128)[:, 0, : own * bsize].reshape(col_panel, bsize)
    inv_col = 1.0 / jnp.sqrt(col_mass_panel)
    pairs = col_panel // 2
    inv_pairs = inv_col.reshape(pairs, 1, 2 * bsize)
    own_pair = jnp.broadcast_to(own_inv.reshape(1, own * bsize), (vecs, own * bsize))
    row_mass_spread = jnp.broadcast_to(row_mass[:, None, :], (own, vecs, bsize)).reshape(vec_rows, LANES)
    fwd_hot = (fwd_ids[None, :] == jnp.arange(row_panel)[:, None]).astype(jnp.bfloat16)
    bwd_hot = (bwd_ids[None, :] == jnp.arange(col_panel)[:, None]).astype(jnp.bfloat16)
    for step in range(ITERS):
        if step == 0:
            scaled = first_panel
        else:
            paired = (current * inv_pairs).astype(jnp.bfloat16)
            scaled = paired.reshape(pairs, vecs, 2, bsize).transpose(0, 2, 1, 3).reshape(col_panel, vecs, bsize)
        forward_taken = jnp.take(scaled, cols_idx, axis=0)
        forward_product = jnp.einsum(
            "bij,bkj->bki", square, forward_taken, preferred_element_type=jnp.bfloat16
        )
        forward_summed = jnp.einsum(
            "rs,ski->rki", fwd_hot, forward_product, preferred_element_type=jnp.float32
        )
        flat = forward_summed.reshape(row_panel * vecs * bsize // LANES, LANES)
        weighted = forward_reduce(flat, row_mass_spread, n_col, 1).reshape(row_panel, vecs, bsize)
        taken = jnp.take(weighted, rows_idx, axis=0)
        product = jnp.einsum("bij,bki->bkj", square, taken, preferred_element_type=jnp.bfloat16)
        summed = jnp.einsum(
            "pbs,skj->pkbj", bwd_hot.reshape(pairs, 2, n_cap), product,
            preferred_element_type=jnp.float32,
        ).reshape(pairs, vecs, 2 * bsize)
        current = backward_reduce(summed, own_pair, n_row, n_col, 1.0 / total_boxes, 2)
    me = lax.axis_index("row")
    mine = lax.dynamic_index_in_dim(current, me, 0, keepdims=False)
    return mine.reshape(vecs, own, bsize).transpose(1, 0, 2).reshape(own, vecs * bsize)


def solution(mesh):
    in_specs = (
        P("row", "col", None, None),
        P("row", "col", None),
        P("row", "col", None),
        P("row", "col"),
        P(("col", "row"), None),
        P(("row", "col"), None),
        P(("col", "row"), None),
    )
    out_specs = P(("col", "row"), None)
    return jax.shard_map(
        per_device, mesh=mesh, in_specs=in_specs, out_specs=out_specs, check_vma=False
    )
```

```python
import functools

import jax
import jax.numpy as jnp
from jax import lax
from jax.experimental import pallas as pl
from jax.experimental.pallas import tpu as pltpu
from jax.sharding import PartitionSpec as P

ITERS = 4
LANES = 512
MESH_ID = pl.DeviceIdType.MESH


def _peer(axis, other, p):
    them = lax.axis_index(other)
    return (p, them) if axis == "row" else (them, p)


def _reduce_kernel(axis, other, n, ch, two_phase, x_ref, o_ref, recv, mine, gath, s1, r1, s2, r2):
    me = lax.axis_index(axis)
    barrier = pltpu.get_barrier_semaphore()
    for d in range(1, n):
        pl.semaphore_signal(
            barrier, 1, device_id=_peer(axis, other, (me + d) % n), device_id_type=MESH_ID
        )
    pl.semaphore_wait(barrier, n - 1)
    if not two_phase:
        sends = []
        for d in range(1, n):
            c = pltpu.make_async_remote_copy(
                x_ref, recv.at[d], s1.at[d], r1.at[d],
                device_id=_peer(axis, other, (me + d) % n), device_id_type=MESH_ID,
            )
            c.start()
            sends.append(c)
        for c in sends:
            c.wait()
        recv[0] = x_ref[...]
        acc = recv[me % n]
        for p in range(1, n):
            acc = acc + recv[(me - p + n) % n]
        o_ref[...] = acc
        return
    sends = []
    for d in range(1, n):
        peer = (me + d) % n
        start = pl.multiple_of(peer * ch, ch)
        c = pltpu.make_async_remote_copy(
            x_ref.at[pl.ds(start, ch)], recv.at[d], s1.at[d], r1.at[d],
            device_id=_peer(axis, other, peer), device_id_type=MESH_ID,
        )
        c.start()
        sends.append(c)
    own = pl.multiple_of(me * ch, ch)
    acc = x_ref[pl.ds(own, ch), :]
    for d, c in enumerate(sends, 1):
        c.wait()
        acc = acc + recv[d]
    mine[...] = acc
    gathers = []
    for d in range(1, n):
        c = pltpu.make_async_remote_copy(
            mine, gath.at[d], s2.at[d], r2.at[d],
            device_id=_peer(axis, other, (me + d) % n), device_id_type=MESH_ID,
        )
        c.start()
        gathers.append(c)
    o_ref[pl.ds(own, ch), :] = acc
    for d, c in enumerate(gathers, 1):
        c.wait()
        src = pl.multiple_of(((me - d + n) % n) * ch, ch)
        o_ref[pl.ds(src, ch), :] = gath[d]


def _gather_kernel(axis, other, n, x_ref, o_ref, gath, s2, r2):
    me = lax.axis_index(axis)
    ch = x_ref.shape[0]
    barrier = pltpu.get_barrier_semaphore()
    for d in range(1, n):
        pl.semaphore_signal(
            barrier, 1, device_id=_peer(axis, other, (me + d) % n), device_id_type=MESH_ID
        )
    pl.semaphore_wait(barrier, n - 1)
    gathers = []
    for d in range(1, n):
        c = pltpu.make_async_remote_copy(
            x_ref, gath.at[d], s2.at[d], r2.at[d],
            device_id=_peer(axis, other, (me + d) % n), device_id_type=MESH_ID,
        )
        c.start()
        gathers.append(c)
    o_ref[pl.ds(pl.multiple_of(me * ch, ch), ch), :] = x_ref[...]
    for d, c in enumerate(gathers, 1):
        c.wait()
        src = pl.multiple_of(((me - d + n) % n) * ch, ch)
        o_ref[pl.ds(src, ch), :] = gath[d]


def all_gather(x, axis, other, n, collective_id):
    ch, lanes = x.shape
    return pl.pallas_call(
        functools.partial(_gather_kernel, axis, other, n),
        out_shape=jax.ShapeDtypeStruct((n * ch, lanes), x.dtype),
        in_specs=[pl.BlockSpec(memory_space=pltpu.VMEM)],
        out_specs=pl.BlockSpec(memory_space=pltpu.VMEM),
        scratch_shapes=[
            pltpu.VMEM((n, ch, lanes), x.dtype),
            pltpu.SemaphoreType.DMA((n,)),
            pltpu.SemaphoreType.DMA((n,)),
        ],
        compiler_params=pltpu.CompilerParams(collective_id=collective_id, has_side_effects=True),
    )(x)


def _forward_kernel(n, ch, x_ref, mass_ref, o_ref, recv, mine, gath, s1, r1, s2, r2):
    axis, other = "col", "row"
    me = lax.axis_index(axis)
    barrier = pltpu.get_barrier_semaphore()
    for d in range(1, n):
        pl.semaphore_signal(
            barrier, 1, device_id=_peer(axis, other, (me + d) % n), device_id_type=MESH_ID
        )
    pl.semaphore_wait(barrier, n - 1)
    sends = []
    for d in range(1, n):
        peer = (me + d) % n
        start = pl.multiple_of(peer * ch, ch)
        c = pltpu.make_async_remote_copy(
            x_ref.at[pl.ds(start, ch)], recv.at[d], s1.at[d], r1.at[d],
            device_id=_peer(axis, other, peer), device_id_type=MESH_ID,
        )
        c.start()
        sends.append(c)
    own = pl.multiple_of(me * ch, ch)
    acc = x_ref[pl.ds(own, ch), :]
    for d, c in enumerate(sends, 1):
        c.wait()
        acc = acc + recv[d]
    mine[...] = (acc * mass_ref[...]).astype(mine.dtype)
    gathers = []
    for d in range(1, n):
        c = pltpu.make_async_remote_copy(
            mine, gath.at[d], s2.at[d], r2.at[d],
            device_id=_peer(axis, other, (me + d) % n), device_id_type=MESH_ID,
        )
        c.start()
        gathers.append(c)
    o_ref[pl.ds(own, ch), :] = mine[...]
    for d, c in enumerate(gathers, 1):
        c.wait()
        src = pl.multiple_of(((me - d + n) % n) * ch, ch)
        o_ref[pl.ds(src, ch), :] = gath[d]


def forward_reduce(x, mass, n, collective_id):
    rows, lanes = x.shape
    ch = rows // n
    return pl.pallas_call(
        functools.partial(_forward_kernel, n, ch),
        out_shape=jax.ShapeDtypeStruct(x.shape, jnp.bfloat16),
        in_specs=[pl.BlockSpec(memory_space=pltpu.VMEM)] * 2,
        out_specs=pl.BlockSpec(memory_space=pltpu.VMEM),
        scratch_shapes=[
            pltpu.VMEM((n, ch, lanes), x.dtype),
            pltpu.VMEM((ch, lanes), jnp.bfloat16),
            pltpu.VMEM((n, ch, lanes), jnp.bfloat16),
            pltpu.SemaphoreType.DMA((n,)),
            pltpu.SemaphoreType.DMA((n,)),
            pltpu.SemaphoreType.DMA((n,)),
            pltpu.SemaphoreType.DMA((n,)),
        ],
        compiler_params=pltpu.CompilerParams(collective_id=collective_id, has_side_effects=True),
    )(x, mass)


def _gather2_kernel(axis, other, n, x_ref, y_ref, o_ref, p_ref, gx, gy, sx, rx, sy, ry):
    me = lax.axis_index(axis)
    cx = x_ref.shape[0]
    cy = y_ref.shape[0]
    barrier = pltpu.get_barrier_semaphore()
    for d in range(1, n):
        pl.semaphore_signal(
            barrier, 1, device_id=_peer(axis, other, (me + d) % n), device_id_type=MESH_ID
        )
    pl.semaphore_wait(barrier, n - 1)
    copies = []
    for d in range(1, n):
        peer = _peer(axis, other, (me + d) % n)
        a = pltpu.make_async_remote_copy(
            x_ref, gx.at[d], sx.at[d], rx.at[d], device_id=peer, device_id_type=MESH_ID
        )
        b = pltpu.make_async_remote_copy(
            y_ref, gy.at[d], sy.at[d], ry.at[d], device_id=peer, device_id_type=MESH_ID
        )
        a.start()
        b.start()
        copies.append((a, b))
    o_ref[pl.ds(pl.multiple_of(me * cx, cx), cx), :] = x_ref[...]
    p_ref[pl.ds(pl.multiple_of(me * cy, cy), cy), :] = y_ref[...]
    for d, (a, b) in enumerate(copies, 1):
        a.wait()
        b.wait()
        src = (me - d + n) % n
        o_ref[pl.ds(pl.multiple_of(src * cx, cx), cx), :] = gx[d]
        p_ref[pl.ds(pl.multiple_of(src * cy, cy), cy), :] = gy[d]


def all_gather2(x, y, axis, other, n, collective_id):
    return pl.pallas_call(
        functools.partial(_gather2_kernel, axis, other, n),
        out_shape=(
            jax.ShapeDtypeStruct((n * x.shape[0], x.shape[1]), x.dtype),
            jax.ShapeDtypeStruct((n * y.shape[0], y.shape[1]), y.dtype),
        ),
        in_specs=[pl.BlockSpec(memory_space=pltpu.VMEM)] * 2,
        out_specs=(pl.BlockSpec(memory_space=pltpu.VMEM),) * 2,
        scratch_shapes=[
            pltpu.VMEM((n,) + x.shape, x.dtype),
            pltpu.VMEM((n,) + y.shape, y.dtype),
            pltpu.SemaphoreType.DMA((n,)),
            pltpu.SemaphoreType.DMA((n,)),
            pltpu.SemaphoreType.DMA((n,)),
            pltpu.SemaphoreType.DMA((n,)),
        ],
        compiler_params=pltpu.CompilerParams(collective_id=collective_id, has_side_effects=True),
    )(x, y)


def _gram_of(a):
    return lax.dot_general(
        a, a, (((1,), (1,)), ((), ())), precision=lax.Precision.HIGHEST,
        preferred_element_type=jnp.float32,
    )


def chol_inverse(a):
    n = a.shape[0]
    r = lax.broadcasted_iota(jnp.int32, (n, n), 0)
    c = lax.broadcasted_iota(jnp.int32, (n, n), 1)
    r1 = lax.broadcasted_iota(jnp.int32, (n, 1), 0)
    c1 = lax.broadcasted_iota(jnp.int32, (1, n), 1)
    x0 = jnp.where(r == c, 1.0, 0.0).astype(jnp.float32)
    d0 = jnp.sum(jnp.where(r == c, a, 0.0), axis=0, keepdims=True)

    def step(j, carry):
        m, x, d = carry
        inv = 1.0 / jnp.sqrt(jnp.sum(jnp.where(c1 == j, d, 0.0), axis=1, keepdims=True))
        col = jnp.sum(jnp.where(c == j, m, 0.0), axis=1, keepdims=True)
        row = jnp.sum(jnp.where(r == j, m, 0.0), axis=0, keepdims=True)
        lcol = jnp.where(r1 >= j, col * inv, 0.0)
        lrow = jnp.where(c1 >= j, row * inv, 0.0)
        m = m - lcol * lrow
        d = d - lrow * lrow
        xrow = jnp.sum(jnp.where(r == j, x, 0.0), axis=0, keepdims=True) * inv
        x = jnp.where(r == j, xrow, x)
        x = x - jnp.where(r1 > j, lcol, 0.0) * xrow
        return m, x, d

    m, x, d = lax.fori_loop(0, n, step, (a, x0, d0))
    return x


def _backward_kernel(n, m, scale, x_ref, icol_ref, o_ref, recv, gath, g3, panel, s1, r1, s2, r2, s3, r3):
    me = lax.axis_index("row")
    mc = lax.axis_index("col")
    barrier = pltpu.get_barrier_semaphore()
    for d in range(1, n):
        pl.semaphore_signal(barrier, 1, device_id=((me + d) % n, mc), device_id_type=MESH_ID)
    for d in range(1, m):
        pl.semaphore_signal(barrier, 1, device_id=(me, (mc + d) % m), device_id_type=MESH_ID)
    pl.semaphore_wait(barrier, n - 1 + m - 1)
    sends = []
    for d in range(1, n):
        peer = (me + d) % n
        c = pltpu.make_async_remote_copy(
            x_ref.at[peer], recv.at[d], s1.at[d], r1.at[d],
            device_id=(peer, mc), device_id_type=MESH_ID,
        )
        c.start()
        sends.append(c)
    acc = x_ref[me]
    for d, c in enumerate(sends, 1):
        c.wait()
        acc = acc + recv[d]
    gath[0] = acc * icol_ref[...]
    gathers = []
    for d in range(1, n):
        c = pltpu.make_async_remote_copy(
            gath.at[0], gath.at[d], s2.at[d], r2.at[d],
            device_id=((me + d) % n, mc), device_id_type=MESH_ID,
        )
        c.start()
        gathers.append(c)
    for c in gathers:
        c.wait()
    lanes = gath.shape[2]
    for p in range(n):
        panel[:, p * lanes:(p + 1) * lanes] = gath[(me - p + n) % n]
    g3[0] = _gram_of(panel[...])
    grams = []
    for d in range(1, m):
        c = pltpu.make_async_remote_copy(
            g3.at[0], g3.at[d], s3.at[d], r3.at[d],
            device_id=(me, (mc + d) % m), device_id_type=MESH_ID,
        )
        c.start()
        grams.append(c)
    for c in grams:
        c.wait()
    total = g3[mc % m]
    for q in range(1, m):
        total = total + g3[(mc - q + m) % m]
    inverse = chol_inverse(total * scale)
    rotated = lax.dot_general(
        inverse, panel[...], (((1,), (0,)), ((), ())),
        precision=lax.Precision.HIGHEST, preferred_element_type=jnp.float32,
    )
    for p in range(n):
        o_ref[p] = rotated[:, p * lanes:(p + 1) * lanes]


def backward_reduce(x, icol, n, m, scale, collective_id):
    chunks, vecs, lanes = x.shape
    return pl.pallas_call(
        functools.partial(_backward_kernel, n, m, scale),
        out_shape=jax.ShapeDtypeStruct(x.shape, jnp.float32),
        in_specs=[pl.BlockSpec(memory_space=pltpu.VMEM)] * 2,
        out_specs=pl.BlockSpec(memory_space=pltpu.VMEM),
        scratch_shapes=[
            pltpu.VMEM((n, vecs, lanes), jnp.float32),
            pltpu.VMEM((n, vecs, lanes), jnp.float32),
            pltpu.VMEM((m, vecs, vecs), jnp.float32),
            pltpu.VMEM((vecs, n * lanes), jnp.float32),
            pltpu.SemaphoreType.DMA((n,)),
            pltpu.SemaphoreType.DMA((n,)),
            pltpu.SemaphoreType.DMA((n,)),
            pltpu.SemaphoreType.DMA((n,)),
            pltpu.SemaphoreType.DMA((m,)),
            pltpu.SemaphoreType.DMA((m,)),
        ],
        compiler_params=pltpu.CompilerParams(collective_id=collective_id, has_side_effects=True),
    )(x, icol)


def all_reduce(x, axis, other, n, collective_id, two_phase=True):
    rows, lanes = x.shape
    ch = rows // n if two_phase else rows
    slots = ch if two_phase else rows
    return pl.pallas_call(
        functools.partial(_reduce_kernel, axis, other, n, ch, two_phase),
        out_shape=jax.ShapeDtypeStruct(x.shape, x.dtype),
        in_specs=[pl.BlockSpec(memory_space=pltpu.VMEM)],
        out_specs=pl.BlockSpec(memory_space=pltpu.VMEM),
        scratch_shapes=[
            pltpu.VMEM((n, slots, lanes), x.dtype),
            pltpu.VMEM((ch, lanes), x.dtype),
            pltpu.VMEM((n, ch, lanes), x.dtype),
            pltpu.SemaphoreType.DMA((n,)),
            pltpu.SemaphoreType.DMA((n,)),
            pltpu.SemaphoreType.DMA((n,)),
            pltpu.SemaphoreType.DMA((n,)),
        ],
        compiler_params=pltpu.CompilerParams(collective_id=collective_id, has_side_effects=True),
    )(x)


def rotate(projected, gram):
    lower = jnp.linalg.cholesky(gram)
    inverse = lax.linalg.triangular_solve(
        lower, jnp.eye(gram.shape[0], dtype=jnp.float32), left_side=True, lower=True
    )
    return jnp.einsum(
        "kl,bli->bki",
        inverse,
        projected,
        precision=lax.Precision.HIGHEST,
        preferred_element_type=jnp.float32,
    )


def rotate_pairs(projected, gram):
    lower = jnp.linalg.cholesky(gram)
    inverse = lax.linalg.triangular_solve(
        lower, jnp.eye(gram.shape[0], dtype=jnp.float32), left_side=True, lower=True
    )
    return jnp.einsum(
        "kl,plx->pkx",
        inverse,
        projected,
        precision=lax.Precision.HIGHEST,
        preferred_element_type=jnp.float32,
    )


def local_gram(projected):
    return jnp.einsum(
        "bki,bli->kl",
        projected,
        projected,
        precision=lax.Precision.HIGHEST,
        preferred_element_type=jnp.float32,
    )


def panel_sum(partial, axis, other, n, collective_id):
    blocks, vecs, bsize = partial.shape
    flat = partial.reshape(blocks * vecs * bsize // LANES, LANES)
    return all_reduce(flat, axis, other, n, collective_id).reshape(blocks, vecs, bsize)


def per_device(blocks, block_row, block_col, counts, vectors, row_mass, col_mass):
    tile = blocks[0, 0]
    n_cap = tile.shape[0]
    bsize = row_mass.shape[1]
    vecs = vectors.shape[1] // bsize
    own = vectors.shape[0]
    n_row = lax.axis_size("row")
    n_col = lax.axis_size("col")
    row_panel = own * n_col
    col_panel = own * n_row
    total_boxes = float(own * bsize * n_row * n_col)
    rows_idx = block_row[0, 0]
    cols_idx = block_col[0, 0]
    live = jnp.arange(n_cap) < counts[0, 0]
    fwd_ids = jnp.where(live, rows_idx, row_panel)
    bwd_ids = jnp.where(live, cols_idx, col_panel)
    square = tile.reshape(n_cap, bsize, bsize)
    vec_rows = own * vecs * bsize // LANES
    own_inv = 1.0 / jnp.sqrt(col_mass)
    first = (vectors.reshape(own, vecs, bsize) * own_inv[:, None, :]).astype(jnp.bfloat16)
    mass_pad = jnp.zeros((8, 128), jnp.float32).at[0, : own * bsize].set(col_mass.reshape(-1))
    got, mass_got = all_gather2(first.reshape(vec_rows, LANES), mass_pad, "row", "col", n_row, 4)
    first_panel = got.reshape(col_panel, vecs, bsize)
    col_mass_panel = mass_got.reshape(n_row, 8, 128)[:, 0, : own * bsize].reshape(col_panel, bsize)
    inv_col = 1.0 / jnp.sqrt(col_mass_panel)
    pairs = col_panel // 2
    inv_pairs = inv_col.reshape(pairs, 1, 2 * bsize)
    own_pair = jnp.broadcast_to(own_inv.reshape(1, own * bsize), (vecs, own * bsize))
    row_mass_spread = jnp.broadcast_to(row_mass[:, None, :], (own, vecs, bsize)).reshape(vec_rows, LANES)
    fwd_hot = (fwd_ids[None, :] == jnp.arange(row_panel)[:, None]).astype(jnp.bfloat16)
    bwd_hot = (bwd_ids[None, :] == jnp.arange(col_panel)[:, None]).astype(jnp.bfloat16)
    for step in range(ITERS):
        if step == 0:
            scaled = first_panel
        else:
            paired = (current * inv_pairs).astype(jnp.bfloat16)
            scaled = paired.reshape(pairs, vecs, 2, bsize).transpose(0, 2, 1, 3).reshape(col_panel, vecs, bsize)
        forward_taken = jnp.take(scaled, cols_idx, axis=0)
        forward_product = jnp.einsum(
            "bij,bkj->bki", square, forward_taken, preferred_element_type=jnp.bfloat16
        )
        forward_summed = jnp.einsum(
            "rs,ski->rki", fwd_hot, forward_product, preferred_element_type=jnp.float32
        )
        flat = forward_summed.reshape(row_panel * vecs * bsize // LANES, LANES)
        weighted = forward_reduce(flat, row_mass_spread, n_col, 1).reshape(row_panel, vecs, bsize)
        taken = jnp.take(weighted, rows_idx, axis=0)
        product = jnp.einsum("bij,bki->bkj", square, taken, preferred_element_type=jnp.bfloat16)
        summed = jnp.einsum(
            "pbs,skj->pkbj", bwd_hot.reshape(pairs, 2, n_cap), product,
            preferred_element_type=jnp.float32,
        ).reshape(pairs, vecs, 2 * bsize)
        current = backward_reduce(summed, own_pair, n_row, n_col, 1.0 / total_boxes, 2)
    me = lax.axis_index("row")
    mine = lax.dynamic_index_in_dim(current, me, 0, keepdims=False)
    return mine.reshape(vecs, own, bsize).transpose(1, 0, 2).reshape(own, vecs * bsize)


def solution(mesh):
    in_specs = (
        P("row", "col", None, None),
        P("row", "col", None),
        P("row", "col", None),
        P("row", "col"),
        P(("col", "row"), None),
        P(("row", "col"), None),
        P(("col", "row"), None),
    )
    out_specs = P(("col", "row"), None)
    return jax.shard_map(
        per_device, mesh=mesh, in_specs=in_specs, out_specs=out_specs, check_vma=False
    )
```

```python
import functools

import jax
import jax.numpy as jnp
from jax import lax
from jax.experimental import pallas as pl
from jax.experimental.pallas import tpu as pltpu
from jax.sharding import PartitionSpec as P

ITERS = 4
LANES = 512
MESH_ID = pl.DeviceIdType.MESH


def _peer(axis, other, p):
    them = lax.axis_index(other)
    return (p, them) if axis == "row" else (them, p)


def _reduce_kernel(axis, other, n, ch, two_phase, x_ref, o_ref, recv, mine, gath, s1, r1, s2, r2):
    me = lax.axis_index(axis)
    barrier = pltpu.get_barrier_semaphore()
    for d in range(1, n):
        pl.semaphore_signal(
            barrier, 1, device_id=_peer(axis, other, (me + d) % n), device_id_type=MESH_ID
        )
    pl.semaphore_wait(barrier, n - 1)
    if not two_phase:
        sends = []
        for d in range(1, n):
            c = pltpu.make_async_remote_copy(
                x_ref, recv.at[d], s1.at[d], r1.at[d],
                device_id=_peer(axis, other, (me + d) % n), device_id_type=MESH_ID,
            )
            c.start()
            sends.append(c)
        for c in sends:
            c.wait()
        recv[0] = x_ref[...]
        acc = recv[me % n]
        for p in range(1, n):
            acc = acc + recv[(me - p + n) % n]
        o_ref[...] = acc
        return
    sends = []
    for d in range(1, n):
        peer = (me + d) % n
        start = pl.multiple_of(peer * ch, ch)
        c = pltpu.make_async_remote_copy(
            x_ref.at[pl.ds(start, ch)], recv.at[d], s1.at[d], r1.at[d],
            device_id=_peer(axis, other, peer), device_id_type=MESH_ID,
        )
        c.start()
        sends.append(c)
    own = pl.multiple_of(me * ch, ch)
    acc = x_ref[pl.ds(own, ch), :]
    for d, c in enumerate(sends, 1):
        c.wait()
        acc = acc + recv[d]
    mine[...] = acc
    gathers = []
    for d in range(1, n):
        c = pltpu.make_async_remote_copy(
            mine, gath.at[d], s2.at[d], r2.at[d],
            device_id=_peer(axis, other, (me + d) % n), device_id_type=MESH_ID,
        )
        c.start()
        gathers.append(c)
    o_ref[pl.ds(own, ch), :] = acc
    for d, c in enumerate(gathers, 1):
        c.wait()
        src = pl.multiple_of(((me - d + n) % n) * ch, ch)
        o_ref[pl.ds(src, ch), :] = gath[d]


def _gather_kernel(axis, other, n, x_ref, o_ref, gath, s2, r2):
    me = lax.axis_index(axis)
    ch = x_ref.shape[0]
    barrier = pltpu.get_barrier_semaphore()
    for d in range(1, n):
        pl.semaphore_signal(
            barrier, 1, device_id=_peer(axis, other, (me + d) % n), device_id_type=MESH_ID
        )
    pl.semaphore_wait(barrier, n - 1)
    gathers = []
    for d in range(1, n):
        c = pltpu.make_async_remote_copy(
            x_ref, gath.at[d], s2.at[d], r2.at[d],
            device_id=_peer(axis, other, (me + d) % n), device_id_type=MESH_ID,
        )
        c.start()
        gathers.append(c)
    o_ref[pl.ds(pl.multiple_of(me * ch, ch), ch), :] = x_ref[...]
    for d, c in enumerate(gathers, 1):
        c.wait()
        src = pl.multiple_of(((me - d + n) % n) * ch, ch)
        o_ref[pl.ds(src, ch), :] = gath[d]


def all_gather(x, axis, other, n, collective_id):
    ch, lanes = x.shape
    return pl.pallas_call(
        functools.partial(_gather_kernel, axis, other, n),
        out_shape=jax.ShapeDtypeStruct((n * ch, lanes), x.dtype),
        in_specs=[pl.BlockSpec(memory_space=pltpu.VMEM)],
        out_specs=pl.BlockSpec(memory_space=pltpu.VMEM),
        scratch_shapes=[
            pltpu.VMEM((n, ch, lanes), x.dtype),
            pltpu.SemaphoreType.DMA((n,)),
            pltpu.SemaphoreType.DMA((n,)),
        ],
        compiler_params=pltpu.CompilerParams(collective_id=collective_id, has_side_effects=True),
    )(x)


def _forward_kernel(n, ch, x_ref, mass_ref, o_ref, recv, mine, gath, s1, r1, s2, r2):
    axis, other = "col", "row"
    me = lax.axis_index(axis)
    barrier = pltpu.get_barrier_semaphore()
    for d in range(1, n):
        pl.semaphore_signal(
            barrier, 1, device_id=_peer(axis, other, (me + d) % n), device_id_type=MESH_ID
        )
    pl.semaphore_wait(barrier, n - 1)
    sends = []
    for d in range(1, n):
        peer = (me + d) % n
        start = pl.multiple_of(peer * ch, ch)
        c = pltpu.make_async_remote_copy(
            x_ref.at[pl.ds(start, ch)], recv.at[d], s1.at[d], r1.at[d],
            device_id=_peer(axis, other, peer), device_id_type=MESH_ID,
        )
        c.start()
        sends.append(c)
    own = pl.multiple_of(me * ch, ch)
    acc = x_ref[pl.ds(own, ch), :]
    for d, c in enumerate(sends, 1):
        c.wait()
        acc = acc + recv[d]
    mine[...] = (acc * mass_ref[...]).astype(mine.dtype)
    gathers = []
    for d in range(1, n):
        c = pltpu.make_async_remote_copy(
            mine, gath.at[d], s2.at[d], r2.at[d],
            device_id=_peer(axis, other, (me + d) % n), device_id_type=MESH_ID,
        )
        c.start()
        gathers.append(c)
    o_ref[pl.ds(own, ch), :] = mine[...]
    for d, c in enumerate(gathers, 1):
        c.wait()
        src = pl.multiple_of(((me - d + n) % n) * ch, ch)
        o_ref[pl.ds(src, ch), :] = gath[d]


def forward_reduce(x, mass, n, collective_id):
    rows, lanes = x.shape
    ch = rows // n
    return pl.pallas_call(
        functools.partial(_forward_kernel, n, ch),
        out_shape=jax.ShapeDtypeStruct(x.shape, jnp.bfloat16),
        in_specs=[pl.BlockSpec(memory_space=pltpu.VMEM)] * 2,
        out_specs=pl.BlockSpec(memory_space=pltpu.VMEM),
        scratch_shapes=[
            pltpu.VMEM((n, ch, lanes), x.dtype),
            pltpu.VMEM((ch, lanes), jnp.bfloat16),
            pltpu.VMEM((n, ch, lanes), jnp.bfloat16),
            pltpu.SemaphoreType.DMA((n,)),
            pltpu.SemaphoreType.DMA((n,)),
            pltpu.SemaphoreType.DMA((n,)),
            pltpu.SemaphoreType.DMA((n,)),
        ],
        compiler_params=pltpu.CompilerParams(collective_id=collective_id, has_side_effects=True),
    )(x, mass)


def _gather2_kernel(axis, other, n, x_ref, y_ref, o_ref, p_ref, gx, gy, sx, rx, sy, ry):
    me = lax.axis_index(axis)
    cx = x_ref.shape[0]
    cy = y_ref.shape[0]
    barrier = pltpu.get_barrier_semaphore()
    for d in range(1, n):
        pl.semaphore_signal(
            barrier, 1, device_id=_peer(axis, other, (me + d) % n), device_id_type=MESH_ID
        )
    pl.semaphore_wait(barrier, n - 1)
    copies = []
    for d in range(1, n):
        peer = _peer(axis, other, (me + d) % n)
        a = pltpu.make_async_remote_copy(
            x_ref, gx.at[d], sx.at[d], rx.at[d], device_id=peer, device_id_type=MESH_ID
        )
        b = pltpu.make_async_remote_copy(
            y_ref, gy.at[d], sy.at[d], ry.at[d], device_id=peer, device_id_type=MESH_ID
        )
        a.start()
        b.start()
        copies.append((a, b))
    o_ref[pl.ds(pl.multiple_of(me * cx, cx), cx), :] = x_ref[...]
    p_ref[pl.ds(pl.multiple_of(me * cy, cy), cy), :] = y_ref[...]
    for d, (a, b) in enumerate(copies, 1):
        a.wait()
        b.wait()
        src = (me - d + n) % n
        o_ref[pl.ds(pl.multiple_of(src * cx, cx), cx), :] = gx[d]
        p_ref[pl.ds(pl.multiple_of(src * cy, cy), cy), :] = gy[d]


def all_gather2(x, y, axis, other, n, collective_id):
    return pl.pallas_call(
        functools.partial(_gather2_kernel, axis, other, n),
        out_shape=(
            jax.ShapeDtypeStruct((n * x.shape[0], x.shape[1]), x.dtype),
            jax.ShapeDtypeStruct((n * y.shape[0], y.shape[1]), y.dtype),
        ),
        in_specs=[pl.BlockSpec(memory_space=pltpu.VMEM)] * 2,
        out_specs=(pl.BlockSpec(memory_space=pltpu.VMEM),) * 2,
        scratch_shapes=[
            pltpu.VMEM((n,) + x.shape, x.dtype),
            pltpu.VMEM((n,) + y.shape, y.dtype),
            pltpu.SemaphoreType.DMA((n,)),
            pltpu.SemaphoreType.DMA((n,)),
            pltpu.SemaphoreType.DMA((n,)),
            pltpu.SemaphoreType.DMA((n,)),
        ],
        compiler_params=pltpu.CompilerParams(collective_id=collective_id, has_side_effects=True),
    )(x, y)


def _gram_of(a):
    return lax.dot_general(
        a, a, (((1,), (1,)), ((), ())), precision=lax.Precision.HIGHEST,
        preferred_element_type=jnp.float32,
    )


def chol_inverse(a):
    n = a.shape[0]
    r = lax.broadcasted_iota(jnp.int32, (n, n), 0)
    c = lax.broadcasted_iota(jnp.int32, (n, n), 1)
    r1 = lax.broadcasted_iota(jnp.int32, (n, 1), 0)
    c1 = lax.broadcasted_iota(jnp.int32, (1, n), 1)
    x0 = jnp.where(r == c, 1.0, 0.0).astype(jnp.float32)
    d0 = jnp.sum(jnp.where(r == c, a, 0.0), axis=0, keepdims=True)

    def step(j, carry):
        m, x, d = carry
        inv = 1.0 / jnp.sqrt(jnp.sum(jnp.where(c1 == j, d, 0.0), axis=1, keepdims=True))
        col = jnp.sum(jnp.where(c == j, m, 0.0), axis=1, keepdims=True)
        row = jnp.sum(jnp.where(r == j, m, 0.0), axis=0, keepdims=True)
        lcol = jnp.where(r1 >= j, col * inv, 0.0)
        lrow = jnp.where(c1 >= j, row * inv, 0.0)
        m = m - lcol * lrow
        d = d - lrow * lrow
        xrow = jnp.sum(jnp.where(r == j, x, 0.0), axis=0, keepdims=True) * inv
        x = jnp.where(r == j, xrow, x)
        x = x - jnp.where(r1 > j, lcol, 0.0) * xrow
        return m, x, d

    m, x, d = lax.fori_loop(0, n, step, (a, x0, d0))
    return x


def _backward_kernel(n, m, scale, x_ref, icol_ref, o_ref, recv, gath, g3, panel, s1, r1, s2, r2, s3, r3):
    me = lax.axis_index("row")
    mc = lax.axis_index("col")
    barrier = pltpu.get_barrier_semaphore()
    for d in range(1, n):
        pl.semaphore_signal(barrier, 1, device_id=((me + d) % n, mc), device_id_type=MESH_ID)
    for d in range(1, m):
        pl.semaphore_signal(barrier, 1, device_id=(me, (mc + d) % m), device_id_type=MESH_ID)
    pl.semaphore_wait(barrier, n - 1 + m - 1)
    sends = []
    for d in range(1, n):
        peer = (me + d) % n
        c = pltpu.make_async_remote_copy(
            x_ref.at[peer], recv.at[d], s1.at[d], r1.at[d],
            device_id=(peer, mc), device_id_type=MESH_ID,
        )
        c.start()
        sends.append(c)
    acc = x_ref[me]
    for d, c in enumerate(sends, 1):
        c.wait()
        acc = acc + recv[d]
    gath[0] = acc * icol_ref[...]
    gathers = []
    for d in range(1, n):
        c = pltpu.make_async_remote_copy(
            gath.at[0], gath.at[d], s2.at[d], r2.at[d],
            device_id=((me + d) % n, mc), device_id_type=MESH_ID,
        )
        c.start()
        gathers.append(c)
    for c in gathers:
        c.wait()
    lanes = gath.shape[2]
    for p in range(n):
        panel[:, p * lanes:(p + 1) * lanes] = gath[(me - p + n) % n]
    g3[0] = _gram_of(panel[...])
    grams = []
    for d in range(1, m):
        c = pltpu.make_async_remote_copy(
            g3.at[0], g3.at[d], s3.at[d], r3.at[d],
            device_id=(me, (mc + d) % m), device_id_type=MESH_ID,
        )
        c.start()
        grams.append(c)
    for c in grams:
        c.wait()
    total = g3[mc % m]
    for q in range(1, m):
        total = total + g3[(mc - q + m) % m]
    inverse = chol_inverse(total * scale)
    rotated = lax.dot_general(
        inverse, panel[...], (((1,), (0,)), ((), ())),
        precision=lax.Precision.HIGHEST, preferred_element_type=jnp.float32,
    )
    for p in range(n):
        o_ref[p] = rotated[:, p * lanes:(p + 1) * lanes]


def backward_reduce(x, icol, n, m, scale, collective_id):
    chunks, vecs, lanes = x.shape
    return pl.pallas_call(
        functools.partial(_backward_kernel, n, m, scale),
        out_shape=jax.ShapeDtypeStruct(x.shape, jnp.float32),
        in_specs=[pl.BlockSpec(memory_space=pltpu.VMEM)] * 2,
        out_specs=pl.BlockSpec(memory_space=pltpu.VMEM),
        scratch_shapes=[
            pltpu.VMEM((n, vecs, lanes), jnp.float32),
            pltpu.VMEM((n, vecs, lanes), jnp.float32),
            pltpu.VMEM((m, vecs, vecs), jnp.float32),
            pltpu.VMEM((vecs, n * lanes), jnp.float32),
            pltpu.SemaphoreType.DMA((n,)),
            pltpu.SemaphoreType.DMA((n,)),
            pltpu.SemaphoreType.DMA((n,)),
            pltpu.SemaphoreType.DMA((n,)),
            pltpu.SemaphoreType.DMA((m,)),
            pltpu.SemaphoreType.DMA((m,)),
        ],
        compiler_params=pltpu.CompilerParams(collective_id=collective_id, has_side_effects=True),
    )(x, icol)


def all_reduce(x, axis, other, n, collective_id, two_phase=True):
    rows, lanes = x.shape
    ch = rows // n if two_phase else rows
    slots = ch if two_phase else rows
    return pl.pallas_call(
        functools.partial(_reduce_kernel, axis, other, n, ch, two_phase),
        out_shape=jax.ShapeDtypeStruct(x.shape, x.dtype),
        in_specs=[pl.BlockSpec(memory_space=pltpu.VMEM)],
        out_specs=pl.BlockSpec(memory_space=pltpu.VMEM),
        scratch_shapes=[
            pltpu.VMEM((n, slots, lanes), x.dtype),
            pltpu.VMEM((ch, lanes), x.dtype),
            pltpu.VMEM((n, ch, lanes), x.dtype),
            pltpu.SemaphoreType.DMA((n,)),
            pltpu.SemaphoreType.DMA((n,)),
            pltpu.SemaphoreType.DMA((n,)),
            pltpu.SemaphoreType.DMA((n,)),
        ],
        compiler_params=pltpu.CompilerParams(collective_id=collective_id, has_side_effects=True),
    )(x)


def rotate(projected, gram):
    lower = jnp.linalg.cholesky(gram)
    inverse = lax.linalg.triangular_solve(
        lower, jnp.eye(gram.shape[0], dtype=jnp.float32), left_side=True, lower=True
    )
    return jnp.einsum(
        "kl,bli->bki",
        inverse,
        projected,
        precision=lax.Precision.HIGHEST,
        preferred_element_type=jnp.float32,
    )


def rotate_pairs(projected, gram):
    lower = jnp.linalg.cholesky(gram)
    inverse = lax.linalg.triangular_solve(
        lower, jnp.eye(gram.shape[0], dtype=jnp.float32), left_side=True, lower=True
    )
    return jnp.einsum(
        "kl,plx->pkx",
        inverse,
        projected,
        precision=lax.Precision.HIGHEST,
        preferred_element_type=jnp.float32,
    )


def local_gram(projected):
    return jnp.einsum(
        "bki,bli->kl",
        projected,
        projected,
        precision=lax.Precision.HIGHEST,
        preferred_element_type=jnp.float32,
    )


def panel_sum(partial, axis, other, n, collective_id):
    blocks, vecs, bsize = partial.shape
    flat = partial.reshape(blocks * vecs * bsize // LANES, LANES)
    return all_reduce(flat, axis, other, n, collective_id).reshape(blocks, vecs, bsize)


def per_device(blocks, block_row, block_col, counts, vectors, row_mass, col_mass):
    tile = blocks[0, 0]
    n_cap = tile.shape[0]
    bsize = row_mass.shape[1]
    vecs = vectors.shape[1] // bsize
    own = vectors.shape[0]
    n_row = lax.axis_size("row")
    n_col = lax.axis_size("col")
    row_panel = own * n_col
    col_panel = own * n_row
    total_boxes = float(own * bsize * n_row * n_col)
    rows_idx = block_row[0, 0]
    cols_idx = block_col[0, 0]
    live = jnp.arange(n_cap) < counts[0, 0]
    fwd_ids = jnp.where(live, rows_idx, row_panel)
    bwd_ids = jnp.where(live, cols_idx, col_panel)
    square = tile.reshape(n_cap, bsize, bsize)
    vec_rows = own * vecs * bsize // LANES
    own_inv = 1.0 / jnp.sqrt(col_mass)
    first = (vectors.reshape(own, vecs, bsize) * own_inv[:, None, :]).astype(jnp.bfloat16)
    mass_pad = jnp.zeros((8, 128), jnp.float32).at[0, : own * bsize].set(col_mass.reshape(-1))
    got, mass_got = all_gather2(first.reshape(vec_rows, LANES), mass_pad, "row", "col", n_row, 4)
    first_panel = got.reshape(col_panel, vecs, bsize)
    col_mass_panel = mass_got.reshape(n_row, 8, 128)[:, 0, : own * bsize].reshape(col_panel, bsize)
    inv_col = 1.0 / jnp.sqrt(col_mass_panel)
    pairs = col_panel // 2
    inv_pairs = inv_col.reshape(pairs, 1, 2 * bsize)
    own_pair = jnp.broadcast_to(own_inv.reshape(1, own * bsize), (vecs, own * bsize))
    row_mass_spread = jnp.broadcast_to(row_mass[:, None, :], (own, vecs, bsize)).reshape(vec_rows, LANES)
    fwd_hot = (fwd_ids[None, :] == jnp.arange(row_panel)[:, None]).astype(jnp.bfloat16)
    bwd_hot = (bwd_ids[None, :] == jnp.arange(col_panel)[:, None]).astype(jnp.bfloat16)
    for step in range(ITERS):
        if step == 0:
            scaled = first_panel
        else:
            paired = (current * inv_pairs).astype(jnp.bfloat16)
            scaled = paired.reshape(pairs, vecs, 2, bsize).transpose(0, 2, 1, 3).reshape(col_panel, vecs, bsize)
        forward_taken = jnp.take(scaled, cols_idx, axis=0)
        forward_product = jnp.einsum(
            "bij,bkj->bki", square, forward_taken, preferred_element_type=jnp.bfloat16
        )
        forward_summed = jnp.einsum(
            "rs,ski->rki", fwd_hot, forward_product, preferred_element_type=jnp.float32
        )
        flat = forward_summed.reshape(row_panel * vecs * bsize // LANES, LANES)
        weighted = forward_reduce(flat, row_mass_spread, n_col, 1).reshape(row_panel, vecs, bsize)
        taken = jnp.take(weighted, rows_idx, axis=0)
        product = jnp.einsum("bij,bki->bkj", square, taken, preferred_element_type=jnp.bfloat16)
        pair_hot = bwd_hot.reshape(pairs, 2, n_cap)
        summed = jnp.concatenate(
            [
                jnp.einsum("ps,skj->pkj", pair_hot[:, half], product, preferred_element_type=jnp.float32)
                for half in range(2)
            ],
            axis=2,
        )
        current = backward_reduce(summed, own_pair, n_row, n_col, 1.0 / total_boxes, 2)
    me = lax.axis_index("row")
    mine = lax.dynamic_index_in_dim(current, me, 0, keepdims=False)
    return mine.reshape(vecs, own, bsize).transpose(1, 0, 2).reshape(own, vecs * bsize)


def solution(mesh):
    in_specs = (
        P("row", "col", None, None),
        P("row", "col", None),
        P("row", "col", None),
        P("row", "col"),
        P(("col", "row"), None),
        P(("row", "col"), None),
        P(("col", "row"), None),
    )
    out_specs = P(("col", "row"), None)
    return jax.shard_map(
        per_device, mesh=mesh, in_specs=in_specs, out_specs=out_specs, check_vma=False
    )
```

```python
import functools

import jax
import jax.numpy as jnp
from jax import lax
from jax.experimental import pallas as pl
from jax.experimental.pallas import tpu as pltpu
from jax.sharding import PartitionSpec as P

ITERS = 4
LANES = 512
MESH_ID = pl.DeviceIdType.MESH


def _peer(axis, other, p):
    them = lax.axis_index(other)
    return (p, them) if axis == "row" else (them, p)


def _reduce_kernel(axis, other, n, ch, two_phase, x_ref, o_ref, recv, mine, gath, s1, r1, s2, r2):
    me = lax.axis_index(axis)
    barrier = pltpu.get_barrier_semaphore()
    for d in range(1, n):
        pl.semaphore_signal(
            barrier, 1, device_id=_peer(axis, other, (me + d) % n), device_id_type=MESH_ID
        )
    pl.semaphore_wait(barrier, n - 1)
    if not two_phase:
        sends = []
        for d in range(1, n):
            c = pltpu.make_async_remote_copy(
                x_ref, recv.at[d], s1.at[d], r1.at[d],
                device_id=_peer(axis, other, (me + d) % n), device_id_type=MESH_ID,
            )
            c.start()
            sends.append(c)
        for c in sends:
            c.wait()
        recv[0] = x_ref[...]
        acc = recv[me % n]
        for p in range(1, n):
            acc = acc + recv[(me - p + n) % n]
        o_ref[...] = acc
        return
    sends = []
    for d in range(1, n):
        peer = (me + d) % n
        start = pl.multiple_of(peer * ch, ch)
        c = pltpu.make_async_remote_copy(
            x_ref.at[pl.ds(start, ch)], recv.at[d], s1.at[d], r1.at[d],
            device_id=_peer(axis, other, peer), device_id_type=MESH_ID,
        )
        c.start()
        sends.append(c)
    own = pl.multiple_of(me * ch, ch)
    acc = x_ref[pl.ds(own, ch), :]
    for d, c in enumerate(sends, 1):
        c.wait()
        acc = acc + recv[d]
    mine[...] = acc
    gathers = []
    for d in range(1, n):
        c = pltpu.make_async_remote_copy(
            mine, gath.at[d], s2.at[d], r2.at[d],
            device_id=_peer(axis, other, (me + d) % n), device_id_type=MESH_ID,
        )
        c.start()
        gathers.append(c)
    o_ref[pl.ds(own, ch), :] = acc
    for d, c in enumerate(gathers, 1):
        c.wait()
        src = pl.multiple_of(((me - d + n) % n) * ch, ch)
        o_ref[pl.ds(src, ch), :] = gath[d]


def _gather_kernel(axis, other, n, x_ref, o_ref, gath, s2, r2):
    me = lax.axis_index(axis)
    ch = x_ref.shape[0]
    barrier = pltpu.get_barrier_semaphore()
    for d in range(1, n):
        pl.semaphore_signal(
            barrier, 1, device_id=_peer(axis, other, (me + d) % n), device_id_type=MESH_ID
        )
    pl.semaphore_wait(barrier, n - 1)
    gathers = []
    for d in range(1, n):
        c = pltpu.make_async_remote_copy(
            x_ref, gath.at[d], s2.at[d], r2.at[d],
            device_id=_peer(axis, other, (me + d) % n), device_id_type=MESH_ID,
        )
        c.start()
        gathers.append(c)
    o_ref[pl.ds(pl.multiple_of(me * ch, ch), ch), :] = x_ref[...]
    for d, c in enumerate(gathers, 1):
        c.wait()
        src = pl.multiple_of(((me - d + n) % n) * ch, ch)
        o_ref[pl.ds(src, ch), :] = gath[d]


def all_gather(x, axis, other, n, collective_id):
    ch, lanes = x.shape
    return pl.pallas_call(
        functools.partial(_gather_kernel, axis, other, n),
        out_shape=jax.ShapeDtypeStruct((n * ch, lanes), x.dtype),
        in_specs=[pl.BlockSpec(memory_space=pltpu.VMEM)],
        out_specs=pl.BlockSpec(memory_space=pltpu.VMEM),
        scratch_shapes=[
            pltpu.VMEM((n, ch, lanes), x.dtype),
            pltpu.SemaphoreType.DMA((n,)),
            pltpu.SemaphoreType.DMA((n,)),
        ],
        compiler_params=pltpu.CompilerParams(collective_id=collective_id, has_side_effects=True),
    )(x)


def _forward_kernel(n, ch, x_ref, mass_ref, o_ref, recv, mine, gath, s1, r1, s2, r2):
    axis, other = "col", "row"
    me = lax.axis_index(axis)
    barrier = pltpu.get_barrier_semaphore()
    for d in range(1, n):
        pl.semaphore_signal(
            barrier, 1, device_id=_peer(axis, other, (me + d) % n), device_id_type=MESH_ID
        )
    pl.semaphore_wait(barrier, n - 1)
    sends = []
    for d in range(1, n):
        peer = (me + d) % n
        start = pl.multiple_of(peer * ch, ch)
        c = pltpu.make_async_remote_copy(
            x_ref.at[pl.ds(start, ch)], recv.at[d], s1.at[d], r1.at[d],
            device_id=_peer(axis, other, peer), device_id_type=MESH_ID,
        )
        c.start()
        sends.append(c)
    own = pl.multiple_of(me * ch, ch)
    acc = x_ref[pl.ds(own, ch), :]
    for d, c in enumerate(sends, 1):
        c.wait()
        acc = acc + recv[d]
    mine[...] = (acc * mass_ref[...]).astype(mine.dtype)
    gathers = []
    for d in range(1, n):
        c = pltpu.make_async_remote_copy(
            mine, gath.at[d], s2.at[d], r2.at[d],
            device_id=_peer(axis, other, (me + d) % n), device_id_type=MESH_ID,
        )
        c.start()
        gathers.append(c)
    o_ref[pl.ds(own, ch), :] = mine[...]
    for d, c in enumerate(gathers, 1):
        c.wait()
        src = pl.multiple_of(((me - d + n) % n) * ch, ch)
        o_ref[pl.ds(src, ch), :] = gath[d]


def forward_reduce(x, mass, n, collective_id):
    rows, lanes = x.shape
    ch = rows // n
    return pl.pallas_call(
        functools.partial(_forward_kernel, n, ch),
        out_shape=jax.ShapeDtypeStruct(x.shape, jnp.bfloat16),
        in_specs=[pl.BlockSpec(memory_space=pltpu.VMEM)] * 2,
        out_specs=pl.BlockSpec(memory_space=pltpu.VMEM),
        scratch_shapes=[
            pltpu.VMEM((n, ch, lanes), x.dtype),
            pltpu.VMEM((ch, lanes), jnp.bfloat16),
            pltpu.VMEM((n, ch, lanes), jnp.bfloat16),
            pltpu.SemaphoreType.DMA((n,)),
            pltpu.SemaphoreType.DMA((n,)),
            pltpu.SemaphoreType.DMA((n,)),
            pltpu.SemaphoreType.DMA((n,)),
        ],
        compiler_params=pltpu.CompilerParams(collective_id=collective_id, has_side_effects=True),
    )(x, mass)


def _gather2_kernel(axis, other, n, x_ref, y_ref, o_ref, p_ref, gx, gy, sx, rx, sy, ry):
    me = lax.axis_index(axis)
    cx = x_ref.shape[0]
    cy = y_ref.shape[0]
    barrier = pltpu.get_barrier_semaphore()
    for d in range(1, n):
        pl.semaphore_signal(
            barrier, 1, device_id=_peer(axis, other, (me + d) % n), device_id_type=MESH_ID
        )
    pl.semaphore_wait(barrier, n - 1)
    copies = []
    for d in range(1, n):
        peer = _peer(axis, other, (me + d) % n)
        a = pltpu.make_async_remote_copy(
            x_ref, gx.at[d], sx.at[d], rx.at[d], device_id=peer, device_id_type=MESH_ID
        )
        b = pltpu.make_async_remote_copy(
            y_ref, gy.at[d], sy.at[d], ry.at[d], device_id=peer, device_id_type=MESH_ID
        )
        a.start()
        b.start()
        copies.append((a, b))
    o_ref[pl.ds(pl.multiple_of(me * cx, cx), cx), :] = x_ref[...]
    p_ref[pl.ds(pl.multiple_of(me * cy, cy), cy), :] = y_ref[...]
    for d, (a, b) in enumerate(copies, 1):
        a.wait()
        b.wait()
        src = (me - d + n) % n
        o_ref[pl.ds(pl.multiple_of(src * cx, cx), cx), :] = gx[d]
        p_ref[pl.ds(pl.multiple_of(src * cy, cy), cy), :] = gy[d]


def all_gather2(x, y, axis, other, n, collective_id):
    return pl.pallas_call(
        functools.partial(_gather2_kernel, axis, other, n),
        out_shape=(
            jax.ShapeDtypeStruct((n * x.shape[0], x.shape[1]), x.dtype),
            jax.ShapeDtypeStruct((n * y.shape[0], y.shape[1]), y.dtype),
        ),
        in_specs=[pl.BlockSpec(memory_space=pltpu.VMEM)] * 2,
        out_specs=(pl.BlockSpec(memory_space=pltpu.VMEM),) * 2,
        scratch_shapes=[
            pltpu.VMEM((n,) + x.shape, x.dtype),
            pltpu.VMEM((n,) + y.shape, y.dtype),
            pltpu.SemaphoreType.DMA((n,)),
            pltpu.SemaphoreType.DMA((n,)),
            pltpu.SemaphoreType.DMA((n,)),
            pltpu.SemaphoreType.DMA((n,)),
        ],
        compiler_params=pltpu.CompilerParams(collective_id=collective_id, has_side_effects=True),
    )(x, y)


def _gram_of(a):
    return lax.dot_general(
        a, a, (((1,), (1,)), ((), ())), precision=lax.Precision.HIGHEST,
        preferred_element_type=jnp.float32,
    )


def chol_inverse(a):
    n = a.shape[0]
    r = lax.broadcasted_iota(jnp.int32, (n, n), 0)
    c = lax.broadcasted_iota(jnp.int32, (n, n), 1)
    r1 = lax.broadcasted_iota(jnp.int32, (n, 1), 0)
    c1 = lax.broadcasted_iota(jnp.int32, (1, n), 1)
    x0 = jnp.where(r == c, 1.0, 0.0).astype(jnp.float32)
    d0 = jnp.sum(jnp.where(r == c, a, 0.0), axis=0, keepdims=True)

    def step(j, carry):
        m, x, d = carry
        inv = 1.0 / jnp.sqrt(jnp.sum(jnp.where(c1 == j, d, 0.0), axis=1, keepdims=True))
        col = jnp.sum(jnp.where(c == j, m, 0.0), axis=1, keepdims=True)
        row = jnp.sum(jnp.where(r == j, m, 0.0), axis=0, keepdims=True)
        lcol = jnp.where(r1 >= j, col * inv, 0.0)
        lrow = jnp.where(c1 >= j, row * inv, 0.0)
        m = m - lcol * lrow
        d = d - lrow * lrow
        xrow = jnp.sum(jnp.where(r == j, x, 0.0), axis=0, keepdims=True) * inv
        x = jnp.where(r == j, xrow, x)
        x = x - jnp.where(r1 > j, lcol, 0.0) * xrow
        return m, x, d

    m, x, d = lax.fori_loop(0, n, step, (a, x0, d0))
    return x


def _backward_kernel(n, m, scale, x_ref, icol_ref, o_ref, recv, gath, g3, panel, s1, r1, s2, r2, s3, r3):
    me = lax.axis_index("row")
    mc = lax.axis_index("col")
    barrier = pltpu.get_barrier_semaphore()
    for d in range(1, n):
        pl.semaphore_signal(barrier, 1, device_id=((me + d) % n, mc), device_id_type=MESH_ID)
    for d in range(1, m):
        pl.semaphore_signal(barrier, 1, device_id=(me, (mc + d) % m), device_id_type=MESH_ID)
    pl.semaphore_wait(barrier, n - 1 + m - 1)
    sends = []
    for d in range(1, n):
        peer = (me + d) % n
        c = pltpu.make_async_remote_copy(
            x_ref.at[peer], recv.at[d], s1.at[d], r1.at[d],
            device_id=(peer, mc), device_id_type=MESH_ID,
        )
        c.start()
        sends.append(c)
    acc = x_ref[me]
    for d, c in enumerate(sends, 1):
        c.wait()
        acc = acc + recv[d]
    gath[0] = acc * icol_ref[...]
    gathers = []
    for d in range(1, n):
        c = pltpu.make_async_remote_copy(
            gath.at[0], gath.at[d], s2.at[d], r2.at[d],
            device_id=((me + d) % n, mc), device_id_type=MESH_ID,
        )
        c.start()
        gathers.append(c)
    for c in gathers:
        c.wait()
    lanes = gath.shape[2]
    for p in range(n):
        panel[:, p * lanes:(p + 1) * lanes] = gath[(me - p + n) % n]
    g3[0] = _gram_of(panel[...])
    grams = []
    for d in range(1, m):
        c = pltpu.make_async_remote_copy(
            g3.at[0], g3.at[d], s3.at[d], r3.at[d],
            device_id=(me, (mc + d) % m), device_id_type=MESH_ID,
        )
        c.start()
        grams.append(c)
    for c in grams:
        c.wait()
    total = g3[mc % m]
    for q in range(1, m):
        total = total + g3[(mc - q + m) % m]
    inverse = chol_inverse(total * scale)
    rotated = lax.dot_general(
        inverse, panel[...], (((1,), (0,)), ((), ())),
        precision=lax.Precision.HIGHEST, preferred_element_type=jnp.float32,
    )
    for p in range(n):
        o_ref[p] = rotated[:, p * lanes:(p + 1) * lanes]


def backward_reduce(x, icol, n, m, scale, collective_id):
    chunks, vecs, lanes = x.shape
    return pl.pallas_call(
        functools.partial(_backward_kernel, n, m, scale),
        out_shape=jax.ShapeDtypeStruct(x.shape, jnp.float32),
        in_specs=[pl.BlockSpec(memory_space=pltpu.VMEM)] * 2,
        out_specs=pl.BlockSpec(memory_space=pltpu.VMEM),
        scratch_shapes=[
            pltpu.VMEM((n, vecs, lanes), jnp.float32),
            pltpu.VMEM((n, vecs, lanes), jnp.float32),
            pltpu.VMEM((m, vecs, vecs), jnp.float32),
            pltpu.VMEM((vecs, n * lanes), jnp.float32),
            pltpu.SemaphoreType.DMA((n,)),
            pltpu.SemaphoreType.DMA((n,)),
            pltpu.SemaphoreType.DMA((n,)),
            pltpu.SemaphoreType.DMA((n,)),
            pltpu.SemaphoreType.DMA((m,)),
            pltpu.SemaphoreType.DMA((m,)),
        ],
        compiler_params=pltpu.CompilerParams(collective_id=collective_id, has_side_effects=True),
    )(x, icol)


def all_reduce(x, axis, other, n, collective_id, two_phase=True):
    rows, lanes = x.shape
    ch = rows // n if two_phase else rows
    slots = ch if two_phase else rows
    return pl.pallas_call(
        functools.partial(_reduce_kernel, axis, other, n, ch, two_phase),
        out_shape=jax.ShapeDtypeStruct(x.shape, x.dtype),
        in_specs=[pl.BlockSpec(memory_space=pltpu.VMEM)],
        out_specs=pl.BlockSpec(memory_space=pltpu.VMEM),
        scratch_shapes=[
            pltpu.VMEM((n, slots, lanes), x.dtype),
            pltpu.VMEM((ch, lanes), x.dtype),
            pltpu.VMEM((n, ch, lanes), x.dtype),
            pltpu.SemaphoreType.DMA((n,)),
            pltpu.SemaphoreType.DMA((n,)),
            pltpu.SemaphoreType.DMA((n,)),
            pltpu.SemaphoreType.DMA((n,)),
        ],
        compiler_params=pltpu.CompilerParams(collective_id=collective_id, has_side_effects=True),
    )(x)


def rotate(projected, gram):
    lower = jnp.linalg.cholesky(gram)
    inverse = lax.linalg.triangular_solve(
        lower, jnp.eye(gram.shape[0], dtype=jnp.float32), left_side=True, lower=True
    )
    return jnp.einsum(
        "kl,bli->bki",
        inverse,
        projected,
        precision=lax.Precision.HIGHEST,
        preferred_element_type=jnp.float32,
    )


def rotate_pairs(projected, gram):
    lower = jnp.linalg.cholesky(gram)
    inverse = lax.linalg.triangular_solve(
        lower, jnp.eye(gram.shape[0], dtype=jnp.float32), left_side=True, lower=True
    )
    return jnp.einsum(
        "kl,plx->pkx",
        inverse,
        projected,
        precision=lax.Precision.HIGHEST,
        preferred_element_type=jnp.float32,
    )


def local_gram(projected):
    return jnp.einsum(
        "bki,bli->kl",
        projected,
        projected,
        precision=lax.Precision.HIGHEST,
        preferred_element_type=jnp.float32,
    )


def panel_sum(partial, axis, other, n, collective_id):
    blocks, vecs, bsize = partial.shape
    flat = partial.reshape(blocks * vecs * bsize // LANES, LANES)
    return all_reduce(flat, axis, other, n, collective_id).reshape(blocks, vecs, bsize)


def per_device(blocks, block_row, block_col, counts, vectors, row_mass, col_mass):
    tile = blocks[0, 0]
    n_cap = tile.shape[0]
    bsize = row_mass.shape[1]
    vecs = vectors.shape[1] // bsize
    own = vectors.shape[0]
    n_row = lax.axis_size("row")
    n_col = lax.axis_size("col")
    row_panel = own * n_col
    col_panel = own * n_row
    total_boxes = float(own * bsize * n_row * n_col)
    rows_idx = block_row[0, 0]
    cols_idx = block_col[0, 0]
    live = jnp.arange(n_cap) < counts[0, 0]
    fwd_ids = jnp.where(live, rows_idx, row_panel)
    bwd_ids = jnp.where(live, cols_idx, col_panel)
    square = tile.reshape(n_cap, bsize, bsize)
    vec_rows = own * vecs * bsize // LANES
    own_inv = 1.0 / jnp.sqrt(col_mass)
    first = (vectors.reshape(own, vecs, bsize) * own_inv[:, None, :]).astype(jnp.bfloat16)
    mass_pad = jnp.zeros((8, 128), jnp.float32).at[0, : own * bsize].set(col_mass.reshape(-1))
    got, mass_got = all_gather2(first.reshape(vec_rows, LANES), mass_pad, "row", "col", n_row, 4)
    first_panel = got.reshape(col_panel, vecs, bsize)
    col_mass_panel = mass_got.reshape(n_row, 8, 128)[:, 0, : own * bsize].reshape(col_panel, bsize)
    inv_col = 1.0 / jnp.sqrt(col_mass_panel)
    pairs = col_panel // 2
    inv_pairs = inv_col.reshape(pairs, 1, 2 * bsize)
    own_pair = jnp.broadcast_to(own_inv.reshape(1, own * bsize), (vecs, own * bsize))
    row_mass_spread = jnp.broadcast_to(row_mass[:, None, :], (own, vecs, bsize)).reshape(vec_rows, LANES)
    col_pick = (cols_idx[:, None] == jnp.arange(col_panel)[None, :]).astype(jnp.bfloat16)
    row_pick = (rows_idx[:, None] == jnp.arange(row_panel)[None, :]).astype(jnp.bfloat16)
    fwd_hot = (fwd_ids[None, :] == jnp.arange(row_panel)[:, None]).astype(jnp.bfloat16)
    bwd_hot = (bwd_ids[None, :] == jnp.arange(col_panel)[:, None]).astype(jnp.bfloat16)
    for step in range(ITERS):
        if step == 0:
            scaled = first_panel
        else:
            paired = (current * inv_pairs).astype(jnp.bfloat16)
            scaled = paired.reshape(pairs, vecs, 2, bsize).transpose(0, 2, 1, 3).reshape(col_panel, vecs, bsize)
        forward_taken = jnp.einsum(
            "sc,ckj->skj", col_pick, scaled, preferred_element_type=jnp.float32
        ).astype(jnp.bfloat16)
        forward_product = jnp.einsum(
            "bij,bkj->bki", square, forward_taken, preferred_element_type=jnp.bfloat16
        )
        forward_summed = jnp.einsum(
            "rs,ski->rki", fwd_hot, forward_product, preferred_element_type=jnp.float32
        )
        flat = forward_summed.reshape(row_panel * vecs * bsize // LANES, LANES)
        weighted = forward_reduce(flat, row_mass_spread, n_col, 1).reshape(row_panel, vecs, bsize)
        taken = jnp.einsum(
            "sr,rki->ski", row_pick, weighted, preferred_element_type=jnp.float32
        ).astype(jnp.bfloat16)
        product = jnp.einsum("bij,bki->bkj", square, taken, preferred_element_type=jnp.bfloat16)
        summed = jnp.einsum(
            "pbs,skj->pkbj", bwd_hot.reshape(pairs, 2, n_cap), product,
            preferred_element_type=jnp.float32,
        ).reshape(pairs, vecs, 2 * bsize)
        current = backward_reduce(summed, own_pair, n_row, n_col, 1.0 / total_boxes, 2)
    me = lax.axis_index("row")
    mine = lax.dynamic_index_in_dim(current, me, 0, keepdims=False)
    return mine.reshape(vecs, own, bsize).transpose(1, 0, 2).reshape(own, vecs * bsize)


def solution(mesh):
    in_specs = (
        P("row", "col", None, None),
        P("row", "col", None),
        P("row", "col", None),
        P("row", "col"),
        P(("col", "row"), None),
        P(("row", "col"), None),
        P(("col", "row"), None),
    )
    out_specs = P(("col", "row"), None)
    return jax.shard_map(
        per_device, mesh=mesh, in_specs=in_specs, out_specs=out_specs, check_vma=False
    )
```

```python
import functools

import jax
import jax.numpy as jnp
from jax import lax
from jax.experimental import pallas as pl
from jax.experimental.pallas import tpu as pltpu
from jax.sharding import PartitionSpec as P

ITERS = 4
LANES = 512
MESH_ID = pl.DeviceIdType.MESH


def _peer(axis, other, p):
    them = lax.axis_index(other)
    return (p, them) if axis == "row" else (them, p)


def _reduce_kernel(axis, other, n, ch, two_phase, x_ref, o_ref, recv, mine, gath, s1, r1, s2, r2):
    me = lax.axis_index(axis)
    barrier = pltpu.get_barrier_semaphore()
    for d in range(1, n):
        pl.semaphore_signal(
            barrier, 1, device_id=_peer(axis, other, (me + d) % n), device_id_type=MESH_ID
        )
    pl.semaphore_wait(barrier, n - 1)
    if not two_phase:
        sends = []
        for d in range(1, n):
            c = pltpu.make_async_remote_copy(
                x_ref, recv.at[d], s1.at[d], r1.at[d],
                device_id=_peer(axis, other, (me + d) % n), device_id_type=MESH_ID,
            )
            c.start()
            sends.append(c)
        for c in sends:
            c.wait()
        recv[0] = x_ref[...]
        acc = recv[me % n]
        for p in range(1, n):
            acc = acc + recv[(me - p + n) % n]
        o_ref[...] = acc
        return
    sends = []
    for d in range(1, n):
        peer = (me + d) % n
        start = pl.multiple_of(peer * ch, ch)
        c = pltpu.make_async_remote_copy(
            x_ref.at[pl.ds(start, ch)], recv.at[d], s1.at[d], r1.at[d],
            device_id=_peer(axis, other, peer), device_id_type=MESH_ID,
        )
        c.start()
        sends.append(c)
    own = pl.multiple_of(me * ch, ch)
    acc = x_ref[pl.ds(own, ch), :]
    for d, c in enumerate(sends, 1):
        c.wait()
        acc = acc + recv[d]
    mine[...] = acc
    gathers = []
    for d in range(1, n):
        c = pltpu.make_async_remote_copy(
            mine, gath.at[d], s2.at[d], r2.at[d],
            device_id=_peer(axis, other, (me + d) % n), device_id_type=MESH_ID,
        )
        c.start()
        gathers.append(c)
    o_ref[pl.ds(own, ch), :] = acc
    for d, c in enumerate(gathers, 1):
        c.wait()
        src = pl.multiple_of(((me - d + n) % n) * ch, ch)
        o_ref[pl.ds(src, ch), :] = gath[d]


def _gather_kernel(axis, other, n, x_ref, o_ref, gath, s2, r2):
    me = lax.axis_index(axis)
    ch = x_ref.shape[0]
    barrier = pltpu.get_barrier_semaphore()
    for d in range(1, n):
        pl.semaphore_signal(
            barrier, 1, device_id=_peer(axis, other, (me + d) % n), device_id_type=MESH_ID
        )
    pl.semaphore_wait(barrier, n - 1)
    gathers = []
    for d in range(1, n):
        c = pltpu.make_async_remote_copy(
            x_ref, gath.at[d], s2.at[d], r2.at[d],
            device_id=_peer(axis, other, (me + d) % n), device_id_type=MESH_ID,
        )
        c.start()
        gathers.append(c)
    o_ref[pl.ds(pl.multiple_of(me * ch, ch), ch), :] = x_ref[...]
    for d, c in enumerate(gathers, 1):
        c.wait()
        src = pl.multiple_of(((me - d + n) % n) * ch, ch)
        o_ref[pl.ds(src, ch), :] = gath[d]


def all_gather(x, axis, other, n, collective_id):
    ch, lanes = x.shape
    return pl.pallas_call(
        functools.partial(_gather_kernel, axis, other, n),
        out_shape=jax.ShapeDtypeStruct((n * ch, lanes), x.dtype),
        in_specs=[pl.BlockSpec(memory_space=pltpu.VMEM)],
        out_specs=pl.BlockSpec(memory_space=pltpu.VMEM),
        scratch_shapes=[
            pltpu.VMEM((n, ch, lanes), x.dtype),
            pltpu.SemaphoreType.DMA((n,)),
            pltpu.SemaphoreType.DMA((n,)),
        ],
        compiler_params=pltpu.CompilerParams(collective_id=collective_id, has_side_effects=True),
    )(x)


def _forward_kernel(n, ch, x_ref, mass_ref, o_ref, recv, mine, gath, s1, r1, s2, r2):
    axis, other = "col", "row"
    me = lax.axis_index(axis)
    barrier = pltpu.get_barrier_semaphore()
    for d in range(1, n):
        pl.semaphore_signal(
            barrier, 1, device_id=_peer(axis, other, (me + d) % n), device_id_type=MESH_ID
        )
    pl.semaphore_wait(barrier, n - 1)
    sends = []
    for d in range(1, n):
        peer = (me + d) % n
        start = pl.multiple_of(peer * ch, ch)
        c = pltpu.make_async_remote_copy(
            x_ref.at[pl.ds(start, ch)], recv.at[d], s1.at[d], r1.at[d],
            device_id=_peer(axis, other, peer), device_id_type=MESH_ID,
        )
        c.start()
        sends.append(c)
    own = pl.multiple_of(me * ch, ch)
    acc = x_ref[pl.ds(own, ch), :]
    for d, c in enumerate(sends, 1):
        c.wait()
        acc = acc + recv[d]
    mine[...] = (acc * mass_ref[...]).astype(mine.dtype)
    gathers = []
    for d in range(1, n):
        c = pltpu.make_async_remote_copy(
            mine, gath.at[d], s2.at[d], r2.at[d],
            device_id=_peer(axis, other, (me + d) % n), device_id_type=MESH_ID,
        )
        c.start()
        gathers.append(c)
    o_ref[pl.ds(own, ch), :] = mine[...]
    for d, c in enumerate(gathers, 1):
        c.wait()
        src = pl.multiple_of(((me - d + n) % n) * ch, ch)
        o_ref[pl.ds(src, ch), :] = gath[d]


def forward_reduce(x, mass, n, collective_id):
    rows, lanes = x.shape
    ch = rows // n
    return pl.pallas_call(
        functools.partial(_forward_kernel, n, ch),
        out_shape=jax.ShapeDtypeStruct(x.shape, jnp.bfloat16),
        in_specs=[pl.BlockSpec(memory_space=pltpu.VMEM)] * 2,
        out_specs=pl.BlockSpec(memory_space=pltpu.VMEM),
        scratch_shapes=[
            pltpu.VMEM((n, ch, lanes), x.dtype),
            pltpu.VMEM((ch, lanes), jnp.bfloat16),
            pltpu.VMEM((n, ch, lanes), jnp.bfloat16),
            pltpu.SemaphoreType.DMA((n,)),
            pltpu.SemaphoreType.DMA((n,)),
            pltpu.SemaphoreType.DMA((n,)),
            pltpu.SemaphoreType.DMA((n,)),
        ],
        compiler_params=pltpu.CompilerParams(collective_id=collective_id, has_side_effects=True),
    )(x, mass)


def _gather2_kernel(axis, other, n, x_ref, y_ref, o_ref, p_ref, gx, gy, sx, rx, sy, ry):
    me = lax.axis_index(axis)
    cx = x_ref.shape[0]
    cy = y_ref.shape[0]
    barrier = pltpu.get_barrier_semaphore()
    for d in range(1, n):
        pl.semaphore_signal(
            barrier, 1, device_id=_peer(axis, other, (me + d) % n), device_id_type=MESH_ID
        )
    pl.semaphore_wait(barrier, n - 1)
    copies = []
    for d in range(1, n):
        peer = _peer(axis, other, (me + d) % n)
        a = pltpu.make_async_remote_copy(
            x_ref, gx.at[d], sx.at[d], rx.at[d], device_id=peer, device_id_type=MESH_ID
        )
        b = pltpu.make_async_remote_copy(
            y_ref, gy.at[d], sy.at[d], ry.at[d], device_id=peer, device_id_type=MESH_ID
        )
        a.start()
        b.start()
        copies.append((a, b))
    o_ref[pl.ds(pl.multiple_of(me * cx, cx), cx), :] = x_ref[...]
    p_ref[pl.ds(pl.multiple_of(me * cy, cy), cy), :] = y_ref[...]
    for d, (a, b) in enumerate(copies, 1):
        a.wait()
        b.wait()
        src = (me - d + n) % n
        o_ref[pl.ds(pl.multiple_of(src * cx, cx), cx), :] = gx[d]
        p_ref[pl.ds(pl.multiple_of(src * cy, cy), cy), :] = gy[d]


def all_gather2(x, y, axis, other, n, collective_id):
    return pl.pallas_call(
        functools.partial(_gather2_kernel, axis, other, n),
        out_shape=(
            jax.ShapeDtypeStruct((n * x.shape[0], x.shape[1]), x.dtype),
            jax.ShapeDtypeStruct((n * y.shape[0], y.shape[1]), y.dtype),
        ),
        in_specs=[pl.BlockSpec(memory_space=pltpu.VMEM)] * 2,
        out_specs=(pl.BlockSpec(memory_space=pltpu.VMEM),) * 2,
        scratch_shapes=[
            pltpu.VMEM((n,) + x.shape, x.dtype),
            pltpu.VMEM((n,) + y.shape, y.dtype),
            pltpu.SemaphoreType.DMA((n,)),
            pltpu.SemaphoreType.DMA((n,)),
            pltpu.SemaphoreType.DMA((n,)),
            pltpu.SemaphoreType.DMA((n,)),
        ],
        compiler_params=pltpu.CompilerParams(collective_id=collective_id, has_side_effects=True),
    )(x, y)


def _gram_of(a):
    return lax.dot_general(
        a, a, (((1,), (1,)), ((), ())), precision=lax.Precision.HIGHEST,
        preferred_element_type=jnp.float32,
    )


def chol_inverse(a):
    n = a.shape[0]
    r = lax.broadcasted_iota(jnp.int32, (n, n), 0)
    c = lax.broadcasted_iota(jnp.int32, (n, n), 1)
    r1 = lax.broadcasted_iota(jnp.int32, (n, 1), 0)
    c1 = lax.broadcasted_iota(jnp.int32, (1, n), 1)
    x0 = jnp.where(r == c, 1.0, 0.0).astype(jnp.float32)
    d0 = jnp.sum(jnp.where(r == c, a, 0.0), axis=0, keepdims=True)

    def step(j, carry):
        m, x, d = carry
        inv = 1.0 / jnp.sqrt(jnp.sum(jnp.where(c1 == j, d, 0.0), axis=1, keepdims=True))
        col = jnp.sum(jnp.where(c == j, m, 0.0), axis=1, keepdims=True)
        row = jnp.sum(jnp.where(r == j, m, 0.0), axis=0, keepdims=True)
        lcol = jnp.where(r1 >= j, col * inv, 0.0)
        lrow = jnp.where(c1 >= j, row * inv, 0.0)
        m = m - lcol * lrow
        d = d - lrow * lrow
        xrow = jnp.sum(jnp.where(r == j, x, 0.0), axis=0, keepdims=True) * inv
        x = jnp.where(r == j, xrow, x)
        x = x - jnp.where(r1 > j, lcol, 0.0) * xrow
        return m, x, d

    m, x, d = lax.fori_loop(0, n, step, (a, x0, d0))
    return x


def _backward_kernel(n, m, scale, x_ref, icol_ref, o_ref, recv, gath, g3, panel, s1, r1, s2, r2, s3, r3):
    me = lax.axis_index("row")
    mc = lax.axis_index("col")
    barrier = pltpu.get_barrier_semaphore()
    for d in range(1, n):
        pl.semaphore_signal(barrier, 1, device_id=((me + d) % n, mc), device_id_type=MESH_ID)
    for d in range(1, m):
        pl.semaphore_signal(barrier, 1, device_id=(me, (mc + d) % m), device_id_type=MESH_ID)
    pl.semaphore_wait(barrier, n - 1 + m - 1)
    sends = []
    for d in range(1, n):
        peer = (me + d) % n
        c = pltpu.make_async_remote_copy(
            x_ref.at[peer], recv.at[d], s1.at[d], r1.at[d],
            device_id=(peer, mc), device_id_type=MESH_ID,
        )
        c.start()
        sends.append(c)
    acc = x_ref[me]
    for d, c in enumerate(sends, 1):
        c.wait()
        acc = acc + recv[d]
    gath[0] = acc * icol_ref[...]
    lanes = gath.shape[2]
    mine = pl.ds(pl.multiple_of(me * lanes, lanes), lanes)
    gathers = []
    for d in range(1, n):
        c = pltpu.make_async_remote_copy(
            gath.at[0], panel.at[:, mine], s2.at[d], r2.at[d],
            device_id=((me + d) % n, mc), device_id_type=MESH_ID,
        )
        c.start()
        gathers.append(c)
    for c in gathers:
        c.wait()
    panel[:, mine] = gath[0]
    g3[0] = _gram_of(panel[...])
    grams = []
    for d in range(1, m):
        c = pltpu.make_async_remote_copy(
            g3.at[0], g3.at[d], s3.at[d], r3.at[d],
            device_id=(me, (mc + d) % m), device_id_type=MESH_ID,
        )
        c.start()
        grams.append(c)
    for c in grams:
        c.wait()
    total = g3[mc % m]
    for q in range(1, m):
        total = total + g3[(mc - q + m) % m]
    inverse = chol_inverse(total * scale)
    rotated = lax.dot_general(
        inverse, panel[...], (((1,), (0,)), ((), ())),
        precision=lax.Precision.HIGHEST, preferred_element_type=jnp.float32,
    )
    for p in range(n):
        o_ref[p] = rotated[:, p * lanes:(p + 1) * lanes]


def backward_reduce(x, icol, n, m, scale, collective_id):
    chunks, vecs, lanes = x.shape
    return pl.pallas_call(
        functools.partial(_backward_kernel, n, m, scale),
        out_shape=jax.ShapeDtypeStruct(x.shape, jnp.float32),
        in_specs=[pl.BlockSpec(memory_space=pltpu.VMEM)] * 2,
        out_specs=pl.BlockSpec(memory_space=pltpu.VMEM),
        scratch_shapes=[
            pltpu.VMEM((n, vecs, lanes), jnp.float32),
            pltpu.VMEM((n, vecs, lanes), jnp.float32),
            pltpu.VMEM((m, vecs, vecs), jnp.float32),
            pltpu.VMEM((vecs, n * lanes), jnp.float32),
            pltpu.SemaphoreType.DMA((n,)),
            pltpu.SemaphoreType.DMA((n,)),
            pltpu.SemaphoreType.DMA((n,)),
            pltpu.SemaphoreType.DMA((n,)),
            pltpu.SemaphoreType.DMA((m,)),
            pltpu.SemaphoreType.DMA((m,)),
        ],
        compiler_params=pltpu.CompilerParams(collective_id=collective_id, has_side_effects=True),
    )(x, icol)


def all_reduce(x, axis, other, n, collective_id, two_phase=True):
    rows, lanes = x.shape
    ch = rows // n if two_phase else rows
    slots = ch if two_phase else rows
    return pl.pallas_call(
        functools.partial(_reduce_kernel, axis, other, n, ch, two_phase),
        out_shape=jax.ShapeDtypeStruct(x.shape, x.dtype),
        in_specs=[pl.BlockSpec(memory_space=pltpu.VMEM)],
        out_specs=pl.BlockSpec(memory_space=pltpu.VMEM),
        scratch_shapes=[
            pltpu.VMEM((n, slots, lanes), x.dtype),
            pltpu.VMEM((ch, lanes), x.dtype),
            pltpu.VMEM((n, ch, lanes), x.dtype),
            pltpu.SemaphoreType.DMA((n,)),
            pltpu.SemaphoreType.DMA((n,)),
            pltpu.SemaphoreType.DMA((n,)),
            pltpu.SemaphoreType.DMA((n,)),
        ],
        compiler_params=pltpu.CompilerParams(collective_id=collective_id, has_side_effects=True),
    )(x)


def rotate(projected, gram):
    lower = jnp.linalg.cholesky(gram)
    inverse = lax.linalg.triangular_solve(
        lower, jnp.eye(gram.shape[0], dtype=jnp.float32), left_side=True, lower=True
    )
    return jnp.einsum(
        "kl,bli->bki",
        inverse,
        projected,
        precision=lax.Precision.HIGHEST,
        preferred_element_type=jnp.float32,
    )


def rotate_pairs(projected, gram):
    lower = jnp.linalg.cholesky(gram)
    inverse = lax.linalg.triangular_solve(
        lower, jnp.eye(gram.shape[0], dtype=jnp.float32), left_side=True, lower=True
    )
    return jnp.einsum(
        "kl,plx->pkx",
        inverse,
        projected,
        precision=lax.Precision.HIGHEST,
        preferred_element_type=jnp.float32,
    )


def local_gram(projected):
    return jnp.einsum(
        "bki,bli->kl",
        projected,
        projected,
        precision=lax.Precision.HIGHEST,
        preferred_element_type=jnp.float32,
    )


def panel_sum(partial, axis, other, n, collective_id):
    blocks, vecs, bsize = partial.shape
    flat = partial.reshape(blocks * vecs * bsize // LANES, LANES)
    return all_reduce(flat, axis, other, n, collective_id).reshape(blocks, vecs, bsize)


def per_device(blocks, block_row, block_col, counts, vectors, row_mass, col_mass):
    tile = blocks[0, 0]
    n_cap = tile.shape[0]
    bsize = row_mass.shape[1]
    vecs = vectors.shape[1] // bsize
    own = vectors.shape[0]
    n_row = lax.axis_size("row")
    n_col = lax.axis_size("col")
    row_panel = own * n_col
    col_panel = own * n_row
    total_boxes = float(own * bsize * n_row * n_col)
    rows_idx = block_row[0, 0]
    cols_idx = block_col[0, 0]
    live = jnp.arange(n_cap) < counts[0, 0]
    fwd_ids = jnp.where(live, rows_idx, row_panel)
    bwd_ids = jnp.where(live, cols_idx, col_panel)
    square = tile.reshape(n_cap, bsize, bsize)
    vec_rows = own * vecs * bsize // LANES
    own_inv = 1.0 / jnp.sqrt(col_mass)
    first = (vectors.reshape(own, vecs, bsize) * own_inv[:, None, :]).astype(jnp.bfloat16)
    mass_pad = jnp.zeros((8, 128), jnp.float32).at[0, : own * bsize].set(col_mass.reshape(-1))
    got, mass_got = all_gather2(first.reshape(vec_rows, LANES), mass_pad, "row", "col", n_row, 4)
    first_panel = got.reshape(col_panel, vecs, bsize)
    col_mass_panel = mass_got.reshape(n_row, 8, 128)[:, 0, : own * bsize].reshape(col_panel, bsize)
    inv_col = 1.0 / jnp.sqrt(col_mass_panel)
    pairs = col_panel // 2
    inv_pairs = inv_col.reshape(pairs, 1, 2 * bsize)
    own_pair = jnp.broadcast_to(own_inv.reshape(1, own * bsize), (vecs, own * bsize))
    row_mass_spread = jnp.broadcast_to(row_mass[:, None, :], (own, vecs, bsize)).reshape(vec_rows, LANES)
    fwd_hot = (fwd_ids[None, :] == jnp.arange(row_panel)[:, None]).astype(jnp.bfloat16)
    bwd_hot = (bwd_ids[None, :] == jnp.arange(col_panel)[:, None]).astype(jnp.bfloat16)
    for step in range(ITERS):
        if step == 0:
            scaled = first_panel
        else:
            paired = (current * inv_pairs).astype(jnp.bfloat16)
            scaled = paired.reshape(pairs, vecs, 2, bsize).transpose(0, 2, 1, 3).reshape(col_panel, vecs, bsize)
        forward_taken = jnp.take(scaled, cols_idx, axis=0)
        forward_product = jnp.einsum(
            "bij,bkj->bki", square, forward_taken, preferred_element_type=jnp.bfloat16
        )
        forward_summed = jnp.einsum(
            "rs,ski->rki", fwd_hot, forward_product, preferred_element_type=jnp.float32
        )
        flat = forward_summed.reshape(row_panel * vecs * bsize // LANES, LANES)
        weighted = forward_reduce(flat, row_mass_spread, n_col, 1).reshape(row_panel, vecs, bsize)
        taken = jnp.take(weighted, rows_idx, axis=0)
        product = jnp.einsum("bij,bki->bkj", square, taken, preferred_element_type=jnp.bfloat16)
        summed = jnp.einsum(
            "pbs,skj->pkbj", bwd_hot.reshape(pairs, 2, n_cap), product,
            preferred_element_type=jnp.float32,
        ).reshape(pairs, vecs, 2 * bsize)
        current = backward_reduce(summed, own_pair, n_row, n_col, 1.0 / total_boxes, 2)
    me = lax.axis_index("row")
    mine = lax.dynamic_index_in_dim(current, me, 0, keepdims=False)
    return mine.reshape(vecs, own, bsize).transpose(1, 0, 2).reshape(own, vecs * bsize)


def solution(mesh):
    in_specs = (
        P("row", "col", None, None),
        P("row", "col", None),
        P("row", "col", None),
        P("row", "col"),
        P(("col", "row"), None),
        P(("row", "col"), None),
        P(("col", "row"), None),
    )
    out_specs = P(("col", "row"), None)
    return jax.shard_map(
        per_device, mesh=mesh, in_specs=in_specs, out_specs=out_specs, check_vma=False
    )
```

```python
import functools

import jax
import jax.numpy as jnp
from jax import lax
from jax.experimental import pallas as pl
from jax.experimental.pallas import tpu as pltpu
from jax.sharding import PartitionSpec as P

ITERS = 4
LANES = 512
MESH_ID = pl.DeviceIdType.MESH


def _peer(axis, other, p):
    them = lax.axis_index(other)
    return (p, them) if axis == "row" else (them, p)


def _reduce_kernel(axis, other, n, ch, two_phase, x_ref, o_ref, recv, mine, gath, s1, r1, s2, r2):
    me = lax.axis_index(axis)
    barrier = pltpu.get_barrier_semaphore()
    for d in range(1, n):
        pl.semaphore_signal(
            barrier, 1, device_id=_peer(axis, other, (me + d) % n), device_id_type=MESH_ID
        )
    pl.semaphore_wait(barrier, n - 1)
    if not two_phase:
        sends = []
        for d in range(1, n):
            c = pltpu.make_async_remote_copy(
                x_ref, recv.at[d], s1.at[d], r1.at[d],
                device_id=_peer(axis, other, (me + d) % n), device_id_type=MESH_ID,
            )
            c.start()
            sends.append(c)
        for c in sends:
            c.wait()
        recv[0] = x_ref[...]
        acc = recv[me % n]
        for p in range(1, n):
            acc = acc + recv[(me - p + n) % n]
        o_ref[...] = acc
        return
    sends = []
    for d in range(1, n):
        peer = (me + d) % n
        start = pl.multiple_of(peer * ch, ch)
        c = pltpu.make_async_remote_copy(
            x_ref.at[pl.ds(start, ch)], recv.at[d], s1.at[d], r1.at[d],
            device_id=_peer(axis, other, peer), device_id_type=MESH_ID,
        )
        c.start()
        sends.append(c)
    own = pl.multiple_of(me * ch, ch)
    acc = x_ref[pl.ds(own, ch), :]
    for d, c in enumerate(sends, 1):
        c.wait()
        acc = acc + recv[d]
    mine[...] = acc
    gathers = []
    for d in range(1, n):
        c = pltpu.make_async_remote_copy(
            mine, gath.at[d], s2.at[d], r2.at[d],
            device_id=_peer(axis, other, (me + d) % n), device_id_type=MESH_ID,
        )
        c.start()
        gathers.append(c)
    o_ref[pl.ds(own, ch), :] = acc
    for d, c in enumerate(gathers, 1):
        c.wait()
        src = pl.multiple_of(((me - d + n) % n) * ch, ch)
        o_ref[pl.ds(src, ch), :] = gath[d]


def _gather_kernel(axis, other, n, x_ref, o_ref, gath, s2, r2):
    me = lax.axis_index(axis)
    ch = x_ref.shape[0]
    barrier = pltpu.get_barrier_semaphore()
    for d in range(1, n):
        pl.semaphore_signal(
            barrier, 1, device_id=_peer(axis, other, (me + d) % n), device_id_type=MESH_ID
        )
    pl.semaphore_wait(barrier, n - 1)
    gathers = []
    for d in range(1, n):
        c = pltpu.make_async_remote_copy(
            x_ref, gath.at[d], s2.at[d], r2.at[d],
            device_id=_peer(axis, other, (me + d) % n), device_id_type=MESH_ID,
        )
        c.start()
        gathers.append(c)
    o_ref[pl.ds(pl.multiple_of(me * ch, ch), ch), :] = x_ref[...]
    for d, c in enumerate(gathers, 1):
        c.wait()
        src = pl.multiple_of(((me - d + n) % n) * ch, ch)
        o_ref[pl.ds(src, ch), :] = gath[d]


def all_gather(x, axis, other, n, collective_id):
    ch, lanes = x.shape
    return pl.pallas_call(
        functools.partial(_gather_kernel, axis, other, n),
        out_shape=jax.ShapeDtypeStruct((n * ch, lanes), x.dtype),
        in_specs=[pl.BlockSpec(memory_space=pltpu.VMEM)],
        out_specs=pl.BlockSpec(memory_space=pltpu.VMEM),
        scratch_shapes=[
            pltpu.VMEM((n, ch, lanes), x.dtype),
            pltpu.SemaphoreType.DMA((n,)),
            pltpu.SemaphoreType.DMA((n,)),
        ],
        compiler_params=pltpu.CompilerParams(collective_id=collective_id, has_side_effects=True),
    )(x)


def _forward_kernel(n, ch, x_ref, mass_ref, o_ref, recv, mine, gath, s1, r1, s2, r2):
    axis, other = "col", "row"
    me = lax.axis_index(axis)
    sends = []
    for d in range(1, n):
        peer = (me + d) % n
        start = pl.multiple_of(peer * ch, ch)
        c = pltpu.make_async_remote_copy(
            x_ref.at[pl.ds(start, ch)], recv.at[d], s1.at[d], r1.at[d],
            device_id=_peer(axis, other, peer), device_id_type=MESH_ID,
        )
        c.start()
        sends.append(c)
    own = pl.multiple_of(me * ch, ch)
    acc = x_ref[pl.ds(own, ch), :]
    for d, c in enumerate(sends, 1):
        c.wait()
        acc = acc + recv[d]
    mine[...] = (acc * mass_ref[...]).astype(mine.dtype)
    gathers = []
    for d in range(1, n):
        c = pltpu.make_async_remote_copy(
            mine, gath.at[d], s2.at[d], r2.at[d],
            device_id=_peer(axis, other, (me + d) % n), device_id_type=MESH_ID,
        )
        c.start()
        gathers.append(c)
    o_ref[pl.ds(own, ch), :] = mine[...]
    for d, c in enumerate(gathers, 1):
        c.wait()
        src = pl.multiple_of(((me - d + n) % n) * ch, ch)
        o_ref[pl.ds(src, ch), :] = gath[d]


def forward_reduce(x, mass, n, collective_id):
    rows, lanes = x.shape
    ch = rows // n
    return pl.pallas_call(
        functools.partial(_forward_kernel, n, ch),
        out_shape=jax.ShapeDtypeStruct(x.shape, jnp.bfloat16),
        in_specs=[pl.BlockSpec(memory_space=pltpu.VMEM)] * 2,
        out_specs=pl.BlockSpec(memory_space=pltpu.VMEM),
        scratch_shapes=[
            pltpu.VMEM((n, ch, lanes), x.dtype),
            pltpu.VMEM((ch, lanes), jnp.bfloat16),
            pltpu.VMEM((n, ch, lanes), jnp.bfloat16),
            pltpu.SemaphoreType.DMA((n,)),
            pltpu.SemaphoreType.DMA((n,)),
            pltpu.SemaphoreType.DMA((n,)),
            pltpu.SemaphoreType.DMA((n,)),
        ],
        compiler_params=pltpu.CompilerParams(has_side_effects=True),
    )(x, mass)


def _gather2_kernel(axis, other, n, x_ref, y_ref, o_ref, p_ref, gx, gy, sx, rx, sy, ry):
    me = lax.axis_index(axis)
    cx = x_ref.shape[0]
    cy = y_ref.shape[0]
    barrier = pltpu.get_barrier_semaphore()
    for d in range(1, n):
        pl.semaphore_signal(
            barrier, 1, device_id=_peer(axis, other, (me + d) % n), device_id_type=MESH_ID
        )
    pl.semaphore_wait(barrier, n - 1)
    copies = []
    for d in range(1, n):
        peer = _peer(axis, other, (me + d) % n)
        a = pltpu.make_async_remote_copy(
            x_ref, gx.at[d], sx.at[d], rx.at[d], device_id=peer, device_id_type=MESH_ID
        )
        b = pltpu.make_async_remote_copy(
            y_ref, gy.at[d], sy.at[d], ry.at[d], device_id=peer, device_id_type=MESH_ID
        )
        a.start()
        b.start()
        copies.append((a, b))
    o_ref[pl.ds(pl.multiple_of(me * cx, cx), cx), :] = x_ref[...]
    p_ref[pl.ds(pl.multiple_of(me * cy, cy), cy), :] = y_ref[...]
    for d, (a, b) in enumerate(copies, 1):
        a.wait()
        b.wait()
        src = (me - d + n) % n
        o_ref[pl.ds(pl.multiple_of(src * cx, cx), cx), :] = gx[d]
        p_ref[pl.ds(pl.multiple_of(src * cy, cy), cy), :] = gy[d]


def all_gather2(x, y, axis, other, n, collective_id):
    return pl.pallas_call(
        functools.partial(_gather2_kernel, axis, other, n),
        out_shape=(
            jax.ShapeDtypeStruct((n * x.shape[0], x.shape[1]), x.dtype),
            jax.ShapeDtypeStruct((n * y.shape[0], y.shape[1]), y.dtype),
        ),
        in_specs=[pl.BlockSpec(memory_space=pltpu.VMEM)] * 2,
        out_specs=(pl.BlockSpec(memory_space=pltpu.VMEM),) * 2,
        scratch_shapes=[
            pltpu.VMEM((n,) + x.shape, x.dtype),
            pltpu.VMEM((n,) + y.shape, y.dtype),
            pltpu.SemaphoreType.DMA((n,)),
            pltpu.SemaphoreType.DMA((n,)),
            pltpu.SemaphoreType.DMA((n,)),
            pltpu.SemaphoreType.DMA((n,)),
        ],
        compiler_params=pltpu.CompilerParams(collective_id=collective_id, has_side_effects=True),
    )(x, y)


def _gram_of(a):
    return lax.dot_general(
        a, a, (((1,), (1,)), ((), ())), precision=lax.Precision.HIGHEST,
        preferred_element_type=jnp.float32,
    )


def chol_inverse(a):
    n = a.shape[0]
    r = lax.broadcasted_iota(jnp.int32, (n, n), 0)
    c = lax.broadcasted_iota(jnp.int32, (n, n), 1)
    r1 = lax.broadcasted_iota(jnp.int32, (n, 1), 0)
    c1 = lax.broadcasted_iota(jnp.int32, (1, n), 1)
    x0 = jnp.where(r == c, 1.0, 0.0).astype(jnp.float32)
    d0 = jnp.sum(jnp.where(r == c, a, 0.0), axis=0, keepdims=True)

    def step(j, carry):
        m, x, d = carry
        inv = 1.0 / jnp.sqrt(jnp.sum(jnp.where(c1 == j, d, 0.0), axis=1, keepdims=True))
        col = jnp.sum(jnp.where(c == j, m, 0.0), axis=1, keepdims=True)
        row = jnp.sum(jnp.where(r == j, m, 0.0), axis=0, keepdims=True)
        lcol = jnp.where(r1 >= j, col * inv, 0.0)
        lrow = jnp.where(c1 >= j, row * inv, 0.0)
        m = m - lcol * lrow
        d = d - lrow * lrow
        xrow = jnp.sum(jnp.where(r == j, x, 0.0), axis=0, keepdims=True) * inv
        x = jnp.where(r == j, xrow, x)
        x = x - jnp.where(r1 > j, lcol, 0.0) * xrow
        return m, x, d

    m, x, d = lax.fori_loop(0, n, step, (a, x0, d0))
    return x


def _backward_kernel(n, m, scale, x_ref, icol_ref, o_ref, recv, gath, g3, panel, s1, r1, s2, r2, s3, r3):
    me = lax.axis_index("row")
    mc = lax.axis_index("col")
    barrier = pltpu.get_barrier_semaphore()
    for d in range(1, n):
        pl.semaphore_signal(barrier, 1, device_id=((me + d) % n, mc), device_id_type=MESH_ID)
    for d in range(1, m):
        pl.semaphore_signal(barrier, 1, device_id=(me, (mc + d) % m), device_id_type=MESH_ID)
    pl.semaphore_wait(barrier, n - 1 + m - 1)
    sends = []
    for d in range(1, n):
        peer = (me + d) % n
        c = pltpu.make_async_remote_copy(
            x_ref.at[peer], recv.at[d], s1.at[d], r1.at[d],
            device_id=(peer, mc), device_id_type=MESH_ID,
        )
        c.start()
        sends.append(c)
    acc = x_ref[me]
    for d, c in enumerate(sends, 1):
        c.wait()
        acc = acc + recv[d]
    gath[0] = acc * icol_ref[...]
    lanes = gath.shape[2]
    mine = pl.ds(pl.multiple_of(me * lanes, lanes), lanes)
    gathers = []
    for d in range(1, n):
        c = pltpu.make_async_remote_copy(
            gath.at[0], panel.at[:, mine], s2.at[d], r2.at[d],
            device_id=((me + d) % n, mc), device_id_type=MESH_ID,
        )
        c.start()
        gathers.append(c)
    for c in gathers:
        c.wait()
    panel[:, mine] = gath[0]
    g3[0] = _gram_of(panel[...])
    grams = []
    for d in range(1, m):
        c = pltpu.make_async_remote_copy(
            g3.at[0], g3.at[d], s3.at[d], r3.at[d],
            device_id=(me, (mc + d) % m), device_id_type=MESH_ID,
        )
        c.start()
        grams.append(c)
    for c in grams:
        c.wait()
    total = g3[mc % m]
    for q in range(1, m):
        total = total + g3[(mc - q + m) % m]
    inverse = chol_inverse(total * scale)
    rotated = lax.dot_general(
        inverse, panel[...], (((1,), (0,)), ((), ())),
        precision=lax.Precision.HIGHEST, preferred_element_type=jnp.float32,
    )
    for p in range(n):
        o_ref[p] = rotated[:, p * lanes:(p + 1) * lanes]


def backward_reduce(x, icol, n, m, scale, collective_id):
    chunks, vecs, lanes = x.shape
    return pl.pallas_call(
        functools.partial(_backward_kernel, n, m, scale),
        out_shape=jax.ShapeDtypeStruct(x.shape, jnp.float32),
        in_specs=[pl.BlockSpec(memory_space=pltpu.VMEM)] * 2,
        out_specs=pl.BlockSpec(memory_space=pltpu.VMEM),
        scratch_shapes=[
            pltpu.VMEM((n, vecs, lanes), jnp.float32),
            pltpu.VMEM((n, vecs, lanes), jnp.float32),
            pltpu.VMEM((m, vecs, vecs), jnp.float32),
            pltpu.VMEM((vecs, n * lanes), jnp.float32),
            pltpu.SemaphoreType.DMA((n,)),
            pltpu.SemaphoreType.DMA((n,)),
            pltpu.SemaphoreType.DMA((n,)),
            pltpu.SemaphoreType.DMA((n,)),
            pltpu.SemaphoreType.DMA((m,)),
            pltpu.SemaphoreType.DMA((m,)),
        ],
        compiler_params=pltpu.CompilerParams(collective_id=collective_id, has_side_effects=True),
    )(x, icol)


def all_reduce(x, axis, other, n, collective_id, two_phase=True):
    rows, lanes = x.shape
    ch = rows // n if two_phase else rows
    slots = ch if two_phase else rows
    return pl.pallas_call(
        functools.partial(_reduce_kernel, axis, other, n, ch, two_phase),
        out_shape=jax.ShapeDtypeStruct(x.shape, x.dtype),
        in_specs=[pl.BlockSpec(memory_space=pltpu.VMEM)],
        out_specs=pl.BlockSpec(memory_space=pltpu.VMEM),
        scratch_shapes=[
            pltpu.VMEM((n, slots, lanes), x.dtype),
            pltpu.VMEM((ch, lanes), x.dtype),
            pltpu.VMEM((n, ch, lanes), x.dtype),
            pltpu.SemaphoreType.DMA((n,)),
            pltpu.SemaphoreType.DMA((n,)),
            pltpu.SemaphoreType.DMA((n,)),
            pltpu.SemaphoreType.DMA((n,)),
        ],
        compiler_params=pltpu.CompilerParams(collective_id=collective_id, has_side_effects=True),
    )(x)


def rotate(projected, gram):
    lower = jnp.linalg.cholesky(gram)
    inverse = lax.linalg.triangular_solve(
        lower, jnp.eye(gram.shape[0], dtype=jnp.float32), left_side=True, lower=True
    )
    return jnp.einsum(
        "kl,bli->bki",
        inverse,
        projected,
        precision=lax.Precision.HIGHEST,
        preferred_element_type=jnp.float32,
    )


def rotate_pairs(projected, gram):
    lower = jnp.linalg.cholesky(gram)
    inverse = lax.linalg.triangular_solve(
        lower, jnp.eye(gram.shape[0], dtype=jnp.float32), left_side=True, lower=True
    )
    return jnp.einsum(
        "kl,plx->pkx",
        inverse,
        projected,
        precision=lax.Precision.HIGHEST,
        preferred_element_type=jnp.float32,
    )


def local_gram(projected):
    return jnp.einsum(
        "bki,bli->kl",
        projected,
        projected,
        precision=lax.Precision.HIGHEST,
        preferred_element_type=jnp.float32,
    )


def panel_sum(partial, axis, other, n, collective_id):
    blocks, vecs, bsize = partial.shape
    flat = partial.reshape(blocks * vecs * bsize // LANES, LANES)
    return all_reduce(flat, axis, other, n, collective_id).reshape(blocks, vecs, bsize)


def per_device(blocks, block_row, block_col, counts, vectors, row_mass, col_mass):
    tile = blocks[0, 0]
    n_cap = tile.shape[0]
    bsize = row_mass.shape[1]
    vecs = vectors.shape[1] // bsize
    own = vectors.shape[0]
    n_row = lax.axis_size("row")
    n_col = lax.axis_size("col")
    row_panel = own * n_col
    col_panel = own * n_row
    total_boxes = float(own * bsize * n_row * n_col)
    rows_idx = block_row[0, 0]
    cols_idx = block_col[0, 0]
    live = jnp.arange(n_cap) < counts[0, 0]
    fwd_ids = jnp.where(live, rows_idx, row_panel)
    bwd_ids = jnp.where(live, cols_idx, col_panel)
    square = tile.reshape(n_cap, bsize, bsize)
    vec_rows = own * vecs * bsize // LANES
    own_inv = 1.0 / jnp.sqrt(col_mass)
    first = (vectors.reshape(own, vecs, bsize) * own_inv[:, None, :]).astype(jnp.bfloat16)
    mass_pad = jnp.zeros((8, 128), jnp.float32).at[0, : own * bsize].set(col_mass.reshape(-1))
    got, mass_got = all_gather2(first.reshape(vec_rows, LANES), mass_pad, "row", "col", n_row, 4)
    first_panel = got.reshape(col_panel, vecs, bsize)
    col_mass_panel = mass_got.reshape(n_row, 8, 128)[:, 0, : own * bsize].reshape(col_panel, bsize)
    inv_col = 1.0 / jnp.sqrt(col_mass_panel)
    pairs = col_panel // 2
    inv_pairs = inv_col.reshape(pairs, 1, 2 * bsize)
    own_pair = jnp.broadcast_to(own_inv.reshape(1, own * bsize), (vecs, own * bsize))
    row_mass_spread = jnp.broadcast_to(row_mass[:, None, :], (own, vecs, bsize)).reshape(vec_rows, LANES)
    fwd_hot = (fwd_ids[None, :] == jnp.arange(row_panel)[:, None]).astype(jnp.bfloat16)
    bwd_hot = (bwd_ids[None, :] == jnp.arange(col_panel)[:, None]).astype(jnp.bfloat16)
    for step in range(ITERS):
        if step == 0:
            scaled = first_panel
        else:
            paired = (current * inv_pairs).astype(jnp.bfloat16)
            scaled = paired.reshape(pairs, vecs, 2, bsize).transpose(0, 2, 1, 3).reshape(col_panel, vecs, bsize)
        forward_taken = jnp.take(scaled, cols_idx, axis=0)
        forward_product = jnp.einsum(
            "bij,bkj->bki", square, forward_taken, preferred_element_type=jnp.bfloat16
        )
        forward_summed = jnp.einsum(
            "rs,ski->rki", fwd_hot, forward_product, preferred_element_type=jnp.float32
        )
        flat = forward_summed.reshape(row_panel * vecs * bsize // LANES, LANES)
        weighted = forward_reduce(flat, row_mass_spread, n_col, 1).reshape(row_panel, vecs, bsize)
        taken = jnp.take(weighted, rows_idx, axis=0)
        product = jnp.einsum("bij,bki->bkj", square, taken, preferred_element_type=jnp.bfloat16)
        summed = jnp.einsum(
            "pbs,skj->pkbj", bwd_hot.reshape(pairs, 2, n_cap), product,
            preferred_element_type=jnp.float32,
        ).reshape(pairs, vecs, 2 * bsize)
        current = backward_reduce(summed, own_pair, n_row, n_col, 1.0 / total_boxes, 2)
    me = lax.axis_index("row")
    mine = lax.dynamic_index_in_dim(current, me, 0, keepdims=False)
    return mine.reshape(vecs, own, bsize).transpose(1, 0, 2).reshape(own, vecs * bsize)


def solution(mesh):
    in_specs = (
        P("row", "col", None, None),
        P("row", "col", None),
        P("row", "col", None),
        P("row", "col"),
        P(("col", "row"), None),
        P(("row", "col"), None),
        P(("col", "row"), None),
    )
    out_specs = P(("col", "row"), None)
    return jax.shard_map(
        per_device, mesh=mesh, in_specs=in_specs, out_specs=out_specs, check_vma=False
    )
```

```python
import functools

import jax
import jax.numpy as jnp
from jax import lax
from jax.experimental import pallas as pl
from jax.experimental.pallas import tpu as pltpu
from jax.sharding import PartitionSpec as P

ITERS = 4
LANES = 512
MESH_ID = pl.DeviceIdType.MESH


def _peer(axis, other, p):
    them = lax.axis_index(other)
    return (p, them) if axis == "row" else (them, p)


def _reduce_kernel(axis, other, n, ch, two_phase, x_ref, o_ref, recv, mine, gath, s1, r1, s2, r2):
    me = lax.axis_index(axis)
    barrier = pltpu.get_barrier_semaphore()
    for d in range(1, n):
        pl.semaphore_signal(
            barrier, 1, device_id=_peer(axis, other, (me + d) % n), device_id_type=MESH_ID
        )
    pl.semaphore_wait(barrier, n - 1)
    if not two_phase:
        sends = []
        for d in range(1, n):
            c = pltpu.make_async_remote_copy(
                x_ref, recv.at[d], s1.at[d], r1.at[d],
                device_id=_peer(axis, other, (me + d) % n), device_id_type=MESH_ID,
            )
            c.start()
            sends.append(c)
        for c in sends:
            c.wait()
        recv[0] = x_ref[...]
        acc = recv[me % n]
        for p in range(1, n):
            acc = acc + recv[(me - p + n) % n]
        o_ref[...] = acc
        return
    sends = []
    for d in range(1, n):
        peer = (me + d) % n
        start = pl.multiple_of(peer * ch, ch)
        c = pltpu.make_async_remote_copy(
            x_ref.at[pl.ds(start, ch)], recv.at[d], s1.at[d], r1.at[d],
            device_id=_peer(axis, other, peer), device_id_type=MESH_ID,
        )
        c.start()
        sends.append(c)
    own = pl.multiple_of(me * ch, ch)
    acc = x_ref[pl.ds(own, ch), :]
    for d, c in enumerate(sends, 1):
        c.wait()
        acc = acc + recv[d]
    mine[...] = acc
    gathers = []
    for d in range(1, n):
        c = pltpu.make_async_remote_copy(
            mine, gath.at[d], s2.at[d], r2.at[d],
            device_id=_peer(axis, other, (me + d) % n), device_id_type=MESH_ID,
        )
        c.start()
        gathers.append(c)
    o_ref[pl.ds(own, ch), :] = acc
    for d, c in enumerate(gathers, 1):
        c.wait()
        src = pl.multiple_of(((me - d + n) % n) * ch, ch)
        o_ref[pl.ds(src, ch), :] = gath[d]


def _gather_kernel(axis, other, n, x_ref, o_ref, gath, s2, r2):
    me = lax.axis_index(axis)
    ch = x_ref.shape[0]
    barrier = pltpu.get_barrier_semaphore()
    for d in range(1, n):
        pl.semaphore_signal(
            barrier, 1, device_id=_peer(axis, other, (me + d) % n), device_id_type=MESH_ID
        )
    pl.semaphore_wait(barrier, n - 1)
    gathers = []
    for d in range(1, n):
        c = pltpu.make_async_remote_copy(
            x_ref, gath.at[d], s2.at[d], r2.at[d],
            device_id=_peer(axis, other, (me + d) % n), device_id_type=MESH_ID,
        )
        c.start()
        gathers.append(c)
    o_ref[pl.ds(pl.multiple_of(me * ch, ch), ch), :] = x_ref[...]
    for d, c in enumerate(gathers, 1):
        c.wait()
        src = pl.multiple_of(((me - d + n) % n) * ch, ch)
        o_ref[pl.ds(src, ch), :] = gath[d]


def all_gather(x, axis, other, n, collective_id):
    ch, lanes = x.shape
    return pl.pallas_call(
        functools.partial(_gather_kernel, axis, other, n),
        out_shape=jax.ShapeDtypeStruct((n * ch, lanes), x.dtype),
        in_specs=[pl.BlockSpec(memory_space=pltpu.VMEM)],
        out_specs=pl.BlockSpec(memory_space=pltpu.VMEM),
        scratch_shapes=[
            pltpu.VMEM((n, ch, lanes), x.dtype),
            pltpu.SemaphoreType.DMA((n,)),
            pltpu.SemaphoreType.DMA((n,)),
        ],
        compiler_params=pltpu.CompilerParams(collective_id=collective_id, has_side_effects=True),
    )(x)


def _forward_kernel(n, ch, x_ref, mass_ref, o_ref, recv, mine, gath, s1, r1, s2, r2):
    axis, other = "col", "row"
    me = lax.axis_index(axis)
    barrier = pltpu.get_barrier_semaphore()
    for d in range(1, n):
        pl.semaphore_signal(
            barrier, 1, device_id=_peer(axis, other, (me + d) % n), device_id_type=MESH_ID
        )
    pl.semaphore_wait(barrier, n - 1)
    sends = []
    for d in range(1, n):
        peer = (me + d) % n
        start = pl.multiple_of(peer * ch, ch)
        c = pltpu.make_async_remote_copy(
            x_ref.at[pl.ds(start, ch)], recv.at[d], s1.at[d], r1.at[d],
            device_id=_peer(axis, other, peer), device_id_type=MESH_ID,
        )
        c.start()
        sends.append(c)
    own = pl.multiple_of(me * ch, ch)
    acc = x_ref[pl.ds(own, ch), :]
    for d, c in enumerate(sends, 1):
        c.wait()
        acc = acc + recv[d]
    mine[...] = (acc * mass_ref[...]).astype(mine.dtype)
    gathers = []
    for d in range(1, n):
        c = pltpu.make_async_remote_copy(
            mine, gath.at[d], s2.at[d], r2.at[d],
            device_id=_peer(axis, other, (me + d) % n), device_id_type=MESH_ID,
        )
        c.start()
        gathers.append(c)
    o_ref[pl.ds(own, ch), :] = mine[...]
    for d, c in enumerate(gathers, 1):
        c.wait()
        src = pl.multiple_of(((me - d + n) % n) * ch, ch)
        o_ref[pl.ds(src, ch), :] = gath[d]


def forward_reduce(x, mass, n, collective_id):
    rows, lanes = x.shape
    ch = rows // n
    return pl.pallas_call(
        functools.partial(_forward_kernel, n, ch),
        out_shape=jax.ShapeDtypeStruct(x.shape, jnp.bfloat16),
        in_specs=[pl.BlockSpec(memory_space=pltpu.VMEM)] * 2,
        out_specs=pl.BlockSpec(memory_space=pltpu.VMEM),
        scratch_shapes=[
            pltpu.VMEM((n, ch, lanes), x.dtype),
            pltpu.VMEM((ch, lanes), jnp.bfloat16),
            pltpu.VMEM((n, ch, lanes), jnp.bfloat16),
            pltpu.SemaphoreType.DMA((n,)),
            pltpu.SemaphoreType.DMA((n,)),
            pltpu.SemaphoreType.DMA((n,)),
            pltpu.SemaphoreType.DMA((n,)),
        ],
        compiler_params=pltpu.CompilerParams(collective_id=collective_id, has_side_effects=True),
    )(x, mass)


def _gather2_kernel(axis, other, n, x_ref, y_ref, o_ref, p_ref, gx, gy, sx, rx, sy, ry):
    me = lax.axis_index(axis)
    cx = x_ref.shape[0]
    cy = y_ref.shape[0]
    barrier = pltpu.get_barrier_semaphore()
    for d in range(1, n):
        pl.semaphore_signal(
            barrier, 1, device_id=_peer(axis, other, (me + d) % n), device_id_type=MESH_ID
        )
    pl.semaphore_wait(barrier, n - 1)
    copies = []
    for d in range(1, n):
        peer = _peer(axis, other, (me + d) % n)
        a = pltpu.make_async_remote_copy(
            x_ref, gx.at[d], sx.at[d], rx.at[d], device_id=peer, device_id_type=MESH_ID
        )
        b = pltpu.make_async_remote_copy(
            y_ref, gy.at[d], sy.at[d], ry.at[d], device_id=peer, device_id_type=MESH_ID
        )
        a.start()
        b.start()
        copies.append((a, b))
    o_ref[pl.ds(pl.multiple_of(me * cx, cx), cx), :] = x_ref[...]
    p_ref[pl.ds(pl.multiple_of(me * cy, cy), cy), :] = y_ref[...]
    for d, (a, b) in enumerate(copies, 1):
        a.wait()
        b.wait()
        src = (me - d + n) % n
        o_ref[pl.ds(pl.multiple_of(src * cx, cx), cx), :] = gx[d]
        p_ref[pl.ds(pl.multiple_of(src * cy, cy), cy), :] = gy[d]


def all_gather2(x, y, axis, other, n, collective_id):
    return pl.pallas_call(
        functools.partial(_gather2_kernel, axis, other, n),
        out_shape=(
            jax.ShapeDtypeStruct((n * x.shape[0], x.shape[1]), x.dtype),
            jax.ShapeDtypeStruct((n * y.shape[0], y.shape[1]), y.dtype),
        ),
        in_specs=[pl.BlockSpec(memory_space=pltpu.VMEM)] * 2,
        out_specs=(pl.BlockSpec(memory_space=pltpu.VMEM),) * 2,
        scratch_shapes=[
            pltpu.VMEM((n,) + x.shape, x.dtype),
            pltpu.VMEM((n,) + y.shape, y.dtype),
            pltpu.SemaphoreType.DMA((n,)),
            pltpu.SemaphoreType.DMA((n,)),
            pltpu.SemaphoreType.DMA((n,)),
            pltpu.SemaphoreType.DMA((n,)),
        ],
        compiler_params=pltpu.CompilerParams(collective_id=collective_id, has_side_effects=True),
    )(x, y)


def _gram_of(a):
    return lax.dot_general(
        a, a, (((1,), (1,)), ((), ())), precision=lax.Precision.HIGHEST,
        preferred_element_type=jnp.float32,
    )


def chol_inverse(a):
    n = a.shape[0]
    r = lax.broadcasted_iota(jnp.int32, (n, n), 0)
    c = lax.broadcasted_iota(jnp.int32, (n, n), 1)
    r1 = lax.broadcasted_iota(jnp.int32, (n, 1), 0)
    c1 = lax.broadcasted_iota(jnp.int32, (1, n), 1)
    x0 = jnp.where(r == c, 1.0, 0.0).astype(jnp.float32)
    d0 = jnp.sum(jnp.where(r == c, a, 0.0), axis=0, keepdims=True)

    def step(j, carry):
        m, x, d = carry
        inv = 1.0 / jnp.sqrt(jnp.sum(jnp.where(c1 == j, d, 0.0), axis=1, keepdims=True))
        col = jnp.sum(jnp.where(c == j, m, 0.0), axis=1, keepdims=True)
        row = jnp.sum(jnp.where(r == j, m, 0.0), axis=0, keepdims=True)
        lcol = jnp.where(r1 >= j, col * inv, 0.0)
        lrow = jnp.where(c1 >= j, row * inv, 0.0)
        m = m - lcol * lrow
        d = d - lrow * lrow
        xrow = jnp.sum(jnp.where(r == j, x, 0.0), axis=0, keepdims=True) * inv
        x = jnp.where(r == j, xrow, x)
        x = x - jnp.where(r1 > j, lcol, 0.0) * xrow
        return m, x, d

    m, x, d = lax.fori_loop(0, n, step, (a, x0, d0), unroll=4)
    return x


def _backward_kernel(n, m, scale, x_ref, icol_ref, o_ref, recv, gath, g3, panel, s1, r1, s2, r2, s3, r3):
    me = lax.axis_index("row")
    mc = lax.axis_index("col")
    barrier = pltpu.get_barrier_semaphore()
    for d in range(1, n):
        pl.semaphore_signal(barrier, 1, device_id=((me + d) % n, mc), device_id_type=MESH_ID)
    for d in range(1, m):
        pl.semaphore_signal(barrier, 1, device_id=(me, (mc + d) % m), device_id_type=MESH_ID)
    pl.semaphore_wait(barrier, n - 1 + m - 1)
    sends = []
    for d in range(1, n):
        peer = (me + d) % n
        c = pltpu.make_async_remote_copy(
            x_ref.at[peer], recv.at[d], s1.at[d], r1.at[d],
            device_id=(peer, mc), device_id_type=MESH_ID,
        )
        c.start()
        sends.append(c)
    acc = x_ref[me]
    for d, c in enumerate(sends, 1):
        c.wait()
        acc = acc + recv[d]
    gath[0] = acc * icol_ref[...]
    gathers = []
    for d in range(1, n):
        c = pltpu.make_async_remote_copy(
            gath.at[0], gath.at[d], s2.at[d], r2.at[d],
            device_id=((me + d) % n, mc), device_id_type=MESH_ID,
        )
        c.start()
        gathers.append(c)
    for c in gathers:
        c.wait()
    lanes = gath.shape[2]
    for p in range(n):
        panel[:, p * lanes:(p + 1) * lanes] = gath[(me - p + n) % n]
    g3[0] = _gram_of(panel[...])
    grams = []
    for d in range(1, m):
        c = pltpu.make_async_remote_copy(
            g3.at[0], g3.at[d], s3.at[d], r3.at[d],
            device_id=(me, (mc + d) % m), device_id_type=MESH_ID,
        )
        c.start()
        grams.append(c)
    for c in grams:
        c.wait()
    total = g3[mc % m]
    for q in range(1, m):
        total = total + g3[(mc - q + m) % m]
    inverse = chol_inverse(total * scale)
    rotated = lax.dot_general(
        inverse, panel[...], (((1,), (0,)), ((), ())),
        precision=lax.Precision.HIGHEST, preferred_element_type=jnp.float32,
    )
    for p in range(n):
        o_ref[p] = rotated[:, p * lanes:(p + 1) * lanes]


def backward_reduce(x, icol, n, m, scale, collective_id):
    chunks, vecs, lanes = x.shape
    return pl.pallas_call(
        functools.partial(_backward_kernel, n, m, scale),
        out_shape=jax.ShapeDtypeStruct(x.shape, jnp.float32),
        in_specs=[pl.BlockSpec(memory_space=pltpu.VMEM)] * 2,
        out_specs=pl.BlockSpec(memory_space=pltpu.VMEM),
        scratch_shapes=[
            pltpu.VMEM((n, vecs, lanes), jnp.float32),
            pltpu.VMEM((n, vecs, lanes), jnp.float32),
            pltpu.VMEM((m, vecs, vecs), jnp.float32),
            pltpu.VMEM((vecs, n * lanes), jnp.float32),
            pltpu.SemaphoreType.DMA((n,)),
            pltpu.SemaphoreType.DMA((n,)),
            pltpu.SemaphoreType.DMA((n,)),
            pltpu.SemaphoreType.DMA((n,)),
            pltpu.SemaphoreType.DMA((m,)),
            pltpu.SemaphoreType.DMA((m,)),
        ],
        compiler_params=pltpu.CompilerParams(collective_id=collective_id, has_side_effects=True),
    )(x, icol)


def all_reduce(x, axis, other, n, collective_id, two_phase=True):
    rows, lanes = x.shape
    ch = rows // n if two_phase else rows
    slots = ch if two_phase else rows
    return pl.pallas_call(
        functools.partial(_reduce_kernel, axis, other, n, ch, two_phase),
        out_shape=jax.ShapeDtypeStruct(x.shape, x.dtype),
        in_specs=[pl.BlockSpec(memory_space=pltpu.VMEM)],
        out_specs=pl.BlockSpec(memory_space=pltpu.VMEM),
        scratch_shapes=[
            pltpu.VMEM((n, slots, lanes), x.dtype),
            pltpu.VMEM((ch, lanes), x.dtype),
            pltpu.VMEM((n, ch, lanes), x.dtype),
            pltpu.SemaphoreType.DMA((n,)),
            pltpu.SemaphoreType.DMA((n,)),
            pltpu.SemaphoreType.DMA((n,)),
            pltpu.SemaphoreType.DMA((n,)),
        ],
        compiler_params=pltpu.CompilerParams(collective_id=collective_id, has_side_effects=True),
    )(x)


def rotate(projected, gram):
    lower = jnp.linalg.cholesky(gram)
    inverse = lax.linalg.triangular_solve(
        lower, jnp.eye(gram.shape[0], dtype=jnp.float32), left_side=True, lower=True
    )
    return jnp.einsum(
        "kl,bli->bki",
        inverse,
        projected,
        precision=lax.Precision.HIGHEST,
        preferred_element_type=jnp.float32,
    )


def rotate_pairs(projected, gram):
    lower = jnp.linalg.cholesky(gram)
    inverse = lax.linalg.triangular_solve(
        lower, jnp.eye(gram.shape[0], dtype=jnp.float32), left_side=True, lower=True
    )
    return jnp.einsum(
        "kl,plx->pkx",
        inverse,
        projected,
        precision=lax.Precision.HIGHEST,
        preferred_element_type=jnp.float32,
    )


def local_gram(projected):
    return jnp.einsum(
        "bki,bli->kl",
        projected,
        projected,
        precision=lax.Precision.HIGHEST,
        preferred_element_type=jnp.float32,
    )


def panel_sum(partial, axis, other, n, collective_id):
    blocks, vecs, bsize = partial.shape
    flat = partial.reshape(blocks * vecs * bsize // LANES, LANES)
    return all_reduce(flat, axis, other, n, collective_id).reshape(blocks, vecs, bsize)


def per_device(blocks, block_row, block_col, counts, vectors, row_mass, col_mass):
    tile = blocks[0, 0]
    n_cap = tile.shape[0]
    bsize = row_mass.shape[1]
    vecs = vectors.shape[1] // bsize
    own = vectors.shape[0]
    n_row = lax.axis_size("row")
    n_col = lax.axis_size("col")
    row_panel = own * n_col
    col_panel = own * n_row
    total_boxes = float(own * bsize * n_row * n_col)
    rows_idx = block_row[0, 0]
    cols_idx = block_col[0, 0]
    live = jnp.arange(n_cap) < counts[0, 0]
    fwd_ids = jnp.where(live, rows_idx, row_panel)
    bwd_ids = jnp.where(live, cols_idx, col_panel)
    square = tile.reshape(n_cap, bsize, bsize)
    vec_rows = own * vecs * bsize // LANES
    own_inv = 1.0 / jnp.sqrt(col_mass)
    first = (vectors.reshape(own, vecs, bsize) * own_inv[:, None, :]).astype(jnp.bfloat16)
    mass_pad = jnp.zeros((8, 128), jnp.float32).at[0, : own * bsize].set(col_mass.reshape(-1))
    got, mass_got = all_gather2(first.reshape(vec_rows, LANES), mass_pad, "row", "col", n_row, 4)
    first_panel = got.reshape(col_panel, vecs, bsize)
    col_mass_panel = mass_got.reshape(n_row, 8, 128)[:, 0, : own * bsize].reshape(col_panel, bsize)
    inv_col = 1.0 / jnp.sqrt(col_mass_panel)
    pairs = col_panel // 2
    inv_pairs = inv_col.reshape(pairs, 1, 2 * bsize)
    own_pair = jnp.broadcast_to(own_inv.reshape(1, own * bsize), (vecs, own * bsize))
    row_mass_spread = jnp.broadcast_to(row_mass[:, None, :], (own, vecs, bsize)).reshape(vec_rows, LANES)
    fwd_hot = (fwd_ids[None, :] == jnp.arange(row_panel)[:, None]).astype(jnp.bfloat16)
    bwd_hot = (bwd_ids[None, :] == jnp.arange(col_panel)[:, None]).astype(jnp.bfloat16)
    for step in range(ITERS):
        if step == 0:
            scaled = first_panel
        else:
            paired = (current * inv_pairs).astype(jnp.bfloat16)
            scaled = paired.reshape(pairs, vecs, 2, bsize).transpose(0, 2, 1, 3).reshape(col_panel, vecs, bsize)
        forward_taken = jnp.take(scaled, cols_idx, axis=0)
        forward_product = jnp.einsum(
            "bij,bkj->bki", square, forward_taken, preferred_element_type=jnp.bfloat16
        )
        forward_summed = jnp.einsum(
            "rs,ski->rki", fwd_hot, forward_product, preferred_element_type=jnp.float32
        )
        flat = forward_summed.reshape(row_panel * vecs * bsize // LANES, LANES)
        weighted = forward_reduce(flat, row_mass_spread, n_col, 1).reshape(row_panel, vecs, bsize)
        taken = jnp.take(weighted, rows_idx, axis=0)
        product = jnp.einsum("bij,bki->bkj", square, taken, preferred_element_type=jnp.bfloat16)
        summed = jnp.einsum(
            "pbs,skj->pkbj", bwd_hot.reshape(pairs, 2, n_cap), product,
            preferred_element_type=jnp.float32,
        ).reshape(pairs, vecs, 2 * bsize)
        current = backward_reduce(summed, own_pair, n_row, n_col, 1.0 / total_boxes, 2)
    me = lax.axis_index("row")
    mine = lax.dynamic_index_in_dim(current, me, 0, keepdims=False)
    return mine.reshape(vecs, own, bsize).transpose(1, 0, 2).reshape(own, vecs * bsize)


def solution(mesh):
    in_specs = (
        P("row", "col", None, None),
        P("row", "col", None),
        P("row", "col", None),
        P("row", "col"),
        P(("col", "row"), None),
        P(("row", "col"), None),
        P(("col", "row"), None),
    )
    out_specs = P(("col", "row"), None)
    return jax.shard_map(
        per_device, mesh=mesh, in_specs=in_specs, out_specs=out_specs, check_vma=False
    )
```

```python
import functools

import jax
import jax.numpy as jnp
from jax import lax
from jax.experimental import pallas as pl
from jax.experimental.pallas import tpu as pltpu
from jax.sharding import PartitionSpec as P

ITERS = 4
LANES = 512
MESH_ID = pl.DeviceIdType.MESH


def _peer(axis, other, p):
    them = lax.axis_index(other)
    return (p, them) if axis == "row" else (them, p)


def _reduce_kernel(axis, other, n, ch, two_phase, x_ref, o_ref, recv, mine, gath, s1, r1, s2, r2):
    me = lax.axis_index(axis)
    barrier = pltpu.get_barrier_semaphore()
    for d in range(1, n):
        pl.semaphore_signal(
            barrier, 1, device_id=_peer(axis, other, (me + d) % n), device_id_type=MESH_ID
        )
    pl.semaphore_wait(barrier, n - 1)
    if not two_phase:
        sends = []
        for d in range(1, n):
            c = pltpu.make_async_remote_copy(
                x_ref, recv.at[d], s1.at[d], r1.at[d],
                device_id=_peer(axis, other, (me + d) % n), device_id_type=MESH_ID,
            )
            c.start()
            sends.append(c)
        for c in sends:
            c.wait()
        recv[0] = x_ref[...]
        acc = recv[me % n]
        for p in range(1, n):
            acc = acc + recv[(me - p + n) % n]
        o_ref[...] = acc
        return
    sends = []
    for d in range(1, n):
        peer = (me + d) % n
        start = pl.multiple_of(peer * ch, ch)
        c = pltpu.make_async_remote_copy(
            x_ref.at[pl.ds(start, ch)], recv.at[d], s1.at[d], r1.at[d],
            device_id=_peer(axis, other, peer), device_id_type=MESH_ID,
        )
        c.start()
        sends.append(c)
    own = pl.multiple_of(me * ch, ch)
    acc = x_ref[pl.ds(own, ch), :]
    for d, c in enumerate(sends, 1):
        c.wait()
        acc = acc + recv[d]
    mine[...] = acc
    gathers = []
    for d in range(1, n):
        c = pltpu.make_async_remote_copy(
            mine, gath.at[d], s2.at[d], r2.at[d],
            device_id=_peer(axis, other, (me + d) % n), device_id_type=MESH_ID,
        )
        c.start()
        gathers.append(c)
    o_ref[pl.ds(own, ch), :] = acc
    for d, c in enumerate(gathers, 1):
        c.wait()
        src = pl.multiple_of(((me - d + n) % n) * ch, ch)
        o_ref[pl.ds(src, ch), :] = gath[d]


def _gather_kernel(axis, other, n, x_ref, o_ref, gath, s2, r2):
    me = lax.axis_index(axis)
    ch = x_ref.shape[0]
    barrier = pltpu.get_barrier_semaphore()
    for d in range(1, n):
        pl.semaphore_signal(
            barrier, 1, device_id=_peer(axis, other, (me + d) % n), device_id_type=MESH_ID
        )
    pl.semaphore_wait(barrier, n - 1)
    gathers = []
    for d in range(1, n):
        c = pltpu.make_async_remote_copy(
            x_ref, gath.at[d], s2.at[d], r2.at[d],
            device_id=_peer(axis, other, (me + d) % n), device_id_type=MESH_ID,
        )
        c.start()
        gathers.append(c)
    o_ref[pl.ds(pl.multiple_of(me * ch, ch), ch), :] = x_ref[...]
    for d, c in enumerate(gathers, 1):
        c.wait()
        src = pl.multiple_of(((me - d + n) % n) * ch, ch)
        o_ref[pl.ds(src, ch), :] = gath[d]


def all_gather(x, axis, other, n, collective_id):
    ch, lanes = x.shape
    return pl.pallas_call(
        functools.partial(_gather_kernel, axis, other, n),
        out_shape=jax.ShapeDtypeStruct((n * ch, lanes), x.dtype),
        in_specs=[pl.BlockSpec(memory_space=pltpu.VMEM)],
        out_specs=pl.BlockSpec(memory_space=pltpu.VMEM),
        scratch_shapes=[
            pltpu.VMEM((n, ch, lanes), x.dtype),
            pltpu.SemaphoreType.DMA((n,)),
            pltpu.SemaphoreType.DMA((n,)),
        ],
        compiler_params=pltpu.CompilerParams(collective_id=collective_id, has_side_effects=True),
    )(x)


def _forward_kernel(n, ch, x_ref, mass_ref, o_ref, recv, mine, gath, s1, r1, s2, r2):
    axis, other = "col", "row"
    me = lax.axis_index(axis)
    barrier = pltpu.get_barrier_semaphore()
    for d in range(1, n):
        pl.semaphore_signal(
            barrier, 1, device_id=_peer(axis, other, (me + d) % n), device_id_type=MESH_ID
        )
    pl.semaphore_wait(barrier, n - 1)
    sends = []
    for d in range(1, n):
        peer = (me + d) % n
        start = pl.multiple_of(peer * ch, ch)
        c = pltpu.make_async_remote_copy(
            x_ref.at[pl.ds(start, ch)], recv.at[d], s1.at[d], r1.at[d],
            device_id=_peer(axis, other, peer), device_id_type=MESH_ID,
        )
        c.start()
        sends.append(c)
    own = pl.multiple_of(me * ch, ch)
    acc = x_ref[pl.ds(own, ch), :]
    for d, c in enumerate(sends, 1):
        c.wait()
        acc = acc + recv[d]
    mine[...] = (acc * mass_ref[...]).astype(mine.dtype)
    gathers = []
    for d in range(1, n):
        c = pltpu.make_async_remote_copy(
            mine, gath.at[d], s2.at[d], r2.at[d],
            device_id=_peer(axis, other, (me + d) % n), device_id_type=MESH_ID,
        )
        c.start()
        gathers.append(c)
    o_ref[pl.ds(own, ch), :] = mine[...]
    for d, c in enumerate(gathers, 1):
        c.wait()
        src = pl.multiple_of(((me - d + n) % n) * ch, ch)
        o_ref[pl.ds(src, ch), :] = gath[d]


def forward_reduce(x, mass, n, collective_id):
    rows, lanes = x.shape
    ch = rows // n
    return pl.pallas_call(
        functools.partial(_forward_kernel, n, ch),
        out_shape=jax.ShapeDtypeStruct(x.shape, jnp.bfloat16),
        in_specs=[pl.BlockSpec(memory_space=pltpu.VMEM)] * 2,
        out_specs=pl.BlockSpec(memory_space=pltpu.VMEM),
        scratch_shapes=[
            pltpu.VMEM((n, ch, lanes), x.dtype),
            pltpu.VMEM((ch, lanes), jnp.bfloat16),
            pltpu.VMEM((n, ch, lanes), jnp.bfloat16),
            pltpu.SemaphoreType.DMA((n,)),
            pltpu.SemaphoreType.DMA((n,)),
            pltpu.SemaphoreType.DMA((n,)),
            pltpu.SemaphoreType.DMA((n,)),
        ],
        compiler_params=pltpu.CompilerParams(collective_id=collective_id, has_side_effects=True),
    )(x, mass)


def _gather2_kernel(axis, other, n, x_ref, y_ref, o_ref, p_ref, gx, gy, sx, rx, sy, ry):
    me = lax.axis_index(axis)
    cx = x_ref.shape[0]
    cy = y_ref.shape[0]
    barrier = pltpu.get_barrier_semaphore()
    for d in range(1, n):
        pl.semaphore_signal(
            barrier, 1, device_id=_peer(axis, other, (me + d) % n), device_id_type=MESH_ID
        )
    pl.semaphore_wait(barrier, n - 1)
    copies = []
    for d in range(1, n):
        peer = _peer(axis, other, (me + d) % n)
        a = pltpu.make_async_remote_copy(
            x_ref, gx.at[d], sx.at[d], rx.at[d], device_id=peer, device_id_type=MESH_ID
        )
        b = pltpu.make_async_remote_copy(
            y_ref, gy.at[d], sy.at[d], ry.at[d], device_id=peer, device_id_type=MESH_ID
        )
        a.start()
        b.start()
        copies.append((a, b))
    o_ref[pl.ds(pl.multiple_of(me * cx, cx), cx), :] = x_ref[...]
    p_ref[pl.ds(pl.multiple_of(me * cy, cy), cy), :] = y_ref[...]
    for d, (a, b) in enumerate(copies, 1):
        a.wait()
        b.wait()
        src = (me - d + n) % n
        o_ref[pl.ds(pl.multiple_of(src * cx, cx), cx), :] = gx[d]
        p_ref[pl.ds(pl.multiple_of(src * cy, cy), cy), :] = gy[d]


def all_gather2(x, y, axis, other, n, collective_id):
    return pl.pallas_call(
        functools.partial(_gather2_kernel, axis, other, n),
        out_shape=(
            jax.ShapeDtypeStruct((n * x.shape[0], x.shape[1]), x.dtype),
            jax.ShapeDtypeStruct((n * y.shape[0], y.shape[1]), y.dtype),
        ),
        in_specs=[pl.BlockSpec(memory_space=pltpu.VMEM)] * 2,
        out_specs=(pl.BlockSpec(memory_space=pltpu.VMEM),) * 2,
        scratch_shapes=[
            pltpu.VMEM((n,) + x.shape, x.dtype),
            pltpu.VMEM((n,) + y.shape, y.dtype),
            pltpu.SemaphoreType.DMA((n,)),
            pltpu.SemaphoreType.DMA((n,)),
            pltpu.SemaphoreType.DMA((n,)),
            pltpu.SemaphoreType.DMA((n,)),
        ],
        compiler_params=pltpu.CompilerParams(collective_id=collective_id, has_side_effects=True),
    )(x, y)


def _gram_of(a):
    return lax.dot_general(
        a, a, (((1,), (1,)), ((), ())), precision=lax.Precision.HIGH,
        preferred_element_type=jnp.float32,
    )


def chol_inverse(a):
    n = a.shape[0]
    r = lax.broadcasted_iota(jnp.int32, (n, n), 0)
    c = lax.broadcasted_iota(jnp.int32, (n, n), 1)
    r1 = lax.broadcasted_iota(jnp.int32, (n, 1), 0)
    c1 = lax.broadcasted_iota(jnp.int32, (1, n), 1)
    x0 = jnp.where(r == c, 1.0, 0.0).astype(jnp.float32)
    d0 = jnp.sum(jnp.where(r == c, a, 0.0), axis=0, keepdims=True)

    def step(j, carry):
        m, x, d = carry
        inv = 1.0 / jnp.sqrt(jnp.sum(jnp.where(c1 == j, d, 0.0), axis=1, keepdims=True))
        col = jnp.sum(jnp.where(c == j, m, 0.0), axis=1, keepdims=True)
        row = jnp.sum(jnp.where(r == j, m, 0.0), axis=0, keepdims=True)
        lcol = jnp.where(r1 >= j, col * inv, 0.0)
        lrow = jnp.where(c1 >= j, row * inv, 0.0)
        m = m - lcol * lrow
        d = d - lrow * lrow
        xrow = jnp.sum(jnp.where(r == j, x, 0.0), axis=0, keepdims=True) * inv
        x = jnp.where(r == j, xrow, x)
        x = x - jnp.where(r1 > j, lcol, 0.0) * xrow
        return m, x, d

    m, x, d = lax.fori_loop(0, n, step, (a, x0, d0))
    return x


def _backward_kernel(n, m, scale, x_ref, icol_ref, o_ref, recv, gath, g3, panel, s1, r1, s2, r2, s3, r3):
    me = lax.axis_index("row")
    mc = lax.axis_index("col")
    barrier = pltpu.get_barrier_semaphore()
    for d in range(1, n):
        pl.semaphore_signal(barrier, 1, device_id=((me + d) % n, mc), device_id_type=MESH_ID)
    for d in range(1, m):
        pl.semaphore_signal(barrier, 1, device_id=(me, (mc + d) % m), device_id_type=MESH_ID)
    pl.semaphore_wait(barrier, n - 1 + m - 1)
    sends = []
    for d in range(1, n):
        peer = (me + d) % n
        c = pltpu.make_async_remote_copy(
            x_ref.at[peer], recv.at[d], s1.at[d], r1.at[d],
            device_id=(peer, mc), device_id_type=MESH_ID,
        )
        c.start()
        sends.append(c)
    acc = x_ref[me]
    for d, c in enumerate(sends, 1):
        c.wait()
        acc = acc + recv[d]
    gath[0] = acc * icol_ref[...]
    gathers = []
    for d in range(1, n):
        c = pltpu.make_async_remote_copy(
            gath.at[0], gath.at[d], s2.at[d], r2.at[d],
            device_id=((me + d) % n, mc), device_id_type=MESH_ID,
        )
        c.start()
        gathers.append(c)
    for c in gathers:
        c.wait()
    lanes = gath.shape[2]
    for p in range(n):
        panel[:, p * lanes:(p + 1) * lanes] = gath[(me - p + n) % n]
    g3[0] = _gram_of(panel[...])
    grams = []
    for d in range(1, m):
        c = pltpu.make_async_remote_copy(
            g3.at[0], g3.at[d], s3.at[d], r3.at[d],
            device_id=(me, (mc + d) % m), device_id_type=MESH_ID,
        )
        c.start()
        grams.append(c)
    for c in grams:
        c.wait()
    total = g3[mc % m]
    for q in range(1, m):
        total = total + g3[(mc - q + m) % m]
    inverse = chol_inverse(total * scale)
    rotated = lax.dot_general(
        inverse, panel[...], (((1,), (0,)), ((), ())),
        precision=lax.Precision.HIGH, preferred_element_type=jnp.float32,
    )
    for p in range(n):
        o_ref[p] = rotated[:, p * lanes:(p + 1) * lanes]


def backward_reduce(x, icol, n, m, scale, collective_id):
    chunks, vecs, lanes = x.shape
    return pl.pallas_call(
        functools.partial(_backward_kernel, n, m, scale),
        out_shape=jax.ShapeDtypeStruct(x.shape, jnp.float32),
        in_specs=[pl.BlockSpec(memory_space=pltpu.VMEM)] * 2,
        out_specs=pl.BlockSpec(memory_space=pltpu.VMEM),
        scratch_shapes=[
            pltpu.VMEM((n, vecs, lanes), jnp.float32),
            pltpu.VMEM((n, vecs, lanes), jnp.float32),
            pltpu.VMEM((m, vecs, vecs), jnp.float32),
            pltpu.VMEM((vecs, n * lanes), jnp.float32),
            pltpu.SemaphoreType.DMA((n,)),
            pltpu.SemaphoreType.DMA((n,)),
            pltpu.SemaphoreType.DMA((n,)),
            pltpu.SemaphoreType.DMA((n,)),
            pltpu.SemaphoreType.DMA((m,)),
            pltpu.SemaphoreType.DMA((m,)),
        ],
        compiler_params=pltpu.CompilerParams(collective_id=collective_id, has_side_effects=True),
    )(x, icol)


def all_reduce(x, axis, other, n, collective_id, two_phase=True):
    rows, lanes = x.shape
    ch = rows // n if two_phase else rows
    slots = ch if two_phase else rows
    return pl.pallas_call(
        functools.partial(_reduce_kernel, axis, other, n, ch, two_phase),
        out_shape=jax.ShapeDtypeStruct(x.shape, x.dtype),
        in_specs=[pl.BlockSpec(memory_space=pltpu.VMEM)],
        out_specs=pl.BlockSpec(memory_space=pltpu.VMEM),
        scratch_shapes=[
            pltpu.VMEM((n, slots, lanes), x.dtype),
            pltpu.VMEM((ch, lanes), x.dtype),
            pltpu.VMEM((n, ch, lanes), x.dtype),
            pltpu.SemaphoreType.DMA((n,)),
            pltpu.SemaphoreType.DMA((n,)),
            pltpu.SemaphoreType.DMA((n,)),
            pltpu.SemaphoreType.DMA((n,)),
        ],
        compiler_params=pltpu.CompilerParams(collective_id=collective_id, has_side_effects=True),
    )(x)


def rotate(projected, gram):
    lower = jnp.linalg.cholesky(gram)
    inverse = lax.linalg.triangular_solve(
        lower, jnp.eye(gram.shape[0], dtype=jnp.float32), left_side=True, lower=True
    )
    return jnp.einsum(
        "kl,bli->bki",
        inverse,
        projected,
        precision=lax.Precision.HIGHEST,
        preferred_element_type=jnp.float32,
    )


def rotate_pairs(projected, gram):
    lower = jnp.linalg.cholesky(gram)
    inverse = lax.linalg.triangular_solve(
        lower, jnp.eye(gram.shape[0], dtype=jnp.float32), left_side=True, lower=True
    )
    return jnp.einsum(
        "kl,plx->pkx",
        inverse,
        projected,
        precision=lax.Precision.HIGHEST,
        preferred_element_type=jnp.float32,
    )


def local_gram(projected):
    return jnp.einsum(
        "bki,bli->kl",
        projected,
        projected,
        precision=lax.Precision.HIGHEST,
        preferred_element_type=jnp.float32,
    )


def panel_sum(partial, axis, other, n, collective_id):
    blocks, vecs, bsize = partial.shape
    flat = partial.reshape(blocks * vecs * bsize // LANES, LANES)
    return all_reduce(flat, axis, other, n, collective_id).reshape(blocks, vecs, bsize)


def per_device(blocks, block_row, block_col, counts, vectors, row_mass, col_mass):
    tile = blocks[0, 0]
    n_cap = tile.shape[0]
    bsize = row_mass.shape[1]
    vecs = vectors.shape[1] // bsize
    own = vectors.shape[0]
    n_row = lax.axis_size("row")
    n_col = lax.axis_size("col")
    row_panel = own * n_col
    col_panel = own * n_row
    total_boxes = float(own * bsize * n_row * n_col)
    rows_idx = block_row[0, 0]
    cols_idx = block_col[0, 0]
    live = jnp.arange(n_cap) < counts[0, 0]
    fwd_ids = jnp.where(live, rows_idx, row_panel)
    bwd_ids = jnp.where(live, cols_idx, col_panel)
    square = tile.reshape(n_cap, bsize, bsize)
    vec_rows = own * vecs * bsize // LANES
    own_inv = 1.0 / jnp.sqrt(col_mass)
    first = (vectors.reshape(own, vecs, bsize) * own_inv[:, None, :]).astype(jnp.bfloat16)
    mass_pad = jnp.zeros((8, 128), jnp.float32).at[0, : own * bsize].set(col_mass.reshape(-1))
    got, mass_got = all_gather2(first.reshape(vec_rows, LANES), mass_pad, "row", "col", n_row, 4)
    first_panel = got.reshape(col_panel, vecs, bsize)
    col_mass_panel = mass_got.reshape(n_row, 8, 128)[:, 0, : own * bsize].reshape(col_panel, bsize)
    inv_col = 1.0 / jnp.sqrt(col_mass_panel)
    pairs = col_panel // 2
    inv_pairs = inv_col.reshape(pairs, 1, 2 * bsize)
    own_pair = jnp.broadcast_to(own_inv.reshape(1, own * bsize), (vecs, own * bsize))
    row_mass_spread = jnp.broadcast_to(row_mass[:, None, :], (own, vecs, bsize)).reshape(vec_rows, LANES)
    fwd_hot = (fwd_ids[None, :] == jnp.arange(row_panel)[:, None]).astype(jnp.bfloat16)
    bwd_hot = (bwd_ids[None, :] == jnp.arange(col_panel)[:, None]).astype(jnp.bfloat16)
    for step in range(ITERS):
        if step == 0:
            scaled = first_panel
        else:
            paired = (current * inv_pairs).astype(jnp.bfloat16)
            scaled = paired.reshape(pairs, vecs, 2, bsize).transpose(0, 2, 1, 3).reshape(col_panel, vecs, bsize)
        forward_taken = jnp.take(scaled, cols_idx, axis=0)
        forward_product = jnp.einsum(
            "bij,bkj->bki", square, forward_taken, preferred_element_type=jnp.bfloat16
        )
        forward_summed = jnp.einsum(
            "rs,ski->rki", fwd_hot, forward_product, preferred_element_type=jnp.float32
        )
        flat = forward_summed.reshape(row_panel * vecs * bsize // LANES, LANES)
        weighted = forward_reduce(flat, row_mass_spread, n_col, 1).reshape(row_panel, vecs, bsize)
        taken = jnp.take(weighted, rows_idx, axis=0)
        product = jnp.einsum("bij,bki->bkj", square, taken, preferred_element_type=jnp.bfloat16)
        summed = jnp.einsum(
            "pbs,skj->pkbj", bwd_hot.reshape(pairs, 2, n_cap), product,
            preferred_element_type=jnp.float32,
        ).reshape(pairs, vecs, 2 * bsize)
        current = backward_reduce(summed, own_pair, n_row, n_col, 1.0 / total_boxes, 2)
    me = lax.axis_index("row")
    mine = lax.dynamic_index_in_dim(current, me, 0, keepdims=False)
    return mine.reshape(vecs, own, bsize).transpose(1, 0, 2).reshape(own, vecs * bsize)


def solution(mesh):
    in_specs = (
        P("row", "col", None, None),
        P("row", "col", None),
        P("row", "col", None),
        P("row", "col"),
        P(("col", "row"), None),
        P(("row", "col"), None),
        P(("col", "row"), None),
    )
    out_specs = P(("col", "row"), None)
    return jax.shard_map(
        per_device, mesh=mesh, in_specs=in_specs, out_specs=out_specs, check_vma=False
    )
```

```python
import functools

import jax
import jax.numpy as jnp
from jax import lax
from jax.experimental import pallas as pl
from jax.experimental.pallas import tpu as pltpu
from jax.sharding import PartitionSpec as P

ITERS = 4
LANES = 512
MESH_ID = pl.DeviceIdType.MESH


def _peer(axis, other, p):
    them = lax.axis_index(other)
    return (p, them) if axis == "row" else (them, p)


def _reduce_kernel(axis, other, n, ch, two_phase, x_ref, o_ref, recv, mine, gath, s1, r1, s2, r2):
    me = lax.axis_index(axis)
    barrier = pltpu.get_barrier_semaphore()
    for d in range(1, n):
        pl.semaphore_signal(
            barrier, 1, device_id=_peer(axis, other, (me + d) % n), device_id_type=MESH_ID
        )
    pl.semaphore_wait(barrier, n - 1)
    if not two_phase:
        sends = []
        for d in range(1, n):
            c = pltpu.make_async_remote_copy(
                x_ref, recv.at[d], s1.at[d], r1.at[d],
                device_id=_peer(axis, other, (me + d) % n), device_id_type=MESH_ID,
            )
            c.start()
            sends.append(c)
        for c in sends:
            c.wait()
        recv[0] = x_ref[...]
        acc = recv[me % n]
        for p in range(1, n):
            acc = acc + recv[(me - p + n) % n]
        o_ref[...] = acc
        return
    sends = []
    for d in range(1, n):
        peer = (me + d) % n
        start = pl.multiple_of(peer * ch, ch)
        c = pltpu.make_async_remote_copy(
            x_ref.at[pl.ds(start, ch)], recv.at[d], s1.at[d], r1.at[d],
            device_id=_peer(axis, other, peer), device_id_type=MESH_ID,
        )
        c.start()
        sends.append(c)
    own = pl.multiple_of(me * ch, ch)
    acc = x_ref[pl.ds(own, ch), :]
    for d, c in enumerate(sends, 1):
        c.wait()
        acc = acc + recv[d]
    mine[...] = acc
    gathers = []
    for d in range(1, n):
        c = pltpu.make_async_remote_copy(
            mine, gath.at[d], s2.at[d], r2.at[d],
            device_id=_peer(axis, other, (me + d) % n), device_id_type=MESH_ID,
        )
        c.start()
        gathers.append(c)
    o_ref[pl.ds(own, ch), :] = acc
    for d, c in enumerate(gathers, 1):
        c.wait()
        src = pl.multiple_of(((me - d + n) % n) * ch, ch)
        o_ref[pl.ds(src, ch), :] = gath[d]


def _gather_kernel(axis, other, n, x_ref, o_ref, gath, s2, r2):
    me = lax.axis_index(axis)
    ch = x_ref.shape[0]
    barrier = pltpu.get_barrier_semaphore()
    for d in range(1, n):
        pl.semaphore_signal(
            barrier, 1, device_id=_peer(axis, other, (me + d) % n), device_id_type=MESH_ID
        )
    pl.semaphore_wait(barrier, n - 1)
    gathers = []
    for d in range(1, n):
        c = pltpu.make_async_remote_copy(
            x_ref, gath.at[d], s2.at[d], r2.at[d],
            device_id=_peer(axis, other, (me + d) % n), device_id_type=MESH_ID,
        )
        c.start()
        gathers.append(c)
    o_ref[pl.ds(pl.multiple_of(me * ch, ch), ch), :] = x_ref[...]
    for d, c in enumerate(gathers, 1):
        c.wait()
        src = pl.multiple_of(((me - d + n) % n) * ch, ch)
        o_ref[pl.ds(src, ch), :] = gath[d]


def all_gather(x, axis, other, n, collective_id):
    ch, lanes = x.shape
    return pl.pallas_call(
        functools.partial(_gather_kernel, axis, other, n),
        out_shape=jax.ShapeDtypeStruct((n * ch, lanes), x.dtype),
        in_specs=[pl.BlockSpec(memory_space=pltpu.VMEM)],
        out_specs=pl.BlockSpec(memory_space=pltpu.VMEM),
        scratch_shapes=[
            pltpu.VMEM((n, ch, lanes), x.dtype),
            pltpu.SemaphoreType.DMA((n,)),
            pltpu.SemaphoreType.DMA((n,)),
        ],
        compiler_params=pltpu.CompilerParams(collective_id=collective_id, has_side_effects=True),
    )(x)


def _forward_kernel(n, ch, x_ref, mass_ref, o_ref, recv, mine, gath, s1, r1, s2, r2):
    axis, other = "col", "row"
    me = lax.axis_index(axis)
    barrier = pltpu.get_barrier_semaphore()
    for d in range(1, n):
        pl.semaphore_signal(
            barrier, 1, device_id=_peer(axis, other, (me + d) % n), device_id_type=MESH_ID
        )
    pl.semaphore_wait(barrier, n - 1)
    sends = []
    for d in range(1, n):
        peer = (me + d) % n
        start = pl.multiple_of(peer * ch, ch)
        c = pltpu.make_async_remote_copy(
            x_ref.at[pl.ds(start, ch)], recv.at[d], s1.at[d], r1.at[d],
            device_id=_peer(axis, other, peer), device_id_type=MESH_ID,
        )
        c.start()
        sends.append(c)
    own = pl.multiple_of(me * ch, ch)
    acc = x_ref[pl.ds(own, ch), :]
    for d, c in enumerate(sends, 1):
        c.wait()
        acc = acc + recv[d]
    mine[...] = (acc * mass_ref[...]).astype(mine.dtype)
    gathers = []
    for d in range(1, n):
        c = pltpu.make_async_remote_copy(
            mine, gath.at[d], s2.at[d], r2.at[d],
            device_id=_peer(axis, other, (me + d) % n), device_id_type=MESH_ID,
        )
        c.start()
        gathers.append(c)
    o_ref[pl.ds(own, ch), :] = mine[...]
    for d, c in enumerate(gathers, 1):
        c.wait()
        src = pl.multiple_of(((me - d + n) % n) * ch, ch)
        o_ref[pl.ds(src, ch), :] = gath[d]


def forward_reduce(x, mass, n, collective_id):
    rows, lanes = x.shape
    ch = rows // n
    return pl.pallas_call(
        functools.partial(_forward_kernel, n, ch),
        out_shape=jax.ShapeDtypeStruct(x.shape, jnp.bfloat16),
        in_specs=[pl.BlockSpec(memory_space=pltpu.VMEM)] * 2,
        out_specs=pl.BlockSpec(memory_space=pltpu.VMEM),
        scratch_shapes=[
            pltpu.VMEM((n, ch, lanes), x.dtype),
            pltpu.VMEM((ch, lanes), jnp.bfloat16),
            pltpu.VMEM((n, ch, lanes), jnp.bfloat16),
            pltpu.SemaphoreType.DMA((n,)),
            pltpu.SemaphoreType.DMA((n,)),
            pltpu.SemaphoreType.DMA((n,)),
            pltpu.SemaphoreType.DMA((n,)),
        ],
        compiler_params=pltpu.CompilerParams(collective_id=collective_id, has_side_effects=True),
    )(x, mass)


def _gather2_kernel(axis, other, n, x_ref, y_ref, o_ref, p_ref, gx, gy, sx, rx, sy, ry):
    me = lax.axis_index(axis)
    cx = x_ref.shape[0]
    cy = y_ref.shape[0]
    barrier = pltpu.get_barrier_semaphore()
    for d in range(1, n):
        pl.semaphore_signal(
            barrier, 1, device_id=_peer(axis, other, (me + d) % n), device_id_type=MESH_ID
        )
    pl.semaphore_wait(barrier, n - 1)
    copies = []
    for d in range(1, n):
        peer = _peer(axis, other, (me + d) % n)
        a = pltpu.make_async_remote_copy(
            x_ref, gx.at[d], sx.at[d], rx.at[d], device_id=peer, device_id_type=MESH_ID
        )
        b = pltpu.make_async_remote_copy(
            y_ref, gy.at[d], sy.at[d], ry.at[d], device_id=peer, device_id_type=MESH_ID
        )
        a.start()
        b.start()
        copies.append((a, b))
    o_ref[pl.ds(pl.multiple_of(me * cx, cx), cx), :] = x_ref[...]
    p_ref[pl.ds(pl.multiple_of(me * cy, cy), cy), :] = y_ref[...]
    for d, (a, b) in enumerate(copies, 1):
        a.wait()
        b.wait()
        src = (me - d + n) % n
        o_ref[pl.ds(pl.multiple_of(src * cx, cx), cx), :] = gx[d]
        p_ref[pl.ds(pl.multiple_of(src * cy, cy), cy), :] = gy[d]


def all_gather2(x, y, axis, other, n, collective_id):
    return pl.pallas_call(
        functools.partial(_gather2_kernel, axis, other, n),
        out_shape=(
            jax.ShapeDtypeStruct((n * x.shape[0], x.shape[1]), x.dtype),
            jax.ShapeDtypeStruct((n * y.shape[0], y.shape[1]), y.dtype),
        ),
        in_specs=[pl.BlockSpec(memory_space=pltpu.VMEM)] * 2,
        out_specs=(pl.BlockSpec(memory_space=pltpu.VMEM),) * 2,
        scratch_shapes=[
            pltpu.VMEM((n,) + x.shape, x.dtype),
            pltpu.VMEM((n,) + y.shape, y.dtype),
            pltpu.SemaphoreType.DMA((n,)),
            pltpu.SemaphoreType.DMA((n,)),
            pltpu.SemaphoreType.DMA((n,)),
            pltpu.SemaphoreType.DMA((n,)),
        ],
        compiler_params=pltpu.CompilerParams(collective_id=collective_id, has_side_effects=True),
    )(x, y)


def _gram_of(a):
    return lax.dot_general(
        a, a, (((1,), (1,)), ((), ())), precision=lax.Precision.HIGH,
        preferred_element_type=jnp.float32,
    )


def chol_inverse(a):
    n = a.shape[0]
    r = lax.broadcasted_iota(jnp.int32, (n, n), 0)
    c = lax.broadcasted_iota(jnp.int32, (n, n), 1)
    r1 = lax.broadcasted_iota(jnp.int32, (n, 1), 0)
    c1 = lax.broadcasted_iota(jnp.int32, (1, n), 1)
    x0 = jnp.where(r == c, 1.0, 0.0).astype(jnp.float32)
    d0 = jnp.sum(jnp.where(r == c, a, 0.0), axis=0, keepdims=True)

    def step(j, carry):
        m, x, d = carry
        inv = 1.0 / jnp.sqrt(jnp.sum(jnp.where(c1 == j, d, 0.0), axis=1, keepdims=True))
        col = jnp.sum(jnp.where(c == j, m, 0.0), axis=1, keepdims=True)
        row = jnp.sum(jnp.where(r == j, m, 0.0), axis=0, keepdims=True)
        lcol = jnp.where(r1 >= j, col * inv, 0.0)
        lrow = jnp.where(c1 >= j, row * inv, 0.0)
        m = m - lcol * lrow
        d = d - lrow * lrow
        xrow = jnp.sum(jnp.where(r == j, x, 0.0), axis=0, keepdims=True) * inv
        x = jnp.where(r == j, xrow, x)
        x = x - jnp.where(r1 > j, lcol, 0.0) * xrow
        return m, x, d

    m, x, d = lax.fori_loop(0, n, step, (a, x0, d0))
    return x


def _backward_kernel(n, m, scale, x_ref, icol_ref, ipan_ref, o_ref, sc_ref, recv, gath, g3, panel, s1, r1, s2, r2, s3, r3):
    me = lax.axis_index("row")
    mc = lax.axis_index("col")
    barrier = pltpu.get_barrier_semaphore()
    for d in range(1, n):
        pl.semaphore_signal(barrier, 1, device_id=((me + d) % n, mc), device_id_type=MESH_ID)
    for d in range(1, m):
        pl.semaphore_signal(barrier, 1, device_id=(me, (mc + d) % m), device_id_type=MESH_ID)
    pl.semaphore_wait(barrier, n - 1 + m - 1)
    sends = []
    for d in range(1, n):
        peer = (me + d) % n
        c = pltpu.make_async_remote_copy(
            x_ref.at[peer], recv.at[d], s1.at[d], r1.at[d],
            device_id=(peer, mc), device_id_type=MESH_ID,
        )
        c.start()
        sends.append(c)
    acc = x_ref[me]
    for d, c in enumerate(sends, 1):
        c.wait()
        acc = acc + recv[d]
    gath[0] = acc * icol_ref[...]
    gathers = []
    for d in range(1, n):
        c = pltpu.make_async_remote_copy(
            gath.at[0], gath.at[d], s2.at[d], r2.at[d],
            device_id=((me + d) % n, mc), device_id_type=MESH_ID,
        )
        c.start()
        gathers.append(c)
    for c in gathers:
        c.wait()
    lanes = gath.shape[2]
    for p in range(n):
        panel[:, p * lanes:(p + 1) * lanes] = gath[(me - p + n) % n]
    g3[0] = _gram_of(panel[...])
    grams = []
    for d in range(1, m):
        c = pltpu.make_async_remote_copy(
            g3.at[0], g3.at[d], s3.at[d], r3.at[d],
            device_id=(me, (mc + d) % m), device_id_type=MESH_ID,
        )
        c.start()
        grams.append(c)
    for c in grams:
        c.wait()
    total = g3[mc % m]
    for q in range(1, m):
        total = total + g3[(mc - q + m) % m]
    inverse = chol_inverse(total * scale)
    rotated = lax.dot_general(
        inverse, panel[...], (((1,), (0,)), ((), ())),
        precision=lax.Precision.HIGH, preferred_element_type=jnp.float32,
    )
    for p in range(n):
        block = rotated[:, p * lanes:(p + 1) * lanes]
        o_ref[p] = block
        sc_ref[p] = (block * ipan_ref[p]).astype(sc_ref.dtype)


def backward_reduce(x, icol, ipan, n, m, scale, collective_id):
    chunks, vecs, lanes = x.shape
    return pl.pallas_call(
        functools.partial(_backward_kernel, n, m, scale),
        out_shape=(
            jax.ShapeDtypeStruct(x.shape, jnp.float32),
            jax.ShapeDtypeStruct(x.shape, jnp.bfloat16),
        ),
        in_specs=[pl.BlockSpec(memory_space=pltpu.VMEM)] * 3,
        out_specs=(pl.BlockSpec(memory_space=pltpu.VMEM),) * 2,
        scratch_shapes=[
            pltpu.VMEM((n, vecs, lanes), jnp.float32),
            pltpu.VMEM((n, vecs, lanes), jnp.float32),
            pltpu.VMEM((m, vecs, vecs), jnp.float32),
            pltpu.VMEM((vecs, n * lanes), jnp.float32),
            pltpu.SemaphoreType.DMA((n,)),
            pltpu.SemaphoreType.DMA((n,)),
            pltpu.SemaphoreType.DMA((n,)),
            pltpu.SemaphoreType.DMA((n,)),
            pltpu.SemaphoreType.DMA((m,)),
            pltpu.SemaphoreType.DMA((m,)),
        ],
        compiler_params=pltpu.CompilerParams(collective_id=collective_id, has_side_effects=True),
    )(x, icol, ipan)


def all_reduce(x, axis, other, n, collective_id, two_phase=True):
    rows, lanes = x.shape
    ch = rows // n if two_phase else rows
    slots = ch if two_phase else rows
    return pl.pallas_call(
        functools.partial(_reduce_kernel, axis, other, n, ch, two_phase),
        out_shape=jax.ShapeDtypeStruct(x.shape, x.dtype),
        in_specs=[pl.BlockSpec(memory_space=pltpu.VMEM)],
        out_specs=pl.BlockSpec(memory_space=pltpu.VMEM),
        scratch_shapes=[
            pltpu.VMEM((n, slots, lanes), x.dtype),
            pltpu.VMEM((ch, lanes), x.dtype),
            pltpu.VMEM((n, ch, lanes), x.dtype),
            pltpu.SemaphoreType.DMA((n,)),
            pltpu.SemaphoreType.DMA((n,)),
            pltpu.SemaphoreType.DMA((n,)),
            pltpu.SemaphoreType.DMA((n,)),
        ],
        compiler_params=pltpu.CompilerParams(collective_id=collective_id, has_side_effects=True),
    )(x)


def rotate(projected, gram):
    lower = jnp.linalg.cholesky(gram)
    inverse = lax.linalg.triangular_solve(
        lower, jnp.eye(gram.shape[0], dtype=jnp.float32), left_side=True, lower=True
    )
    return jnp.einsum(
        "kl,bli->bki",
        inverse,
        projected,
        precision=lax.Precision.HIGHEST,
        preferred_element_type=jnp.float32,
    )


def rotate_pairs(projected, gram):
    lower = jnp.linalg.cholesky(gram)
    inverse = lax.linalg.triangular_solve(
        lower, jnp.eye(gram.shape[0], dtype=jnp.float32), left_side=True, lower=True
    )
    return jnp.einsum(
        "kl,plx->pkx",
        inverse,
        projected,
        precision=lax.Precision.HIGHEST,
        preferred_element_type=jnp.float32,
    )


def local_gram(projected):
    return jnp.einsum(
        "bki,bli->kl",
        projected,
        projected,
        precision=lax.Precision.HIGHEST,
        preferred_element_type=jnp.float32,
    )


def panel_sum(partial, axis, other, n, collective_id):
    blocks, vecs, bsize = partial.shape
    flat = partial.reshape(blocks * vecs * bsize // LANES, LANES)
    return all_reduce(flat, axis, other, n, collective_id).reshape(blocks, vecs, bsize)


def per_device(blocks, block_row, block_col, counts, vectors, row_mass, col_mass):
    tile = blocks[0, 0]
    n_cap = tile.shape[0]
    bsize = row_mass.shape[1]
    vecs = vectors.shape[1] // bsize
    own = vectors.shape[0]
    n_row = lax.axis_size("row")
    n_col = lax.axis_size("col")
    row_panel = own * n_col
    col_panel = own * n_row
    total_boxes = float(own * bsize * n_row * n_col)
    rows_idx = block_row[0, 0]
    cols_idx = block_col[0, 0]
    live = jnp.arange(n_cap) < counts[0, 0]
    fwd_ids = jnp.where(live, rows_idx, row_panel)
    bwd_ids = jnp.where(live, cols_idx, col_panel)
    square = tile.reshape(n_cap, bsize, bsize)
    vec_rows = own * vecs * bsize // LANES
    own_inv = 1.0 / jnp.sqrt(col_mass)
    first = (vectors.reshape(own, vecs, bsize) * own_inv[:, None, :]).astype(jnp.bfloat16)
    mass_pad = jnp.zeros((8, 128), jnp.float32).at[0, : own * bsize].set(col_mass.reshape(-1))
    got, mass_got = all_gather2(first.reshape(vec_rows, LANES), mass_pad, "row", "col", n_row, 4)
    first_panel = got.reshape(col_panel, vecs, bsize)
    col_mass_panel = mass_got.reshape(n_row, 8, 128)[:, 0, : own * bsize].reshape(col_panel, bsize)
    inv_col = 1.0 / jnp.sqrt(col_mass_panel)
    pairs = col_panel // 2
    inv_pairs = inv_col.reshape(pairs, 1, 2 * bsize)
    own_pair = jnp.broadcast_to(own_inv.reshape(1, own * bsize), (vecs, own * bsize))
    row_mass_spread = jnp.broadcast_to(row_mass[:, None, :], (own, vecs, bsize)).reshape(vec_rows, LANES)
    fwd_hot = (fwd_ids[None, :] == jnp.arange(row_panel)[:, None]).astype(jnp.bfloat16)
    bwd_hot = (bwd_ids[None, :] == jnp.arange(col_panel)[:, None]).astype(jnp.bfloat16)
    for step in range(ITERS):
        if step == 0:
            scaled = first_panel
        else:
            scaled = paired.reshape(pairs, vecs, 2, bsize).transpose(0, 2, 1, 3).reshape(col_panel, vecs, bsize)
        forward_taken = jnp.take(scaled, cols_idx, axis=0)
        forward_product = jnp.einsum(
            "bij,bkj->bki", square, forward_taken, preferred_element_type=jnp.bfloat16
        )
        forward_summed = jnp.einsum(
            "rs,ski->rki", fwd_hot, forward_product, preferred_element_type=jnp.float32
        )
        flat = forward_summed.reshape(row_panel * vecs * bsize // LANES, LANES)
        weighted = forward_reduce(flat, row_mass_spread, n_col, 1).reshape(row_panel, vecs, bsize)
        taken = jnp.take(weighted, rows_idx, axis=0)
        product = jnp.einsum("bij,bki->bkj", square, taken, preferred_element_type=jnp.bfloat16)
        summed = jnp.einsum(
            "pbs,skj->pkbj", bwd_hot.reshape(pairs, 2, n_cap), product,
            preferred_element_type=jnp.float32,
        ).reshape(pairs, vecs, 2 * bsize)
        current, paired = backward_reduce(summed, own_pair, inv_pairs, n_row, n_col, 1.0 / total_boxes, 2)
    me = lax.axis_index("row")
    mine = lax.dynamic_index_in_dim(current, me, 0, keepdims=False)
    return mine.reshape(vecs, own, bsize).transpose(1, 0, 2).reshape(own, vecs * bsize)


def solution(mesh):
    in_specs = (
        P("row", "col", None, None),
        P("row", "col", None),
        P("row", "col", None),
        P("row", "col"),
        P(("col", "row"), None),
        P(("row", "col"), None),
        P(("col", "row"), None),
    )
    out_specs = P(("col", "row"), None)
    return jax.shard_map(
        per_device, mesh=mesh, in_specs=in_specs, out_specs=out_specs, check_vma=False
    )
```

```python
import functools

import jax
import jax.numpy as jnp
from jax import lax
from jax.experimental import pallas as pl
from jax.experimental.pallas import tpu as pltpu
from jax.sharding import PartitionSpec as P

ITERS = 4
LANES = 512
MESH_ID = pl.DeviceIdType.MESH


def _peer(axis, other, p):
    them = lax.axis_index(other)
    return (p, them) if axis == "row" else (them, p)


def _reduce_kernel(axis, other, n, ch, two_phase, x_ref, o_ref, recv, mine, gath, s1, r1, s2, r2):
    me = lax.axis_index(axis)
    barrier = pltpu.get_barrier_semaphore()
    for d in range(1, n):
        pl.semaphore_signal(
            barrier, 1, device_id=_peer(axis, other, (me + d) % n), device_id_type=MESH_ID
        )
    pl.semaphore_wait(barrier, n - 1)
    if not two_phase:
        sends = []
        for d in range(1, n):
            c = pltpu.make_async_remote_copy(
                x_ref, recv.at[d], s1.at[d], r1.at[d],
                device_id=_peer(axis, other, (me + d) % n), device_id_type=MESH_ID,
            )
            c.start()
            sends.append(c)
        for c in sends:
            c.wait()
        recv[0] = x_ref[...]
        acc = recv[me % n]
        for p in range(1, n):
            acc = acc + recv[(me - p + n) % n]
        o_ref[...] = acc
        return
    sends = []
    for d in range(1, n):
        peer = (me + d) % n
        start = pl.multiple_of(peer * ch, ch)
        c = pltpu.make_async_remote_copy(
            x_ref.at[pl.ds(start, ch)], recv.at[d], s1.at[d], r1.at[d],
            device_id=_peer(axis, other, peer), device_id_type=MESH_ID,
        )
        c.start()
        sends.append(c)
    own = pl.multiple_of(me * ch, ch)
    acc = x_ref[pl.ds(own, ch), :]
    for d, c in enumerate(sends, 1):
        c.wait()
        acc = acc + recv[d]
    mine[...] = acc
    gathers = []
    for d in range(1, n):
        c = pltpu.make_async_remote_copy(
            mine, gath.at[d], s2.at[d], r2.at[d],
            device_id=_peer(axis, other, (me + d) % n), device_id_type=MESH_ID,
        )
        c.start()
        gathers.append(c)
    o_ref[pl.ds(own, ch), :] = acc
    for d, c in enumerate(gathers, 1):
        c.wait()
        src = pl.multiple_of(((me - d + n) % n) * ch, ch)
        o_ref[pl.ds(src, ch), :] = gath[d]


def _gather_kernel(axis, other, n, x_ref, o_ref, gath, s2, r2):
    me = lax.axis_index(axis)
    ch = x_ref.shape[0]
    barrier = pltpu.get_barrier_semaphore()
    for d in range(1, n):
        pl.semaphore_signal(
            barrier, 1, device_id=_peer(axis, other, (me + d) % n), device_id_type=MESH_ID
        )
    pl.semaphore_wait(barrier, n - 1)
    gathers = []
    for d in range(1, n):
        c = pltpu.make_async_remote_copy(
            x_ref, gath.at[d], s2.at[d], r2.at[d],
            device_id=_peer(axis, other, (me + d) % n), device_id_type=MESH_ID,
        )
        c.start()
        gathers.append(c)
    o_ref[pl.ds(pl.multiple_of(me * ch, ch), ch), :] = x_ref[...]
    for d, c in enumerate(gathers, 1):
        c.wait()
        src = pl.multiple_of(((me - d + n) % n) * ch, ch)
        o_ref[pl.ds(src, ch), :] = gath[d]


def all_gather(x, axis, other, n, collective_id):
    ch, lanes = x.shape
    return pl.pallas_call(
        functools.partial(_gather_kernel, axis, other, n),
        out_shape=jax.ShapeDtypeStruct((n * ch, lanes), x.dtype),
        in_specs=[pl.BlockSpec(memory_space=pltpu.VMEM)],
        out_specs=pl.BlockSpec(memory_space=pltpu.VMEM),
        scratch_shapes=[
            pltpu.VMEM((n, ch, lanes), x.dtype),
            pltpu.SemaphoreType.DMA((n,)),
            pltpu.SemaphoreType.DMA((n,)),
        ],
        compiler_params=pltpu.CompilerParams(collective_id=collective_id, has_side_effects=True),
    )(x)


def _forward_kernel(n, ch, x_ref, mass_ref, o_ref, recv, mine, gath, s1, r1, s2, r2):
    axis, other = "col", "row"
    me = lax.axis_index(axis)
    barrier = pltpu.get_barrier_semaphore()
    for d in range(1, n):
        pl.semaphore_signal(
            barrier, 1, device_id=_peer(axis, other, (me + d) % n), device_id_type=MESH_ID
        )
    pl.semaphore_wait(barrier, n - 1)
    sends = []
    for d in range(1, n):
        peer = (me + d) % n
        start = pl.multiple_of(peer * ch, ch)
        c = pltpu.make_async_remote_copy(
            x_ref.at[pl.ds(start, ch)], recv.at[d], s1.at[d], r1.at[d],
            device_id=_peer(axis, other, peer), device_id_type=MESH_ID,
        )
        c.start()
        sends.append(c)
    own = pl.multiple_of(me * ch, ch)
    acc = x_ref[pl.ds(own, ch), :]
    for d, c in enumerate(sends, 1):
        c.wait()
        acc = acc + recv[d]
    mine[...] = (acc * mass_ref[...]).astype(mine.dtype)
    gathers = []
    for d in range(1, n):
        c = pltpu.make_async_remote_copy(
            mine, gath.at[d], s2.at[d], r2.at[d],
            device_id=_peer(axis, other, (me + d) % n), device_id_type=MESH_ID,
        )
        c.start()
        gathers.append(c)
    o_ref[pl.ds(own, ch), :] = mine[...]
    for d, c in enumerate(gathers, 1):
        c.wait()
        src = pl.multiple_of(((me - d + n) % n) * ch, ch)
        o_ref[pl.ds(src, ch), :] = gath[d]


def forward_reduce(x, mass, n, collective_id):
    rows, lanes = x.shape
    ch = rows // n
    return pl.pallas_call(
        functools.partial(_forward_kernel, n, ch),
        out_shape=jax.ShapeDtypeStruct(x.shape, jnp.bfloat16),
        in_specs=[pl.BlockSpec(memory_space=pltpu.VMEM)] * 2,
        out_specs=pl.BlockSpec(memory_space=pltpu.VMEM),
        scratch_shapes=[
            pltpu.VMEM((n, ch, lanes), x.dtype),
            pltpu.VMEM((ch, lanes), jnp.bfloat16),
            pltpu.VMEM((n, ch, lanes), jnp.bfloat16),
            pltpu.SemaphoreType.DMA((n,)),
            pltpu.SemaphoreType.DMA((n,)),
            pltpu.SemaphoreType.DMA((n,)),
            pltpu.SemaphoreType.DMA((n,)),
        ],
        compiler_params=pltpu.CompilerParams(collective_id=collective_id, has_side_effects=True),
    )(x, mass)


def _gather2_kernel(axis, other, n, x_ref, y_ref, o_ref, p_ref, gx, gy, sx, rx, sy, ry):
    me = lax.axis_index(axis)
    cx = x_ref.shape[0]
    cy = y_ref.shape[0]
    barrier = pltpu.get_barrier_semaphore()
    for d in range(1, n):
        pl.semaphore_signal(
            barrier, 1, device_id=_peer(axis, other, (me + d) % n), device_id_type=MESH_ID
        )
    pl.semaphore_wait(barrier, n - 1)
    copies = []
    for d in range(1, n):
        peer = _peer(axis, other, (me + d) % n)
        a = pltpu.make_async_remote_copy(
            x_ref, gx.at[d], sx.at[d], rx.at[d], device_id=peer, device_id_type=MESH_ID
        )
        b = pltpu.make_async_remote_copy(
            y_ref, gy.at[d], sy.at[d], ry.at[d], device_id=peer, device_id_type=MESH_ID
        )
        a.start()
        b.start()
        copies.append((a, b))
    o_ref[pl.ds(pl.multiple_of(me * cx, cx), cx), :] = x_ref[...]
    p_ref[pl.ds(pl.multiple_of(me * cy, cy), cy), :] = y_ref[...]
    for d, (a, b) in enumerate(copies, 1):
        a.wait()
        b.wait()
        src = (me - d + n) % n
        o_ref[pl.ds(pl.multiple_of(src * cx, cx), cx), :] = gx[d]
        p_ref[pl.ds(pl.multiple_of(src * cy, cy), cy), :] = gy[d]


def all_gather2(x, y, axis, other, n, collective_id):
    return pl.pallas_call(
        functools.partial(_gather2_kernel, axis, other, n),
        out_shape=(
            jax.ShapeDtypeStruct((n * x.shape[0], x.shape[1]), x.dtype),
            jax.ShapeDtypeStruct((n * y.shape[0], y.shape[1]), y.dtype),
        ),
        in_specs=[pl.BlockSpec(memory_space=pltpu.VMEM)] * 2,
        out_specs=(pl.BlockSpec(memory_space=pltpu.VMEM),) * 2,
        scratch_shapes=[
            pltpu.VMEM((n,) + x.shape, x.dtype),
            pltpu.VMEM((n,) + y.shape, y.dtype),
            pltpu.SemaphoreType.DMA((n,)),
            pltpu.SemaphoreType.DMA((n,)),
            pltpu.SemaphoreType.DMA((n,)),
            pltpu.SemaphoreType.DMA((n,)),
        ],
        compiler_params=pltpu.CompilerParams(collective_id=collective_id, has_side_effects=True),
    )(x, y)


def _gram_of(a):
    return lax.dot_general(
        a, a, (((1,), (1,)), ((), ())), precision=lax.Precision.HIGH,
        preferred_element_type=jnp.float32,
    )


def chol_inverse(a):
    n = a.shape[0]
    r = lax.broadcasted_iota(jnp.int32, (n, n), 0)
    c = lax.broadcasted_iota(jnp.int32, (n, n), 1)
    r1 = lax.broadcasted_iota(jnp.int32, (n, 1), 0)
    c1 = lax.broadcasted_iota(jnp.int32, (1, n), 1)
    x0 = jnp.where(r == c, 1.0, 0.0).astype(jnp.float32)
    d0 = jnp.sum(jnp.where(r == c, a, 0.0), axis=0, keepdims=True)

    def step(j, carry):
        m, x, d = carry
        inv = lax.rsqrt(jnp.sum(jnp.where(c1 == j, d, 0.0), axis=1, keepdims=True))
        col = jnp.sum(jnp.where(c == j, m, 0.0), axis=1, keepdims=True)
        row = jnp.sum(jnp.where(r == j, m, 0.0), axis=0, keepdims=True)
        lcol = jnp.where(r1 >= j, col * inv, 0.0)
        lrow = jnp.where(c1 >= j, row * inv, 0.0)
        m = m - lcol * lrow
        d = d - lrow * lrow
        xrow = jnp.sum(jnp.where(r == j, x, 0.0), axis=0, keepdims=True) * inv
        x = jnp.where(r == j, xrow, x)
        x = x - jnp.where(r1 > j, lcol, 0.0) * xrow
        return m, x, d

    m, x, d = lax.fori_loop(0, n, step, (a, x0, d0))
    return x


def _backward_kernel(n, m, scale, x_ref, icol_ref, o_ref, recv, gath, g3, panel, s1, r1, s2, r2, s3, r3):
    me = lax.axis_index("row")
    mc = lax.axis_index("col")
    barrier = pltpu.get_barrier_semaphore()
    for d in range(1, n):
        pl.semaphore_signal(barrier, 1, device_id=((me + d) % n, mc), device_id_type=MESH_ID)
    for d in range(1, m):
        pl.semaphore_signal(barrier, 1, device_id=(me, (mc + d) % m), device_id_type=MESH_ID)
    pl.semaphore_wait(barrier, n - 1 + m - 1)
    sends = []
    for d in range(1, n):
        peer = (me + d) % n
        c = pltpu.make_async_remote_copy(
            x_ref.at[peer], recv.at[d], s1.at[d], r1.at[d],
            device_id=(peer, mc), device_id_type=MESH_ID,
        )
        c.start()
        sends.append(c)
    acc = x_ref[me]
    for d, c in enumerate(sends, 1):
        c.wait()
        acc = acc + recv[d]
    gath[0] = acc * icol_ref[...]
    gathers = []
    for d in range(1, n):
        c = pltpu.make_async_remote_copy(
            gath.at[0], gath.at[d], s2.at[d], r2.at[d],
            device_id=((me + d) % n, mc), device_id_type=MESH_ID,
        )
        c.start()
        gathers.append(c)
    for c in gathers:
        c.wait()
    lanes = gath.shape[2]
    for p in range(n):
        panel[:, p * lanes:(p + 1) * lanes] = gath[(me - p + n) % n]
    g3[0] = _gram_of(panel[...])
    grams = []
    for d in range(1, m):
        c = pltpu.make_async_remote_copy(
            g3.at[0], g3.at[d], s3.at[d], r3.at[d],
            device_id=(me, (mc + d) % m), device_id_type=MESH_ID,
        )
        c.start()
        grams.append(c)
    for c in grams:
        c.wait()
    total = g3[mc % m]
    for q in range(1, m):
        total = total + g3[(mc - q + m) % m]
    inverse = chol_inverse(total * scale)
    rotated = lax.dot_general(
        inverse, panel[...], (((1,), (0,)), ((), ())),
        precision=lax.Precision.HIGH, preferred_element_type=jnp.float32,
    )
    for p in range(n):
        o_ref[p] = rotated[:, p * lanes:(p + 1) * lanes]


def backward_reduce(x, icol, n, m, scale, collective_id):
    chunks, vecs, lanes = x.shape
    return pl.pallas_call(
        functools.partial(_backward_kernel, n, m, scale),
        out_shape=jax.ShapeDtypeStruct(x.shape, jnp.float32),
        in_specs=[pl.BlockSpec(memory_space=pltpu.VMEM)] * 2,
        out_specs=pl.BlockSpec(memory_space=pltpu.VMEM),
        scratch_shapes=[
            pltpu.VMEM((n, vecs, lanes), jnp.float32),
            pltpu.VMEM((n, vecs, lanes), jnp.float32),
            pltpu.VMEM((m, vecs, vecs), jnp.float32),
            pltpu.VMEM((vecs, n * lanes), jnp.float32),
            pltpu.SemaphoreType.DMA((n,)),
            pltpu.SemaphoreType.DMA((n,)),
            pltpu.SemaphoreType.DMA((n,)),
            pltpu.SemaphoreType.DMA((n,)),
            pltpu.SemaphoreType.DMA((m,)),
            pltpu.SemaphoreType.DMA((m,)),
        ],
        compiler_params=pltpu.CompilerParams(collective_id=collective_id, has_side_effects=True),
    )(x, icol)


def all_reduce(x, axis, other, n, collective_id, two_phase=True):
    rows, lanes = x.shape
    ch = rows // n if two_phase else rows
    slots = ch if two_phase else rows
    return pl.pallas_call(
        functools.partial(_reduce_kernel, axis, other, n, ch, two_phase),
        out_shape=jax.ShapeDtypeStruct(x.shape, x.dtype),
        in_specs=[pl.BlockSpec(memory_space=pltpu.VMEM)],
        out_specs=pl.BlockSpec(memory_space=pltpu.VMEM),
        scratch_shapes=[
            pltpu.VMEM((n, slots, lanes), x.dtype),
            pltpu.VMEM((ch, lanes), x.dtype),
            pltpu.VMEM((n, ch, lanes), x.dtype),
            pltpu.SemaphoreType.DMA((n,)),
            pltpu.SemaphoreType.DMA((n,)),
            pltpu.SemaphoreType.DMA((n,)),
            pltpu.SemaphoreType.DMA((n,)),
        ],
        compiler_params=pltpu.CompilerParams(collective_id=collective_id, has_side_effects=True),
    )(x)


def rotate(projected, gram):
    lower = jnp.linalg.cholesky(gram)
    inverse = lax.linalg.triangular_solve(
        lower, jnp.eye(gram.shape[0], dtype=jnp.float32), left_side=True, lower=True
    )
    return jnp.einsum(
        "kl,bli->bki",
        inverse,
        projected,
        precision=lax.Precision.HIGHEST,
        preferred_element_type=jnp.float32,
    )


def rotate_pairs(projected, gram):
    lower = jnp.linalg.cholesky(gram)
    inverse = lax.linalg.triangular_solve(
        lower, jnp.eye(gram.shape[0], dtype=jnp.float32), left_side=True, lower=True
    )
    return jnp.einsum(
        "kl,plx->pkx",
        inverse,
        projected,
        precision=lax.Precision.HIGHEST,
        preferred_element_type=jnp.float32,
    )


def local_gram(projected):
    return jnp.einsum(
        "bki,bli->kl",
        projected,
        projected,
        precision=lax.Precision.HIGHEST,
        preferred_element_type=jnp.float32,
    )


def panel_sum(partial, axis, other, n, collective_id):
    blocks, vecs, bsize = partial.shape
    flat = partial.reshape(blocks * vecs * bsize // LANES, LANES)
    return all_reduce(flat, axis, other, n, collective_id).reshape(blocks, vecs, bsize)


def per_device(blocks, block_row, block_col, counts, vectors, row_mass, col_mass):
    tile = blocks[0, 0]
    n_cap = tile.shape[0]
    bsize = row_mass.shape[1]
    vecs = vectors.shape[1] // bsize
    own = vectors.shape[0]
    n_row = lax.axis_size("row")
    n_col = lax.axis_size("col")
    row_panel = own * n_col
    col_panel = own * n_row
    total_boxes = float(own * bsize * n_row * n_col)
    rows_idx = block_row[0, 0]
    cols_idx = block_col[0, 0]
    live = jnp.arange(n_cap) < counts[0, 0]
    fwd_ids = jnp.where(live, rows_idx, row_panel)
    bwd_ids = jnp.where(live, cols_idx, col_panel)
    square = tile.reshape(n_cap, bsize, bsize)
    vec_rows = own * vecs * bsize // LANES
    own_inv = 1.0 / jnp.sqrt(col_mass)
    first = (vectors.reshape(own, vecs, bsize) * own_inv[:, None, :]).astype(jnp.bfloat16)
    mass_pad = jnp.zeros((8, 128), jnp.float32).at[0, : own * bsize].set(col_mass.reshape(-1))
    got, mass_got = all_gather2(first.reshape(vec_rows, LANES), mass_pad, "row", "col", n_row, 4)
    first_panel = got.reshape(col_panel, vecs, bsize)
    col_mass_panel = mass_got.reshape(n_row, 8, 128)[:, 0, : own * bsize].reshape(col_panel, bsize)
    inv_col = 1.0 / jnp.sqrt(col_mass_panel)
    pairs = col_panel // 2
    inv_pairs = inv_col.reshape(pairs, 1, 2 * bsize)
    own_pair = jnp.broadcast_to(own_inv.reshape(1, own * bsize), (vecs, own * bsize))
    row_mass_spread = jnp.broadcast_to(row_mass[:, None, :], (own, vecs, bsize)).reshape(vec_rows, LANES)
    fwd_hot = (fwd_ids[None, :] == jnp.arange(row_panel)[:, None]).astype(jnp.bfloat16)
    bwd_hot = (bwd_ids[None, :] == jnp.arange(col_panel)[:, None]).astype(jnp.bfloat16)
    for step in range(ITERS):
        if step == 0:
            scaled = first_panel
        else:
            paired = (current * inv_pairs).astype(jnp.bfloat16)
            scaled = paired.reshape(pairs, vecs, 2, bsize).transpose(0, 2, 1, 3).reshape(col_panel, vecs, bsize)
        forward_taken = jnp.take(scaled, cols_idx, axis=0)
        forward_product = jnp.einsum(
            "bij,bkj->bki", square, forward_taken, preferred_element_type=jnp.bfloat16
        )
        forward_summed = jnp.einsum(
            "rs,ski->rki", fwd_hot, forward_product, preferred_element_type=jnp.float32
        )
        flat = forward_summed.reshape(row_panel * vecs * bsize // LANES, LANES)
        weighted = forward_reduce(flat, row_mass_spread, n_col, 1).reshape(row_panel, vecs, bsize)
        taken = jnp.take(weighted, rows_idx, axis=0)
        product = jnp.einsum("bij,bki->bkj", square, taken, preferred_element_type=jnp.bfloat16)
        summed = jnp.einsum(
            "pbs,skj->pkbj", bwd_hot.reshape(pairs, 2, n_cap), product,
            preferred_element_type=jnp.float32,
        ).reshape(pairs, vecs, 2 * bsize)
        current = backward_reduce(summed, own_pair, n_row, n_col, 1.0 / total_boxes, 2)
    me = lax.axis_index("row")
    mine = lax.dynamic_index_in_dim(current, me, 0, keepdims=False)
    return mine.reshape(vecs, own, bsize).transpose(1, 0, 2).reshape(own, vecs * bsize)


def solution(mesh):
    in_specs = (
        P("row", "col", None, None),
        P("row", "col", None),
        P("row", "col", None),
        P("row", "col"),
        P(("col", "row"), None),
        P(("row", "col"), None),
        P(("col", "row"), None),
    )
    out_specs = P(("col", "row"), None)
    return jax.shard_map(
        per_device, mesh=mesh, in_specs=in_specs, out_specs=out_specs, check_vma=False
    )
```

```python
import functools

import jax
import jax.numpy as jnp
from jax import lax
from jax.experimental import pallas as pl
from jax.experimental.pallas import tpu as pltpu
from jax.sharding import PartitionSpec as P

ITERS = 4
LANES = 512
MESH_ID = pl.DeviceIdType.MESH


def _peer(axis, other, p):
    them = lax.axis_index(other)
    return (p, them) if axis == "row" else (them, p)


def _reduce_kernel(axis, other, n, ch, two_phase, x_ref, o_ref, recv, mine, gath, s1, r1, s2, r2):
    me = lax.axis_index(axis)
    barrier = pltpu.get_barrier_semaphore()
    for d in range(1, n):
        pl.semaphore_signal(
            barrier, 1, device_id=_peer(axis, other, (me + d) % n), device_id_type=MESH_ID
        )
    pl.semaphore_wait(barrier, n - 1)
    if not two_phase:
        sends = []
        for d in range(1, n):
            c = pltpu.make_async_remote_copy(
                x_ref, recv.at[d], s1.at[d], r1.at[d],
                device_id=_peer(axis, other, (me + d) % n), device_id_type=MESH_ID,
            )
            c.start()
            sends.append(c)
        for c in sends:
            c.wait()
        recv[0] = x_ref[...]
        acc = recv[me % n]
        for p in range(1, n):
            acc = acc + recv[(me - p + n) % n]
        o_ref[...] = acc
        return
    sends = []
    for d in range(1, n):
        peer = (me + d) % n
        start = pl.multiple_of(peer * ch, ch)
        c = pltpu.make_async_remote_copy(
            x_ref.at[pl.ds(start, ch)], recv.at[d], s1.at[d], r1.at[d],
            device_id=_peer(axis, other, peer), device_id_type=MESH_ID,
        )
        c.start()
        sends.append(c)
    own = pl.multiple_of(me * ch, ch)
    acc = x_ref[pl.ds(own, ch), :]
    for d, c in enumerate(sends, 1):
        c.wait()
        acc = acc + recv[d]
    mine[...] = acc
    gathers = []
    for d in range(1, n):
        c = pltpu.make_async_remote_copy(
            mine, gath.at[d], s2.at[d], r2.at[d],
            device_id=_peer(axis, other, (me + d) % n), device_id_type=MESH_ID,
        )
        c.start()
        gathers.append(c)
    o_ref[pl.ds(own, ch), :] = acc
    for d, c in enumerate(gathers, 1):
        c.wait()
        src = pl.multiple_of(((me - d + n) % n) * ch, ch)
        o_ref[pl.ds(src, ch), :] = gath[d]


def _gather_kernel(axis, other, n, x_ref, o_ref, gath, s2, r2):
    me = lax.axis_index(axis)
    ch = x_ref.shape[0]
    barrier = pltpu.get_barrier_semaphore()
    for d in range(1, n):
        pl.semaphore_signal(
            barrier, 1, device_id=_peer(axis, other, (me + d) % n), device_id_type=MESH_ID
        )
    pl.semaphore_wait(barrier, n - 1)
    gathers = []
    for d in range(1, n):
        c = pltpu.make_async_remote_copy(
            x_ref, gath.at[d], s2.at[d], r2.at[d],
            device_id=_peer(axis, other, (me + d) % n), device_id_type=MESH_ID,
        )
        c.start()
        gathers.append(c)
    o_ref[pl.ds(pl.multiple_of(me * ch, ch), ch), :] = x_ref[...]
    for d, c in enumerate(gathers, 1):
        c.wait()
        src = pl.multiple_of(((me - d + n) % n) * ch, ch)
        o_ref[pl.ds(src, ch), :] = gath[d]


def all_gather(x, axis, other, n, collective_id):
    ch, lanes = x.shape
    return pl.pallas_call(
        functools.partial(_gather_kernel, axis, other, n),
        out_shape=jax.ShapeDtypeStruct((n * ch, lanes), x.dtype),
        in_specs=[pl.BlockSpec(memory_space=pltpu.VMEM)],
        out_specs=pl.BlockSpec(memory_space=pltpu.VMEM),
        scratch_shapes=[
            pltpu.VMEM((n, ch, lanes), x.dtype),
            pltpu.SemaphoreType.DMA((n,)),
            pltpu.SemaphoreType.DMA((n,)),
        ],
        compiler_params=pltpu.CompilerParams(collective_id=collective_id, has_side_effects=True),
    )(x)


def _forward_kernel(n, ch, x_ref, mass_ref, o_ref, recv, mine, gath, s1, r1, s2, r2):
    axis, other = "col", "row"
    me = lax.axis_index(axis)
    barrier = pltpu.get_barrier_semaphore()
    for d in range(1, n):
        pl.semaphore_signal(
            barrier, 1, device_id=_peer(axis, other, (me + d) % n), device_id_type=MESH_ID
        )
    pl.semaphore_wait(barrier, n - 1)
    sends = []
    for d in range(1, n):
        peer = (me + d) % n
        start = pl.multiple_of(peer * ch, ch)
        c = pltpu.make_async_remote_copy(
            x_ref.at[pl.ds(start, ch)], recv.at[d], s1.at[d], r1.at[d],
            device_id=_peer(axis, other, peer), device_id_type=MESH_ID,
        )
        c.start()
        sends.append(c)
    own = pl.multiple_of(me * ch, ch)
    acc = x_ref[pl.ds(own, ch), :]
    for d, c in enumerate(sends, 1):
        c.wait()
        acc = acc + recv[d]
    mine[...] = (acc * mass_ref[...]).astype(mine.dtype)
    gathers = []
    for d in range(1, n):
        c = pltpu.make_async_remote_copy(
            mine, gath.at[d], s2.at[d], r2.at[d],
            device_id=_peer(axis, other, (me + d) % n), device_id_type=MESH_ID,
        )
        c.start()
        gathers.append(c)
    o_ref[pl.ds(own, ch), :] = mine[...]
    for d, c in enumerate(gathers, 1):
        c.wait()
        src = pl.multiple_of(((me - d + n) % n) * ch, ch)
        o_ref[pl.ds(src, ch), :] = gath[d]


def forward_reduce(x, mass, n, collective_id):
    rows, lanes = x.shape
    ch = rows // n
    return pl.pallas_call(
        functools.partial(_forward_kernel, n, ch),
        out_shape=jax.ShapeDtypeStruct(x.shape, jnp.bfloat16),
        in_specs=[pl.BlockSpec(memory_space=pltpu.VMEM)] * 2,
        out_specs=pl.BlockSpec(memory_space=pltpu.VMEM),
        scratch_shapes=[
            pltpu.VMEM((n, ch, lanes), x.dtype),
            pltpu.VMEM((ch, lanes), jnp.bfloat16),
            pltpu.VMEM((n, ch, lanes), jnp.bfloat16),
            pltpu.SemaphoreType.DMA((n,)),
            pltpu.SemaphoreType.DMA((n,)),
            pltpu.SemaphoreType.DMA((n,)),
            pltpu.SemaphoreType.DMA((n,)),
        ],
        compiler_params=pltpu.CompilerParams(collective_id=collective_id, has_side_effects=True),
    )(x, mass)


def _gather2_kernel(axis, other, n, x_ref, y_ref, o_ref, p_ref, gx, gy, sx, rx, sy, ry):
    me = lax.axis_index(axis)
    cx = x_ref.shape[0]
    cy = y_ref.shape[0]
    barrier = pltpu.get_barrier_semaphore()
    for d in range(1, n):
        pl.semaphore_signal(
            barrier, 1, device_id=_peer(axis, other, (me + d) % n), device_id_type=MESH_ID
        )
    pl.semaphore_wait(barrier, n - 1)
    copies = []
    for d in range(1, n):
        peer = _peer(axis, other, (me + d) % n)
        a = pltpu.make_async_remote_copy(
            x_ref, gx.at[d], sx.at[d], rx.at[d], device_id=peer, device_id_type=MESH_ID
        )
        b = pltpu.make_async_remote_copy(
            y_ref, gy.at[d], sy.at[d], ry.at[d], device_id=peer, device_id_type=MESH_ID
        )
        a.start()
        b.start()
        copies.append((a, b))
    o_ref[pl.ds(pl.multiple_of(me * cx, cx), cx), :] = x_ref[...]
    p_ref[pl.ds(pl.multiple_of(me * cy, cy), cy), :] = y_ref[...]
    for d, (a, b) in enumerate(copies, 1):
        a.wait()
        b.wait()
        src = (me - d + n) % n
        o_ref[pl.ds(pl.multiple_of(src * cx, cx), cx), :] = gx[d]
        p_ref[pl.ds(pl.multiple_of(src * cy, cy), cy), :] = gy[d]


def all_gather2(x, y, axis, other, n, collective_id):
    return pl.pallas_call(
        functools.partial(_gather2_kernel, axis, other, n),
        out_shape=(
            jax.ShapeDtypeStruct((n * x.shape[0], x.shape[1]), x.dtype),
            jax.ShapeDtypeStruct((n * y.shape[0], y.shape[1]), y.dtype),
        ),
        in_specs=[pl.BlockSpec(memory_space=pltpu.VMEM)] * 2,
        out_specs=(pl.BlockSpec(memory_space=pltpu.VMEM),) * 2,
        scratch_shapes=[
            pltpu.VMEM((n,) + x.shape, x.dtype),
            pltpu.VMEM((n,) + y.shape, y.dtype),
            pltpu.SemaphoreType.DMA((n,)),
            pltpu.SemaphoreType.DMA((n,)),
            pltpu.SemaphoreType.DMA((n,)),
            pltpu.SemaphoreType.DMA((n,)),
        ],
        compiler_params=pltpu.CompilerParams(collective_id=collective_id, has_side_effects=True),
    )(x, y)


def _gram_of(a):
    return lax.dot_general(
        a, a, (((1,), (1,)), ((), ())), precision=lax.Precision.HIGH,
        preferred_element_type=jnp.float32,
    )


def chol_inverse(a):
    n = a.shape[0]
    r = lax.broadcasted_iota(jnp.int32, (n, n), 0)
    c = lax.broadcasted_iota(jnp.int32, (n, n), 1)
    r1 = lax.broadcasted_iota(jnp.int32, (n, 1), 0)
    c1 = lax.broadcasted_iota(jnp.int32, (1, n), 1)
    x0 = jnp.where(r == c, 1.0, 0.0).astype(jnp.float32)
    d0 = jnp.sum(jnp.where(r == c, a, 0.0), axis=0, keepdims=True)

    def step(j, carry):
        m, x, d = carry
        inv = lax.rsqrt(jnp.sum(jnp.where(c1 == j, d, 0.0), axis=1, keepdims=True))
        col = jnp.sum(jnp.where(c == j, m, 0.0), axis=1, keepdims=True)
        row = jnp.sum(jnp.where(r == j, m, 0.0), axis=0, keepdims=True)
        colm = jnp.where(r1 >= j, col, 0.0)
        rowm = jnp.where(c1 >= j, row, 0.0)
        inv2 = inv * inv
        m = m - (colm * rowm) * inv2
        d = d - (rowm * rowm) * inv2
        lcol = colm * inv
        xrow = jnp.sum(jnp.where(r == j, x, 0.0), axis=0, keepdims=True) * inv
        x = jnp.where(r == j, xrow, x)
        x = x - jnp.where(r1 > j, lcol, 0.0) * xrow
        return m, x, d

    m, x, d = lax.fori_loop(0, n, step, (a, x0, d0))
    return x


def _backward_kernel(n, m, scale, x_ref, icol_ref, o_ref, recv, gath, g3, panel, s1, r1, s2, r2, s3, r3):
    me = lax.axis_index("row")
    mc = lax.axis_index("col")
    barrier = pltpu.get_barrier_semaphore()
    for d in range(1, n):
        pl.semaphore_signal(barrier, 1, device_id=((me + d) % n, mc), device_id_type=MESH_ID)
    for d in range(1, m):
        pl.semaphore_signal(barrier, 1, device_id=(me, (mc + d) % m), device_id_type=MESH_ID)
    pl.semaphore_wait(barrier, n - 1 + m - 1)
    sends = []
    for d in range(1, n):
        peer = (me + d) % n
        c = pltpu.make_async_remote_copy(
            x_ref.at[peer], recv.at[d], s1.at[d], r1.at[d],
            device_id=(peer, mc), device_id_type=MESH_ID,
        )
        c.start()
        sends.append(c)
    acc = x_ref[me]
    for d, c in enumerate(sends, 1):
        c.wait()
        acc = acc + recv[d]
    gath[0] = acc * icol_ref[...]
    gathers = []
    for d in range(1, n):
        c = pltpu.make_async_remote_copy(
            gath.at[0], gath.at[d], s2.at[d], r2.at[d],
            device_id=((me + d) % n, mc), device_id_type=MESH_ID,
        )
        c.start()
        gathers.append(c)
    for c in gathers:
        c.wait()
    lanes = gath.shape[2]
    for p in range(n):
        panel[:, p * lanes:(p + 1) * lanes] = gath[(me - p + n) % n]
    g3[0] = _gram_of(panel[...])
    grams = []
    for d in range(1, m):
        c = pltpu.make_async_remote_copy(
            g3.at[0], g3.at[d], s3.at[d], r3.at[d],
            device_id=(me, (mc + d) % m), device_id_type=MESH_ID,
        )
        c.start()
        grams.append(c)
    for c in grams:
        c.wait()
    total = g3[mc % m]
    for q in range(1, m):
        total = total + g3[(mc - q + m) % m]
    inverse = chol_inverse(total * scale)
    rotated = lax.dot_general(
        inverse, panel[...], (((1,), (0,)), ((), ())),
        precision=lax.Precision.HIGH, preferred_element_type=jnp.float32,
    )
    for p in range(n):
        o_ref[p] = rotated[:, p * lanes:(p + 1) * lanes]


def backward_reduce(x, icol, n, m, scale, collective_id):
    chunks, vecs, lanes = x.shape
    return pl.pallas_call(
        functools.partial(_backward_kernel, n, m, scale),
        out_shape=jax.ShapeDtypeStruct(x.shape, jnp.float32),
        in_specs=[pl.BlockSpec(memory_space=pltpu.VMEM)] * 2,
        out_specs=pl.BlockSpec(memory_space=pltpu.VMEM),
        scratch_shapes=[
            pltpu.VMEM((n, vecs, lanes), jnp.float32),
            pltpu.VMEM((n, vecs, lanes), jnp.float32),
            pltpu.VMEM((m, vecs, vecs), jnp.float32),
            pltpu.VMEM((vecs, n * lanes), jnp.float32),
            pltpu.SemaphoreType.DMA((n,)),
            pltpu.SemaphoreType.DMA((n,)),
            pltpu.SemaphoreType.DMA((n,)),
            pltpu.SemaphoreType.DMA((n,)),
            pltpu.SemaphoreType.DMA((m,)),
            pltpu.SemaphoreType.DMA((m,)),
        ],
        compiler_params=pltpu.CompilerParams(collective_id=collective_id, has_side_effects=True),
    )(x, icol)


def all_reduce(x, axis, other, n, collective_id, two_phase=True):
    rows, lanes = x.shape
    ch = rows // n if two_phase else rows
    slots = ch if two_phase else rows
    return pl.pallas_call(
        functools.partial(_reduce_kernel, axis, other, n, ch, two_phase),
        out_shape=jax.ShapeDtypeStruct(x.shape, x.dtype),
        in_specs=[pl.BlockSpec(memory_space=pltpu.VMEM)],
        out_specs=pl.BlockSpec(memory_space=pltpu.VMEM),
        scratch_shapes=[
            pltpu.VMEM((n, slots, lanes), x.dtype),
            pltpu.VMEM((ch, lanes), x.dtype),
            pltpu.VMEM((n, ch, lanes), x.dtype),
            pltpu.SemaphoreType.DMA((n,)),
            pltpu.SemaphoreType.DMA((n,)),
            pltpu.SemaphoreType.DMA((n,)),
            pltpu.SemaphoreType.DMA((n,)),
        ],
        compiler_params=pltpu.CompilerParams(collective_id=collective_id, has_side_effects=True),
    )(x)


def rotate(projected, gram):
    lower = jnp.linalg.cholesky(gram)
    inverse = lax.linalg.triangular_solve(
        lower, jnp.eye(gram.shape[0], dtype=jnp.float32), left_side=True, lower=True
    )
    return jnp.einsum(
        "kl,bli->bki",
        inverse,
        projected,
        precision=lax.Precision.HIGHEST,
        preferred_element_type=jnp.float32,
    )


def rotate_pairs(projected, gram):
    lower = jnp.linalg.cholesky(gram)
    inverse = lax.linalg.triangular_solve(
        lower, jnp.eye(gram.shape[0], dtype=jnp.float32), left_side=True, lower=True
    )
    return jnp.einsum(
        "kl,plx->pkx",
        inverse,
        projected,
        precision=lax.Precision.HIGHEST,
        preferred_element_type=jnp.float32,
    )


def local_gram(projected):
    return jnp.einsum(
        "bki,bli->kl",
        projected,
        projected,
        precision=lax.Precision.HIGHEST,
        preferred_element_type=jnp.float32,
    )


def panel_sum(partial, axis, other, n, collective_id):
    blocks, vecs, bsize = partial.shape
    flat = partial.reshape(blocks * vecs * bsize // LANES, LANES)
    return all_reduce(flat, axis, other, n, collective_id).reshape(blocks, vecs, bsize)


def per_device(blocks, block_row, block_col, counts, vectors, row_mass, col_mass):
    tile = blocks[0, 0]
    n_cap = tile.shape[0]
    bsize = row_mass.shape[1]
    vecs = vectors.shape[1] // bsize
    own = vectors.shape[0]
    n_row = lax.axis_size("row")
    n_col = lax.axis_size("col")
    row_panel = own * n_col
    col_panel = own * n_row
    total_boxes = float(own * bsize * n_row * n_col)
    rows_idx = block_row[0, 0]
    cols_idx = block_col[0, 0]
    live = jnp.arange(n_cap) < counts[0, 0]
    fwd_ids = jnp.where(live, rows_idx, row_panel)
    bwd_ids = jnp.where(live, cols_idx, col_panel)
    square = tile.reshape(n_cap, bsize, bsize)
    vec_rows = own * vecs * bsize // LANES
    own_inv = 1.0 / jnp.sqrt(col_mass)
    first = (vectors.reshape(own, vecs, bsize) * own_inv[:, None, :]).astype(jnp.bfloat16)
    mass_pad = jnp.zeros((8, 128), jnp.float32).at[0, : own * bsize].set(col_mass.reshape(-1))
    got, mass_got = all_gather2(first.reshape(vec_rows, LANES), mass_pad, "row", "col", n_row, 4)
    first_panel = got.reshape(col_panel, vecs, bsize)
    col_mass_panel = mass_got.reshape(n_row, 8, 128)[:, 0, : own * bsize].reshape(col_panel, bsize)
    inv_col = 1.0 / jnp.sqrt(col_mass_panel)
    pairs = col_panel // 2
    inv_pairs = inv_col.reshape(pairs, 1, 2 * bsize)
    own_pair = jnp.broadcast_to(own_inv.reshape(1, own * bsize), (vecs, own * bsize))
    row_mass_spread = jnp.broadcast_to(row_mass[:, None, :], (own, vecs, bsize)).reshape(vec_rows, LANES)
    fwd_hot = (fwd_ids[None, :] == jnp.arange(row_panel)[:, None]).astype(jnp.bfloat16)
    bwd_hot = (bwd_ids[None, :] == jnp.arange(col_panel)[:, None]).astype(jnp.bfloat16)
    for step in range(ITERS):
        if step == 0:
            scaled = first_panel
        else:
            paired = (current * inv_pairs).astype(jnp.bfloat16)
            scaled = paired.reshape(pairs, vecs, 2, bsize).transpose(0, 2, 1, 3).reshape(col_panel, vecs, bsize)
        forward_taken = jnp.take(scaled, cols_idx, axis=0)
        forward_product = jnp.einsum(
            "bij,bkj->bki", square, forward_taken, preferred_element_type=jnp.bfloat16
        )
        forward_summed = jnp.einsum(
            "rs,ski->rki", fwd_hot, forward_product, preferred_element_type=jnp.float32
        )
        flat = forward_summed.reshape(row_panel * vecs * bsize // LANES, LANES)
        weighted = forward_reduce(flat, row_mass_spread, n_col, 1).reshape(row_panel, vecs, bsize)
        taken = jnp.take(weighted, rows_idx, axis=0)
        product = jnp.einsum("bij,bki->bkj", square, taken, preferred_element_type=jnp.bfloat16)
        summed = jnp.einsum(
            "pbs,skj->pkbj", bwd_hot.reshape(pairs, 2, n_cap), product,
            preferred_element_type=jnp.float32,
        ).reshape(pairs, vecs, 2 * bsize)
        current = backward_reduce(summed, own_pair, n_row, n_col, 1.0 / total_boxes, 2)
    me = lax.axis_index("row")
    mine = lax.dynamic_index_in_dim(current, me, 0, keepdims=False)
    return mine.reshape(vecs, own, bsize).transpose(1, 0, 2).reshape(own, vecs * bsize)


def solution(mesh):
    in_specs = (
        P("row", "col", None, None),
        P("row", "col", None),
        P("row", "col", None),
        P("row", "col"),
        P(("col", "row"), None),
        P(("row", "col"), None),
        P(("col", "row"), None),
    )
    out_specs = P(("col", "row"), None)
    return jax.shard_map(
        per_device, mesh=mesh, in_specs=in_specs, out_specs=out_specs, check_vma=False
    )
```

```python
import functools

import jax
import jax.numpy as jnp
from jax import lax
from jax.experimental import pallas as pl
from jax.experimental.pallas import tpu as pltpu
from jax.sharding import PartitionSpec as P

ITERS = 4
LANES = 512
MESH_ID = pl.DeviceIdType.MESH


def _peer(axis, other, p):
    them = lax.axis_index(other)
    return (p, them) if axis == "row" else (them, p)


def _reduce_kernel(axis, other, n, ch, two_phase, x_ref, o_ref, recv, mine, gath, s1, r1, s2, r2):
    me = lax.axis_index(axis)
    barrier = pltpu.get_barrier_semaphore()
    for d in range(1, n):
        pl.semaphore_signal(
            barrier, 1, device_id=_peer(axis, other, (me + d) % n), device_id_type=MESH_ID
        )
    pl.semaphore_wait(barrier, n - 1)
    if not two_phase:
        sends = []
        for d in range(1, n):
            c = pltpu.make_async_remote_copy(
                x_ref, recv.at[d], s1.at[d], r1.at[d],
                device_id=_peer(axis, other, (me + d) % n), device_id_type=MESH_ID,
            )
            c.start()
            sends.append(c)
        for c in sends:
            c.wait()
        recv[0] = x_ref[...]
        acc = recv[me % n]
        for p in range(1, n):
            acc = acc + recv[(me - p + n) % n]
        o_ref[...] = acc
        return
    sends = []
    for d in range(1, n):
        peer = (me + d) % n
        start = pl.multiple_of(peer * ch, ch)
        c = pltpu.make_async_remote_copy(
            x_ref.at[pl.ds(start, ch)], recv.at[d], s1.at[d], r1.at[d],
            device_id=_peer(axis, other, peer), device_id_type=MESH_ID,
        )
        c.start()
        sends.append(c)
    own = pl.multiple_of(me * ch, ch)
    acc = x_ref[pl.ds(own, ch), :]
    for d, c in enumerate(sends, 1):
        c.wait()
        acc = acc + recv[d]
    mine[...] = acc
    gathers = []
    for d in range(1, n):
        c = pltpu.make_async_remote_copy(
            mine, gath.at[d], s2.at[d], r2.at[d],
            device_id=_peer(axis, other, (me + d) % n), device_id_type=MESH_ID,
        )
        c.start()
        gathers.append(c)
    o_ref[pl.ds(own, ch), :] = acc
    for d, c in enumerate(gathers, 1):
        c.wait()
        src = pl.multiple_of(((me - d + n) % n) * ch, ch)
        o_ref[pl.ds(src, ch), :] = gath[d]


def _gather_kernel(axis, other, n, x_ref, o_ref, gath, s2, r2):
    me = lax.axis_index(axis)
    ch = x_ref.shape[0]
    barrier = pltpu.get_barrier_semaphore()
    for d in range(1, n):
        pl.semaphore_signal(
            barrier, 1, device_id=_peer(axis, other, (me + d) % n), device_id_type=MESH_ID
        )
    pl.semaphore_wait(barrier, n - 1)
    gathers = []
    for d in range(1, n):
        c = pltpu.make_async_remote_copy(
            x_ref, gath.at[d], s2.at[d], r2.at[d],
            device_id=_peer(axis, other, (me + d) % n), device_id_type=MESH_ID,
        )
        c.start()
        gathers.append(c)
    o_ref[pl.ds(pl.multiple_of(me * ch, ch), ch), :] = x_ref[...]
    for d, c in enumerate(gathers, 1):
        c.wait()
        src = pl.multiple_of(((me - d + n) % n) * ch, ch)
        o_ref[pl.ds(src, ch), :] = gath[d]


def all_gather(x, axis, other, n, collective_id):
    ch, lanes = x.shape
    return pl.pallas_call(
        functools.partial(_gather_kernel, axis, other, n),
        out_shape=jax.ShapeDtypeStruct((n * ch, lanes), x.dtype),
        in_specs=[pl.BlockSpec(memory_space=pltpu.VMEM)],
        out_specs=pl.BlockSpec(memory_space=pltpu.VMEM),
        scratch_shapes=[
            pltpu.VMEM((n, ch, lanes), x.dtype),
            pltpu.SemaphoreType.DMA((n,)),
            pltpu.SemaphoreType.DMA((n,)),
        ],
        compiler_params=pltpu.CompilerParams(collective_id=collective_id, has_side_effects=True),
    )(x)


def _forward_kernel(n, ch, x_ref, mass_ref, o_ref, recv, mine, gath, s1, r1, s2, r2):
    axis, other = "col", "row"
    me = lax.axis_index(axis)
    barrier = pltpu.get_barrier_semaphore()
    for d in range(1, n):
        pl.semaphore_signal(
            barrier, 1, device_id=_peer(axis, other, (me + d) % n), device_id_type=MESH_ID
        )
    pl.semaphore_wait(barrier, n - 1)
    sends = []
    for d in range(1, n):
        peer = (me + d) % n
        start = pl.multiple_of(peer * ch, ch)
        c = pltpu.make_async_remote_copy(
            x_ref.at[pl.ds(start, ch)], recv.at[d], s1.at[d], r1.at[d],
            device_id=_peer(axis, other, peer), device_id_type=MESH_ID,
        )
        c.start()
        sends.append(c)
    own = pl.multiple_of(me * ch, ch)
    acc = x_ref[pl.ds(own, ch), :]
    for d, c in enumerate(sends, 1):
        c.wait()
        acc = acc + recv[d]
    mine[...] = (acc * mass_ref[...]).astype(mine.dtype)
    gathers = []
    for d in range(1, n):
        c = pltpu.make_async_remote_copy(
            mine, gath.at[d], s2.at[d], r2.at[d],
            device_id=_peer(axis, other, (me + d) % n), device_id_type=MESH_ID,
        )
        c.start()
        gathers.append(c)
    o_ref[pl.ds(own, ch), :] = mine[...]
    for d, c in enumerate(gathers, 1):
        c.wait()
        src = pl.multiple_of(((me - d + n) % n) * ch, ch)
        o_ref[pl.ds(src, ch), :] = gath[d]


def forward_reduce(x, mass, n, collective_id):
    rows, lanes = x.shape
    ch = rows // n
    return pl.pallas_call(
        functools.partial(_forward_kernel, n, ch),
        out_shape=jax.ShapeDtypeStruct(x.shape, jnp.bfloat16),
        in_specs=[pl.BlockSpec(memory_space=pltpu.VMEM)] * 2,
        out_specs=pl.BlockSpec(memory_space=pltpu.VMEM),
        scratch_shapes=[
            pltpu.VMEM((n, ch, lanes), x.dtype),
            pltpu.VMEM((ch, lanes), jnp.bfloat16),
            pltpu.VMEM((n, ch, lanes), jnp.bfloat16),
            pltpu.SemaphoreType.DMA((n,)),
            pltpu.SemaphoreType.DMA((n,)),
            pltpu.SemaphoreType.DMA((n,)),
            pltpu.SemaphoreType.DMA((n,)),
        ],
        compiler_params=pltpu.CompilerParams(collective_id=collective_id, has_side_effects=True),
    )(x, mass)


def _gather2_kernel(axis, other, n, x_ref, y_ref, o_ref, p_ref, gx, gy, sx, rx, sy, ry):
    me = lax.axis_index(axis)
    cx = x_ref.shape[0]
    cy = y_ref.shape[0]
    barrier = pltpu.get_barrier_semaphore()
    for d in range(1, n):
        pl.semaphore_signal(
            barrier, 1, device_id=_peer(axis, other, (me + d) % n), device_id_type=MESH_ID
        )
    pl.semaphore_wait(barrier, n - 1)
    copies = []
    for d in range(1, n):
        peer = _peer(axis, other, (me + d) % n)
        a = pltpu.make_async_remote_copy(
            x_ref, gx.at[d], sx.at[d], rx.at[d], device_id=peer, device_id_type=MESH_ID
        )
        b = pltpu.make_async_remote_copy(
            y_ref, gy.at[d], sy.at[d], ry.at[d], device_id=peer, device_id_type=MESH_ID
        )
        a.start()
        b.start()
        copies.append((a, b))
    o_ref[pl.ds(pl.multiple_of(me * cx, cx), cx), :] = x_ref[...]
    p_ref[pl.ds(pl.multiple_of(me * cy, cy), cy), :] = y_ref[...]
    for d, (a, b) in enumerate(copies, 1):
        a.wait()
        b.wait()
        src = (me - d + n) % n
        o_ref[pl.ds(pl.multiple_of(src * cx, cx), cx), :] = gx[d]
        p_ref[pl.ds(pl.multiple_of(src * cy, cy), cy), :] = gy[d]


def all_gather2(x, y, axis, other, n, collective_id):
    return pl.pallas_call(
        functools.partial(_gather2_kernel, axis, other, n),
        out_shape=(
            jax.ShapeDtypeStruct((n * x.shape[0], x.shape[1]), x.dtype),
            jax.ShapeDtypeStruct((n * y.shape[0], y.shape[1]), y.dtype),
        ),
        in_specs=[pl.BlockSpec(memory_space=pltpu.VMEM)] * 2,
        out_specs=(pl.BlockSpec(memory_space=pltpu.VMEM),) * 2,
        scratch_shapes=[
            pltpu.VMEM((n,) + x.shape, x.dtype),
            pltpu.VMEM((n,) + y.shape, y.dtype),
            pltpu.SemaphoreType.DMA((n,)),
            pltpu.SemaphoreType.DMA((n,)),
            pltpu.SemaphoreType.DMA((n,)),
            pltpu.SemaphoreType.DMA((n,)),
        ],
        compiler_params=pltpu.CompilerParams(collective_id=collective_id, has_side_effects=True),
    )(x, y)


def _gram_of(a):
    return lax.dot_general(
        a, a, (((1,), (1,)), ((), ())), precision=lax.Precision.HIGH,
        preferred_element_type=jnp.float32,
    )


def chol_inverse(a):
    n = a.shape[0]
    r = lax.broadcasted_iota(jnp.int32, (n, n), 0)
    c = lax.broadcasted_iota(jnp.int32, (n, n), 1)
    r1 = lax.broadcasted_iota(jnp.int32, (n, 1), 0)
    c1 = lax.broadcasted_iota(jnp.int32, (1, n), 1)
    x0 = jnp.where(r == c, 1.0, 0.0).astype(jnp.float32)
    d0 = jnp.sum(jnp.where(r == c, a, 0.0), axis=0, keepdims=True)

    def step(j, carry):
        m, x, d = carry
        inv = lax.rsqrt(jnp.sum(jnp.where(c1 == j, d, 0.0), axis=1, keepdims=True))
        col = jnp.sum(jnp.where(c == j, m, 0.0), axis=1, keepdims=True)
        row = jnp.sum(jnp.where(r == j, m, 0.0), axis=0, keepdims=True)
        colm = jnp.where(r1 >= j, col, 0.0)
        rowm = jnp.where(c1 >= j, row, 0.0)
        inv2 = inv * inv
        m = m - (colm * rowm) * inv2
        d = d - (rowm * rowm) * inv2
        lcol = colm * inv
        xrow = jnp.sum(jnp.where(r == j, x, 0.0), axis=0, keepdims=True) * inv
        x = jnp.where(r == j, xrow, x)
        x = x - jnp.where(r1 > j, lcol, 0.0) * xrow
        return m, x, d

    m, x, d = lax.fori_loop(0, n, step, (a, x0, d0), unroll=2)
    return x


def _backward_kernel(n, m, scale, x_ref, icol_ref, o_ref, recv, gath, g3, panel, s1, r1, s2, r2, s3, r3):
    me = lax.axis_index("row")
    mc = lax.axis_index("col")
    barrier = pltpu.get_barrier_semaphore()
    for d in range(1, n):
        pl.semaphore_signal(barrier, 1, device_id=((me + d) % n, mc), device_id_type=MESH_ID)
    for d in range(1, m):
        pl.semaphore_signal(barrier, 1, device_id=(me, (mc + d) % m), device_id_type=MESH_ID)
    pl.semaphore_wait(barrier, n - 1 + m - 1)
    sends = []
    for d in range(1, n):
        peer = (me + d) % n
        c = pltpu.make_async_remote_copy(
            x_ref.at[peer], recv.at[d], s1.at[d], r1.at[d],
            device_id=(peer, mc), device_id_type=MESH_ID,
        )
        c.start()
        sends.append(c)
    acc = x_ref[me]
    for d, c in enumerate(sends, 1):
        c.wait()
        acc = acc + recv[d]
    gath[0] = acc * icol_ref[...]
    gathers = []
    for d in range(1, n):
        c = pltpu.make_async_remote_copy(
            gath.at[0], gath.at[d], s2.at[d], r2.at[d],
            device_id=((me + d) % n, mc), device_id_type=MESH_ID,
        )
        c.start()
        gathers.append(c)
    for c in gathers:
        c.wait()
    lanes = gath.shape[2]
    for p in range(n):
        panel[:, p * lanes:(p + 1) * lanes] = gath[(me - p + n) % n]
    g3[0] = _gram_of(panel[...])
    grams = []
    for d in range(1, m):
        c = pltpu.make_async_remote_copy(
            g3.at[0], g3.at[d], s3.at[d], r3.at[d],
            device_id=(me, (mc + d) % m), device_id_type=MESH_ID,
        )
        c.start()
        grams.append(c)
    for c in grams:
        c.wait()
    total = g3[mc % m]
    for q in range(1, m):
        total = total + g3[(mc - q + m) % m]
    inverse = chol_inverse(total * scale)
    rotated = lax.dot_general(
        inverse, panel[...], (((1,), (0,)), ((), ())),
        precision=lax.Precision.HIGH, preferred_element_type=jnp.float32,
    )
    for p in range(n):
        o_ref[p] = rotated[:, p * lanes:(p + 1) * lanes]


def backward_reduce(x, icol, n, m, scale, collective_id):
    chunks, vecs, lanes = x.shape
    return pl.pallas_call(
        functools.partial(_backward_kernel, n, m, scale),
        out_shape=jax.ShapeDtypeStruct(x.shape, jnp.float32),
        in_specs=[pl.BlockSpec(memory_space=pltpu.VMEM)] * 2,
        out_specs=pl.BlockSpec(memory_space=pltpu.VMEM),
        scratch_shapes=[
            pltpu.VMEM((n, vecs, lanes), jnp.float32),
            pltpu.VMEM((n, vecs, lanes), jnp.float32),
            pltpu.VMEM((m, vecs, vecs), jnp.float32),
            pltpu.VMEM((vecs, n * lanes), jnp.float32),
            pltpu.SemaphoreType.DMA((n,)),
            pltpu.SemaphoreType.DMA((n,)),
            pltpu.SemaphoreType.DMA((n,)),
            pltpu.SemaphoreType.DMA((n,)),
            pltpu.SemaphoreType.DMA((m,)),
            pltpu.SemaphoreType.DMA((m,)),
        ],
        compiler_params=pltpu.CompilerParams(collective_id=collective_id, has_side_effects=True),
    )(x, icol)


def all_reduce(x, axis, other, n, collective_id, two_phase=True):
    rows, lanes = x.shape
    ch = rows // n if two_phase else rows
    slots = ch if two_phase else rows
    return pl.pallas_call(
        functools.partial(_reduce_kernel, axis, other, n, ch, two_phase),
        out_shape=jax.ShapeDtypeStruct(x.shape, x.dtype),
        in_specs=[pl.BlockSpec(memory_space=pltpu.VMEM)],
        out_specs=pl.BlockSpec(memory_space=pltpu.VMEM),
        scratch_shapes=[
            pltpu.VMEM((n, slots, lanes), x.dtype),
            pltpu.VMEM((ch, lanes), x.dtype),
            pltpu.VMEM((n, ch, lanes), x.dtype),
            pltpu.SemaphoreType.DMA((n,)),
            pltpu.SemaphoreType.DMA((n,)),
            pltpu.SemaphoreType.DMA((n,)),
            pltpu.SemaphoreType.DMA((n,)),
        ],
        compiler_params=pltpu.CompilerParams(collective_id=collective_id, has_side_effects=True),
    )(x)


def rotate(projected, gram):
    lower = jnp.linalg.cholesky(gram)
    inverse = lax.linalg.triangular_solve(
        lower, jnp.eye(gram.shape[0], dtype=jnp.float32), left_side=True, lower=True
    )
    return jnp.einsum(
        "kl,bli->bki",
        inverse,
        projected,
        precision=lax.Precision.HIGHEST,
        preferred_element_type=jnp.float32,
    )


def rotate_pairs(projected, gram):
    lower = jnp.linalg.cholesky(gram)
    inverse = lax.linalg.triangular_solve(
        lower, jnp.eye(gram.shape[0], dtype=jnp.float32), left_side=True, lower=True
    )
    return jnp.einsum(
        "kl,plx->pkx",
        inverse,
        projected,
        precision=lax.Precision.HIGHEST,
        preferred_element_type=jnp.float32,
    )


def local_gram(projected):
    return jnp.einsum(
        "bki,bli->kl",
        projected,
        projected,
        precision=lax.Precision.HIGHEST,
        preferred_element_type=jnp.float32,
    )


def panel_sum(partial, axis, other, n, collective_id):
    blocks, vecs, bsize = partial.shape
    flat = partial.reshape(blocks * vecs * bsize // LANES, LANES)
    return all_reduce(flat, axis, other, n, collective_id).reshape(blocks, vecs, bsize)


def per_device(blocks, block_row, block_col, counts, vectors, row_mass, col_mass):
    tile = blocks[0, 0]
    n_cap = tile.shape[0]
    bsize = row_mass.shape[1]
    vecs = vectors.shape[1] // bsize
    own = vectors.shape[0]
    n_row = lax.axis_size("row")
    n_col = lax.axis_size("col")
    row_panel = own * n_col
    col_panel = own * n_row
    total_boxes = float(own * bsize * n_row * n_col)
    rows_idx = block_row[0, 0]
    cols_idx = block_col[0, 0]
    live = jnp.arange(n_cap) < counts[0, 0]
    fwd_ids = jnp.where(live, rows_idx, row_panel)
    bwd_ids = jnp.where(live, cols_idx, col_panel)
    square = tile.reshape(n_cap, bsize, bsize)
    vec_rows = own * vecs * bsize // LANES
    own_inv = 1.0 / jnp.sqrt(col_mass)
    first = (vectors.reshape(own, vecs, bsize) * own_inv[:, None, :]).astype(jnp.bfloat16)
    mass_pad = jnp.zeros((8, 128), jnp.float32).at[0, : own * bsize].set(col_mass.reshape(-1))
    got, mass_got = all_gather2(first.reshape(vec_rows, LANES), mass_pad, "row", "col", n_row, 4)
    first_panel = got.reshape(col_panel, vecs, bsize)
    col_mass_panel = mass_got.reshape(n_row, 8, 128)[:, 0, : own * bsize].reshape(col_panel, bsize)
    inv_col = 1.0 / jnp.sqrt(col_mass_panel)
    pairs = col_panel // 2
    inv_pairs = inv_col.reshape(pairs, 1, 2 * bsize)
    own_pair = jnp.broadcast_to(own_inv.reshape(1, own * bsize), (vecs, own * bsize))
    row_mass_spread = jnp.broadcast_to(row_mass[:, None, :], (own, vecs, bsize)).reshape(vec_rows, LANES)
    fwd_hot = (fwd_ids[None, :] == jnp.arange(row_panel)[:, None]).astype(jnp.bfloat16)
    bwd_hot = (bwd_ids[None, :] == jnp.arange(col_panel)[:, None]).astype(jnp.bfloat16)
    for step in range(ITERS):
        if step == 0:
            scaled = first_panel
        else:
            paired = (current * inv_pairs).astype(jnp.bfloat16)
            scaled = paired.reshape(pairs, vecs, 2, bsize).transpose(0, 2, 1, 3).reshape(col_panel, vecs, bsize)
        forward_taken = jnp.take(scaled, cols_idx, axis=0)
        forward_product = jnp.einsum(
            "bij,bkj->bki", square, forward_taken, preferred_element_type=jnp.bfloat16
        )
        forward_summed = jnp.einsum(
            "rs,ski->rki", fwd_hot, forward_product, preferred_element_type=jnp.float32
        )
        flat = forward_summed.reshape(row_panel * vecs * bsize // LANES, LANES)
        weighted = forward_reduce(flat, row_mass_spread, n_col, 1).reshape(row_panel, vecs, bsize)
        taken = jnp.take(weighted, rows_idx, axis=0)
        product = jnp.einsum("bij,bki->bkj", square, taken, preferred_element_type=jnp.bfloat16)
        summed = jnp.einsum(
            "pbs,skj->pkbj", bwd_hot.reshape(pairs, 2, n_cap), product,
            preferred_element_type=jnp.float32,
        ).reshape(pairs, vecs, 2 * bsize)
        current = backward_reduce(summed, own_pair, n_row, n_col, 1.0 / total_boxes, 2)
    me = lax.axis_index("row")
    mine = lax.dynamic_index_in_dim(current, me, 0, keepdims=False)
    return mine.reshape(vecs, own, bsize).transpose(1, 0, 2).reshape(own, vecs * bsize)


def solution(mesh):
    in_specs = (
        P("row", "col", None, None),
        P("row", "col", None),
        P("row", "col", None),
        P("row", "col"),
        P(("col", "row"), None),
        P(("row", "col"), None),
        P(("col", "row"), None),
    )
    out_specs = P(("col", "row"), None)
    return jax.shard_map(
        per_device, mesh=mesh, in_specs=in_specs, out_specs=out_specs, check_vma=False
    )
```

```python
import functools

import jax
import jax.numpy as jnp
from jax import lax
from jax.experimental import pallas as pl
from jax.experimental.pallas import tpu as pltpu
from jax.sharding import PartitionSpec as P

ITERS = 4
LANES = 512
MESH_ID = pl.DeviceIdType.MESH


def _peer(axis, other, p):
    them = lax.axis_index(other)
    return (p, them) if axis == "row" else (them, p)


def _reduce_kernel(axis, other, n, ch, two_phase, x_ref, o_ref, recv, mine, gath, s1, r1, s2, r2):
    me = lax.axis_index(axis)
    barrier = pltpu.get_barrier_semaphore()
    for d in range(1, n):
        pl.semaphore_signal(
            barrier, 1, device_id=_peer(axis, other, (me + d) % n), device_id_type=MESH_ID
        )
    pl.semaphore_wait(barrier, n - 1)
    if not two_phase:
        sends = []
        for d in range(1, n):
            c = pltpu.make_async_remote_copy(
                x_ref, recv.at[d], s1.at[d], r1.at[d],
                device_id=_peer(axis, other, (me + d) % n), device_id_type=MESH_ID,
            )
            c.start()
            sends.append(c)
        for c in sends:
            c.wait()
        recv[0] = x_ref[...]
        acc = recv[me % n]
        for p in range(1, n):
            acc = acc + recv[(me - p + n) % n]
        o_ref[...] = acc
        return
    sends = []
    for d in range(1, n):
        peer = (me + d) % n
        start = pl.multiple_of(peer * ch, ch)
        c = pltpu.make_async_remote_copy(
            x_ref.at[pl.ds(start, ch)], recv.at[d], s1.at[d], r1.at[d],
            device_id=_peer(axis, other, peer), device_id_type=MESH_ID,
        )
        c.start()
        sends.append(c)
    own = pl.multiple_of(me * ch, ch)
    acc = x_ref[pl.ds(own, ch), :]
    for d, c in enumerate(sends, 1):
        c.wait()
        acc = acc + recv[d]
    mine[...] = acc
    gathers = []
    for d in range(1, n):
        c = pltpu.make_async_remote_copy(
            mine, gath.at[d], s2.at[d], r2.at[d],
            device_id=_peer(axis, other, (me + d) % n), device_id_type=MESH_ID,
        )
        c.start()
        gathers.append(c)
    o_ref[pl.ds(own, ch), :] = acc
    for d, c in enumerate(gathers, 1):
        c.wait()
        src = pl.multiple_of(((me - d + n) % n) * ch, ch)
        o_ref[pl.ds(src, ch), :] = gath[d]


def _gather_kernel(axis, other, n, x_ref, o_ref, gath, s2, r2):
    me = lax.axis_index(axis)
    ch = x_ref.shape[0]
    barrier = pltpu.get_barrier_semaphore()
    for d in range(1, n):
        pl.semaphore_signal(
            barrier, 1, device_id=_peer(axis, other, (me + d) % n), device_id_type=MESH_ID
        )
    pl.semaphore_wait(barrier, n - 1)
    gathers = []
    for d in range(1, n):
        c = pltpu.make_async_remote_copy(
            x_ref, gath.at[d], s2.at[d], r2.at[d],
            device_id=_peer(axis, other, (me + d) % n), device_id_type=MESH_ID,
        )
        c.start()
        gathers.append(c)
    o_ref[pl.ds(pl.multiple_of(me * ch, ch), ch), :] = x_ref[...]
    for d, c in enumerate(gathers, 1):
        c.wait()
        src = pl.multiple_of(((me - d + n) % n) * ch, ch)
        o_ref[pl.ds(src, ch), :] = gath[d]


def all_gather(x, axis, other, n, collective_id):
    ch, lanes = x.shape
    return pl.pallas_call(
        functools.partial(_gather_kernel, axis, other, n),
        out_shape=jax.ShapeDtypeStruct((n * ch, lanes), x.dtype),
        in_specs=[pl.BlockSpec(memory_space=pltpu.VMEM)],
        out_specs=pl.BlockSpec(memory_space=pltpu.VMEM),
        scratch_shapes=[
            pltpu.VMEM((n, ch, lanes), x.dtype),
            pltpu.SemaphoreType.DMA((n,)),
            pltpu.SemaphoreType.DMA((n,)),
        ],
        compiler_params=pltpu.CompilerParams(collective_id=collective_id, has_side_effects=True),
    )(x)


def _forward_kernel(n, ch, x_ref, mass_ref, o_ref, recv, mine, gath, s1, r1, s2, r2):
    axis, other = "col", "row"
    me = lax.axis_index(axis)
    barrier = pltpu.get_barrier_semaphore()
    for d in range(1, n):
        pl.semaphore_signal(
            barrier, 1, device_id=_peer(axis, other, (me + d) % n), device_id_type=MESH_ID
        )
    pl.semaphore_wait(barrier, n - 1)
    sends = []
    for d in range(1, n):
        peer = (me + d) % n
        start = pl.multiple_of(peer * ch, ch)
        c = pltpu.make_async_remote_copy(
            x_ref.at[pl.ds(start, ch)], recv.at[d], s1.at[d], r1.at[d],
            device_id=_peer(axis, other, peer), device_id_type=MESH_ID,
        )
        c.start()
        sends.append(c)
    own = pl.multiple_of(me * ch, ch)
    acc = x_ref[pl.ds(own, ch), :]
    for d, c in enumerate(sends, 1):
        c.wait()
        acc = acc + recv[d]
    mine[...] = (acc * mass_ref[...]).astype(mine.dtype)
    gathers = []
    for d in range(1, n):
        c = pltpu.make_async_remote_copy(
            mine, gath.at[d], s2.at[d], r2.at[d],
            device_id=_peer(axis, other, (me + d) % n), device_id_type=MESH_ID,
        )
        c.start()
        gathers.append(c)
    o_ref[pl.ds(own, ch), :] = mine[...]
    for d, c in enumerate(gathers, 1):
        c.wait()
        src = pl.multiple_of(((me - d + n) % n) * ch, ch)
        o_ref[pl.ds(src, ch), :] = gath[d]


def forward_reduce(x, mass, n, collective_id):
    rows, lanes = x.shape
    ch = rows // n
    return pl.pallas_call(
        functools.partial(_forward_kernel, n, ch),
        out_shape=jax.ShapeDtypeStruct(x.shape, jnp.bfloat16),
        in_specs=[pl.BlockSpec(memory_space=pltpu.VMEM)] * 2,
        out_specs=pl.BlockSpec(memory_space=pltpu.VMEM),
        scratch_shapes=[
            pltpu.VMEM((n, ch, lanes), x.dtype),
            pltpu.VMEM((ch, lanes), jnp.bfloat16),
            pltpu.VMEM((n, ch, lanes), jnp.bfloat16),
            pltpu.SemaphoreType.DMA((n,)),
            pltpu.SemaphoreType.DMA((n,)),
            pltpu.SemaphoreType.DMA((n,)),
            pltpu.SemaphoreType.DMA((n,)),
        ],
        compiler_params=pltpu.CompilerParams(collective_id=collective_id, has_side_effects=True),
    )(x, mass)


def _gather2_kernel(axis, other, n, x_ref, y_ref, o_ref, p_ref, gx, gy, sx, rx, sy, ry):
    me = lax.axis_index(axis)
    cx = x_ref.shape[0]
    cy = y_ref.shape[0]
    barrier = pltpu.get_barrier_semaphore()
    for d in range(1, n):
        pl.semaphore_signal(
            barrier, 1, device_id=_peer(axis, other, (me + d) % n), device_id_type=MESH_ID
        )
    pl.semaphore_wait(barrier, n - 1)
    copies = []
    for d in range(1, n):
        peer = _peer(axis, other, (me + d) % n)
        a = pltpu.make_async_remote_copy(
            x_ref, gx.at[d], sx.at[d], rx.at[d], device_id=peer, device_id_type=MESH_ID
        )
        b = pltpu.make_async_remote_copy(
            y_ref, gy.at[d], sy.at[d], ry.at[d], device_id=peer, device_id_type=MESH_ID
        )
        a.start()
        b.start()
        copies.append((a, b))
    o_ref[pl.ds(pl.multiple_of(me * cx, cx), cx), :] = x_ref[...]
    p_ref[pl.ds(pl.multiple_of(me * cy, cy), cy), :] = y_ref[...]
    for d, (a, b) in enumerate(copies, 1):
        a.wait()
        b.wait()
        src = (me - d + n) % n
        o_ref[pl.ds(pl.multiple_of(src * cx, cx), cx), :] = gx[d]
        p_ref[pl.ds(pl.multiple_of(src * cy, cy), cy), :] = gy[d]


def all_gather2(x, y, axis, other, n, collective_id):
    return pl.pallas_call(
        functools.partial(_gather2_kernel, axis, other, n),
        out_shape=(
            jax.ShapeDtypeStruct((n * x.shape[0], x.shape[1]), x.dtype),
            jax.ShapeDtypeStruct((n * y.shape[0], y.shape[1]), y.dtype),
        ),
        in_specs=[pl.BlockSpec(memory_space=pltpu.VMEM)] * 2,
        out_specs=(pl.BlockSpec(memory_space=pltpu.VMEM),) * 2,
        scratch_shapes=[
            pltpu.VMEM((n,) + x.shape, x.dtype),
            pltpu.VMEM((n,) + y.shape, y.dtype),
            pltpu.SemaphoreType.DMA((n,)),
            pltpu.SemaphoreType.DMA((n,)),
            pltpu.SemaphoreType.DMA((n,)),
            pltpu.SemaphoreType.DMA((n,)),
        ],
        compiler_params=pltpu.CompilerParams(collective_id=collective_id, has_side_effects=True),
    )(x, y)


def _gram_of(a):
    return lax.dot_general(
        a, a, (((1,), (1,)), ((), ())), precision=lax.Precision.HIGH,
        preferred_element_type=jnp.float32,
    )


def chol_inverse(a):
    n = a.shape[0]
    r = lax.broadcasted_iota(jnp.int32, (n, n), 0)
    c = lax.broadcasted_iota(jnp.int32, (n, n), 1)
    r1 = lax.broadcasted_iota(jnp.int32, (n, 1), 0)
    c1 = lax.broadcasted_iota(jnp.int32, (1, n), 1)
    x0 = jnp.where(r == c, 1.0, 0.0).astype(jnp.float32)
    d0 = jnp.sum(jnp.where(r == c, a, 0.0), axis=0, keepdims=True)

    def step(j, carry):
        m, x, d = carry
        inv = lax.rsqrt(jnp.sum(jnp.where(c1 == j, d, 0.0), axis=1, keepdims=True))
        col = jnp.sum(jnp.where(c == j, m, 0.0), axis=1, keepdims=True)
        row = jnp.sum(jnp.where(r == j, m, 0.0), axis=0, keepdims=True)
        colm = jnp.where(r1 >= j, col, 0.0)
        rowm = jnp.where(c1 >= j, row, 0.0)
        inv2 = inv * inv
        m = m - (colm * rowm) * inv2
        d = d - (rowm * rowm) * inv2
        xraw = jnp.sum(jnp.where(r == j, x, 0.0), axis=0, keepdims=True)
        x = jnp.where(r == j, xraw * inv, x)
        x = x - (jnp.where(r1 > j, col, 0.0) * xraw) * inv2
        return m, x, d

    m, x, d = lax.fori_loop(0, n, step, (a, x0, d0))
    return x


def _backward_kernel(n, m, scale, x_ref, icol_ref, o_ref, recv, gath, g3, panel, s1, r1, s2, r2, s3, r3):
    me = lax.axis_index("row")
    mc = lax.axis_index("col")
    barrier = pltpu.get_barrier_semaphore()
    for d in range(1, n):
        pl.semaphore_signal(barrier, 1, device_id=((me + d) % n, mc), device_id_type=MESH_ID)
    for d in range(1, m):
        pl.semaphore_signal(barrier, 1, device_id=(me, (mc + d) % m), device_id_type=MESH_ID)
    pl.semaphore_wait(barrier, n - 1 + m - 1)
    sends = []
    for d in range(1, n):
        peer = (me + d) % n
        c = pltpu.make_async_remote_copy(
            x_ref.at[peer], recv.at[d], s1.at[d], r1.at[d],
            device_id=(peer, mc), device_id_type=MESH_ID,
        )
        c.start()
        sends.append(c)
    acc = x_ref[me]
    for d, c in enumerate(sends, 1):
        c.wait()
        acc = acc + recv[d]
    gath[0] = acc * icol_ref[...]
    gathers = []
    for d in range(1, n):
        c = pltpu.make_async_remote_copy(
            gath.at[0], gath.at[d], s2.at[d], r2.at[d],
            device_id=((me + d) % n, mc), device_id_type=MESH_ID,
        )
        c.start()
        gathers.append(c)
    for c in gathers:
        c.wait()
    lanes = gath.shape[2]
    for p in range(n):
        panel[:, p * lanes:(p + 1) * lanes] = gath[(me - p + n) % n]
    g3[0] = _gram_of(panel[...])
    grams = []
    for d in range(1, m):
        c = pltpu.make_async_remote_copy(
            g3.at[0], g3.at[d], s3.at[d], r3.at[d],
            device_id=(me, (mc + d) % m), device_id_type=MESH_ID,
        )
        c.start()
        grams.append(c)
    for c in grams:
        c.wait()
    total = g3[mc % m]
    for q in range(1, m):
        total = total + g3[(mc - q + m) % m]
    inverse = chol_inverse(total * scale)
    rotated = lax.dot_general(
        inverse, panel[...], (((1,), (0,)), ((), ())),
        precision=lax.Precision.HIGH, preferred_element_type=jnp.float32,
    )
    for p in range(n):
        o_ref[p] = rotated[:, p * lanes:(p + 1) * lanes]


def backward_reduce(x, icol, n, m, scale, collective_id):
    chunks, vecs, lanes = x.shape
    return pl.pallas_call(
        functools.partial(_backward_kernel, n, m, scale),
        out_shape=jax.ShapeDtypeStruct(x.shape, jnp.float32),
        in_specs=[pl.BlockSpec(memory_space=pltpu.VMEM)] * 2,
        out_specs=pl.BlockSpec(memory_space=pltpu.VMEM),
        scratch_shapes=[
            pltpu.VMEM((n, vecs, lanes), jnp.float32),
            pltpu.VMEM((n, vecs, lanes), jnp.float32),
            pltpu.VMEM((m, vecs, vecs), jnp.float32),
            pltpu.VMEM((vecs, n * lanes), jnp.float32),
            pltpu.SemaphoreType.DMA((n,)),
            pltpu.SemaphoreType.DMA((n,)),
            pltpu.SemaphoreType.DMA((n,)),
            pltpu.SemaphoreType.DMA((n,)),
            pltpu.SemaphoreType.DMA((m,)),
            pltpu.SemaphoreType.DMA((m,)),
        ],
        compiler_params=pltpu.CompilerParams(collective_id=collective_id, has_side_effects=True),
    )(x, icol)


def all_reduce(x, axis, other, n, collective_id, two_phase=True):
    rows, lanes = x.shape
    ch = rows // n if two_phase else rows
    slots = ch if two_phase else rows
    return pl.pallas_call(
        functools.partial(_reduce_kernel, axis, other, n, ch, two_phase),
        out_shape=jax.ShapeDtypeStruct(x.shape, x.dtype),
        in_specs=[pl.BlockSpec(memory_space=pltpu.VMEM)],
        out_specs=pl.BlockSpec(memory_space=pltpu.VMEM),
        scratch_shapes=[
            pltpu.VMEM((n, slots, lanes), x.dtype),
            pltpu.VMEM((ch, lanes), x.dtype),
            pltpu.VMEM((n, ch, lanes), x.dtype),
            pltpu.SemaphoreType.DMA((n,)),
            pltpu.SemaphoreType.DMA((n,)),
            pltpu.SemaphoreType.DMA((n,)),
            pltpu.SemaphoreType.DMA((n,)),
        ],
        compiler_params=pltpu.CompilerParams(collective_id=collective_id, has_side_effects=True),
    )(x)


def rotate(projected, gram):
    lower = jnp.linalg.cholesky(gram)
    inverse = lax.linalg.triangular_solve(
        lower, jnp.eye(gram.shape[0], dtype=jnp.float32), left_side=True, lower=True
    )
    return jnp.einsum(
        "kl,bli->bki",
        inverse,
        projected,
        precision=lax.Precision.HIGHEST,
        preferred_element_type=jnp.float32,
    )


def rotate_pairs(projected, gram):
    lower = jnp.linalg.cholesky(gram)
    inverse = lax.linalg.triangular_solve(
        lower, jnp.eye(gram.shape[0], dtype=jnp.float32), left_side=True, lower=True
    )
    return jnp.einsum(
        "kl,plx->pkx",
        inverse,
        projected,
        precision=lax.Precision.HIGHEST,
        preferred_element_type=jnp.float32,
    )


def local_gram(projected):
    return jnp.einsum(
        "bki,bli->kl",
        projected,
        projected,
        precision=lax.Precision.HIGHEST,
        preferred_element_type=jnp.float32,
    )


def panel_sum(partial, axis, other, n, collective_id):
    blocks, vecs, bsize = partial.shape
    flat = partial.reshape(blocks * vecs * bsize // LANES, LANES)
    return all_reduce(flat, axis, other, n, collective_id).reshape(blocks, vecs, bsize)


def per_device(blocks, block_row, block_col, counts, vectors, row_mass, col_mass):
    tile = blocks[0, 0]
    n_cap = tile.shape[0]
    bsize = row_mass.shape[1]
    vecs = vectors.shape[1] // bsize
    own = vectors.shape[0]
    n_row = lax.axis_size("row")
    n_col = lax.axis_size("col")
    row_panel = own * n_col
    col_panel = own * n_row
    total_boxes = float(own * bsize * n_row * n_col)
    rows_idx = block_row[0, 0]
    cols_idx = block_col[0, 0]
    live = jnp.arange(n_cap) < counts[0, 0]
    fwd_ids = jnp.where(live, rows_idx, row_panel)
    bwd_ids = jnp.where(live, cols_idx, col_panel)
    square = tile.reshape(n_cap, bsize, bsize)
    vec_rows = own * vecs * bsize // LANES
    own_inv = 1.0 / jnp.sqrt(col_mass)
    first = (vectors.reshape(own, vecs, bsize) * own_inv[:, None, :]).astype(jnp.bfloat16)
    mass_pad = jnp.zeros((8, 128), jnp.float32).at[0, : own * bsize].set(col_mass.reshape(-1))
    got, mass_got = all_gather2(first.reshape(vec_rows, LANES), mass_pad, "row", "col", n_row, 4)
    first_panel = got.reshape(col_panel, vecs, bsize)
    col_mass_panel = mass_got.reshape(n_row, 8, 128)[:, 0, : own * bsize].reshape(col_panel, bsize)
    inv_col = 1.0 / jnp.sqrt(col_mass_panel)
    pairs = col_panel // 2
    inv_pairs = inv_col.reshape(pairs, 1, 2 * bsize)
    own_pair = jnp.broadcast_to(own_inv.reshape(1, own * bsize), (vecs, own * bsize))
    row_mass_spread = jnp.broadcast_to(row_mass[:, None, :], (own, vecs, bsize)).reshape(vec_rows, LANES)
    fwd_hot = (fwd_ids[None, :] == jnp.arange(row_panel)[:, None]).astype(jnp.bfloat16)
    bwd_hot = (bwd_ids[None, :] == jnp.arange(col_panel)[:, None]).astype(jnp.bfloat16)
    for step in range(ITERS):
        if step == 0:
            scaled = first_panel
        else:
            paired = (current * inv_pairs).astype(jnp.bfloat16)
            scaled = paired.reshape(pairs, vecs, 2, bsize).transpose(0, 2, 1, 3).reshape(col_panel, vecs, bsize)
        forward_taken = jnp.take(scaled, cols_idx, axis=0)
        forward_product = jnp.einsum(
            "bij,bkj->bki", square, forward_taken, preferred_element_type=jnp.bfloat16
        )
        forward_summed = jnp.einsum(
            "rs,ski->rki", fwd_hot, forward_product, preferred_element_type=jnp.float32
        )
        flat = forward_summed.reshape(row_panel * vecs * bsize // LANES, LANES)
        weighted = forward_reduce(flat, row_mass_spread, n_col, 1).reshape(row_panel, vecs, bsize)
        taken = jnp.take(weighted, rows_idx, axis=0)
        product = jnp.einsum("bij,bki->bkj", square, taken, preferred_element_type=jnp.bfloat16)
        summed = jnp.einsum(
            "pbs,skj->pkbj", bwd_hot.reshape(pairs, 2, n_cap), product,
            preferred_element_type=jnp.float32,
        ).reshape(pairs, vecs, 2 * bsize)
        current = backward_reduce(summed, own_pair, n_row, n_col, 1.0 / total_boxes, 2)
    me = lax.axis_index("row")
    mine = lax.dynamic_index_in_dim(current, me, 0, keepdims=False)
    return mine.reshape(vecs, own, bsize).transpose(1, 0, 2).reshape(own, vecs * bsize)


def solution(mesh):
    in_specs = (
        P("row", "col", None, None),
        P("row", "col", None),
        P("row", "col", None),
        P("row", "col"),
        P(("col", "row"), None),
        P(("row", "col"), None),
        P(("col", "row"), None),
    )
    out_specs = P(("col", "row"), None)
    return jax.shard_map(
        per_device, mesh=mesh, in_specs=in_specs, out_specs=out_specs, check_vma=False
    )
```

```python
import functools

import jax
import jax.numpy as jnp
from jax import lax
from jax.experimental import pallas as pl
from jax.experimental.pallas import tpu as pltpu
from jax.sharding import PartitionSpec as P

ITERS = 4
LANES = 512
MESH_ID = pl.DeviceIdType.MESH


def _peer(axis, other, p):
    them = lax.axis_index(other)
    return (p, them) if axis == "row" else (them, p)


def _reduce_kernel(axis, other, n, ch, two_phase, x_ref, o_ref, recv, mine, gath, s1, r1, s2, r2):
    me = lax.axis_index(axis)
    barrier = pltpu.get_barrier_semaphore()
    for d in range(1, n):
        pl.semaphore_signal(
            barrier, 1, device_id=_peer(axis, other, (me + d) % n), device_id_type=MESH_ID
        )
    pl.semaphore_wait(barrier, n - 1)
    if not two_phase:
        sends = []
        for d in range(1, n):
            c = pltpu.make_async_remote_copy(
                x_ref, recv.at[d], s1.at[d], r1.at[d],
                device_id=_peer(axis, other, (me + d) % n), device_id_type=MESH_ID,
            )
            c.start()
            sends.append(c)
        for c in sends:
            c.wait()
        recv[0] = x_ref[...]
        acc = recv[me % n]
        for p in range(1, n):
            acc = acc + recv[(me - p + n) % n]
        o_ref[...] = acc
        return
    sends = []
    for d in range(1, n):
        peer = (me + d) % n
        start = pl.multiple_of(peer * ch, ch)
        c = pltpu.make_async_remote_copy(
            x_ref.at[pl.ds(start, ch)], recv.at[d], s1.at[d], r1.at[d],
            device_id=_peer(axis, other, peer), device_id_type=MESH_ID,
        )
        c.start()
        sends.append(c)
    own = pl.multiple_of(me * ch, ch)
    acc = x_ref[pl.ds(own, ch), :]
    for d, c in enumerate(sends, 1):
        c.wait()
        acc = acc + recv[d]
    mine[...] = acc
    gathers = []
    for d in range(1, n):
        c = pltpu.make_async_remote_copy(
            mine, gath.at[d], s2.at[d], r2.at[d],
            device_id=_peer(axis, other, (me + d) % n), device_id_type=MESH_ID,
        )
        c.start()
        gathers.append(c)
    o_ref[pl.ds(own, ch), :] = acc
    for d, c in enumerate(gathers, 1):
        c.wait()
        src = pl.multiple_of(((me - d + n) % n) * ch, ch)
        o_ref[pl.ds(src, ch), :] = gath[d]


def _gather_kernel(axis, other, n, x_ref, o_ref, gath, s2, r2):
    me = lax.axis_index(axis)
    ch = x_ref.shape[0]
    barrier = pltpu.get_barrier_semaphore()
    for d in range(1, n):
        pl.semaphore_signal(
            barrier, 1, device_id=_peer(axis, other, (me + d) % n), device_id_type=MESH_ID
        )
    pl.semaphore_wait(barrier, n - 1)
    gathers = []
    for d in range(1, n):
        c = pltpu.make_async_remote_copy(
            x_ref, gath.at[d], s2.at[d], r2.at[d],
            device_id=_peer(axis, other, (me + d) % n), device_id_type=MESH_ID,
        )
        c.start()
        gathers.append(c)
    o_ref[pl.ds(pl.multiple_of(me * ch, ch), ch), :] = x_ref[...]
    for d, c in enumerate(gathers, 1):
        c.wait()
        src = pl.multiple_of(((me - d + n) % n) * ch, ch)
        o_ref[pl.ds(src, ch), :] = gath[d]


def all_gather(x, axis, other, n, collective_id):
    ch, lanes = x.shape
    return pl.pallas_call(
        functools.partial(_gather_kernel, axis, other, n),
        out_shape=jax.ShapeDtypeStruct((n * ch, lanes), x.dtype),
        in_specs=[pl.BlockSpec(memory_space=pltpu.VMEM)],
        out_specs=pl.BlockSpec(memory_space=pltpu.VMEM),
        scratch_shapes=[
            pltpu.VMEM((n, ch, lanes), x.dtype),
            pltpu.SemaphoreType.DMA((n,)),
            pltpu.SemaphoreType.DMA((n,)),
        ],
        compiler_params=pltpu.CompilerParams(collective_id=collective_id, has_side_effects=True),
    )(x)


def _forward_kernel(n, ch, x_ref, mass_ref, o_ref, recv, mine, gath, s1, r1, s2, r2):
    axis, other = "col", "row"
    me = lax.axis_index(axis)
    barrier = pltpu.get_barrier_semaphore()
    for d in range(1, n):
        pl.semaphore_signal(
            barrier, 1, device_id=_peer(axis, other, (me + d) % n), device_id_type=MESH_ID
        )
    pl.semaphore_wait(barrier, n - 1)
    sends = []
    for d in range(1, n):
        peer = (me + d) % n
        start = pl.multiple_of(peer * ch, ch)
        c = pltpu.make_async_remote_copy(
            x_ref.at[pl.ds(start, ch)], recv.at[d], s1.at[d], r1.at[d],
            device_id=_peer(axis, other, peer), device_id_type=MESH_ID,
        )
        c.start()
        sends.append(c)
    own = pl.multiple_of(me * ch, ch)
    acc = x_ref[pl.ds(own, ch), :]
    for d, c in enumerate(sends, 1):
        c.wait()
        acc = acc + recv[d]
    mine[...] = (acc * mass_ref[...]).astype(mine.dtype)
    gathers = []
    for d in range(1, n):
        c = pltpu.make_async_remote_copy(
            mine, gath.at[d], s2.at[d], r2.at[d],
            device_id=_peer(axis, other, (me + d) % n), device_id_type=MESH_ID,
        )
        c.start()
        gathers.append(c)
    o_ref[pl.ds(own, ch), :] = mine[...]
    for d, c in enumerate(gathers, 1):
        c.wait()
        src = pl.multiple_of(((me - d + n) % n) * ch, ch)
        o_ref[pl.ds(src, ch), :] = gath[d]


def forward_reduce(x, mass, n, collective_id):
    rows, lanes = x.shape
    ch = rows // n
    return pl.pallas_call(
        functools.partial(_forward_kernel, n, ch),
        out_shape=jax.ShapeDtypeStruct(x.shape, jnp.bfloat16),
        in_specs=[pl.BlockSpec(memory_space=pltpu.VMEM)] * 2,
        out_specs=pl.BlockSpec(memory_space=pltpu.VMEM),
        scratch_shapes=[
            pltpu.VMEM((n, ch, lanes), x.dtype),
            pltpu.VMEM((ch, lanes), jnp.bfloat16),
            pltpu.VMEM((n, ch, lanes), jnp.bfloat16),
            pltpu.SemaphoreType.DMA((n,)),
            pltpu.SemaphoreType.DMA((n,)),
            pltpu.SemaphoreType.DMA((n,)),
            pltpu.SemaphoreType.DMA((n,)),
        ],
        compiler_params=pltpu.CompilerParams(collective_id=collective_id, has_side_effects=True),
    )(x, mass)


def _gather2_kernel(axis, other, n, x_ref, y_ref, o_ref, p_ref, gx, gy, sx, rx, sy, ry):
    me = lax.axis_index(axis)
    cx = x_ref.shape[0]
    cy = y_ref.shape[0]
    barrier = pltpu.get_barrier_semaphore()
    for d in range(1, n):
        pl.semaphore_signal(
            barrier, 1, device_id=_peer(axis, other, (me + d) % n), device_id_type=MESH_ID
        )
    pl.semaphore_wait(barrier, n - 1)
    copies = []
    for d in range(1, n):
        peer = _peer(axis, other, (me + d) % n)
        a = pltpu.make_async_remote_copy(
            x_ref, gx.at[d], sx.at[d], rx.at[d], device_id=peer, device_id_type=MESH_ID
        )
        b = pltpu.make_async_remote_copy(
            y_ref, gy.at[d], sy.at[d], ry.at[d], device_id=peer, device_id_type=MESH_ID
        )
        a.start()
        b.start()
        copies.append((a, b))
    o_ref[pl.ds(pl.multiple_of(me * cx, cx), cx), :] = x_ref[...]
    p_ref[pl.ds(pl.multiple_of(me * cy, cy), cy), :] = y_ref[...]
    for d, (a, b) in enumerate(copies, 1):
        a.wait()
        b.wait()
        src = (me - d + n) % n
        o_ref[pl.ds(pl.multiple_of(src * cx, cx), cx), :] = gx[d]
        p_ref[pl.ds(pl.multiple_of(src * cy, cy), cy), :] = gy[d]


def all_gather2(x, y, axis, other, n, collective_id):
    return pl.pallas_call(
        functools.partial(_gather2_kernel, axis, other, n),
        out_shape=(
            jax.ShapeDtypeStruct((n * x.shape[0], x.shape[1]), x.dtype),
            jax.ShapeDtypeStruct((n * y.shape[0], y.shape[1]), y.dtype),
        ),
        in_specs=[pl.BlockSpec(memory_space=pltpu.VMEM)] * 2,
        out_specs=(pl.BlockSpec(memory_space=pltpu.VMEM),) * 2,
        scratch_shapes=[
            pltpu.VMEM((n,) + x.shape, x.dtype),
            pltpu.VMEM((n,) + y.shape, y.dtype),
            pltpu.SemaphoreType.DMA((n,)),
            pltpu.SemaphoreType.DMA((n,)),
            pltpu.SemaphoreType.DMA((n,)),
            pltpu.SemaphoreType.DMA((n,)),
        ],
        compiler_params=pltpu.CompilerParams(collective_id=collective_id, has_side_effects=True),
    )(x, y)


def _gram_of(a):
    return lax.dot_general(
        a, a, (((1,), (1,)), ((), ())), precision=lax.Precision.HIGH,
        preferred_element_type=jnp.float32,
    )


def chol_inverse(a):
    n = a.shape[0]
    r = lax.broadcasted_iota(jnp.int32, (n, n), 0)
    c = lax.broadcasted_iota(jnp.int32, (n, n), 1)
    r1 = lax.broadcasted_iota(jnp.int32, (n, 1), 0)
    c1 = lax.broadcasted_iota(jnp.int32, (1, n), 1)
    x0 = jnp.where(r == c, 1.0, 0.0).astype(jnp.float32)
    d0 = jnp.sum(jnp.where(r == c, a, 0.0), axis=0, keepdims=True)

    def step(j, carry):
        m, x, d = carry
        pivot = jnp.sum(jnp.where(c1 == j, d, 0.0), axis=1, keepdims=True)
        inv = lax.rsqrt(pivot)
        col = jnp.sum(jnp.where(c == j, m, 0.0), axis=1, keepdims=True)
        row = jnp.sum(jnp.where(r == j, m, 0.0), axis=0, keepdims=True)
        colm = jnp.where(r1 >= j, col, 0.0)
        rowm = jnp.where(c1 >= j, row, 0.0)
        inv2 = 1.0 / pivot
        m = m - (colm * rowm) * inv2
        d = d - (rowm * rowm) * inv2
        xraw = jnp.sum(jnp.where(r == j, x, 0.0), axis=0, keepdims=True)
        x = jnp.where(r == j, xraw * inv, x)
        x = x - (jnp.where(r1 > j, col, 0.0) * xraw) * inv2
        return m, x, d

    m, x, d = lax.fori_loop(0, n, step, (a, x0, d0))
    return x


def _backward_kernel(n, m, scale, x_ref, icol_ref, o_ref, recv, gath, g3, panel, s1, r1, s2, r2, s3, r3):
    me = lax.axis_index("row")
    mc = lax.axis_index("col")
    barrier = pltpu.get_barrier_semaphore()
    for d in range(1, n):
        pl.semaphore_signal(barrier, 1, device_id=((me + d) % n, mc), device_id_type=MESH_ID)
    for d in range(1, m):
        pl.semaphore_signal(barrier, 1, device_id=(me, (mc + d) % m), device_id_type=MESH_ID)
    pl.semaphore_wait(barrier, n - 1 + m - 1)
    sends = []
    for d in range(1, n):
        peer = (me + d) % n
        c = pltpu.make_async_remote_copy(
            x_ref.at[peer], recv.at[d], s1.at[d], r1.at[d],
            device_id=(peer, mc), device_id_type=MESH_ID,
        )
        c.start()
        sends.append(c)
    acc = x_ref[me]
    for d, c in enumerate(sends, 1):
        c.wait()
        acc = acc + recv[d]
    gath[0] = acc * icol_ref[...]
    gathers = []
    for d in range(1, n):
        c = pltpu.make_async_remote_copy(
            gath.at[0], gath.at[d], s2.at[d], r2.at[d],
            device_id=((me + d) % n, mc), device_id_type=MESH_ID,
        )
        c.start()
        gathers.append(c)
    for c in gathers:
        c.wait()
    lanes = gath.shape[2]
    for p in range(n):
        panel[:, p * lanes:(p + 1) * lanes] = gath[(me - p + n) % n]
    g3[0] = _gram_of(panel[...])
    grams = []
    for d in range(1, m):
        c = pltpu.make_async_remote_copy(
            g3.at[0], g3.at[d], s3.at[d], r3.at[d],
            device_id=(me, (mc + d) % m), device_id_type=MESH_ID,
        )
        c.start()
        grams.append(c)
    for c in grams:
        c.wait()
    total = g3[mc % m]
    for q in range(1, m):
        total = total + g3[(mc - q + m) % m]
    inverse = chol_inverse(total * scale)
    rotated = lax.dot_general(
        inverse, panel[...], (((1,), (0,)), ((), ())),
        precision=lax.Precision.HIGH, preferred_element_type=jnp.float32,
    )
    for p in range(n):
        o_ref[p] = rotated[:, p * lanes:(p + 1) * lanes]


def backward_reduce(x, icol, n, m, scale, collective_id):
    chunks, vecs, lanes = x.shape
    return pl.pallas_call(
        functools.partial(_backward_kernel, n, m, scale),
        out_shape=jax.ShapeDtypeStruct(x.shape, jnp.float32),
        in_specs=[pl.BlockSpec(memory_space=pltpu.VMEM)] * 2,
        out_specs=pl.BlockSpec(memory_space=pltpu.VMEM),
        scratch_shapes=[
            pltpu.VMEM((n, vecs, lanes), jnp.float32),
            pltpu.VMEM((n, vecs, lanes), jnp.float32),
            pltpu.VMEM((m, vecs, vecs), jnp.float32),
            pltpu.VMEM((vecs, n * lanes), jnp.float32),
            pltpu.SemaphoreType.DMA((n,)),
            pltpu.SemaphoreType.DMA((n,)),
            pltpu.SemaphoreType.DMA((n,)),
            pltpu.SemaphoreType.DMA((n,)),
            pltpu.SemaphoreType.DMA((m,)),
            pltpu.SemaphoreType.DMA((m,)),
        ],
        compiler_params=pltpu.CompilerParams(collective_id=collective_id, has_side_effects=True),
    )(x, icol)


def all_reduce(x, axis, other, n, collective_id, two_phase=True):
    rows, lanes = x.shape
    ch = rows // n if two_phase else rows
    slots = ch if two_phase else rows
    return pl.pallas_call(
        functools.partial(_reduce_kernel, axis, other, n, ch, two_phase),
        out_shape=jax.ShapeDtypeStruct(x.shape, x.dtype),
        in_specs=[pl.BlockSpec(memory_space=pltpu.VMEM)],
        out_specs=pl.BlockSpec(memory_space=pltpu.VMEM),
        scratch_shapes=[
            pltpu.VMEM((n, slots, lanes), x.dtype),
            pltpu.VMEM((ch, lanes), x.dtype),
            pltpu.VMEM((n, ch, lanes), x.dtype),
            pltpu.SemaphoreType.DMA((n,)),
            pltpu.SemaphoreType.DMA((n,)),
            pltpu.SemaphoreType.DMA((n,)),
            pltpu.SemaphoreType.DMA((n,)),
        ],
        compiler_params=pltpu.CompilerParams(collective_id=collective_id, has_side_effects=True),
    )(x)


def rotate(projected, gram):
    lower = jnp.linalg.cholesky(gram)
    inverse = lax.linalg.triangular_solve(
        lower, jnp.eye(gram.shape[0], dtype=jnp.float32), left_side=True, lower=True
    )
    return jnp.einsum(
        "kl,bli->bki",
        inverse,
        projected,
        precision=lax.Precision.HIGHEST,
        preferred_element_type=jnp.float32,
    )


def rotate_pairs(projected, gram):
    lower = jnp.linalg.cholesky(gram)
    inverse = lax.linalg.triangular_solve(
        lower, jnp.eye(gram.shape[0], dtype=jnp.float32), left_side=True, lower=True
    )
    return jnp.einsum(
        "kl,plx->pkx",
        inverse,
        projected,
        precision=lax.Precision.HIGHEST,
        preferred_element_type=jnp.float32,
    )


def local_gram(projected):
    return jnp.einsum(
        "bki,bli->kl",
        projected,
        projected,
        precision=lax.Precision.HIGHEST,
        preferred_element_type=jnp.float32,
    )


def panel_sum(partial, axis, other, n, collective_id):
    blocks, vecs, bsize = partial.shape
    flat = partial.reshape(blocks * vecs * bsize // LANES, LANES)
    return all_reduce(flat, axis, other, n, collective_id).reshape(blocks, vecs, bsize)


def per_device(blocks, block_row, block_col, counts, vectors, row_mass, col_mass):
    tile = blocks[0, 0]
    n_cap = tile.shape[0]
    bsize = row_mass.shape[1]
    vecs = vectors.shape[1] // bsize
    own = vectors.shape[0]
    n_row = lax.axis_size("row")
    n_col = lax.axis_size("col")
    row_panel = own * n_col
    col_panel = own * n_row
    total_boxes = float(own * bsize * n_row * n_col)
    rows_idx = block_row[0, 0]
    cols_idx = block_col[0, 0]
    live = jnp.arange(n_cap) < counts[0, 0]
    fwd_ids = jnp.where(live, rows_idx, row_panel)
    bwd_ids = jnp.where(live, cols_idx, col_panel)
    square = tile.reshape(n_cap, bsize, bsize)
    vec_rows = own * vecs * bsize // LANES
    own_inv = 1.0 / jnp.sqrt(col_mass)
    first = (vectors.reshape(own, vecs, bsize) * own_inv[:, None, :]).astype(jnp.bfloat16)
    mass_pad = jnp.zeros((8, 128), jnp.float32).at[0, : own * bsize].set(col_mass.reshape(-1))
    got, mass_got = all_gather2(first.reshape(vec_rows, LANES), mass_pad, "row", "col", n_row, 4)
    first_panel = got.reshape(col_panel, vecs, bsize)
    col_mass_panel = mass_got.reshape(n_row, 8, 128)[:, 0, : own * bsize].reshape(col_panel, bsize)
    inv_col = 1.0 / jnp.sqrt(col_mass_panel)
    pairs = col_panel // 2
    inv_pairs = inv_col.reshape(pairs, 1, 2 * bsize)
    own_pair = jnp.broadcast_to(own_inv.reshape(1, own * bsize), (vecs, own * bsize))
    row_mass_spread = jnp.broadcast_to(row_mass[:, None, :], (own, vecs, bsize)).reshape(vec_rows, LANES)
    fwd_hot = (fwd_ids[None, :] == jnp.arange(row_panel)[:, None]).astype(jnp.bfloat16)
    bwd_hot = (bwd_ids[None, :] == jnp.arange(col_panel)[:, None]).astype(jnp.bfloat16)
    for step in range(ITERS):
        if step == 0:
            scaled = first_panel
        else:
            paired = (current * inv_pairs).astype(jnp.bfloat16)
            scaled = paired.reshape(pairs, vecs, 2, bsize).transpose(0, 2, 1, 3).reshape(col_panel, vecs, bsize)
        forward_taken = jnp.take(scaled, cols_idx, axis=0)
        forward_product = jnp.einsum(
            "bij,bkj->bki", square, forward_taken, preferred_element_type=jnp.bfloat16
        )
        forward_summed = jnp.einsum(
            "rs,ski->rki", fwd_hot, forward_product, preferred_element_type=jnp.float32
        )
        flat = forward_summed.reshape(row_panel * vecs * bsize // LANES, LANES)
        weighted = forward_reduce(flat, row_mass_spread, n_col, 1).reshape(row_panel, vecs, bsize)
        taken = jnp.take(weighted, rows_idx, axis=0)
        product = jnp.einsum("bij,bki->bkj", square, taken, preferred_element_type=jnp.bfloat16)
        summed = jnp.einsum(
            "pbs,skj->pkbj", bwd_hot.reshape(pairs, 2, n_cap), product,
            preferred_element_type=jnp.float32,
        ).reshape(pairs, vecs, 2 * bsize)
        current = backward_reduce(summed, own_pair, n_row, n_col, 1.0 / total_boxes, 2)
    me = lax.axis_index("row")
    mine = lax.dynamic_index_in_dim(current, me, 0, keepdims=False)
    return mine.reshape(vecs, own, bsize).transpose(1, 0, 2).reshape(own, vecs * bsize)


def solution(mesh):
    in_specs = (
        P("row", "col", None, None),
        P("row", "col", None),
        P("row", "col", None),
        P("row", "col"),
        P(("col", "row"), None),
        P(("row", "col"), None),
        P(("col", "row"), None),
    )
    out_specs = P(("col", "row"), None)
    return jax.shard_map(
        per_device, mesh=mesh, in_specs=in_specs, out_specs=out_specs, check_vma=False
    )
```
